32 devices in a mesh: seq: 8 (over z, x), head: 4 (over y, core).
Axes of the slice: x: 2, y: 2, z: 4, core: 2. Of those that a mesh axis runs over, the one named last changes fastest.
Arguments:
- tokens: bfloat16 [2, 8, 896, 768], P(None, None, 'seq'), may hold values from -6 to 6
- prev_logits: bfloat16 [2, 8, 896, 12, 896], P(None, None, 'seq', 'head'), may hold values from -6 to 6
- lengths: int32 [2, 8], replicated, may hold values from 128 to 896, as said below
- dealing: int32 [2, 8], replicated, may hold values from 0 to 7, each once within a row
- w_query: bfloat16 [768, 768], P('seq', 'head'), may hold values from -0.21875 to 0.21875
- b_query: bfloat16 [12, 64], P('head', 'seq'), may hold values from -3 to 3
- w_key: bfloat16 [768, 768], P('seq', 'head'), may hold values from -0.21875 to 0.21875
- w_value: bfloat16 [768, 768], P('seq', 'head'), may hold values from -0.21875 to 0.21875
- b_value: bfloat16 [12, 64], P('head', 'seq'), may hold values from -1.75 to 1.75
- w_out: bfloat16 [768, 768], P('head', 'seq'), may hold values from -1.75 to 1.75
- b_out: bfloat16 [768], P('seq'), may hold values from -3 to 3
- gain_one: bfloat16 [768], P('seq'), may hold values from 0.5 to 1.5
- shift_one: bfloat16 [768], P('seq'), may hold values from -3 to 3
- w_up: bfloat16 [768, 3072], P('seq', 'head'), may hold values from -0.21875 to 0.21875
- b_up: bfloat16 [12, 256], P('head', 'seq'), may hold values from -3 to 3
- w_down: bfloat16 [3072, 768], P('head', 'seq'), may hold values from -0.109375 to 0.109375
- b_down: bfloat16 [768], P('seq'), may hold values from -3 to 3
- gain_two: bfloat16 [768], P('seq'), may hold values from 0.5 to 1.5
- shift_two: bfloat16 [768], P('seq'), may hold values from -3 to 3
- cot_tokens: bfloat16 [2, 8, 896, 768], P(None, None, 'seq'), may hold values from -6 to 6
- cot_logits: bfloat16 [2, 8, 896, 12, 896], P(None, 'seq', None, 'head'), may hold values from -1.75 to 1.75
Outputs:
- out_tokens: bfloat16 [2, 8, 896, 768], P(None, None, 'seq')
- out_logits: bfloat16 [2, 8, 896, 12, 896], P(None, 'seq', None, 'head')
- grad_tokens: bfloat16 [2, 8, 896, 768], P(None, None, 'seq', 'head')
- grad_logits: bfloat16 [2, 8, 896, 12, 896], P(None, None, 'seq', 'head')
- grad_w_query: float32 [768, 768], P('seq', 'head')
- grad_b_query: float32 [12, 64], P('head', 'seq')
- grad_w_key: float32 [768, 768], P('seq', 'head')
- grad_w_value: float32 [768, 768], P('seq', 'head')
- grad_b_value: float32 [12, 64], P('head', 'seq')
- grad_w_out: float32 [768, 768], P('head', 'seq')
- grad_b_out: float32 [768], P('seq')
- grad_gain_one: float32 [768], P('seq')
- grad_shift_one: float32 [768], P('seq')
- grad_w_up: float32 [768, 3072], P('seq', 'head')
- grad_b_up: float32 [12, 256], P('head', 'seq')
- grad_w_down: float32 [3072, 768], P('head', 'seq')
- grad_b_down: float32 [768], P('seq')
- grad_gain_two: float32 [768], P('seq')
- grad_shift_two: float32 [768], P('seq')
The draws below stay inside these ranges and needn't reach their ends.
Inputs may be any that keep to these rules, and one draw needn't show every extreme that they name: `lengths`: in every micro-batch some sequence has exactly 896 tokens. `dealing`: each row names every slot 0 to 7 once.
All inputs are finite; a program needn't handle non-finite values.
Results may differ from the reference program's by a relative error of at most 0.014.
Values may be sent and summed in bfloat16 or wider, within the bound.
A program may use at most 256 MiB of HBM per device.

```python
import jax
import jax.numpy as jnp
from jax import lax

D = 768
HEADS = 12
HEAD_DIM = 64
FF = 3072
MAXLEN = 896
MINLEN = 128
MICRO = 2
SEQS = 8


def draw_lengths(key, part):
    draw_key = jax.random.fold_in(key, 11)
    pick_key = jax.random.fold_in(key, 23)
    lengths_drawn = jax.random.randint(draw_key, (MICRO, SEQS), MINLEN, MAXLEN + 1)
    longest = jax.random.randint(pick_key, (MICRO, 1), 0, SEQS)
    column = jnp.arange(SEQS)[None, :]
    return jnp.where(column == longest, MAXLEN, lengths_drawn).astype(jnp.int32)


def levels(stream_key, shape, pieces, least, top_value):
    factor_of = 1.0
    for axis_at, shards_of in pieces:
        draws = jax.random.uniform(jax.random.fold_in(jax.random.fold_in(stream_key, 6), axis_at), (shards_of,), jnp.float32, least / len(pieces), top_value / len(pieces))
        factor_of = factor_of * jnp.repeat(jnp.exp(draws), shape[axis_at] // shards_of).reshape((-1,) + (1,) * (len(shape) - 1 - axis_at))
    return factor_of


def scatter_about(own_key, shape, deviation, reach, shards=(), kind=jnp.bfloat16):
    values = deviation * jax.random.normal(own_key, shape, jnp.float32)
    if shards:
        values = values * levels(own_key, shape, shards, -0.22, 0.18)
    return jnp.clip(values, -reach, reach).astype(kind)


def setup_inputs(seed: int = 0) -> dict:
    splits = jax.random.split(jax.random.key(seed), 22)
    tokens = scatter_about(splits[0], (MICRO, SEQS, MAXLEN, D), 1.0, 6.0, ((2, 8),))
    prev_logits = scatter_about(splits[1], (MICRO, SEQS, MAXLEN, HEADS, MAXLEN), 1.0, 6.0, ((2, 8), (3, 4)))
    lengths = draw_lengths(jax.random.fold_in(splits[21], 71), 0)
    dealing = jax.vmap(lambda own: jax.random.permutation(own, SEQS))(jax.random.split(splits[3], MICRO)).reshape((MICRO, SEQS)).astype(jnp.int32)
    w_query = scatter_about(splits[4], (D, D), D ** -0.5, 0.21875, ((0, 8), (1, 4)))
    b_query = scatter_about(splits[5], (HEADS, HEAD_DIM), 0.5, 3.0, ((0, 4), (1, 8)))
    w_key = scatter_about(splits[6], (D, D), D ** -0.5, 0.21875, ((0, 8), (1, 4)))
    w_value = scatter_about(splits[7], (D, D), D ** -0.5, 0.21875, ((0, 8), (1, 4)))
    b_value = scatter_about(splits[8], (HEADS, HEAD_DIM), 0.3, 1.75, ((0, 4), (1, 8)))
    w_out = scatter_about(splits[9], (D, D), (max(1, D * 16 // MAXLEN)) ** -0.5, 1.75, ((0, 4), (1, 8)))
    b_out = scatter_about(splits[10], (D,), 0.5, 3.0, ((0, 8),))
    gain_one = jnp.clip(1.0 + 0.1 * jax.random.normal(splits[11], (D,), jnp.float32), 0.5, 1.5).astype(jnp.bfloat16)
    shift_one = scatter_about(splits[12], (D,), 0.5, 3.0, ((0, 8),))
    w_up = scatter_about(splits[13], (D, FF), D ** -0.5, 0.21875, ((0, 8), (1, 4)))
    b_up = scatter_about(splits[14], (HEADS, FF // HEADS), 0.5, 3.0, ((0, 4), (1, 8)))
    w_down = scatter_about(splits[15], (FF, D), FF ** -0.5, 0.109375, ((0, 4), (1, 8)))
    b_down = scatter_about(splits[16], (D,), 0.5, 3.0, ((0, 8),))
    gain_two = jnp.clip(1.0 + 0.1 * jax.random.normal(splits[17], (D,), jnp.float32), 0.5, 1.5).astype(jnp.bfloat16)
    shift_two = scatter_about(splits[18], (D,), 0.5, 3.0, ((0, 8),))
    cot_tokens = scatter_about(splits[19], (MICRO, SEQS, MAXLEN, D), 1.0, 6.0, ((2, 8),))
    cot_logits = scatter_about(splits[20], (MICRO, SEQS, MAXLEN, HEADS, MAXLEN), 0.3, 1.75, ((1, 8), (3, 4)))
    return dict(tokens=tokens, prev_logits=prev_logits, lengths=lengths, dealing=dealing, w_query=w_query, b_query=b_query, w_key=w_key, w_value=w_value, b_value=b_value, w_out=w_out, b_out=b_out, gain_one=gain_one, shift_one=shift_one, w_up=w_up, b_up=b_up, w_down=w_down, b_down=b_down, gain_two=gain_two, shift_two=shift_two, cot_tokens=cot_tokens, cot_logits=cot_logits)


@jax.custom_vjp
def low(v):
    return lax.optimization_barrier(v.astype(jnp.bfloat16)).astype(jnp.float32)

@jax.custom_vjp
def low_back(v):
    return v

def low_keep(v):
    return (low(v), None)

def low_pass(kept, grad):
    return (grad,)

def back_keep(v):
    return (v, None)

def back_low(kept, grad):
    return (low(grad),)
low.defvjp(low_keep, low_pass)
low_back.defvjp(back_keep, back_low)
epsilon = 1e-12

def layer_norm(values, gain, shift):
    center = values - lax.optimization_barrier(jnp.mean(values, axis=-1, keepdims=True))
    spread = lax.optimization_barrier(jnp.mean(center * center, axis=-1, keepdims=True))
    return center * lax.rsqrt(spread + epsilon) * gain + shift

def matmul(left, right):
    return jnp.dot(left, right, precision=lax.Precision.HIGHEST)

def layer(params, tokens_in, prev_in, length):
    w_query, b_query, w_key, w_value, b_value, w_out, b_out, gain_one, shift_one, w_up, b_up, w_down, b_down, gain_two, shift_two = params
    extent = tokens_in.shape[0]
    queries = low(low_back(matmul(tokens_in, w_query)) + b_query.reshape(D))
    keys_all = low(low_back(matmul(tokens_in, w_key)))
    values = low(low_back(matmul(tokens_in, w_value)) + b_value.reshape(D))
    query_heads = queries.reshape(extent, HEADS, HEAD_DIM)
    key_heads = keys_all.reshape(extent, HEADS, HEAD_DIM)
    value_heads = values.reshape(extent, HEADS, HEAD_DIM)
    raw_logits = low_back(jnp.einsum('qhd,khd->qhk', query_heads, key_heads, precision=lax.Precision.HIGHEST) * HEAD_DIM ** (-0.5) + prev_in)
    key_valid = jnp.arange(extent) < length
    masked = jnp.where(key_valid[None, None, :], raw_logits, -jnp.inf)
    attend = jax.nn.softmax(masked, axis=-1)
    context = low(low_back(jnp.einsum('qhk,khd->qhd', low(attend), value_heads, precision=lax.Precision.HIGHEST))).reshape(extent, D)
    branch = low_back(matmul(context, w_out)) + b_out
    hidden = layer_norm(tokens_in + branch, gain_one, shift_one)
    before_gelu = low_back(matmul(low(hidden), w_up)) + b_up.reshape(FF)
    active = low(jax.nn.gelu(before_gelu, approximate=False))
    output = low_back(matmul(active, w_down)) + b_down
    return (layer_norm(hidden + output, gain_two, shift_two), raw_logits)

def reference(tokens, prev_logits, lengths, dealing, w_query, b_query, w_key, w_value, b_value, w_out, b_out, gain_one, shift_one, w_up, b_up, w_down, b_down, gain_two, shift_two, cot_tokens, cot_logits):
    params = tuple((weight.astype(jnp.float32) for weight in (w_query, b_query, w_key, w_value, b_value, w_out, b_out, gain_one, shift_one, w_up, b_up, w_down, b_down, gain_two, shift_two)))
    flat_tokens = tokens.reshape(MICRO * SEQS, MAXLEN, D)
    flat_prev = prev_logits.reshape(MICRO * SEQS, MAXLEN, HEADS, MAXLEN)
    flat_cot = cot_tokens.reshape(MICRO * SEQS, MAXLEN, D)

    def step(totals, counter):
        micro_batch = counter // SEQS
        sequence = counter % SEQS
        dealt_slot = dealing[micro_batch, sequence]
        length = lengths[micro_batch, sequence]
        tokens_in = flat_tokens[counter].astype(jnp.float32)
        prev_in = flat_prev[counter].astype(jnp.float32)
        cot_out = flat_cot[counter].astype(jnp.float32)
        cot_raw = cot_logits[micro_batch, dealt_slot].astype(jnp.float32)

        def forward(params_in, tokens_arg, prev_arg):
            return layer(params_in, tokens_arg, prev_arg, length)
        (result, raw_logits), pullback = jax.vjp(forward, params, tokens_in, prev_in)
        grad_params, grad_in, grad_prev = pullback((cot_out, cot_raw))
        totals = jax.tree.map(lambda total, extra: total + extra, totals, grad_params)
        return (totals, (result.astype(jnp.bfloat16), raw_logits.astype(jnp.bfloat16), grad_in.astype(jnp.bfloat16), grad_prev.astype(jnp.bfloat16)))
    zero_grads = tuple((jnp.zeros(weight.shape, jnp.float32) for weight in params))
    totals, (results, raws, grads_in, grads_prev) = lax.scan(step, zero_grads, jnp.arange(MICRO * SEQS, dtype=jnp.int32))
    out_tokens = results.reshape(MICRO, SEQS, MAXLEN, D)
    raws = raws.reshape(MICRO, SEQS, MAXLEN, HEADS, MAXLEN)
    micro_rows = jnp.arange(MICRO, dtype=jnp.int32)[:, None]
    out_logits = jnp.zeros_like(raws).at[micro_rows, dealing].set(raws)
    grad_tokens = grads_in.reshape(MICRO, SEQS, MAXLEN, D)
    grad_logits = grads_prev.reshape(MICRO, SEQS, MAXLEN, HEADS, MAXLEN)
    return (out_tokens, out_logits, grad_tokens, grad_logits, totals[0], totals[1], totals[2], totals[3], totals[4], totals[5], totals[6], totals[7], totals[8], totals[9], totals[10], totals[11], totals[12], totals[13], totals[14])
```

```python
import functools

import jax
import jax.numpy as jnp
from jax import lax
from jax.experimental import pallas as pl
from jax.experimental.pallas import tpu as pltpu
from jax.sharding import PartitionSpec as P

HEAD_DIM = 64
BF16, F32 = jnp.bfloat16, jnp.float32
VMEM_LIMIT = 60 * 1024 * 1024


epsilon = 1e-12


def cut_along(x, dim, peers):
    before, after = (x.shape[:dim], x.shape[dim + 1 :])
    return jnp.moveaxis(x.reshape(*before, peers, -1, *after), dim, 0)


def sum_at_owner(x, axis, dim):
    blocks = cut_along(x, dim, lax.axis_size(axis))
    arrived = lax.all_to_all(blocks, axis, split_axis=0, concat_axis=0, tiled=True)
    return arrived.astype(jnp.float32).sum(axis=0)


def side_by_side(arrays, axis, dim, along):
    both = jnp.concatenate(arrays, axis=along)
    result, at, finished = (sum_at_owner(both, axis, dim), 0, [])
    for a in arrays:
        finished.append(lax.slice_in_dim(result, at, at + a.shape[along], axis=along))
        at += a.shape[along]
    return tuple(finished)


def side_by_side_2(arrays, axis, dim, along):
    columns = [a.reshape(*a.shape[:along], -1) for a in arrays]
    both = jnp.concatenate(columns, axis=along)
    result, at, finished = (sum_at_owner(both, axis, dim), 0, [])
    for a, column in zip(arrays, columns):
        slab = result[..., at : at + column.shape[along]]
        finished.append(slab.reshape(*slab.shape[:along], *a.shape[along:]))
        at += column.shape[along]
    return tuple(finished)


def layer_norm(values, gain, shift):
    center = values - jnp.mean(values, axis=-1, keepdims=True)
    spread = jnp.mean(center * center, axis=-1, keepdims=True)
    return center * lax.rsqrt(spread + epsilon) * gain + shift


def exact_gelu(values):
    return jax.nn.gelu(values, approximate=False)


def mask_scores(raw_scores, length):
    key_valid = jnp.arange(raw_scores.shape[2]) < length
    return jnp.where(key_valid[None, None, :], raw_scores, -jnp.inf)


def on_device_general(
    tokens,
    prev_logits,
    lengths,
    dealing,
    w_query,
    b_query,
    w_key,
    w_value,
    b_value,
    w_out,
    b_out,
    gain_one,
    shift_one,
    w_up,
    b_up,
    w_down,
    b_down,
    gain_two,
    shift_two,
    cot_tokens,
    cot_logits,
):
    micro_count = tokens.shape[0]
    seq_count = tokens.shape[1]
    piece_rows = tokens.shape[2]
    model_width = tokens.shape[3]
    extent = piece_rows * seq_count
    heads_here = prev_logits.shape[3]
    width_here = model_width // lax.axis_size("head")
    score_scale = HEAD_DIM ** (-0.5)
    owner_slot = lax.axis_index("seq")
    head_slot = lax.axis_index("head")
    zero_shift = jnp.zeros((model_width,), jnp.float32)
    out_token_list = []
    out_logit_list = []
    grad_token_list = []
    grad_logit_list = []
    grad_totals = None
    for micro_batch in range(micro_count):
        full_weights = (
            lax.all_gather(w_query, "seq", axis=0, tiled=True),
            lax.all_gather(w_key, "seq", axis=0, tiled=True),
            lax.all_gather(w_value, "seq", axis=0, tiled=True),
            lax.all_gather(w_out, "seq", axis=1, tiled=True),
            lax.all_gather(w_up, "seq", axis=0, tiled=True),
            lax.all_gather(w_down, "seq", axis=1, tiled=True),
            lax.all_gather(b_query, "seq", axis=1, tiled=True),
            lax.all_gather(b_value, "seq", axis=1, tiled=True),
            lax.all_gather(b_out, "seq", axis=0, tiled=True),
            lax.all_gather(gain_one, "seq", axis=0, tiled=True),
            lax.all_gather(shift_one, "seq", axis=0, tiled=True),
            lax.all_gather(b_up, "seq", axis=1, tiled=True),
            lax.all_gather(b_down, "seq", axis=0, tiled=True),
            lax.all_gather(gain_two, "seq", axis=0, tiled=True),
            lax.all_gather(shift_two, "seq", axis=0, tiled=True),
        )
        (
            query_full,
            key_full,
            value_full,
            out_full,
            up_full,
            down_full,
            bias_query,
            bias_value,
            bias_out,
            gain_first,
            shift_first,
            bias_up,
            bias_down,
            gain_second,
            shift_second,
        ) = full_weights
        inverse = (
            jnp.zeros((seq_count,), jnp.int32)
            .at[dealing[micro_batch]]
            .set(jnp.arange(seq_count, dtype=jnp.int32))
        )
        own_sequence = inverse[owner_slot]
        own_length = lengths[micro_batch, own_sequence]
        send_tokens = jnp.take(tokens[micro_batch], inverse, axis=0)
        send_prev = jnp.take(prev_logits[micro_batch], inverse, axis=0).reshape(
            seq_count, piece_rows, heads_here * extent
        )
        send_cot = jnp.take(cot_tokens[micro_batch], inverse, axis=0)
        got_tokens, got_prev, got_cot = (
            lax.all_to_all(send_tokens, "seq", split_axis=0, concat_axis=1, tiled=True),
            lax.all_to_all(send_prev, "seq", split_axis=0, concat_axis=1, tiled=True),
            lax.all_to_all(send_cot, "seq", split_axis=0, concat_axis=1, tiled=True),
        )
        rows_in = got_tokens.reshape(extent, model_width)
        prev_rows = got_prev.reshape(extent, heads_here, extent).astype(jnp.float32)
        cot_rows = got_cot.reshape(extent, model_width).astype(jnp.float32)
        query_pre = jnp.dot(rows_in, query_full, preferred_element_type=jnp.float32)
        queries = (query_pre + bias_query.reshape(-1).astype(jnp.float32)).astype(jnp.bfloat16)
        keys_all = jnp.dot(rows_in, key_full, preferred_element_type=jnp.float32).astype(
            jnp.bfloat16
        )
        value_pre = jnp.dot(rows_in, value_full, preferred_element_type=jnp.float32)
        values = (value_pre + bias_value.reshape(-1).astype(jnp.float32)).astype(jnp.bfloat16)
        query_heads = queries.reshape(extent, heads_here, HEAD_DIM)
        key_heads = keys_all.reshape(extent, heads_here, HEAD_DIM)
        value_heads = values.reshape(extent, heads_here, HEAD_DIM)
        raw_scores = (
            jnp.einsum("qhd,khd->qhk", query_heads, key_heads, preferred_element_type=jnp.float32)
            * score_scale
            + prev_rows
        )
        masked = mask_scores(raw_scores, own_length)
        row_top = jnp.max(masked, axis=-1, keepdims=True)
        shifted_exp = jnp.exp(masked - row_top)
        row_total = jnp.sum(shifted_exp, axis=-1, keepdims=True)
        attend = shifted_exp / row_total
        log_total = row_top + jnp.log(row_total)
        out_logit_list.append(raw_scores.astype(jnp.bfloat16)[None])
        context = (
            jnp.einsum(
                "qhk,khd->qhd",
                attend.astype(jnp.bfloat16),
                value_heads,
                preferred_element_type=jnp.float32,
            )
            .astype(jnp.bfloat16)
            .reshape(extent, heads_here * HEAD_DIM)
        )
        out_part = jnp.dot(context, out_full, preferred_element_type=jnp.float32)
        branch = lax.psum(out_part, "head") + bias_out.astype(jnp.float32)
        resid_one = rows_in.astype(jnp.float32) + branch
        hidden = layer_norm(
            resid_one, gain_first.astype(jnp.float32), shift_first.astype(jnp.float32)
        )
        hidden_low = hidden.astype(jnp.bfloat16)
        before_gelu = jnp.dot(
            hidden_low, up_full, preferred_element_type=jnp.float32
        ) + bias_up.reshape(-1).astype(jnp.float32)
        active = exact_gelu(before_gelu).astype(jnp.bfloat16)
        down_part = jnp.dot(active, down_full, preferred_element_type=jnp.float32)
        resid_two = hidden + (
            lax.psum(down_part.astype(jnp.bfloat16), "head").astype(jnp.float32)
            + bias_down.astype(jnp.float32)
        )
        result = layer_norm(
            resid_two, gain_second.astype(jnp.float32), shift_second.astype(jnp.float32)
        )
        out_rows = result.astype(jnp.bfloat16)
        (
            back_query,
            back_key,
            back_value,
            back_out,
            back_up,
            back_down,
            back_gain_first,
            back_gain_second,
        ) = (
            lax.all_gather(w_query, "seq", axis=0, tiled=True),
            lax.all_gather(w_key, "seq", axis=0, tiled=True),
            lax.all_gather(w_value, "seq", axis=0, tiled=True),
            lax.all_gather(w_out, "seq", axis=1, tiled=True),
            lax.all_gather(w_up, "seq", axis=0, tiled=True),
            lax.all_gather(w_down, "seq", axis=1, tiled=True),
            lax.all_gather(gain_one, "seq", axis=0, tiled=True),
            lax.all_gather(gain_two, "seq", axis=0, tiled=True),
        )
        norm_two_value, norm_two_back = jax.vjp(
            layer_norm, resid_two, back_gain_second.astype(jnp.float32), zero_shift
        )
        d_resid_two, d_gain_two, d_shift_two = norm_two_back(cot_rows)
        d_b_down = jnp.sum(d_resid_two, axis=0)
        grad_two_low = d_resid_two.astype(jnp.bfloat16)
        d_w_down = jnp.einsum("rf,rd->fd", active, grad_two_low, preferred_element_type=jnp.float32)
        d_active = jnp.einsum(
            "rd,fd->rf", grad_two_low, back_down, preferred_element_type=jnp.float32
        )
        gelu_value, gelu_back = jax.vjp(exact_gelu, before_gelu)
        d_before = gelu_back(d_active)[0]
        d_b_up = jnp.sum(d_before, axis=0).reshape(heads_here, -1)
        before_low = d_before.astype(jnp.bfloat16)
        d_w_up = jnp.einsum("rd,rf->df", hidden_low, before_low, preferred_element_type=jnp.float32)
        up_part = jnp.einsum("rf,df->rd", before_low, back_up, preferred_element_type=jnp.float32)
        d_hidden = d_resid_two + lax.psum(up_part.astype(jnp.bfloat16), "head").astype(jnp.float32)
        norm_one_value, norm_one_back = jax.vjp(
            layer_norm, resid_one, back_gain_first.astype(jnp.float32), zero_shift
        )
        d_resid_one, d_gain_one, d_shift_one = norm_one_back(d_hidden)
        d_b_out = jnp.sum(d_resid_one, axis=0)
        grad_one_low = d_resid_one.astype(jnp.bfloat16)
        d_w_out = jnp.einsum("rc,rd->cd", context, grad_one_low, preferred_element_type=jnp.float32)
        d_context = (
            jnp.einsum("rd,cd->rc", grad_one_low, back_out, preferred_element_type=jnp.float32)
            .astype(jnp.bfloat16)
            .reshape(extent, heads_here, HEAD_DIM)
        )
        raw_again = (
            jnp.einsum("qhd,khd->qhk", query_heads, key_heads, preferred_element_type=jnp.float32)
            * score_scale
            + prev_rows
        )
        attend_again = jnp.exp(mask_scores(raw_again, own_length) - log_total)
        d_attend = jnp.einsum(
            "qhd,khd->qhk", d_context, value_heads, preferred_element_type=jnp.float32
        )
        d_values = jnp.einsum(
            "qhk,qhd->khd",
            attend_again.astype(jnp.bfloat16),
            d_context,
            preferred_element_type=jnp.float32,
        )
        d_scores = attend_again * (
            d_attend - jnp.sum(attend_again * d_attend, axis=-1, keepdims=True)
        ) + cot_logits[micro_batch, 0].astype(jnp.float32)
        scores_low = d_scores.astype(jnp.bfloat16)
        d_queries = (
            jnp.einsum("qhk,khd->qhd", scores_low, key_heads, preferred_element_type=jnp.float32)
            * score_scale
        )
        d_keys = (
            jnp.einsum("qhk,qhd->khd", scores_low, query_heads, preferred_element_type=jnp.float32)
            * score_scale
        )
        d_b_query = jnp.sum(d_queries, axis=0)
        d_b_value = jnp.sum(d_values, axis=0)
        queries_low = d_queries.astype(jnp.bfloat16).reshape(extent, heads_here * HEAD_DIM)
        keys_low = d_keys.astype(jnp.bfloat16).reshape(extent, heads_here * HEAD_DIM)
        values_low = d_values.astype(jnp.bfloat16).reshape(extent, heads_here * HEAD_DIM)
        d_w_query = jnp.einsum(
            "rd,rc->dc", rows_in, queries_low, preferred_element_type=jnp.float32
        )
        d_w_key = jnp.einsum("rd,rc->dc", rows_in, keys_low, preferred_element_type=jnp.float32)
        d_w_value = jnp.einsum("rd,rc->dc", rows_in, values_low, preferred_element_type=jnp.float32)
        input_part = jnp.einsum(
            "rc,dc->rd", queries_low, back_query, preferred_element_type=jnp.float32
        )
        input_part = input_part + jnp.einsum(
            "rc,dc->rd", keys_low, back_key, preferred_element_type=jnp.float32
        )
        input_part = input_part + jnp.einsum(
            "rc,dc->rd", values_low, back_value, preferred_element_type=jnp.float32
        )
        input_share = lax.psum_scatter(
            input_part.astype(jnp.bfloat16), "head", scatter_dimension=1, tiled=True
        ).astype(jnp.float32)
        resid_share = lax.dynamic_slice_in_dim(d_resid_one, head_slot * width_here, width_here, 1)
        grad_rows = (resid_share + input_share).astype(jnp.bfloat16)
        back_tokens, back_grads, back_logits = (
            lax.all_to_all(
                out_rows.reshape(seq_count, piece_rows, model_width),
                "seq",
                split_axis=0,
                concat_axis=0,
                tiled=True,
            ),
            lax.all_to_all(
                grad_rows.reshape(seq_count, piece_rows, width_here),
                "seq",
                split_axis=0,
                concat_axis=0,
                tiled=True,
            ),
            lax.all_to_all(
                scores_low.reshape(seq_count, piece_rows, heads_here * extent),
                "seq",
                split_axis=0,
                concat_axis=0,
                tiled=True,
            ),
        )
        out_token_list.append(jnp.take(back_tokens, dealing[micro_batch], axis=0))
        grad_token_list.append(jnp.take(back_grads, dealing[micro_batch], axis=0))
        grad_logit_list.append(
            jnp.take(back_logits, dealing[micro_batch], axis=0).reshape(
                seq_count, piece_rows, heads_here, extent
            )
        )
        local_grads = (
            d_w_query,
            d_b_query,
            d_w_key,
            d_w_value,
            d_b_value,
            d_w_out,
            d_b_out,
            d_gain_one,
            d_shift_one,
            d_w_up,
            d_b_up,
            d_w_down,
            d_b_down,
            d_gain_two,
            d_shift_two,
        )
        if grad_totals is None:
            grad_totals = local_grads
        else:
            grad_totals = tuple((total + extra for total, extra in zip(grad_totals, local_grads)))
    final_grads = (
        sum_at_owner(grad_totals[0].astype(jnp.bfloat16), "seq", 0),
        sum_at_owner(grad_totals[1].astype(jnp.bfloat16), "seq", 1),
        *side_by_side(
            (grad_totals[2].astype(jnp.bfloat16), grad_totals[3].astype(jnp.bfloat16)), "seq", 0, 1
        ),
        sum_at_owner(grad_totals[4].astype(jnp.bfloat16), "seq", 1),
        sum_at_owner(grad_totals[5].astype(jnp.bfloat16), "seq", 1),
        sum_at_owner(grad_totals[6].astype(jnp.bfloat16), "seq", 0),
        sum_at_owner(grad_totals[7].astype(jnp.bfloat16), "seq", 0),
        *side_by_side_2(
            (grad_totals[8].astype(jnp.bfloat16), grad_totals[9].astype(jnp.bfloat16)), "seq", 0, 1
        ),
        sum_at_owner(grad_totals[10].astype(jnp.bfloat16), "seq", 1),
        sum_at_owner(grad_totals[11].astype(jnp.bfloat16), "seq", 1),
        sum_at_owner(grad_totals[12].astype(jnp.bfloat16), "seq", 0),
        sum_at_owner(grad_totals[13].astype(jnp.bfloat16), "seq", 0),
        sum_at_owner(grad_totals[14].astype(jnp.bfloat16), "seq", 0),
    )
    out_tokens = jnp.stack(out_token_list, axis=0)
    out_logits = jnp.stack(out_logit_list, axis=0)
    grad_tokens = jnp.stack(grad_token_list, axis=0)
    grad_logits = jnp.stack(grad_logit_list, axis=0)
    return (
        out_tokens,
        out_logits,
        grad_tokens,
        grad_logits,
        final_grads[0],
        final_grads[1],
        final_grads[2],
        final_grads[3],
        final_grads[4],
        final_grads[5],
        final_grads[6],
        final_grads[7],
        final_grads[8],
        final_grads[9],
        final_grads[10],
        final_grads[11],
        final_grads[12],
        final_grads[13],
        final_grads[14],
    )

def cost(flops, moved):
    return pl.CostEstimate(flops=int(flops), bytes_accessed=int(moved), transcendentals=0)


def params(**more):
    return pltpu.CompilerParams(vmem_limit_bytes=VMEM_LIMIT, **more)


def dot(a, b, ca, cb):
    return lax.dot_general(a, b, (((ca,), (cb,)), ((), ())), preferred_element_type=F32)


def whole(x):
    return pl.BlockSpec(x.shape, lambda *_: (0,) * len(x.shape))


def pick_kernel(index_ref, x_ref, o_ref):
    o_ref[0] = x_ref[0, 0]


def pick_blocks(stacked, micro, index):
    _, count, heads, rows, extent = stacked.shape
    block = (heads, rows, extent)
    return pl.pallas_call(
        pick_kernel,
        out_shape=jax.ShapeDtypeStruct((count, *block), stacked.dtype),
        grid_spec=pltpu.PrefetchScalarGridSpec(
            num_scalar_prefetch=1,
            grid=(count,),
            in_specs=[pl.BlockSpec((1, 1, *block), lambda i, ix: (micro, ix[i], 0, 0, 0))],
            out_specs=pl.BlockSpec((1, *block), lambda i, ix: (i, 0, 0, 0)),
        ),
        compiler_params=params(),
        cost_estimate=cost(0, 4 * count * heads * rows * extent),
        name="pick_blocks",
    )(index, stacked)


def place_kernel(index_ref, x_ref, *rest):
    rest[-1][0, 0] = x_ref[0]


def place_blocks(blocks, micro, micros, index, into):
    count, heads, rows, extent = blocks.shape
    block = (heads, rows, extent)
    others = [] if into is None else [into]
    return pl.pallas_call(
        place_kernel,
        out_shape=jax.ShapeDtypeStruct((micros, count, *block), blocks.dtype),
        grid_spec=pltpu.PrefetchScalarGridSpec(
            num_scalar_prefetch=1,
            grid=(count,),
            in_specs=[pl.BlockSpec((1, *block), lambda i, ix: (ix[i], 0, 0, 0))]
            + [pl.BlockSpec(memory_space=pl.ANY) for _ in others],
            out_specs=pl.BlockSpec((1, 1, *block), lambda i, ix: (micro, i, 0, 0, 0)),
        ),
        input_output_aliases={2: 0} if others else {},
        compiler_params=params(),
        cost_estimate=cost(0, 4 * count * heads * rows * extent),
        name="place_blocks",
    )(index, blocks, *others)


def project_kernel(x_ref, w_ref, b_ref, o_ref):
    columns = o_ref.shape[2]
    o_ref[0] = (dot(x_ref[...], w_ref[0, :, :columns], 1, 0) + b_ref[0]).astype(BF16)


def project(x, weights, bias):
    rows, width = x.shape
    groups, _, columns = bias.shape
    return pl.pallas_call(
        project_kernel,
        out_shape=jax.ShapeDtypeStruct((groups, rows, columns), BF16),
        grid=(groups,),
        in_specs=[
            whole(x),
            pl.BlockSpec((1, width, width), lambda h: (h, 0, 0)),
            pl.BlockSpec((1, 1, columns), lambda h: (h, 0, 0)),
        ],
        out_specs=pl.BlockSpec((1, rows, columns), lambda h: (h, 0, 0)),
        compiler_params=params(),
        cost_estimate=cost(2 * groups * rows * width * columns, 2 * groups * columns * (width + rows)),
        name="project",
    )(x, weights, bias)


def head_mask(shape, head):
    lane = lax.broadcasted_iota(jnp.int32, shape, len(shape) - 1)
    return lane // HEAD_DIM == head


def gather_rows(info_ref, qkv_ref, groups, rows, width, q_scr, k_scr, v_scr):
    for g in range(groups):
        block = qkv_ref[(info_ref[1] + g) % groups, 0]
        q_scr[g * rows : (g + 1) * rows] = block[:, :width]
        k_scr[g * rows : (g + 1) * rows] = block[:, width : 2 * width]
        v_scr[g * rows : (g + 1) * rows] = block[:, 2 * width :]


def forward_kernel(heads, info_ref, qkv_ref, prev_ref, *rest):
    logit_ref, attend_ref, context_ref, q_scr, k_scr, v_scr = rest[-6:]
    step = pl.program_id(0)
    groups, _, rows, columns = qkv_ref.shape
    piece, extent = prev_ref.shape[2:]
    width = columns // 3

    @pl.when(step == 0)
    def _():
        gather_rows(info_ref, qkv_ref, groups, rows, width, q_scr, k_scr, v_scr)

    q = q_scr[pl.ds(pl.multiple_of(step * piece, 16), piece), :]
    key_valid = lax.broadcasted_iota(jnp.int32, (1, extent), 1) < info_ref[0]
    total = jnp.zeros((piece, width), F32)
    for h in range(heads):
        mine = head_mask((1, width), h)
        q_head = jnp.where(mine, q, jnp.zeros_like(q))
        raw = dot(q_head, k_scr[...], 1, 1) * HEAD_DIM ** (-0.5) + prev_ref[0, h].astype(F32)
        logit_ref[0, h] = raw.astype(BF16)
        masked = jnp.where(key_valid, raw, -jnp.inf)
        top = jnp.max(masked, axis=-1, keepdims=True)
        grown = jnp.exp(masked - top)
        attend = grown * (1.0 / jnp.sum(grown, axis=-1, keepdims=True))
        low = attend.astype(BF16)
        attend_ref[0, h] = low
        total = total + jnp.where(mine, dot(low, v_scr[...], 1, 0), 0.0)
    context_ref[0] = total.astype(BF16)


def attention_forward(info, qkv, prev, micro, micros, logits_into):
    groups, _, rows, columns = qkv.shape
    pieces, heads, piece, extent = prev.shape
    width = columns // 3
    per = rows // piece
    others = [] if logits_into is None else [logits_into]
    return pl.pallas_call(
        functools.partial(forward_kernel, heads),
        out_shape=(
            jax.ShapeDtypeStruct((micros, heads, extent, extent), BF16),
            jax.ShapeDtypeStruct(prev.shape, BF16),
            jax.ShapeDtypeStruct((groups, rows, width), BF16),
        ),
        grid_spec=pltpu.PrefetchScalarGridSpec(
            num_scalar_prefetch=1,
            grid=(pieces,),
            in_specs=[
                pl.BlockSpec((groups, 1, rows, columns), lambda j, i: (0, micro, 0, 0)),
                pl.BlockSpec((1, heads, piece, extent), lambda j, i: (j, 0, 0, 0)),
            ]
            + [pl.BlockSpec(memory_space=pl.ANY) for _ in others],
            out_specs=(
                pl.BlockSpec((1, heads, piece, extent), lambda j, i: (micro, 0, j, 0)),
                pl.BlockSpec((1, heads, piece, extent), lambda j, i: (j, 0, 0, 0)),
                pl.BlockSpec((1, piece, width), lambda j, i: ((j // per + i[1]) % groups, j % per, 0)),
            ),
            scratch_shapes=[pltpu.VMEM((extent, width), BF16)] * 3,
        ),
        input_output_aliases={3: 0} if others else {},
        compiler_params=params(),
        cost_estimate=cost(4 * heads * extent * extent * HEAD_DIM * 4, 6 * heads * extent * extent),
        name="attention_forward",
    )(info, qkv, prev, *others)


def backward_kernel(
    heads, info_ref, qkv_ref, attend_ref, context_ref, dcon_ref, cot_ref,
    send_ref, dqkv_ref, sums_ref, q_scr, k_scr, v_scr, dq_scr, dk_scr, dv_scr,
):
    step = pl.program_id(0)
    groups, _, rows, columns = qkv_ref.shape
    piece, extent = attend_ref.shape[2:]
    width = columns // 3
    scale = HEAD_DIM ** (-0.5)

    @pl.when(step == 0)
    def _():
        gather_rows(info_ref, qkv_ref, groups, rows, width, q_scr, k_scr, v_scr)
        dk_scr[...] = jnp.zeros_like(dk_scr)
        dv_scr[...] = jnp.zeros_like(dv_scr)

    here = pl.ds(pl.multiple_of(step * piece, 16), piece)
    q = q_scr[here, :]
    dcon = dcon_ref[0]
    both = dcon.astype(F32) * context_ref[0].astype(F32)
    dq = jnp.zeros((piece, width), F32)
    for h in range(heads):
        mine = head_mask((1, width), h)
        dcon_head = jnp.where(mine, dcon, jnp.zeros_like(dcon))
        q_head = jnp.where(mine, q, jnp.zeros_like(q))
        low = attend_ref[0, h]
        delta = jnp.sum(jnp.where(mine, both, 0.0), axis=-1, keepdims=True)
        dprob = dot(dcon_head, v_scr[...], 1, 1)
        dscore = low.astype(F32) * (dprob - delta) + cot_ref[0, h].astype(F32)
        dlow = dscore.astype(BF16)
        send_ref[0, h] = dlow
        dq = dq + jnp.where(mine, dot(dlow, k_scr[...], 1, 0), 0.0)
        dk_scr[...] += dot(dlow, q_head, 0, 0)
        dv_scr[...] += dot(low, dcon_head, 0, 0)
    dq_scr[here, :] = dq * scale

    @pl.when(step == pl.num_programs(0) - 1)
    def _():
        sums_ref[0:1, :] = jnp.sum(dq_scr[...], axis=0, keepdims=True)
        sums_ref[1:2, :] = jnp.sum(dv_scr[...], axis=0, keepdims=True)
        for g in range(groups):
            part = slice(g * rows, (g + 1) * rows)
            dqkv_ref[(info_ref[1] + g) % groups] = jnp.concatenate(
                [dq_scr[part], dk_scr[part] * scale, dv_scr[part]], axis=1
            ).astype(BF16)


def attention_backward(info, qkv, attend, context, dcontext, cot, micro):
    groups, _, rows, columns = qkv.shape
    pieces, heads, piece, extent = attend.shape
    width = columns // 3
    per = rows // piece
    rotated = pl.BlockSpec((1, piece, width), lambda j, i: ((j // per + i[1]) % groups, j % per, 0))
    square = pl.BlockSpec((1, heads, piece, extent), lambda j, i: (j, 0, 0, 0))
    return pl.pallas_call(
        functools.partial(backward_kernel, heads),
        out_shape=(
            jax.ShapeDtypeStruct(attend.shape, BF16),
            jax.ShapeDtypeStruct((groups, rows, columns), BF16),
            jax.ShapeDtypeStruct((2, width), F32),
        ),
        grid_spec=pltpu.PrefetchScalarGridSpec(
            num_scalar_prefetch=1,
            grid=(pieces,),
            in_specs=[
                pl.BlockSpec((groups, 1, rows, columns), lambda j, i: (0, micro, 0, 0)),
                square,
                rotated,
                rotated,
                pl.BlockSpec((1, heads, piece, extent), lambda j, i: (micro, 0, j, 0)),
            ],
            out_specs=(
                square,
                pl.BlockSpec((groups, rows, columns), lambda j, i: (0, 0, 0)),
                pl.BlockSpec((2, width), lambda j, i: (0, 0)),
            ),
            scratch_shapes=[pltpu.VMEM((extent, width), BF16)] * 3
            + [pltpu.VMEM((extent, width), F32)] * 3,
        ),
        compiler_params=params(),
        cost_estimate=cost(8 * heads * extent * extent * HEAD_DIM * 4, 6 * heads * extent * extent),
        name="attention_backward",
    )(info, qkv, attend, context, dcontext, cot)


def normal(values):
    center = values - jnp.mean(values, axis=-1, keepdims=True)
    spread = jnp.mean(center * center, axis=-1, keepdims=True)
    inverse = lax.rsqrt(spread + epsilon)
    return center * inverse, inverse


def normal_back(grad, gain, unit, inverse):
    scaled = grad * gain
    return inverse * (
        scaled
        - jnp.mean(scaled, axis=-1, keepdims=True)
        - unit * jnp.mean(scaled * unit, axis=-1, keepdims=True)
    )


def rows_kernel(
    cuts, con_ref, x_ref, cot_ref, w_ref, bup_ref, vec_ref,
    y_ref, dz_ref, dcon_ref, h1_ref, act_ref, b1_ref, b2_ref, b0_ref, sums_ref, dbup_ref,
    slope, acc, hidden, unit_scr, inv_scr,
):
    groups, rows, width = con_ref.shape
    qkv_end, out_end, up_end, down_end = cuts
    b_out, gain_one, shift_one = vec_ref[0:1, :], vec_ref[1:2, :], vec_ref[2:3, :]
    b_down, gain_two, shift_two = vec_ref[3:4, :], vec_ref[4:5, :], vec_ref[5:6, :]

    branch = b_out + x_ref[...].astype(F32)
    for h in range(groups):
        branch = branch + dot(con_ref[h], w_ref[h, :, qkv_end:out_end], 1, 1)
    unit_one, inverse_one = normal(branch)
    unit_scr[...] = unit_one
    inv_scr[...] = inverse_one
    hid = unit_one * gain_one + shift_one
    hidden[...] = hid
    h1_ref[...] = hid.astype(BF16)
    acc[...] = hid + b_down

    def up(h, carry):
        u = dot(h1_ref[...], w_ref[h, :, out_end:up_end], 1, 0) + bup_ref[h]
        half = 0.5 * (1.0 + lax.erf(u * 0.7071067811865476))
        act_ref[h] = (u * half).astype(BF16)
        slope[h] = half + u * (jnp.exp(u * u * -0.5) * 0.3989422804014327)
        acc[...] += dot(act_ref[h], w_ref[h, :, up_end:down_end], 1, 1)
        return carry

    lax.fori_loop(0, groups, up, 0)
    unit_two, inverse_two = normal(acc[...])
    y_ref[...] = (unit_two * gain_two + shift_two).astype(BF16)
    cot = cot_ref[...].astype(F32)
    sums_ref[4:5, :] = jnp.sum(cot * unit_two, axis=0, keepdims=True)
    sums_ref[5:6, :] = jnp.sum(cot, axis=0, keepdims=True)
    dz_two = normal_back(cot, gain_two, unit_two, inverse_two)
    sums_ref[3:4, :] = jnp.sum(dz_two, axis=0, keepdims=True)
    b2_ref[...] = dz_two.astype(BF16)
    acc[...] = dz_two

    def down(h, carry):
        du = dot(b2_ref[...], w_ref[h, :, up_end:down_end], 1, 0) * slope[h]
        dbup_ref[h] = jnp.sum(du, axis=0, keepdims=True)
        b1_ref[h] = du.astype(BF16)
        acc[...] += dot(b1_ref[h], w_ref[h, :, out_end:up_end], 1, 1)
        return carry

    lax.fori_loop(0, groups, down, 0)
    dh = acc[...]
    unit_one = unit_scr[...]
    sums_ref[1:2, :] = jnp.sum(dh * unit_one, axis=0, keepdims=True)
    sums_ref[2:3, :] = jnp.sum(dh, axis=0, keepdims=True)
    dz_one = normal_back(dh, gain_one, unit_one, inv_scr[...])
    sums_ref[0:1, :] = jnp.sum(dz_one, axis=0, keepdims=True)
    sums_ref[6:8, :] = jnp.zeros_like(sums_ref[6:8, :])
    dz_ref[...] = dz_one
    b0_ref[...] = dz_one.astype(BF16)
    for h in range(groups):
        dcon_ref[h] = dot(b0_ref[...], w_ref[h, :, qkv_end:out_end], 1, 0).astype(BF16)


def row_work(cuts, context, x, cot, weights, bias_up, vectors):
    groups, rows, width = context.shape
    model = x.shape[1]
    unit = bias_up.shape[2]
    shape = jax.ShapeDtypeStruct
    args = (context, x, cot, weights, bias_up, vectors)
    return pl.pallas_call(
        functools.partial(rows_kernel, cuts),
        out_shape=(
            shape((rows, model), BF16),
            shape((rows, model), F32),
            shape(context.shape, BF16),
            shape((rows, model), BF16),
            shape((groups, rows, unit), BF16),
            shape((groups, rows, unit), BF16),
            shape((rows, model), BF16),
            shape((rows, model), BF16),
            shape((8, model), F32),
            shape((groups, 1, unit), F32),
        ),
        in_specs=[pl.BlockSpec(memory_space=pltpu.VMEM)] * len(args),
        out_specs=(pl.BlockSpec(memory_space=pltpu.VMEM),) * 10,
        scratch_shapes=[
            pltpu.VMEM((groups, rows, unit), F32),
            pltpu.VMEM((rows, model), F32),
            pltpu.VMEM((rows, model), F32),
            pltpu.VMEM((rows, model), F32),
            pltpu.VMEM((rows, 1), F32),
        ],
        compiler_params=params(),
        cost_estimate=cost(8 * groups * rows * model * (unit + width), 2 * weights.size),
        name="row_work",
    )(*args)


def input_kernel(dqkv_ref, w_ref, dz_ref, o_ref):
    total = dz_ref[...]
    for h in range(dqkv_ref.shape[0]):
        total = total + dot(dqkv_ref[h], w_ref[h, :, : dqkv_ref.shape[2]], 1, 1)
    o_ref[...] = total.astype(BF16)


def input_grad(dqkv, weights, dz):
    groups, rows, columns = dqkv.shape
    model = dz.shape[1]
    return pl.pallas_call(
        input_kernel,
        out_shape=jax.ShapeDtypeStruct((rows, model), BF16),
        grid=(1,),
        in_specs=[
            whole(dqkv),
            pl.BlockSpec((groups, model, model), lambda i: (0, 0, 0)),
            whole(dz),
        ],
        out_specs=pl.BlockSpec((rows, model), lambda i: (0, 0)),
        compiler_params=params(),
        cost_estimate=cost(2 * groups * rows * columns * model, 2 * groups * columns * model),
        name="input_grad",
    )(dqkv, weights, dz)


def weight_kernel(cuts, micros, *refs):
    out_ref = refs[-1]
    qkv_end, out_end, up_end, down_end = cuts

    def product(lefts, rights):
        total = None
        for left, right in zip(lefts, rights):
            term = dot(left[...], right[0], 0, 0)
            total = term if total is None else total + term
        return total.astype(BF16)

    x, b0, h1, b2, dqkv, con, b1, act = (refs[i * micros : (i + 1) * micros] for i in range(8))
    out_ref[0, :, 0:qkv_end] = product(x, dqkv)
    out_ref[0, :, qkv_end:out_end] = product(b0, con)
    out_ref[0, :, out_end:up_end] = product(h1, b1)
    out_ref[0, :, up_end:down_end] = product(b2, act)


def weight_grads(cuts, lefts, rights):
    micros = len(lefts[0])
    groups = rights[0][0].shape[0]
    model = lefts[0][0].shape[1]
    flat_left = [a for family in lefts for a in family]
    flat_right = [a for family in rights for a in family]
    rows = flat_left[0].shape[0]
    return pl.pallas_call(
        functools.partial(weight_kernel, cuts, micros),
        out_shape=jax.ShapeDtypeStruct((groups, model, cuts[-1]), BF16),
        grid=(groups,),
        in_specs=[whole(a) for a in flat_left]
        + [pl.BlockSpec((1, *a.shape[1:]), lambda h: (h, 0, 0)) for a in flat_right],
        out_specs=pl.BlockSpec((1, model, cuts[-1]), lambda h: (h, 0, 0)),
        compiler_params=params(),
        cost_estimate=cost(2 * micros * groups * rows * model * cuts[-1], 2 * groups * model * cuts[-1]),
        name="weight_grads",
    )(*flat_left, *flat_right)


def by_step(step, groups, slots):
    pairs = []
    for home in range(slots):
        for h in range(groups):
            slot = (h - home // 2) % groups + groups * ((home + step) % 2)
            pairs.append((home * groups + h, slot * groups + h))
    return pairs


def fits(mesh):
    return dict(mesh.shape) == {"seq": 8, "head": 4}


def on_device(
    tokens,
    prev_logits,
    lengths,
    dealing,
    w_query,
    b_query,
    w_key,
    w_value,
    b_value,
    w_out,
    b_out,
    gain_one,
    shift_one,
    w_up,
    b_up,
    w_down,
    b_down,
    gain_two,
    shift_two,
    cot_tokens,
    cot_logits,
):
    slots, groups = lax.axis_size("seq"), lax.axis_size("head")
    grid = ("seq", "head")
    here, head = lax.axis_index("seq"), lax.axis_index("head")
    micros, _, piece, model = tokens.shape
    heads = prev_logits.shape[3]
    extent = piece * slots
    width = heads * HEAD_DIM
    unit = w_up.shape[1]
    per = slots // groups
    cuts = (3 * width, 3 * width + width, 3 * width + width + unit, 3 * width + width + 2 * unit)
    own_rows = model // slots

    inverse = [
        jnp.sum(
            jnp.where(
                dealing[m][None, :] == jnp.arange(slots, dtype=jnp.int32)[:, None],
                jnp.arange(slots, dtype=jnp.int32)[None, :],
                0,
            ),
            axis=1,
        ).astype(jnp.int32)
        for m in range(micros)
    ]
    info = [
        jnp.stack([lengths[m, inverse[m][here]], here % groups]).astype(jnp.int32)
        for m in range(micros)
    ]
    prev = jnp.transpose(prev_logits, (0, 1, 3, 2, 4))
    cot_square = jnp.transpose(cot_logits[:, 0], (0, 2, 1, 3))

    vector = jnp.concatenate(
        [
            b_query.reshape(-1),
            b_value.reshape(-1),
            b_out,
            gain_one,
            shift_one,
            b_up.reshape(-1),
            b_down,
            gain_two,
            shift_two,
        ]
    )
    lots = 8
    vector = jnp.pad(vector, (0, lots * own_rows - vector.shape[0])).reshape(own_rows, lots)
    packed = jnp.concatenate(
        [
            w_query,
            w_key,
            w_value,
            w_out.T,
            w_up,
            w_down.T,
            jnp.pad(vector, ((0, 0), (0, 128 - lots))),
        ],
        axis=1,
    )
    gathered = lax.all_gather(packed, grid, axis=0).reshape(slots, groups, own_rows, -1)
    vectors = gathered[..., cuts[-1] : cuts[-1] + lots].reshape(slots, groups, -1).astype(F32)
    weights = jnp.transpose(gathered, (1, 0, 2, 3)).reshape(groups, model, -1)
    q_len = heads * HEAD_DIM // slots
    offsets = [0, q_len, 2 * q_len]
    for _ in range(7):
        offsets.append(offsets[-1] + own_rows)

    def plain(i):
        return vectors[:, 0, offsets[i] : offsets[i + 1]].reshape(1, -1)

    def by_head(i):
        part = vectors[:, :, offsets[i] : offsets[i + 1]].reshape(slots, groups, heads, -1)
        return jnp.transpose(part, (1, 2, 0, 3)).reshape(groups, 1, -1)

    bias_query, bias_value, bias_up = by_head(0), by_head(1), by_head(5)
    bias_qkv = jnp.concatenate([bias_query, jnp.zeros_like(bias_query), bias_value], axis=2)
    row_vectors = jnp.concatenate(
        [plain(2), plain(3), plain(4), plain(6), plain(7), plain(8), jnp.zeros((2, model), F32)], axis=0
    )

    def slot_of(step):
        return (head - here // 2) % groups + groups * ((here + step) % 2)

    def to_slots(array):
        arrived = []
        for step in range(2):
            slot = slot_of(step)
            out = jnp.stack(
                [
                    lax.dynamic_index_in_dim(array[m], inverse[m][slot], 0, keepdims=False)
                    for m in range(micros)
                ]
            )
            arrived.append(lax.ppermute(out, grid, by_step(step, groups, slots)))
        swap = here // groups == 1
        first = jnp.where(swap, arrived[1], arrived[0])
        second = jnp.where(swap, arrived[0], arrived[1])
        return jnp.concatenate([first, second], axis=1)

    rows_in = to_slots(tokens)
    cot_rows = to_slots(cot_tokens)

    def across_heads(array):
        return lax.all_to_all(array, "head", split_axis=0, concat_axis=0, tiled=True)

    got_prev, after = [], None
    for m in range(micros):
        send = pick_blocks(prev, m, inverse[m])
        if after is not None:
            send, _ = lax.optimization_barrier((send, after))
        got = lax.all_to_all(send, "seq", split_axis=0, concat_axis=0, tiled=True)
        got_prev.append(got)
        after = got

    rows = per * piece
    qkv = project(rows_in.reshape(micros * rows, model), weights, bias_qkv)
    qkv = across_heads(qkv).reshape(groups, micros, rows, 3 * width)

    logits, grad_logits = None, None
    kept, sums_own, sums_rows, sums_up, returned = [], [], [], [], []
    for m in range(micros):
        logits, attend, context = attention_forward(info[m], qkv, got_prev[m], m, micros, logits)
        context_rows = across_heads(context)
        y, dz, dcon, h1, act, b1, b2, b0, sums, dbup = row_work(
            cuts, context_rows, rows_in[m], cot_rows[m], weights, bias_up, row_vectors
        )
        dcontext = across_heads(dcon)
        send, dqkv, own = attention_backward(
            info[m], qkv, attend, context, dcontext, cot_square, m
        )
        got = lax.all_to_all(send, "seq", split_axis=0, concat_axis=0, tiled=True)
        dqkv = across_heads(dqkv)
        dx = input_grad(dqkv, weights, dz)
        kept.append((rows_in[m], b0, h1, b2, dqkv, context_rows, b1, act))
        sums_own.append(own)
        sums_rows.append(sums)
        sums_up.append(dbup)
        returned.append((y, dx))
        grad_logits = place_blocks(got, m, micros, dealing[m], grad_logits)

    families = list(zip(*kept))
    part = weight_grads(cuts, families[:4], families[4:])
    part = lax.psum_scatter(part, "head", scatter_dimension=0, tiled=True).reshape(slots, own_rows, -1)
    part = lax.all_to_all(part, "seq", split_axis=0, concat_axis=0, tiled=True)
    part = part.astype(F32).sum(axis=0)

    own = sums_own[0]
    rows_sum = sums_rows[0]
    up_sum = sums_up[0]
    for m in range(1, micros):
        own, rows_sum, up_sum = own + sums_own[m], rows_sum + sums_rows[m], up_sum + sums_up[m]
    mine = (jnp.arange(groups) == head)[None, :, None]

    def spread_own(row):
        piece_of = jnp.transpose(row.reshape(heads, slots, -1), (1, 0, 2)).reshape(slots, 1, -1)
        return jnp.where(mine, piece_of, 0.0)

    def spread_plain(row):
        return jnp.broadcast_to(row.reshape(slots, 1, -1), (slots, groups, own_rows))

    up_part = jnp.transpose(up_sum.reshape(groups, heads, slots, -1), (2, 0, 1, 3))
    out_vectors = jnp.concatenate(
        [
            spread_own(own[0]),
            spread_own(own[1]),
            spread_plain(rows_sum[0]),
            spread_plain(rows_sum[1]),
            spread_plain(rows_sum[2]),
            up_part.reshape(slots, groups, own_rows),
            spread_plain(rows_sum[3]),
            spread_plain(rows_sum[4]),
            spread_plain(rows_sum[5]),
        ],
        axis=2,
    ).reshape(slots * groups, -1)
    out_vectors = lax.all_to_all(out_vectors, grid, split_axis=0, concat_axis=0, tiled=True).sum(axis=0)

    def vector_out(i):
        return out_vectors[offsets[i] : offsets[i + 1]]

    sent = []
    for m in range(micros):
        y, dx = returned[m]
        sent.append(jnp.stack([y.reshape(per, piece, model), dx.reshape(per, piece, model)], axis=1))
    sent = jnp.stack(sent, axis=1)
    back = []
    for step in range(2):
        block = lax.dynamic_index_in_dim(sent, (here // groups + step) % 2, 0, keepdims=False)
        pairs = [(b, a) for a, b in by_step(step, groups, slots)]
        back.append(lax.ppermute(block, grid, pairs))
    back = jnp.stack(back)
    all_y = lax.all_gather(back[:, :, 0], "head", axis=0).reshape(-1, micros, piece, model)
    dx_send = back[:, :, 1].reshape(2, micros, piece, groups, -1)
    dx_send = jnp.transpose(dx_send, (3, 0, 1, 2, 4))
    all_dx = across_heads(dx_send).reshape(-1, micros, piece, model // groups)
    out_tokens, grad_tokens = [], []
    for m in range(micros):
        slot = dealing[m]
        which = ((slot + here // 2) % groups) * 2 + (slot // groups + here) % 2
        out_tokens.append(jnp.take(all_y[:, m], which, axis=0, mode="clip"))
        grad_tokens.append(jnp.take(all_dx[:, m], which, axis=0, mode="clip"))

    def columns(start, count):
        return part[:, start : start + count]

    return (
        jnp.stack(out_tokens),
        jnp.transpose(logits, (0, 2, 1, 3))[:, None],
        jnp.stack(grad_tokens),
        jnp.transpose(grad_logits, (0, 1, 3, 2, 4)),
        columns(0, width),
        vector_out(0).reshape(heads, -1),
        columns(width, width),
        columns(2 * width, width),
        vector_out(1).reshape(heads, -1),
        columns(3 * width, width).T,
        vector_out(2),
        vector_out(3),
        vector_out(4),
        columns(cuts[1], unit),
        vector_out(5).reshape(heads, -1),
        columns(cuts[2], unit).T,
        vector_out(6),
        vector_out(7),
        vector_out(8),
    )


def solution(mesh):
    placed = (
        P(None, None, "seq", None),
        P(None, None, "seq", "head", None),
        P(),
        P(),
        P("seq", "head"),
        P("head", "seq"),
        P("seq", "head"),
        P("seq", "head"),
        P("head", "seq"),
        P("head", "seq"),
        P("seq"),
        P("seq"),
        P("seq"),
        P("seq", "head"),
        P("head", "seq"),
        P("head", "seq"),
        P("seq"),
        P("seq"),
        P("seq"),
        P(None, None, "seq", None),
        P(None, "seq", None, "head", None),
    )
    return jax.shard_map(
        on_device if fits(mesh) else on_device_general,
        mesh=mesh,
        in_specs=placed,
        out_specs=(
            P(None, None, "seq", None),
            P(None, "seq", None, "head", None),
            P(None, None, "seq", "head"),
            P(None, None, "seq", "head", None),
            P("seq", "head"),
            P("head", "seq"),
            P("seq", "head"),
            P("seq", "head"),
            P("head", "seq"),
            P("head", "seq"),
            P("seq"),
            P("seq"),
            P("seq"),
            P("seq", "head"),
            P("head", "seq"),
            P("head", "seq"),
            P("seq"),
            P("seq"),
            P("seq"),
        ),
        check_vma=False,
    )
```

```python
import functools

import jax
import jax.numpy as jnp
from jax import lax
from jax.experimental import pallas as pl
from jax.experimental.pallas import tpu as pltpu
from jax.sharding import PartitionSpec as P

HEAD_DIM = 64
BF16, F32 = jnp.bfloat16, jnp.float32
VMEM_LIMIT = 60 * 1024 * 1024


epsilon = 1e-12


def cut_along(x, dim, peers):
    before, after = (x.shape[:dim], x.shape[dim + 1 :])
    return jnp.moveaxis(x.reshape(*before, peers, -1, *after), dim, 0)


def sum_at_owner(x, axis, dim):
    blocks = cut_along(x, dim, lax.axis_size(axis))
    arrived = lax.all_to_all(blocks, axis, split_axis=0, concat_axis=0, tiled=True)
    return arrived.astype(jnp.float32).sum(axis=0)


def side_by_side(arrays, axis, dim, along):
    both = jnp.concatenate(arrays, axis=along)
    result, at, finished = (sum_at_owner(both, axis, dim), 0, [])
    for a in arrays:
        finished.append(lax.slice_in_dim(result, at, at + a.shape[along], axis=along))
        at += a.shape[along]
    return tuple(finished)


def side_by_side_2(arrays, axis, dim, along):
    columns = [a.reshape(*a.shape[:along], -1) for a in arrays]
    both = jnp.concatenate(columns, axis=along)
    result, at, finished = (sum_at_owner(both, axis, dim), 0, [])
    for a, column in zip(arrays, columns):
        slab = result[..., at : at + column.shape[along]]
        finished.append(slab.reshape(*slab.shape[:along], *a.shape[along:]))
        at += column.shape[along]
    return tuple(finished)


def layer_norm(values, gain, shift):
    center = values - jnp.mean(values, axis=-1, keepdims=True)
    spread = jnp.mean(center * center, axis=-1, keepdims=True)
    return center * lax.rsqrt(spread + epsilon) * gain + shift


def exact_gelu(values):
    return jax.nn.gelu(values, approximate=False)


def mask_scores(raw_scores, length):
    key_valid = jnp.arange(raw_scores.shape[2]) < length
    return jnp.where(key_valid[None, None, :], raw_scores, -jnp.inf)


def on_device_general(
    tokens,
    prev_logits,
    lengths,
    dealing,
    w_query,
    b_query,
    w_key,
    w_value,
    b_value,
    w_out,
    b_out,
    gain_one,
    shift_one,
    w_up,
    b_up,
    w_down,
    b_down,
    gain_two,
    shift_two,
    cot_tokens,
    cot_logits,
):
    micro_count = tokens.shape[0]
    seq_count = tokens.shape[1]
    piece_rows = tokens.shape[2]
    model_width = tokens.shape[3]
    extent = piece_rows * seq_count
    heads_here = prev_logits.shape[3]
    width_here = model_width // lax.axis_size("head")
    score_scale = HEAD_DIM ** (-0.5)
    owner_slot = lax.axis_index("seq")
    head_slot = lax.axis_index("head")
    zero_shift = jnp.zeros((model_width,), jnp.float32)
    out_token_list = []
    out_logit_list = []
    grad_token_list = []
    grad_logit_list = []
    grad_totals = None
    for micro_batch in range(micro_count):
        full_weights = (
            lax.all_gather(w_query, "seq", axis=0, tiled=True),
            lax.all_gather(w_key, "seq", axis=0, tiled=True),
            lax.all_gather(w_value, "seq", axis=0, tiled=True),
            lax.all_gather(w_out, "seq", axis=1, tiled=True),
            lax.all_gather(w_up, "seq", axis=0, tiled=True),
            lax.all_gather(w_down, "seq", axis=1, tiled=True),
            lax.all_gather(b_query, "seq", axis=1, tiled=True),
            lax.all_gather(b_value, "seq", axis=1, tiled=True),
            lax.all_gather(b_out, "seq", axis=0, tiled=True),
            lax.all_gather(gain_one, "seq", axis=0, tiled=True),
            lax.all_gather(shift_one, "seq", axis=0, tiled=True),
            lax.all_gather(b_up, "seq", axis=1, tiled=True),
            lax.all_gather(b_down, "seq", axis=0, tiled=True),
            lax.all_gather(gain_two, "seq", axis=0, tiled=True),
            lax.all_gather(shift_two, "seq", axis=0, tiled=True),
        )
        (
            query_full,
            key_full,
            value_full,
            out_full,
            up_full,
            down_full,
            bias_query,
            bias_value,
            bias_out,
            gain_first,
            shift_first,
            bias_up,
            bias_down,
            gain_second,
            shift_second,
        ) = full_weights
        inverse = (
            jnp.zeros((seq_count,), jnp.int32)
            .at[dealing[micro_batch]]
            .set(jnp.arange(seq_count, dtype=jnp.int32))
        )
        own_sequence = inverse[owner_slot]
        own_length = lengths[micro_batch, own_sequence]
        send_tokens = jnp.take(tokens[micro_batch], inverse, axis=0)
        send_prev = jnp.take(prev_logits[micro_batch], inverse, axis=0).reshape(
            seq_count, piece_rows, heads_here * extent
        )
        send_cot = jnp.take(cot_tokens[micro_batch], inverse, axis=0)
        got_tokens, got_prev, got_cot = (
            lax.all_to_all(send_tokens, "seq", split_axis=0, concat_axis=1, tiled=True),
            lax.all_to_all(send_prev, "seq", split_axis=0, concat_axis=1, tiled=True),
            lax.all_to_all(send_cot, "seq", split_axis=0, concat_axis=1, tiled=True),
        )
        rows_in = got_tokens.reshape(extent, model_width)
        prev_rows = got_prev.reshape(extent, heads_here, extent).astype(jnp.float32)
        cot_rows = got_cot.reshape(extent, model_width).astype(jnp.float32)
        query_pre = jnp.dot(rows_in, query_full, preferred_element_type=jnp.float32)
        queries = (query_pre + bias_query.reshape(-1).astype(jnp.float32)).astype(jnp.bfloat16)
        keys_all = jnp.dot(rows_in, key_full, preferred_element_type=jnp.float32).astype(
            jnp.bfloat16
        )
        value_pre = jnp.dot(rows_in, value_full, preferred_element_type=jnp.float32)
        values = (value_pre + bias_value.reshape(-1).astype(jnp.float32)).astype(jnp.bfloat16)
        query_heads = queries.reshape(extent, heads_here, HEAD_DIM)
        key_heads = keys_all.reshape(extent, heads_here, HEAD_DIM)
        value_heads = values.reshape(extent, heads_here, HEAD_DIM)
        raw_scores = (
            jnp.einsum("qhd,khd->qhk", query_heads, key_heads, preferred_element_type=jnp.float32)
            * score_scale
            + prev_rows
        )
        masked = mask_scores(raw_scores, own_length)
        row_top = jnp.max(masked, axis=-1, keepdims=True)
        shifted_exp = jnp.exp(masked - row_top)
        row_total = jnp.sum(shifted_exp, axis=-1, keepdims=True)
        attend = shifted_exp / row_total
        log_total = row_top + jnp.log(row_total)
        out_logit_list.append(raw_scores.astype(jnp.bfloat16)[None])
        context = (
            jnp.einsum(
                "qhk,khd->qhd",
                attend.astype(jnp.bfloat16),
                value_heads,
                preferred_element_type=jnp.float32,
            )
            .astype(jnp.bfloat16)
            .reshape(extent, heads_here * HEAD_DIM)
        )
        out_part = jnp.dot(context, out_full, preferred_element_type=jnp.float32)
        branch = lax.psum(out_part, "head") + bias_out.astype(jnp.float32)
        resid_one = rows_in.astype(jnp.float32) + branch
        hidden = layer_norm(
            resid_one, gain_first.astype(jnp.float32), shift_first.astype(jnp.float32)
        )
        hidden_low = hidden.astype(jnp.bfloat16)
        before_gelu = jnp.dot(
            hidden_low, up_full, preferred_element_type=jnp.float32
        ) + bias_up.reshape(-1).astype(jnp.float32)
        active = exact_gelu(before_gelu).astype(jnp.bfloat16)
        down_part = jnp.dot(active, down_full, preferred_element_type=jnp.float32)
        resid_two = hidden + (
            lax.psum(down_part.astype(jnp.bfloat16), "head").astype(jnp.float32)
            + bias_down.astype(jnp.float32)
        )
        result = layer_norm(
            resid_two, gain_second.astype(jnp.float32), shift_second.astype(jnp.float32)
        )
        out_rows = result.astype(jnp.bfloat16)
        (
            back_query,
            back_key,
            back_value,
            back_out,
            back_up,
            back_down,
            back_gain_first,
            back_gain_second,
        ) = (
            lax.all_gather(w_query, "seq", axis=0, tiled=True),
            lax.all_gather(w_key, "seq", axis=0, tiled=True),
            lax.all_gather(w_value, "seq", axis=0, tiled=True),
            lax.all_gather(w_out, "seq", axis=1, tiled=True),
            lax.all_gather(w_up, "seq", axis=0, tiled=True),
            lax.all_gather(w_down, "seq", axis=1, tiled=True),
            lax.all_gather(gain_one, "seq", axis=0, tiled=True),
            lax.all_gather(gain_two, "seq", axis=0, tiled=True),
        )
        norm_two_value, norm_two_back = jax.vjp(
            layer_norm, resid_two, back_gain_second.astype(jnp.float32), zero_shift
        )
        d_resid_two, d_gain_two, d_shift_two = norm_two_back(cot_rows)
        d_b_down = jnp.sum(d_resid_two, axis=0)
        grad_two_low = d_resid_two.astype(jnp.bfloat16)
        d_w_down = jnp.einsum("rf,rd->fd", active, grad_two_low, preferred_element_type=jnp.float32)
        d_active = jnp.einsum(
            "rd,fd->rf", grad_two_low, back_down, preferred_element_type=jnp.float32
        )
        gelu_value, gelu_back = jax.vjp(exact_gelu, before_gelu)
        d_before = gelu_back(d_active)[0]
        d_b_up = jnp.sum(d_before, axis=0).reshape(heads_here, -1)
        before_low = d_before.astype(jnp.bfloat16)
        d_w_up = jnp.einsum("rd,rf->df", hidden_low, before_low, preferred_element_type=jnp.float32)
        up_part = jnp.einsum("rf,df->rd", before_low, back_up, preferred_element_type=jnp.float32)
        d_hidden = d_resid_two + lax.psum(up_part.astype(jnp.bfloat16), "head").astype(jnp.float32)
        norm_one_value, norm_one_back = jax.vjp(
            layer_norm, resid_one, back_gain_first.astype(jnp.float32), zero_shift
        )
        d_resid_one, d_gain_one, d_shift_one = norm_one_back(d_hidden)
        d_b_out = jnp.sum(d_resid_one, axis=0)
        grad_one_low = d_resid_one.astype(jnp.bfloat16)
        d_w_out = jnp.einsum("rc,rd->cd", context, grad_one_low, preferred_element_type=jnp.float32)
        d_context = (
            jnp.einsum("rd,cd->rc", grad_one_low, back_out, preferred_element_type=jnp.float32)
            .astype(jnp.bfloat16)
            .reshape(extent, heads_here, HEAD_DIM)
        )
        raw_again = (
            jnp.einsum("qhd,khd->qhk", query_heads, key_heads, preferred_element_type=jnp.float32)
            * score_scale
            + prev_rows
        )
        attend_again = jnp.exp(mask_scores(raw_again, own_length) - log_total)
        d_attend = jnp.einsum(
            "qhd,khd->qhk", d_context, value_heads, preferred_element_type=jnp.float32
        )
        d_values = jnp.einsum(
            "qhk,qhd->khd",
            attend_again.astype(jnp.bfloat16),
            d_context,
            preferred_element_type=jnp.float32,
        )
        d_scores = attend_again * (
            d_attend - jnp.sum(attend_again * d_attend, axis=-1, keepdims=True)
        ) + cot_logits[micro_batch, 0].astype(jnp.float32)
        scores_low = d_scores.astype(jnp.bfloat16)
        d_queries = (
            jnp.einsum("qhk,khd->qhd", scores_low, key_heads, preferred_element_type=jnp.float32)
            * score_scale
        )
        d_keys = (
            jnp.einsum("qhk,qhd->khd", scores_low, query_heads, preferred_element_type=jnp.float32)
            * score_scale
        )
        d_b_query = jnp.sum(d_queries, axis=0)
        d_b_value = jnp.sum(d_values, axis=0)
        queries_low = d_queries.astype(jnp.bfloat16).reshape(extent, heads_here * HEAD_DIM)
        keys_low = d_keys.astype(jnp.bfloat16).reshape(extent, heads_here * HEAD_DIM)
        values_low = d_values.astype(jnp.bfloat16).reshape(extent, heads_here * HEAD_DIM)
        d_w_query = jnp.einsum(
            "rd,rc->dc", rows_in, queries_low, preferred_element_type=jnp.float32
        )
        d_w_key = jnp.einsum("rd,rc->dc", rows_in, keys_low, preferred_element_type=jnp.float32)
        d_w_value = jnp.einsum("rd,rc->dc", rows_in, values_low, preferred_element_type=jnp.float32)
        input_part = jnp.einsum(
            "rc,dc->rd", queries_low, back_query, preferred_element_type=jnp.float32
        )
        input_part = input_part + jnp.einsum(
            "rc,dc->rd", keys_low, back_key, preferred_element_type=jnp.float32
        )
        input_part = input_part + jnp.einsum(
            "rc,dc->rd", values_low, back_value, preferred_element_type=jnp.float32
        )
        input_share = lax.psum_scatter(
            input_part.astype(jnp.bfloat16), "head", scatter_dimension=1, tiled=True
        ).astype(jnp.float32)
        resid_share = lax.dynamic_slice_in_dim(d_resid_one, head_slot * width_here, width_here, 1)
        grad_rows = (resid_share + input_share).astype(jnp.bfloat16)
        back_tokens, back_grads, back_logits = (
            lax.all_to_all(
                out_rows.reshape(seq_count, piece_rows, model_width),
                "seq",
                split_axis=0,
                concat_axis=0,
                tiled=True,
            ),
            lax.all_to_all(
                grad_rows.reshape(seq_count, piece_rows, width_here),
                "seq",
                split_axis=0,
                concat_axis=0,
                tiled=True,
            ),
            lax.all_to_all(
                scores_low.reshape(seq_count, piece_rows, heads_here * extent),
                "seq",
                split_axis=0,
                concat_axis=0,
                tiled=True,
            ),
        )
        out_token_list.append(jnp.take(back_tokens, dealing[micro_batch], axis=0))
        grad_token_list.append(jnp.take(back_grads, dealing[micro_batch], axis=0))
        grad_logit_list.append(
            jnp.take(back_logits, dealing[micro_batch], axis=0).reshape(
                seq_count, piece_rows, heads_here, extent
            )
        )
        local_grads = (
            d_w_query,
            d_b_query,
            d_w_key,
            d_w_value,
            d_b_value,
            d_w_out,
            d_b_out,
            d_gain_one,
            d_shift_one,
            d_w_up,
            d_b_up,
            d_w_down,
            d_b_down,
            d_gain_two,
            d_shift_two,
        )
        if grad_totals is None:
            grad_totals = local_grads
        else:
            grad_totals = tuple((total + extra for total, extra in zip(grad_totals, local_grads)))
    final_grads = (
        sum_at_owner(grad_totals[0].astype(jnp.bfloat16), "seq", 0),
        sum_at_owner(grad_totals[1].astype(jnp.bfloat16), "seq", 1),
        *side_by_side(
            (grad_totals[2].astype(jnp.bfloat16), grad_totals[3].astype(jnp.bfloat16)), "seq", 0, 1
        ),
        sum_at_owner(grad_totals[4].astype(jnp.bfloat16), "seq", 1),
        sum_at_owner(grad_totals[5].astype(jnp.bfloat16), "seq", 1),
        sum_at_owner(grad_totals[6].astype(jnp.bfloat16), "seq", 0),
        sum_at_owner(grad_totals[7].astype(jnp.bfloat16), "seq", 0),
        *side_by_side_2(
            (grad_totals[8].astype(jnp.bfloat16), grad_totals[9].astype(jnp.bfloat16)), "seq", 0, 1
        ),
        sum_at_owner(grad_totals[10].astype(jnp.bfloat16), "seq", 1),
        sum_at_owner(grad_totals[11].astype(jnp.bfloat16), "seq", 1),
        sum_at_owner(grad_totals[12].astype(jnp.bfloat16), "seq", 0),
        sum_at_owner(grad_totals[13].astype(jnp.bfloat16), "seq", 0),
        sum_at_owner(grad_totals[14].astype(jnp.bfloat16), "seq", 0),
    )
    out_tokens = jnp.stack(out_token_list, axis=0)
    out_logits = jnp.stack(out_logit_list, axis=0)
    grad_tokens = jnp.stack(grad_token_list, axis=0)
    grad_logits = jnp.stack(grad_logit_list, axis=0)
    return (
        out_tokens,
        out_logits,
        grad_tokens,
        grad_logits,
        final_grads[0],
        final_grads[1],
        final_grads[2],
        final_grads[3],
        final_grads[4],
        final_grads[5],
        final_grads[6],
        final_grads[7],
        final_grads[8],
        final_grads[9],
        final_grads[10],
        final_grads[11],
        final_grads[12],
        final_grads[13],
        final_grads[14],
    )

def cost(flops, moved):
    return pl.CostEstimate(flops=int(flops) // 100, bytes_accessed=int(moved) // 100, transcendentals=0)


def params(**more):
    return pltpu.CompilerParams(vmem_limit_bytes=VMEM_LIMIT, **more)


def dot(a, b, ca, cb):
    return lax.dot_general(a, b, (((ca,), (cb,)), ((), ())), preferred_element_type=F32)


def whole(x):
    return pl.BlockSpec(x.shape, lambda *_: (0,) * len(x.shape))


def pick_kernel(index_ref, x_ref, o_ref):
    o_ref[0] = x_ref[0, 0]


def pick_blocks(stacked, micro, index):
    _, count, heads, rows, extent = stacked.shape
    block = (heads, rows, extent)
    return pl.pallas_call(
        pick_kernel,
        out_shape=jax.ShapeDtypeStruct((count, *block), stacked.dtype),
        grid_spec=pltpu.PrefetchScalarGridSpec(
            num_scalar_prefetch=1,
            grid=(count,),
            in_specs=[pl.BlockSpec((1, 1, *block), lambda i, ix: (micro, ix[i], 0, 0, 0))],
            out_specs=pl.BlockSpec((1, *block), lambda i, ix: (i, 0, 0, 0)),
        ),
        compiler_params=params(),
        cost_estimate=cost(0, 4 * count * heads * rows * extent),
        name="pick_blocks",
    )(index, stacked)


def place_kernel(index_ref, x_ref, *rest):
    rest[-1][0, 0] = x_ref[0]


def place_blocks(blocks, micro, micros, index, into):
    count, heads, rows, extent = blocks.shape
    block = (heads, rows, extent)
    others = [] if into is None else [into]
    return pl.pallas_call(
        place_kernel,
        out_shape=jax.ShapeDtypeStruct((micros, count, *block), blocks.dtype),
        grid_spec=pltpu.PrefetchScalarGridSpec(
            num_scalar_prefetch=1,
            grid=(count,),
            in_specs=[pl.BlockSpec((1, *block), lambda i, ix: (ix[i], 0, 0, 0))]
            + [pl.BlockSpec(memory_space=pl.ANY) for _ in others],
            out_specs=pl.BlockSpec((1, 1, *block), lambda i, ix: (micro, i, 0, 0, 0)),
        ),
        input_output_aliases={2: 0} if others else {},
        compiler_params=params(),
        cost_estimate=cost(0, 4 * count * heads * rows * extent),
        name="place_blocks",
    )(index, blocks, *others)


def project_kernel(x_ref, w_ref, b_ref, o_ref):
    columns = o_ref.shape[2]
    o_ref[0] = (dot(x_ref[...], w_ref[0, :, :columns], 1, 0) + b_ref[0]).astype(BF16)


def project(x, weights, bias):
    rows, width = x.shape
    groups, _, columns = bias.shape
    return pl.pallas_call(
        project_kernel,
        out_shape=jax.ShapeDtypeStruct((groups, rows, columns), BF16),
        grid=(groups,),
        in_specs=[
            whole(x),
            pl.BlockSpec((1, width, width), lambda h: (h, 0, 0)),
            pl.BlockSpec((1, 1, columns), lambda h: (h, 0, 0)),
        ],
        out_specs=pl.BlockSpec((1, rows, columns), lambda h: (h, 0, 0)),
        compiler_params=params(),
        cost_estimate=cost(2 * groups * rows * width * columns, 2 * groups * columns * (width + rows)),
        name="project",
    )(x, weights, bias)


def head_mask(shape, head):
    lane = lax.broadcasted_iota(jnp.int32, shape, len(shape) - 1)
    return lane // HEAD_DIM == head


def gather_rows(info_ref, qkv_ref, groups, rows, width, q_scr, k_scr, v_scr):
    for g in range(groups):
        block = qkv_ref[(info_ref[1] + g) % groups, 0]
        q_scr[g * rows : (g + 1) * rows] = block[:, :width]
        k_scr[g * rows : (g + 1) * rows] = block[:, width : 2 * width]
        v_scr[g * rows : (g + 1) * rows] = block[:, 2 * width :]


def forward_kernel(heads, info_ref, qkv_ref, prev_ref, *rest):
    logit_ref, attend_ref, context_ref, q_scr, k_scr, v_scr = rest[-6:]
    step = pl.program_id(0)
    groups, _, rows, columns = qkv_ref.shape
    piece, extent = prev_ref.shape[2:]
    width = columns // 3

    @pl.when(step == 0)
    def _():
        gather_rows(info_ref, qkv_ref, groups, rows, width, q_scr, k_scr, v_scr)

    q = q_scr[pl.ds(pl.multiple_of(step * piece, 16), piece), :]
    key_valid = lax.broadcasted_iota(jnp.int32, (1, extent), 1) < info_ref[0]
    total = jnp.zeros((piece, width), F32)
    for h in range(heads):
        mine = head_mask((1, width), h)
        q_head = jnp.where(mine, q, jnp.zeros_like(q))
        raw = dot(q_head, k_scr[...], 1, 1) * HEAD_DIM ** (-0.5) + prev_ref[0, h].astype(F32)
        logit_ref[0, h] = raw.astype(BF16)
        masked = jnp.where(key_valid, raw, -jnp.inf)
        top = jnp.max(masked, axis=-1, keepdims=True)
        grown = jnp.exp(masked - top)
        attend = grown * (1.0 / jnp.sum(grown, axis=-1, keepdims=True))
        low = attend.astype(BF16)
        attend_ref[0, h] = low
        total = total + jnp.where(mine, dot(low, v_scr[...], 1, 0), 0.0)
    context_ref[0] = total.astype(BF16)


def attention_forward(info, qkv, prev, micro, micros, logits_into):
    groups, _, rows, columns = qkv.shape
    pieces, heads, piece, extent = prev.shape
    width = columns // 3
    per = rows // piece
    others = [] if logits_into is None else [logits_into]
    return pl.pallas_call(
        functools.partial(forward_kernel, heads),
        out_shape=(
            jax.ShapeDtypeStruct((micros, heads, extent, extent), BF16),
            jax.ShapeDtypeStruct(prev.shape, BF16),
            jax.ShapeDtypeStruct((groups, rows, width), BF16),
        ),
        grid_spec=pltpu.PrefetchScalarGridSpec(
            num_scalar_prefetch=1,
            grid=(pieces,),
            in_specs=[
                pl.BlockSpec((groups, 1, rows, columns), lambda j, i: (0, micro, 0, 0)),
                pl.BlockSpec((1, heads, piece, extent), lambda j, i: (j, 0, 0, 0)),
            ]
            + [pl.BlockSpec(memory_space=pl.ANY) for _ in others],
            out_specs=(
                pl.BlockSpec((1, heads, piece, extent), lambda j, i: (micro, 0, j, 0)),
                pl.BlockSpec((1, heads, piece, extent), lambda j, i: (j, 0, 0, 0)),
                pl.BlockSpec((1, piece, width), lambda j, i: ((j // per + i[1]) % groups, j % per, 0)),
            ),
            scratch_shapes=[pltpu.VMEM((extent, width), BF16)] * 3,
        ),
        input_output_aliases={3: 0} if others else {},
        compiler_params=params(),
        cost_estimate=cost(4 * heads * extent * extent * HEAD_DIM * 4, 6 * heads * extent * extent),
        name="attention_forward",
    )(info, qkv, prev, *others)


def backward_kernel(
    heads, info_ref, qkv_ref, attend_ref, context_ref, dcon_ref, cot_ref,
    send_ref, dqkv_ref, sums_ref, q_scr, k_scr, v_scr, dq_scr, dk_scr, dv_scr,
):
    step = pl.program_id(0)
    groups, _, rows, columns = qkv_ref.shape
    piece, extent = attend_ref.shape[2:]
    width = columns // 3
    scale = HEAD_DIM ** (-0.5)

    @pl.when(step == 0)
    def _():
        gather_rows(info_ref, qkv_ref, groups, rows, width, q_scr, k_scr, v_scr)
        dk_scr[...] = jnp.zeros_like(dk_scr)
        dv_scr[...] = jnp.zeros_like(dv_scr)

    here = pl.ds(pl.multiple_of(step * piece, 16), piece)
    q = q_scr[here, :]
    dcon = dcon_ref[0]
    both = dcon.astype(F32) * context_ref[0].astype(F32)
    dq = jnp.zeros((piece, width), F32)
    for h in range(heads):
        mine = head_mask((1, width), h)
        dcon_head = jnp.where(mine, dcon, jnp.zeros_like(dcon))
        q_head = jnp.where(mine, q, jnp.zeros_like(q))
        low = attend_ref[0, h]
        delta = jnp.sum(jnp.where(mine, both, 0.0), axis=-1, keepdims=True)
        dprob = dot(dcon_head, v_scr[...], 1, 1)
        dscore = low.astype(F32) * (dprob - delta) + cot_ref[0, h].astype(F32)
        dlow = dscore.astype(BF16)
        send_ref[0, h] = dlow
        dq = dq + jnp.where(mine, dot(dlow, k_scr[...], 1, 0), 0.0)
        dk_scr[...] += dot(dlow, q_head, 0, 0)
        dv_scr[...] += dot(low, dcon_head, 0, 0)
    dq_scr[here, :] = dq * scale

    @pl.when(step == pl.num_programs(0) - 1)
    def _():
        sums_ref[0:1, :] = jnp.sum(dq_scr[...], axis=0, keepdims=True)
        sums_ref[1:2, :] = jnp.sum(dv_scr[...], axis=0, keepdims=True)
        for g in range(groups):
            part = slice(g * rows, (g + 1) * rows)
            dqkv_ref[(info_ref[1] + g) % groups] = jnp.concatenate(
                [dq_scr[part], dk_scr[part] * scale, dv_scr[part]], axis=1
            ).astype(BF16)


def attention_backward(info, qkv, attend, context, dcontext, cot, micro):
    groups, _, rows, columns = qkv.shape
    pieces, heads, piece, extent = attend.shape
    width = columns // 3
    per = rows // piece
    rotated = pl.BlockSpec((1, piece, width), lambda j, i: ((j // per + i[1]) % groups, j % per, 0))
    square = pl.BlockSpec((1, heads, piece, extent), lambda j, i: (j, 0, 0, 0))
    return pl.pallas_call(
        functools.partial(backward_kernel, heads),
        out_shape=(
            jax.ShapeDtypeStruct(attend.shape, BF16),
            jax.ShapeDtypeStruct((groups, rows, columns), BF16),
            jax.ShapeDtypeStruct((2, width), F32),
        ),
        grid_spec=pltpu.PrefetchScalarGridSpec(
            num_scalar_prefetch=1,
            grid=(pieces,),
            in_specs=[
                pl.BlockSpec((groups, 1, rows, columns), lambda j, i: (0, micro, 0, 0)),
                square,
                rotated,
                rotated,
                pl.BlockSpec((1, heads, piece, extent), lambda j, i: (micro, 0, j, 0)),
            ],
            out_specs=(
                square,
                pl.BlockSpec((groups, rows, columns), lambda j, i: (0, 0, 0)),
                pl.BlockSpec((2, width), lambda j, i: (0, 0)),
            ),
            scratch_shapes=[pltpu.VMEM((extent, width), BF16)] * 3
            + [pltpu.VMEM((extent, width), F32)] * 3,
        ),
        compiler_params=params(),
        cost_estimate=cost(8 * heads * extent * extent * HEAD_DIM * 4, 6 * heads * extent * extent),
        name="attention_backward",
    )(info, qkv, attend, context, dcontext, cot)


def normal(values):
    center = values - jnp.mean(values, axis=-1, keepdims=True)
    spread = jnp.mean(center * center, axis=-1, keepdims=True)
    inverse = lax.rsqrt(spread + epsilon)
    return center * inverse, inverse


def normal_back(grad, gain, unit, inverse):
    scaled = grad * gain
    return inverse * (
        scaled
        - jnp.mean(scaled, axis=-1, keepdims=True)
        - unit * jnp.mean(scaled * unit, axis=-1, keepdims=True)
    )


def rows_kernel(
    cuts, con_ref, x_ref, cot_ref, w_ref, bup_ref, vec_ref,
    y_ref, dz_ref, dcon_ref, h1_ref, act_ref, b1_ref, b2_ref, b0_ref, sums_ref, dbup_ref,
    slope, acc, hidden, unit_scr, inv_scr,
):
    groups, rows, width = con_ref.shape
    qkv_end, out_end, up_end, down_end = cuts
    b_out, gain_one, shift_one = vec_ref[0:1, :], vec_ref[1:2, :], vec_ref[2:3, :]
    b_down, gain_two, shift_two = vec_ref[3:4, :], vec_ref[4:5, :], vec_ref[5:6, :]

    branch = b_out + x_ref[...].astype(F32)
    for h in range(groups):
        branch = branch + dot(con_ref[h], w_ref[h, :, qkv_end:out_end], 1, 1)
    unit_one, inverse_one = normal(branch)
    unit_scr[...] = unit_one
    inv_scr[...] = inverse_one
    hid = unit_one * gain_one + shift_one
    hidden[...] = hid
    h1_ref[...] = hid.astype(BF16)
    acc[...] = hid + b_down

    def up(h, carry):
        u = dot(h1_ref[...], w_ref[h, :, out_end:up_end], 1, 0) + bup_ref[h]
        half = 0.5 * (1.0 + lax.erf(u * 0.7071067811865476))
        act_ref[h] = (u * half).astype(BF16)
        slope[h] = half + u * (jnp.exp(u * u * -0.5) * 0.3989422804014327)
        acc[...] += dot(act_ref[h], w_ref[h, :, up_end:down_end], 1, 1)
        return carry

    lax.fori_loop(0, groups, up, 0)
    unit_two, inverse_two = normal(acc[...])
    y_ref[...] = (unit_two * gain_two + shift_two).astype(BF16)
    cot = cot_ref[...].astype(F32)
    sums_ref[4:5, :] = jnp.sum(cot * unit_two, axis=0, keepdims=True)
    sums_ref[5:6, :] = jnp.sum(cot, axis=0, keepdims=True)
    dz_two = normal_back(cot, gain_two, unit_two, inverse_two)
    sums_ref[3:4, :] = jnp.sum(dz_two, axis=0, keepdims=True)
    b2_ref[...] = dz_two.astype(BF16)
    acc[...] = dz_two

    def down(h, carry):
        du = dot(b2_ref[...], w_ref[h, :, up_end:down_end], 1, 0) * slope[h]
        dbup_ref[h] = jnp.sum(du, axis=0, keepdims=True)
        b1_ref[h] = du.astype(BF16)
        acc[...] += dot(b1_ref[h], w_ref[h, :, out_end:up_end], 1, 1)
        return carry

    lax.fori_loop(0, groups, down, 0)
    dh = acc[...]
    unit_one = unit_scr[...]
    sums_ref[1:2, :] = jnp.sum(dh * unit_one, axis=0, keepdims=True)
    sums_ref[2:3, :] = jnp.sum(dh, axis=0, keepdims=True)
    dz_one = normal_back(dh, gain_one, unit_one, inv_scr[...])
    sums_ref[0:1, :] = jnp.sum(dz_one, axis=0, keepdims=True)
    sums_ref[6:8, :] = jnp.zeros_like(sums_ref[6:8, :])
    dz_ref[...] = dz_one
    b0_ref[...] = dz_one.astype(BF16)
    for h in range(groups):
        dcon_ref[h] = dot(b0_ref[...], w_ref[h, :, qkv_end:out_end], 1, 0).astype(BF16)


def row_work(cuts, context, x, cot, weights, bias_up, vectors):
    groups, rows, width = context.shape
    model = x.shape[1]
    unit = bias_up.shape[2]
    shape = jax.ShapeDtypeStruct
    args = (context, x, cot, weights, bias_up, vectors)
    return pl.pallas_call(
        functools.partial(rows_kernel, cuts),
        out_shape=(
            shape((rows, model), BF16),
            shape((rows, model), F32),
            shape(context.shape, BF16),
            shape((rows, model), BF16),
            shape((groups, rows, unit), BF16),
            shape((groups, rows, unit), BF16),
            shape((rows, model), BF16),
            shape((rows, model), BF16),
            shape((8, model), F32),
            shape((groups, 1, unit), F32),
        ),
        in_specs=[pl.BlockSpec(memory_space=pltpu.VMEM)] * len(args),
        out_specs=(pl.BlockSpec(memory_space=pltpu.VMEM),) * 10,
        scratch_shapes=[
            pltpu.VMEM((groups, rows, unit), F32),
            pltpu.VMEM((rows, model), F32),
            pltpu.VMEM((rows, model), F32),
            pltpu.VMEM((rows, model), F32),
            pltpu.VMEM((rows, 1), F32),
        ],
        compiler_params=params(),
        cost_estimate=cost(8 * groups * rows * model * (unit + width), 2 * weights.size),
        name="row_work",
    )(*args)


def input_kernel(dqkv_ref, w_ref, dz_ref, o_ref):
    total = dz_ref[...]
    for h in range(dqkv_ref.shape[0]):
        total = total + dot(dqkv_ref[h], w_ref[h, :, : dqkv_ref.shape[2]], 1, 1)
    share = o_ref.shape[2]
    for h in range(o_ref.shape[0]):
        o_ref[h] = total[:, h * share : (h + 1) * share].astype(BF16)


def input_grad(dqkv, weights, dz):
    groups, rows, columns = dqkv.shape
    model = dz.shape[1]
    return pl.pallas_call(
        input_kernel,
        out_shape=jax.ShapeDtypeStruct((groups, rows, model // groups), BF16),
        grid=(1,),
        in_specs=[
            whole(dqkv),
            pl.BlockSpec((groups, model, model), lambda i: (0, 0, 0)),
            whole(dz),
        ],
        out_specs=pl.BlockSpec((groups, rows, model // groups), lambda i: (0, 0, 0)),
        compiler_params=params(),
        cost_estimate=cost(2 * groups * rows * columns * model, 2 * groups * columns * model),
        name="input_grad",
    )(dqkv, weights, dz)


def weight_kernel(cuts, micros, vector_ref, *refs):
    out_ref = refs[-1]
    out_ref[0, :, cuts[-1] :] = vector_ref[0]
    qkv_end, out_end, up_end, down_end = cuts

    def product(lefts, rights):
        total = None
        for left, right in zip(lefts, rights):
            term = dot(left[...], right[0], 0, 0)
            total = term if total is None else total + term
        return total.astype(BF16)

    x, b0, h1, b2, dqkv, con, b1, act = (refs[i * micros : (i + 1) * micros] for i in range(8))
    out_ref[0, :, 0:qkv_end] = product(x, dqkv)
    out_ref[0, :, qkv_end:out_end] = product(b0, con)
    out_ref[0, :, out_end:up_end] = product(h1, b1)
    out_ref[0, :, up_end:down_end] = product(b2, act)


def weight_grads(cuts, lefts, rights, vectors):
    micros = len(lefts[0])
    groups = rights[0][0].shape[0]
    model = lefts[0][0].shape[1]
    flat_left = [a for family in lefts for a in family]
    flat_right = [a for family in rights for a in family]
    rows = flat_left[0].shape[0]
    columns = cuts[-1] + vectors.shape[2]
    return pl.pallas_call(
        functools.partial(weight_kernel, cuts, micros),
        out_shape=jax.ShapeDtypeStruct((groups, model, columns), BF16),
        grid=(groups,),
        in_specs=[pl.BlockSpec((1, *vectors.shape[1:]), lambda h: (h, 0, 0))]
        + [whole(a) for a in flat_left]
        + [pl.BlockSpec((1, *a.shape[1:]), lambda h: (h, 0, 0)) for a in flat_right],
        out_specs=pl.BlockSpec((1, model, columns), lambda h: (h, 0, 0)),
        compiler_params=params(),
        cost_estimate=cost(2 * micros * groups * rows * model * cuts[-1], 2 * groups * model * cuts[-1]),
        name="weight_grads",
    )(vectors, *flat_left, *flat_right)


MESH = pl.DeviceIdType.MESH
SIDE = 2


def remote(source, target, send_sem, recv_sem, device):
    return pltpu.make_async_remote_copy(
        src_ref=source,
        dst_ref=target,
        send_sem=send_sem,
        recv_sem=recv_sem,
        device_id=device,
        device_id_type=MESH,
    )


def signal(device):
    pl.semaphore_signal(
        pltpu.get_barrier_semaphore(), inc=1, device_id=device, device_id_type=MESH
    )


def greet(devices):
    for device in devices:
        signal(device)
    pl.semaphore_wait(pltpu.get_barrier_semaphore(), len(devices))


def cross_kernel(groups, x_ref, o_ref, send_sem, recv_sem, own_sem):
    me = lax.axis_index("head")
    peers = [lax.rem(me + i, groups) for i in range(1, groups)]
    greet([{"head": peer} for peer in peers])
    copies = []
    for i, peer in enumerate(peers):
        copy = remote(x_ref.at[peer], o_ref.at[me], send_sem.at[i], recv_sem.at[i], {"head": peer})
        copy.start()
        copies.append(copy)
    own = pltpu.make_async_copy(x_ref.at[me], o_ref.at[me], own_sem)
    own.start()
    own.wait()
    for copy in copies:
        copy.wait()


def across_heads(x, number):
    groups = x.shape[0]
    return pl.pallas_call(
        functools.partial(cross_kernel, groups),
        out_shape=jax.ShapeDtypeStruct(x.shape, x.dtype),
        in_specs=[pl.BlockSpec(memory_space=pltpu.VMEM)],
        out_specs=pl.BlockSpec(memory_space=pl.ANY),
        scratch_shapes=[
            pltpu.SemaphoreType.DMA((groups - 1,)),
            pltpu.SemaphoreType.DMA((groups - 1,)),
            pltpu.SemaphoreType.DMA,
        ],
        compiler_params=params(collective_id=number, has_side_effects=True),
        cost_estimate=cost(0, 40 * x.size),
        name="across_heads",
    )(x)


SIDES = 2
LINE = 4


class Place:
    def __init__(self):
        self.here, self.head = lax.axis_index("seq"), lax.axis_index("head")
        self.z, self.x = self.here // SIDES, lax.rem(self.here, SIDES)
        self.y, self.c = self.head // 2, lax.rem(self.head, 2)
        self.up, self.down = {"seq": self.here + SIDES}, {"seq": self.here - SIDES}
        self.across = {"seq": self.z * SIDES + (1 - self.x)}
        self.over = {"head": (1 - self.y) * 2 + self.c}
        self.beside = {"head": self.y * 2 + (1 - self.c)}
        self.not_last, self.not_first = self.z < LINE - 1, self.z > 0
        half = (LINE - 1 - self.z) // 2
        self.order = [self.z, self.z + 1 - 2 * lax.rem(self.z, 2), 1 + half, (LINE - 1) * half]

    def greet_neighbours(self):
        pl.when(self.not_last)(lambda: signal(self.up))
        pl.when(self.not_first)(lambda: signal(self.down))
        for device in (self.across, self.over, self.beside):
            signal(device)
        return 3 + self.not_last.astype(jnp.int32) + self.not_first.astype(jnp.int32)


def arrived(block, send_sem, recv_sem, device):
    remote(block, block, send_sem, recv_sem, device).wait_recv()


def gather_kernel(
    slots, groups, pack_ref, piece_ref, all_ref, rows_ref,
    z_s, z_r, x_s, x_r, y_s, y_r, c_s, c_r, piece_s, piece_r, own_sem,
):
    me = Place()
    here, head, x, y, c = me.here, me.head, me.x, me.y, me.c
    group = lax.rem(head - here + slots, groups)
    homes = [group * SIDE + p for p in range(SIDE)]
    targets = [
        lax.rem(head - me.z + groups, groups) + groups * lax.rem(here + step, 2) for step in range(2)
    ]
    expected = me.greet_neighbours()
    for home in homes:
        pl.when(home != here)(lambda home=home: signal({"seq": home}))
    for target in targets:
        expected = expected + (target != here).astype(jnp.int32)
    pl.semaphore_wait(pltpu.get_barrier_semaphore(), expected)

    def at(i, side, row, core=c):
        return all_ref.at[row * 2 + core, i * SIDES + side]

    def half(i, side, row, part):
        return all_ref.at[row * 2 + c, i * SIDES + side, part]

    def source(k):
        return pack_ref if k == 0 else at(me.order[k], x, y)

    def upward(k):
        i = me.order[k]
        return remote(source(k), at(i, x, y), z_s.at[i], z_r.at[i], me.up)

    def downward(k):
        i = me.order[k]
        return remote(source(k), at(i, x, y), z_s.at[LINE + i], z_r.at[i], me.down)

    def goes_up(k):
        return (me.order[k] <= me.z) & me.not_last

    def goes_down(k):
        return (me.order[k] >= me.z) & me.not_first

    def over_x(k, kind):
        i = me.order[k]
        n = kind * LINE + i
        if kind < 2:
            return remote(source(k).at[kind], half(i, x, y, kind), x_s.at[n], x_r.at[n], me.across)
        block = half(i, x, 1 - y, 1)
        return remote(block, block, x_s.at[n], x_r.at[n], me.across)

    def over_y(k, kind):
        i = me.order[k]
        n = kind * LINE + i
        if kind < 2:
            return remote(source(k).at[1 - kind], half(i, x, y, 1 - kind), y_s.at[n], y_r.at[n], me.over)
        block = half(i, 1 - x, y, 0)
        return remote(block, block, y_s.at[n], y_r.at[n], me.over)

    def to_core(k, kind):
        i = me.order[k]
        n = kind * LINE + i
        if kind == 0:
            return remote(source(k), at(i, x, y), c_s.at[n], c_r.at[n], me.beside)
        block = at(i, *((1 - x, y), (x, 1 - y), (1 - x, 1 - y))[kind - 1])
        return remote(block, block, c_s.at[n], c_r.at[n], me.beside)

    def second(k):
        i = me.order[k]
        arrived(half(i, 1 - x, y, 0), x_s.at[i], x_r.at[i], me.across)
        over_y(k, 2).start()
        arrived(half(i, x, 1 - y, 1), y_s.at[i], y_r.at[i], me.over)
        over_x(k, 2).start()

    def piece(step):
        return remote(
            piece_ref.at[step], rows_ref.at[:, x], piece_s.at[step], piece_r.at[x], {"seq": targets[step]}
        )

    def piece_here(step):
        return pltpu.make_async_copy(piece_ref.at[step], rows_ref.at[:, x], own_sem.at[1])

    own = pltpu.make_async_copy(pack_ref, at(me.z, x, y), own_sem.at[0])
    own.start()
    for k in range(LINE):
        i = me.order[k]
        if k:
            arrived(at(i, x, y), z_s.at[i], z_r.at[i], me.up)
        pl.when(goes_up(k))(lambda k=k: upward(k).start())
        pl.when(goes_down(k))(lambda k=k: downward(k).start())
        over_x(k, 0).start()
        over_y(k, 0).start()
        if k:
            second(k - 1)
        over_x(k, 1).start()
        over_y(k, 1).start()
        to_core(k, 0).start()
        if k == 2:
            for step, target in enumerate(targets):
                pl.when(target != here)(lambda step=step: piece(step).start())
                pl.when(target == here)(lambda step=step: piece_here(step).start())
    second(LINE - 1)
    for k in range(LINE):
        i = me.order[k]
        n = LINE + i
        arrived(half(i, 1 - x, y, 1), x_s.at[n], x_r.at[n], me.across)
        to_core(k, 1).start()
        arrived(half(i, x, 1 - y, 0), y_s.at[n], y_r.at[n], me.over)
        to_core(k, 2).start()
        n = 2 * LINE + i
        arrived(half(i, 1 - x, 1 - y, 1), x_s.at[n], x_r.at[n], me.across)
        arrived(half(i, 1 - x, 1 - y, 0), y_s.at[n], y_r.at[n], me.over)
        to_core(k, 3).start()
    for kind, (side, row) in enumerate(((x, y), (1 - x, y), (x, 1 - y), (1 - x, 1 - y))):
        for k in range(LINE):
            i = me.order[k]
            n = kind * LINE + i
            arrived(at(i, side, row, 1 - c), c_s.at[n], c_r.at[n], me.beside)
    for p, home in enumerate(homes):
        block = rows_ref.at[:, p]
        pl.when(home != here)(
            lambda block=block, p=p, home=home: arrived(
                block, piece_s.at[p], piece_r.at[p], {"seq": home}
            )
        )
    for step, target in enumerate(targets):
        pl.when(target != here)(lambda step=step: piece(step).wait_send())
        pl.when(target == here)(lambda step=step: piece_here(step).wait())
    own.wait()
    for k in range(LINE):
        pl.when(goes_up(k))(lambda k=k: upward(k).wait_send())
        pl.when(goes_down(k))(lambda k=k: downward(k).wait_send())
        for kind in range(3):
            over_x(k, kind).wait_send()
            over_y(k, kind).wait_send()
        for kind in range(4):
            to_core(k, kind).wait_send()


def gather_all(packed, pieces, slots, groups, number):
    dma = pltpu.SemaphoreType.DMA
    return pl.pallas_call(
        functools.partial(gather_kernel, slots, groups),
        out_shape=(
            jax.ShapeDtypeStruct((groups, slots, *packed.shape), packed.dtype),
            jax.ShapeDtypeStruct((pieces.shape[1], SIDE, *pieces.shape[2:]), pieces.dtype),
        ),
        in_specs=[pl.BlockSpec(memory_space=pltpu.VMEM)] * 2,
        out_specs=(pl.BlockSpec(memory_space=pl.ANY),) * 2,
        scratch_shapes=[dma((2 * LINE,)), dma((LINE,))]
        + [dma((3 * LINE,))] * 4
        + [dma((4 * LINE,))] * 2
        + [dma((2,))] * 3,
        compiler_params=params(collective_id=number, has_side_effects=True),
        cost_estimate=cost(0, 3000000 * 40),
        name="gather_all",
    )(packed, pieces)


def add_into(target, terms, shape):
    rows = shape[-2]
    tile = 16
    steps = rows // tile
    outer = 1
    for n in shape[:-2]:
        outer *= n

    def body(i, carry):
        at = pl.ds(pl.multiple_of(lax.rem(i, steps) * tile, tile), tile)
        rest = i // steps
        index = []
        for n in reversed(shape[:-2]):
            index.insert(0, lax.rem(rest, n))
            rest = rest // n
        index = (*index, at)
        total = terms[0][index].astype(F32)
        for term in terms[1:]:
            total = total + term[index].astype(F32)
        target[index] = total.astype(target.dtype)
        return carry

    lax.fori_loop(0, outer * steps, body, 0)


def finish_kernel(
    slots, groups, micros, part_ref, y_ref, dx_ref, sum_ref, tokens_ref, grads_ref,
    held, first_a, first_b, second_a, second_b, line,
    c_s, c_r, x_s, x_r, y_s, y_r, z_s, z_r, home_s, home_r, over_s, over_r, near_s, near_r, pass_s, pass_r,
    grad_s, grad_r, own_sem,
):
    me = Place()
    here, head, x, y, z, c = me.here, me.head, me.x, me.y, me.z, me.c
    order = me.order[::-1]
    group = lax.rem(head - here + slots, groups)
    homes = [group * SIDE + p for p in range(SIDE)]
    mine = lax.rem(head - z + groups, groups)
    senders = [lax.rem(slot + z, groups) for slot in range(slots)]

    def is_me(slot, other):
        return (slot == here) & (other == head)

    expected = me.greet_neighbours()
    for slot in range(slots):
        pl.when(jnp.logical_not(is_me(slot, senders[slot])))(
            lambda slot=slot: signal({"seq": slot, "head": senders[slot]})
        )
    for home in homes:
        for h in range(groups):
            expected = expected + 1 - is_me(home, h).astype(jnp.int32)
    pl.semaphore_wait(pltpu.get_barrier_semaphore(), expected)

    def to_core(k, row):
        i = order[k]
        n = row * LINE + i
        return remote(
            part_ref.at[row * 2 + (1 - c), i], held.at[i, row], c_s.at[n], c_r.at[n], me.beside
        )

    def first_y(k):
        i = order[k]
        return remote(held.at[i, 1 - y, :, 0], first_a.at[i], y_s.at[i], y_r.at[i], me.over)

    def first_x(k):
        i = order[k]
        return remote(held.at[i, :, 1 - x, 1], first_b.at[i], x_s.at[i], x_r.at[i], me.across)

    def second_x(k):
        i = order[k]
        n = LINE + i
        return remote(held.at[i, y, 1 - x, 0], second_a.at[i], x_s.at[n], x_r.at[n], me.across)

    def second_y(k):
        i = order[k]
        n = LINE + i
        return remote(held.at[i, 1 - y, x, 1], second_b.at[i], y_s.at[n], y_r.at[n], me.over)

    def upward(k):
        i = order[k]
        return remote(held.at[i, y, x], line.at[0, i], z_s.at[i], z_r.at[i], me.up)

    def downward(k):
        i = order[k]
        n = LINE + i
        return remote(held.at[i, y, x], line.at[1, i], z_s.at[n], z_r.at[n], me.down)

    rows, columns = sum_ref.shape[1:]

    def begin(k):
        i = order[k]
        for row in range(2):
            arrived(held.at[i, row], c_s.at[row * LINE + i], c_r.at[row * LINE + i], me.beside)
            add_into(
                held.at[i, row], [held.at[i, row], part_ref.at[row * 2 + c, i]], (SIDES, 2, rows, columns)
            )
        first_y(k).start()
        first_x(k).start()

    def middle(k):
        i = order[k]
        arrived(first_a.at[i], y_s.at[i], y_r.at[i], me.over)
        for side in range(SIDES):
            block = held.at[i, y, side, 0]
            add_into(block, [block, first_a.at[i, side]], (rows, columns))
        second_x(k).start()
        arrived(first_b.at[i], x_s.at[i], x_r.at[i], me.across)
        for row in range(2):
            block = held.at[i, row, x, 1]
            add_into(block, [block, first_b.at[i, row]], (rows, columns))
        second_y(k).start()

    def end(k):
        i = order[k]
        n = LINE + i
        last = k == LINE - 1
        arrived(second_a.at[i], x_s.at[n], x_r.at[n], me.across)
        arrived(second_b.at[i], y_s.at[n], y_r.at[n], me.over)
        for part, other in enumerate((second_a, second_b)):
            block = held.at[i, y, x, part]
            add_into(sum_ref.at[part] if last else block, [block, other.at[i]], (rows, columns))
        target = sum_ref if last else held.at[i, y, x]

        def below():
            arrived(line.at[0, i], z_s.at[i], z_r.at[i], me.up)
            add_into(target, [target, line.at[0, i]], (2, rows, columns))

        def above():
            arrived(line.at[1, i], z_s.at[n], z_r.at[n], me.up)
            add_into(target, [target, line.at[1, i]], (2, rows, columns))

        pl.when((i >= z) & me.not_first)(below)
        pl.when((i <= z) & me.not_last)(above)
        if not last:
            pl.when(i > z)(lambda: upward(k).start())
            pl.when(i < z)(lambda: downward(k).start())

    def home_copy(m, p):
        n = m * SIDE + p
        return remote(
            y_ref.at[m, p], tokens_ref.at[m, here], home_s.at[n], home_r.at[m * 2 + here // groups], {"seq": homes[p]}
        )

    def home_here(m, p):
        return pltpu.make_async_copy(y_ref.at[m, p], tokens_ref.at[m, here], own_sem.at[m])

    def grad_copy(m, p, h):
        n = (m * SIDE + p) * groups + h
        return remote(
            dx_ref.at[m, h, p], grads_ref.at[m, here], grad_s.at[n], grad_r.at[m * slots + here],
            {"seq": homes[p], "head": h},
        )

    def grad_here(m, p, h):
        return pltpu.make_async_copy(dx_ref.at[m, h, p], grads_ref.at[m, here], own_sem.at[micros + m])

    def slot_of(other, j):
        return lax.rem(other - z + groups, groups) + groups * j

    far_head, near_head = (1 - y) * 2 + c, y * 2 + (1 - c)
    last_head = (1 - y) * 2 + (1 - c)

    def far(m, j):
        n, block = m * 2 + j, tokens_ref.at[m, slot_of(head, j)]
        return remote(block, block, over_s.at[n], over_r.at[n], me.over)

    def near(m, j):
        n, block = m * 2 + j, tokens_ref.at[m, slot_of(head, j)]
        return remote(block, block, near_s.at[n], near_r.at[n], me.beside)

    def passed(m, j):
        n, block = m * 2 + j, tokens_ref.at[m, slot_of(far_head, j)]
        return remote(block, block, pass_s.at[n], pass_r.at[n], me.beside)

    for k in range(LINE):
        for row in range(2):
            to_core(k, row).start()
    for m in range(micros):
        for p, home in enumerate(homes):
            pl.when(home != here)(lambda m=m, p=p: home_copy(m, p).start())
            pl.when(home == here)(lambda m=m, p=p: home_here(m, p).start())
            for h in range(groups):
                same = is_me(home, h)
                pl.when(jnp.logical_not(same))(lambda m=m, p=p, h=h: grad_copy(m, p, h).start())
                pl.when(same)(lambda m=m, p=p, h=h: grad_here(m, p, h).start())
    for k in range(LINE):
        begin(k)
        if k >= 1:
            middle(k - 1)
        if k >= 2:
            end(k - 2)
    middle(LINE - 1)
    end(LINE - 2)
    for m in range(micros):
        for p, home in enumerate(homes):
            pl.when(home == here)(lambda m=m, p=p: home_here(m, p).wait())
        for j in range(2):
            slot = slot_of(head, j)
            pl.when(slot != here)(
                lambda m=m, j=j, slot=slot: arrived(
                    tokens_ref.at[m, slot], home_s.at[m * 2 + j], home_r.at[m * 2 + j], {"seq": slot}
                )
            )
            far(m, j).start()
            near(m, j).start()
    end(LINE - 1)
    for m in range(micros):
        for j in range(2):
            n = m * 2 + j
            arrived(tokens_ref.at[m, slot_of(far_head, j)], over_s.at[n], over_r.at[n], me.over)
            passed(m, j).start()
    for m in range(micros):
        for j in range(2):
            n = m * 2 + j
            arrived(tokens_ref.at[m, slot_of(near_head, j)], near_s.at[n], near_r.at[n], me.beside)
            arrived(tokens_ref.at[m, slot_of(last_head, j)], pass_s.at[n], pass_r.at[n], me.beside)
        for slot in range(slots):
            n = m * slots + slot
            pl.when(jnp.logical_not(is_me(slot, senders[slot])))(
                lambda m=m, n=n, slot=slot: arrived(
                    grads_ref.at[m, slot], grad_s.at[0], grad_r.at[n], {"seq": slot, "head": senders[slot]}
                )
            )
    for m in range(micros):
        for p, home in enumerate(homes):
            pl.when(home != here)(lambda m=m, p=p: home_copy(m, p).wait_send())
            for h in range(groups):
                same = is_me(home, h)
                pl.when(jnp.logical_not(same))(lambda m=m, p=p, h=h: grad_copy(m, p, h).wait_send())
                pl.when(same)(lambda m=m, p=p, h=h: grad_here(m, p, h).wait())
        for j in range(2):
            far(m, j).wait_send()
            near(m, j).wait_send()
            passed(m, j).wait_send()
    for k in range(LINE):
        for row in range(2):
            to_core(k, row).wait_send()
        for copy in (first_y, first_x, second_x, second_y):
            copy(k).wait_send()
        if k < LINE - 1:
            i = order[k]
            pl.when(i > z)(lambda k=k: upward(k).wait_send())
            pl.when(i < z)(lambda k=k: downward(k).wait_send())


def finish(part, y, dx, slots, groups, number):
    columns = part.shape[-1]
    micros, _, piece, model = y.shape
    rows = part.shape[-2]
    dma = pltpu.SemaphoreType.DMA
    vmem = pltpu.VMEM
    part = part.reshape(groups, LINE, SIDES, 2, rows, columns)
    return pl.pallas_call(
        functools.partial(finish_kernel, slots, groups, micros),
        out_shape=(
            jax.ShapeDtypeStruct((2, rows, columns), F32),
            jax.ShapeDtypeStruct((micros, slots, piece, model), BF16),
            jax.ShapeDtypeStruct((micros, slots, piece, dx.shape[-1]), BF16),
        ),
        in_specs=[pl.BlockSpec(memory_space=pltpu.VMEM)] * 3,
        out_specs=(pl.BlockSpec(memory_space=pltpu.VMEM),) + (pl.BlockSpec(memory_space=pl.ANY),) * 2,
        scratch_shapes=[
            vmem((LINE, 2, SIDES, 2, rows, columns), BF16),
            vmem((LINE, SIDES, rows, columns), BF16),
            vmem((LINE, 2, rows, columns), BF16),
            vmem((LINE, rows, columns), BF16),
            vmem((LINE, rows, columns), BF16),
            vmem((2, LINE, 2, rows, columns), BF16),
        ]
        + [dma((2 * LINE,))] * 8
        + [dma((2 * micros,))] * 8
        + [dma((2 * groups * micros,)), dma((slots * micros,)), dma((2 * micros,))],
        compiler_params=params(collective_id=number, has_side_effects=True),
        cost_estimate=cost(0, 3000000 * 40),
        name="finish",
    )(part, y, dx)


def order_kernel(micros, index_ref, *refs):
    inputs, outputs = refs[: 2 * micros], refs[2 * micros :]
    for n, out in enumerate(outputs):
        for m in range(micros):
            out[m, 0] = inputs[n * micros + m][0, 0]


def in_order(arrays, index):
    micros, slots = arrays[0].shape[:2]

    def source(m):
        return lambda i, ix: (m, ix[m, i], 0, 0)

    return pl.pallas_call(
        functools.partial(order_kernel, micros),
        out_shape=tuple(jax.ShapeDtypeStruct(a.shape, a.dtype) for a in arrays),
        grid_spec=pltpu.PrefetchScalarGridSpec(
            num_scalar_prefetch=1,
            grid=(slots,),
            in_specs=[
                pl.BlockSpec((1, 1, *a.shape[2:]), source(m)) for a in arrays for m in range(micros)
            ],
            out_specs=tuple(
                pl.BlockSpec((micros, 1, *a.shape[2:]), lambda i, ix: (0, i, 0, 0)) for a in arrays
            ),
        ),
        compiler_params=params(),
        cost_estimate=cost(0, 4 * sum(a.size for a in arrays)),
        name="in_order",
    )(index, *[a for a in arrays for _ in range(micros)])


def fits(mesh):
    return dict(mesh.shape) == {"seq": 8, "head": 4}


def on_device(
    tokens,
    prev_logits,
    lengths,
    dealing,
    w_query,
    b_query,
    w_key,
    w_value,
    b_value,
    w_out,
    b_out,
    gain_one,
    shift_one,
    w_up,
    b_up,
    w_down,
    b_down,
    gain_two,
    shift_two,
    cot_tokens,
    cot_logits,
):
    slots, groups = lax.axis_size("seq"), lax.axis_size("head")
    grid = ("seq", "head")
    here, head = lax.axis_index("seq"), lax.axis_index("head")
    micros, _, piece, model = tokens.shape
    heads = prev_logits.shape[3]
    extent = piece * slots
    width = heads * HEAD_DIM
    unit = w_up.shape[1]
    per = slots // groups
    cuts = (3 * width, 3 * width + width, 3 * width + width + unit, 3 * width + width + 2 * unit)
    own_rows = model // slots

    inverse = [
        jnp.sum(
            jnp.where(
                dealing[m][None, :] == jnp.arange(slots, dtype=jnp.int32)[:, None],
                jnp.arange(slots, dtype=jnp.int32)[None, :],
                0,
            ),
            axis=1,
        ).astype(jnp.int32)
        for m in range(micros)
    ]
    info = [
        jnp.stack([lengths[m, inverse[m][here]], here % groups]).astype(jnp.int32)
        for m in range(micros)
    ]
    prev = jnp.transpose(prev_logits, (0, 1, 3, 2, 4))
    cot_square = jnp.transpose(cot_logits[:, 0], (0, 2, 1, 3))

    vector = jnp.concatenate(
        [
            b_query.reshape(-1),
            b_value.reshape(-1),
            b_out,
            gain_one,
            shift_one,
            b_up.reshape(-1),
            b_down,
            gain_two,
            shift_two,
        ]
    )
    lots = 8
    vector = jnp.pad(vector, (0, lots * own_rows - vector.shape[0])).reshape(own_rows, lots)
    packed = jnp.concatenate(
        [
            w_query,
            w_key,
            w_value,
            w_out.T,
            w_up,
            w_down.T,
            jnp.pad(vector, ((0, 0), (0, 128 - lots))),
        ],
        axis=1,
    )
    pieces = jnp.stack(
        [
            jnp.stack(
                [
                    lax.dynamic_index_in_dim(array[m], inverse[m][slot], 0, keepdims=False)
                    for array in (tokens, cot_tokens)
                    for m in range(micros)
                ]
            )
            for slot in (
                (head - here // 2) % groups + groups * ((here + step) % 2) for step in range(2)
            )
        ]
    )
    weights, rows_all = gather_all(packed.reshape(2, own_rows // 2, -1), pieces, slots, groups, 1)
    rows = per * piece
    rows_all = rows_all.reshape(2 * micros, rows, model)
    rows_in, cot_rows = rows_all[:micros], rows_all[micros:]

    weights = weights.reshape(groups, slots, own_rows, -1)
    vectors = jnp.transpose(weights[..., cuts[-1] : cuts[-1] + lots], (1, 0, 2, 3))
    vectors = vectors.reshape(slots, groups, -1).astype(F32)
    weights = weights.reshape(groups, model, -1)
    q_len = heads * HEAD_DIM // slots
    offsets = [0, q_len, 2 * q_len]
    for _ in range(7):
        offsets.append(offsets[-1] + own_rows)

    def plain(i):
        return vectors[:, 0, offsets[i] : offsets[i + 1]].reshape(1, -1)

    def by_head(i):
        part = vectors[:, :, offsets[i] : offsets[i + 1]].reshape(slots, groups, heads, -1)
        return jnp.transpose(part, (1, 2, 0, 3)).reshape(groups, 1, -1)

    bias_query, bias_value, bias_up = by_head(0), by_head(1), by_head(5)
    bias_qkv = jnp.concatenate([bias_query, jnp.zeros_like(bias_query), bias_value], axis=2)
    row_vectors = jnp.concatenate(
        [plain(2), plain(3), plain(4), plain(6), plain(7), plain(8), jnp.zeros((2, model), F32)], axis=0
    )

    qkv = project(rows_in.reshape(micros * rows, model), weights, bias_qkv)
    qkv = across_heads(qkv, 3).reshape(groups, micros, rows, 3 * width)

    got_prev, after = [], None
    for m in range(micros):
        send = pick_blocks(prev, m, inverse[m])
        if after is not None:
            send, _ = lax.optimization_barrier((send, after))
        got = lax.all_to_all(send, "seq", split_axis=0, concat_axis=0, tiled=True)
        got_prev.append(got)
        after = (got, qkv)

    logits, grad_logits = None, None
    kept, sums_own, sums_rows, sums_up, returned = [], [], [], [], []
    for m in range(micros):
        logits, attend, context = attention_forward(info[m], qkv, got_prev[m], m, micros, logits)
        context_rows = across_heads(context, 4)
        y, dz, dcon, h1, act, b1, b2, b0, sums, dbup = row_work(
            cuts, context_rows, rows_in[m], cot_rows[m], weights, bias_up, row_vectors
        )
        dcontext = across_heads(dcon, 4)
        send, dqkv, own = attention_backward(
            info[m], qkv, attend, context, dcontext, cot_square, m
        )
        if m:
            send, _ = lax.optimization_barrier((send, first_grads))
        got = lax.all_to_all(send, "seq", split_axis=0, concat_axis=0, tiled=True)
        dqkv = across_heads(dqkv, 5)
        if m:
            dqkv, _ = lax.optimization_barrier((dqkv, first_grads))
        else:
            first_grads = got
        dx = input_grad(dqkv, weights, dz)
        kept.append((rows_in[m], b0, h1, b2, dqkv, context_rows, b1, act))
        sums_own.append(own)
        sums_rows.append(sums)
        sums_up.append(dbup)
        returned.append((y, dx))
        grad_logits = place_blocks(got, m, micros, dealing[m], grad_logits)

    own = sums_own[0]
    rows_sum = sums_rows[0]
    up_sum = sums_up[0]
    for m in range(1, micros):
        own, rows_sum, up_sum = own + sums_own[m], rows_sum + sums_rows[m], up_sum + sums_up[m]
    mine = (jnp.arange(groups) == head)[None, :, None]

    def spread_own(row):
        piece_of = jnp.transpose(row.reshape(heads, slots, -1), (1, 0, 2)).reshape(slots, 1, -1)
        return jnp.where(mine, piece_of, 0.0)

    def spread_plain(row):
        return jnp.broadcast_to(row.reshape(slots, 1, -1), (slots, groups, own_rows))

    up_part = jnp.transpose(up_sum.reshape(groups, heads, slots, -1), (2, 0, 1, 3))
    out_vectors = jnp.concatenate(
        [
            spread_own(own[0]),
            spread_own(own[1]),
            spread_plain(rows_sum[0]),
            spread_plain(rows_sum[1]),
            spread_plain(rows_sum[2]),
            up_part.reshape(slots, groups, own_rows),
            spread_plain(rows_sum[3]),
            spread_plain(rows_sum[4]),
            spread_plain(rows_sum[5]),
        ],
        axis=2,
    ).reshape(slots * groups, -1)
    out_vectors = jnp.pad(out_vectors, ((0, 0), (0, lots * own_rows - out_vectors.shape[1])))
    out_vectors = out_vectors.astype(BF16).reshape(slots, groups, own_rows, lots)
    out_vectors = jnp.transpose(out_vectors, (1, 0, 2, 3)).reshape(groups, model, lots)
    out_vectors = jnp.pad(out_vectors, ((0, 0), (0, 0), (0, 128 - lots)))

    families = list(zip(*kept))
    part = weight_grads(cuts, families[:4], families[4:], out_vectors)
    ys = jnp.stack([y for y, _ in returned]).reshape(micros, per, piece, model)
    dxs = jnp.stack([dx for _, dx in returned]).reshape(micros, groups, per, piece, -1)
    part = part.reshape(groups, slots, 2, own_rows // 2, -1)
    part, all_y, all_dx = finish(part, ys, dxs, slots, groups, 7)
    part = part.reshape(own_rows, -1)
    out_tokens, grad_tokens = in_order((all_y, all_dx), dealing)
    out_vectors = part[:, cuts[-1] : cuts[-1] + lots].reshape(-1)

    def vector_out(i):
        return out_vectors[offsets[i] : offsets[i + 1]]

    def columns(start, count):
        return part[:, start : start + count]

    return (
        out_tokens,
        jnp.transpose(logits, (0, 2, 1, 3))[:, None],
        grad_tokens,
        jnp.transpose(grad_logits, (0, 1, 3, 2, 4)),
        columns(0, width),
        vector_out(0).reshape(heads, -1),
        columns(width, width),
        columns(2 * width, width),
        vector_out(1).reshape(heads, -1),
        columns(3 * width, width).T,
        vector_out(2),
        vector_out(3),
        vector_out(4),
        columns(cuts[1], unit),
        vector_out(5).reshape(heads, -1),
        columns(cuts[2], unit).T,
        vector_out(6),
        vector_out(7),
        vector_out(8),
    )


def solution(mesh):
    placed = (
        P(None, None, "seq", None),
        P(None, None, "seq", "head", None),
        P(),
        P(),
        P("seq", "head"),
        P("head", "seq"),
        P("seq", "head"),
        P("seq", "head"),
        P("head", "seq"),
        P("head", "seq"),
        P("seq"),
        P("seq"),
        P("seq"),
        P("seq", "head"),
        P("head", "seq"),
        P("head", "seq"),
        P("seq"),
        P("seq"),
        P("seq"),
        P(None, None, "seq", None),
        P(None, "seq", None, "head", None),
    )
    return jax.shard_map(
        on_device if fits(mesh) else on_device_general,
        mesh=mesh,
        in_specs=placed,
        out_specs=(
            P(None, None, "seq", None),
            P(None, "seq", None, "head", None),
            P(None, None, "seq", "head"),
            P(None, None, "seq", "head", None),
            P("seq", "head"),
            P("head", "seq"),
            P("seq", "head"),
            P("seq", "head"),
            P("head", "seq"),
            P("head", "seq"),
            P("seq"),
            P("seq"),
            P("seq"),
            P("seq", "head"),
            P("head", "seq"),
            P("head", "seq"),
            P("seq"),
            P("seq"),
            P("seq"),
        ),
        check_vma=False,
    )
```

```python
import functools

import jax
import jax.numpy as jnp
from jax import lax
from jax.experimental import pallas as pl
from jax.experimental.pallas import tpu as pltpu
from jax.sharding import PartitionSpec as P

HEAD_DIM = 64
BF16, F32 = jnp.bfloat16, jnp.float32
VMEM_LIMIT = 60 * 1024 * 1024


epsilon = 1e-12


def cut_along(x, dim, peers):
    before, after = (x.shape[:dim], x.shape[dim + 1 :])
    return jnp.moveaxis(x.reshape(*before, peers, -1, *after), dim, 0)


def sum_at_owner(x, axis, dim):
    blocks = cut_along(x, dim, lax.axis_size(axis))
    arrived = lax.all_to_all(blocks, axis, split_axis=0, concat_axis=0, tiled=True)
    return arrived.astype(jnp.float32).sum(axis=0)


def side_by_side(arrays, axis, dim, along):
    both = jnp.concatenate(arrays, axis=along)
    result, at, finished = (sum_at_owner(both, axis, dim), 0, [])
    for a in arrays:
        finished.append(lax.slice_in_dim(result, at, at + a.shape[along], axis=along))
        at += a.shape[along]
    return tuple(finished)


def side_by_side_2(arrays, axis, dim, along):
    columns = [a.reshape(*a.shape[:along], -1) for a in arrays]
    both = jnp.concatenate(columns, axis=along)
    result, at, finished = (sum_at_owner(both, axis, dim), 0, [])
    for a, column in zip(arrays, columns):
        slab = result[..., at : at + column.shape[along]]
        finished.append(slab.reshape(*slab.shape[:along], *a.shape[along:]))
        at += column.shape[along]
    return tuple(finished)


def layer_norm(values, gain, shift):
    center = values - jnp.mean(values, axis=-1, keepdims=True)
    spread = jnp.mean(center * center, axis=-1, keepdims=True)
    return center * lax.rsqrt(spread + epsilon) * gain + shift


def exact_gelu(values):
    return jax.nn.gelu(values, approximate=False)


def mask_scores(raw_scores, length):
    key_valid = jnp.arange(raw_scores.shape[2]) < length
    return jnp.where(key_valid[None, None, :], raw_scores, -jnp.inf)


def on_device_general(
    tokens,
    prev_logits,
    lengths,
    dealing,
    w_query,
    b_query,
    w_key,
    w_value,
    b_value,
    w_out,
    b_out,
    gain_one,
    shift_one,
    w_up,
    b_up,
    w_down,
    b_down,
    gain_two,
    shift_two,
    cot_tokens,
    cot_logits,
):
    micro_count = tokens.shape[0]
    seq_count = tokens.shape[1]
    piece_rows = tokens.shape[2]
    model_width = tokens.shape[3]
    extent = piece_rows * seq_count
    heads_here = prev_logits.shape[3]
    width_here = model_width // lax.axis_size("head")
    score_scale = HEAD_DIM ** (-0.5)
    owner_slot = lax.axis_index("seq")
    head_slot = lax.axis_index("head")
    zero_shift = jnp.zeros((model_width,), jnp.float32)
    out_token_list = []
    out_logit_list = []
    grad_token_list = []
    grad_logit_list = []
    grad_totals = None
    for micro_batch in range(micro_count):
        full_weights = (
            lax.all_gather(w_query, "seq", axis=0, tiled=True),
            lax.all_gather(w_key, "seq", axis=0, tiled=True),
            lax.all_gather(w_value, "seq", axis=0, tiled=True),
            lax.all_gather(w_out, "seq", axis=1, tiled=True),
            lax.all_gather(w_up, "seq", axis=0, tiled=True),
            lax.all_gather(w_down, "seq", axis=1, tiled=True),
            lax.all_gather(b_query, "seq", axis=1, tiled=True),
            lax.all_gather(b_value, "seq", axis=1, tiled=True),
            lax.all_gather(b_out, "seq", axis=0, tiled=True),
            lax.all_gather(gain_one, "seq", axis=0, tiled=True),
            lax.all_gather(shift_one, "seq", axis=0, tiled=True),
            lax.all_gather(b_up, "seq", axis=1, tiled=True),
            lax.all_gather(b_down, "seq", axis=0, tiled=True),
            lax.all_gather(gain_two, "seq", axis=0, tiled=True),
            lax.all_gather(shift_two, "seq", axis=0, tiled=True),
        )
        (
            query_full,
            key_full,
            value_full,
            out_full,
            up_full,
            down_full,
            bias_query,
            bias_value,
            bias_out,
            gain_first,
            shift_first,
            bias_up,
            bias_down,
            gain_second,
            shift_second,
        ) = full_weights
        inverse = (
            jnp.zeros((seq_count,), jnp.int32)
            .at[dealing[micro_batch]]
            .set(jnp.arange(seq_count, dtype=jnp.int32))
        )
        own_sequence = inverse[owner_slot]
        own_length = lengths[micro_batch, own_sequence]
        send_tokens = jnp.take(tokens[micro_batch], inverse, axis=0)
        send_prev = jnp.take(prev_logits[micro_batch], inverse, axis=0).reshape(
            seq_count, piece_rows, heads_here * extent
        )
        send_cot = jnp.take(cot_tokens[micro_batch], inverse, axis=0)
        got_tokens, got_prev, got_cot = (
            lax.all_to_all(send_tokens, "seq", split_axis=0, concat_axis=1, tiled=True),
            lax.all_to_all(send_prev, "seq", split_axis=0, concat_axis=1, tiled=True),
            lax.all_to_all(send_cot, "seq", split_axis=0, concat_axis=1, tiled=True),
        )
        rows_in = got_tokens.reshape(extent, model_width)
        prev_rows = got_prev.reshape(extent, heads_here, extent).astype(jnp.float32)
        cot_rows = got_cot.reshape(extent, model_width).astype(jnp.float32)
        query_pre = jnp.dot(rows_in, query_full, preferred_element_type=jnp.float32)
        queries = (query_pre + bias_query.reshape(-1).astype(jnp.float32)).astype(jnp.bfloat16)
        keys_all = jnp.dot(rows_in, key_full, preferred_element_type=jnp.float32).astype(
            jnp.bfloat16
        )
        value_pre = jnp.dot(rows_in, value_full, preferred_element_type=jnp.float32)
        values = (value_pre + bias_value.reshape(-1).astype(jnp.float32)).astype(jnp.bfloat16)
        query_heads = queries.reshape(extent, heads_here, HEAD_DIM)
        key_heads = keys_all.reshape(extent, heads_here, HEAD_DIM)
        value_heads = values.reshape(extent, heads_here, HEAD_DIM)
        raw_scores = (
            jnp.einsum("qhd,khd->qhk", query_heads, key_heads, preferred_element_type=jnp.float32)
            * score_scale
            + prev_rows
        )
        masked = mask_scores(raw_scores, own_length)
        row_top = jnp.max(masked, axis=-1, keepdims=True)
        shifted_exp = jnp.exp(masked - row_top)
        row_total = jnp.sum(shifted_exp, axis=-1, keepdims=True)
        attend = shifted_exp / row_total
        log_total = row_top + jnp.log(row_total)
        out_logit_list.append(raw_scores.astype(jnp.bfloat16)[None])
        context = (
            jnp.einsum(
                "qhk,khd->qhd",
                attend.astype(jnp.bfloat16),
                value_heads,
                preferred_element_type=jnp.float32,
            )
            .astype(jnp.bfloat16)
            .reshape(extent, heads_here * HEAD_DIM)
        )
        out_part = jnp.dot(context, out_full, preferred_element_type=jnp.float32)
        branch = lax.psum(out_part, "head") + bias_out.astype(jnp.float32)
        resid_one = rows_in.astype(jnp.float32) + branch
        hidden = layer_norm(
            resid_one, gain_first.astype(jnp.float32), shift_first.astype(jnp.float32)
        )
        hidden_low = hidden.astype(jnp.bfloat16)
        before_gelu = jnp.dot(
            hidden_low, up_full, preferred_element_type=jnp.float32
        ) + bias_up.reshape(-1).astype(jnp.float32)
        active = exact_gelu(before_gelu).astype(jnp.bfloat16)
        down_part = jnp.dot(active, down_full, preferred_element_type=jnp.float32)
        resid_two = hidden + (
            lax.psum(down_part.astype(jnp.bfloat16), "head").astype(jnp.float32)
            + bias_down.astype(jnp.float32)
        )
        result = layer_norm(
            resid_two, gain_second.astype(jnp.float32), shift_second.astype(jnp.float32)
        )
        out_rows = result.astype(jnp.bfloat16)
        (
            back_query,
            back_key,
            back_value,
            back_out,
            back_up,
            back_down,
            back_gain_first,
            back_gain_second,
        ) = (
            lax.all_gather(w_query, "seq", axis=0, tiled=True),
            lax.all_gather(w_key, "seq", axis=0, tiled=True),
            lax.all_gather(w_value, "seq", axis=0, tiled=True),
            lax.all_gather(w_out, "seq", axis=1, tiled=True),
            lax.all_gather(w_up, "seq", axis=0, tiled=True),
            lax.all_gather(w_down, "seq", axis=1, tiled=True),
            lax.all_gather(gain_one, "seq", axis=0, tiled=True),
            lax.all_gather(gain_two, "seq", axis=0, tiled=True),
        )
        norm_two_value, norm_two_back = jax.vjp(
            layer_norm, resid_two, back_gain_second.astype(jnp.float32), zero_shift
        )
        d_resid_two, d_gain_two, d_shift_two = norm_two_back(cot_rows)
        d_b_down = jnp.sum(d_resid_two, axis=0)
        grad_two_low = d_resid_two.astype(jnp.bfloat16)
        d_w_down = jnp.einsum("rf,rd->fd", active, grad_two_low, preferred_element_type=jnp.float32)
        d_active = jnp.einsum(
            "rd,fd->rf", grad_two_low, back_down, preferred_element_type=jnp.float32
        )
        gelu_value, gelu_back = jax.vjp(exact_gelu, before_gelu)
        d_before = gelu_back(d_active)[0]
        d_b_up = jnp.sum(d_before, axis=0).reshape(heads_here, -1)
        before_low = d_before.astype(jnp.bfloat16)
        d_w_up = jnp.einsum("rd,rf->df", hidden_low, before_low, preferred_element_type=jnp.float32)
        up_part = jnp.einsum("rf,df->rd", before_low, back_up, preferred_element_type=jnp.float32)
        d_hidden = d_resid_two + lax.psum(up_part.astype(jnp.bfloat16), "head").astype(jnp.float32)
        norm_one_value, norm_one_back = jax.vjp(
            layer_norm, resid_one, back_gain_first.astype(jnp.float32), zero_shift
        )
        d_resid_one, d_gain_one, d_shift_one = norm_one_back(d_hidden)
        d_b_out = jnp.sum(d_resid_one, axis=0)
        grad_one_low = d_resid_one.astype(jnp.bfloat16)
        d_w_out = jnp.einsum("rc,rd->cd", context, grad_one_low, preferred_element_type=jnp.float32)
        d_context = (
            jnp.einsum("rd,cd->rc", grad_one_low, back_out, preferred_element_type=jnp.float32)
            .astype(jnp.bfloat16)
            .reshape(extent, heads_here, HEAD_DIM)
        )
        raw_again = (
            jnp.einsum("qhd,khd->qhk", query_heads, key_heads, preferred_element_type=jnp.float32)
            * score_scale
            + prev_rows
        )
        attend_again = jnp.exp(mask_scores(raw_again, own_length) - log_total)
        d_attend = jnp.einsum(
            "qhd,khd->qhk", d_context, value_heads, preferred_element_type=jnp.float32
        )
        d_values = jnp.einsum(
            "qhk,qhd->khd",
            attend_again.astype(jnp.bfloat16),
            d_context,
            preferred_element_type=jnp.float32,
        )
        d_scores = attend_again * (
            d_attend - jnp.sum(attend_again * d_attend, axis=-1, keepdims=True)
        ) + cot_logits[micro_batch, 0].astype(jnp.float32)
        scores_low = d_scores.astype(jnp.bfloat16)
        d_queries = (
            jnp.einsum("qhk,khd->qhd", scores_low, key_heads, preferred_element_type=jnp.float32)
            * score_scale
        )
        d_keys = (
            jnp.einsum("qhk,qhd->khd", scores_low, query_heads, preferred_element_type=jnp.float32)
            * score_scale
        )
        d_b_query = jnp.sum(d_queries, axis=0)
        d_b_value = jnp.sum(d_values, axis=0)
        queries_low = d_queries.astype(jnp.bfloat16).reshape(extent, heads_here * HEAD_DIM)
        keys_low = d_keys.astype(jnp.bfloat16).reshape(extent, heads_here * HEAD_DIM)
        values_low = d_values.astype(jnp.bfloat16).reshape(extent, heads_here * HEAD_DIM)
        d_w_query = jnp.einsum(
            "rd,rc->dc", rows_in, queries_low, preferred_element_type=jnp.float32
        )
        d_w_key = jnp.einsum("rd,rc->dc", rows_in, keys_low, preferred_element_type=jnp.float32)
        d_w_value = jnp.einsum("rd,rc->dc", rows_in, values_low, preferred_element_type=jnp.float32)
        input_part = jnp.einsum(
            "rc,dc->rd", queries_low, back_query, preferred_element_type=jnp.float32
        )
        input_part = input_part + jnp.einsum(
            "rc,dc->rd", keys_low, back_key, preferred_element_type=jnp.float32
        )
        input_part = input_part + jnp.einsum(
            "rc,dc->rd", values_low, back_value, preferred_element_type=jnp.float32
        )
        input_share = lax.psum_scatter(
            input_part.astype(jnp.bfloat16), "head", scatter_dimension=1, tiled=True
        ).astype(jnp.float32)
        resid_share = lax.dynamic_slice_in_dim(d_resid_one, head_slot * width_here, width_here, 1)
        grad_rows = (resid_share + input_share).astype(jnp.bfloat16)
        back_tokens, back_grads, back_logits = (
            lax.all_to_all(
                out_rows.reshape(seq_count, piece_rows, model_width),
                "seq",
                split_axis=0,
                concat_axis=0,
                tiled=True,
            ),
            lax.all_to_all(
                grad_rows.reshape(seq_count, piece_rows, width_here),
                "seq",
                split_axis=0,
                concat_axis=0,
                tiled=True,
            ),
            lax.all_to_all(
                scores_low.reshape(seq_count, piece_rows, heads_here * extent),
                "seq",
                split_axis=0,
                concat_axis=0,
                tiled=True,
            ),
        )
        out_token_list.append(jnp.take(back_tokens, dealing[micro_batch], axis=0))
        grad_token_list.append(jnp.take(back_grads, dealing[micro_batch], axis=0))
        grad_logit_list.append(
            jnp.take(back_logits, dealing[micro_batch], axis=0).reshape(
                seq_count, piece_rows, heads_here, extent
            )
        )
        local_grads = (
            d_w_query,
            d_b_query,
            d_w_key,
            d_w_value,
            d_b_value,
            d_w_out,
            d_b_out,
            d_gain_one,
            d_shift_one,
            d_w_up,
            d_b_up,
            d_w_down,
            d_b_down,
            d_gain_two,
            d_shift_two,
        )
        if grad_totals is None:
            grad_totals = local_grads
        else:
            grad_totals = tuple((total + extra for total, extra in zip(grad_totals, local_grads)))
    final_grads = (
        sum_at_owner(grad_totals[0].astype(jnp.bfloat16), "seq", 0),
        sum_at_owner(grad_totals[1].astype(jnp.bfloat16), "seq", 1),
        *side_by_side(
            (grad_totals[2].astype(jnp.bfloat16), grad_totals[3].astype(jnp.bfloat16)), "seq", 0, 1
        ),
        sum_at_owner(grad_totals[4].astype(jnp.bfloat16), "seq", 1),
        sum_at_owner(grad_totals[5].astype(jnp.bfloat16), "seq", 1),
        sum_at_owner(grad_totals[6].astype(jnp.bfloat16), "seq", 0),
        sum_at_owner(grad_totals[7].astype(jnp.bfloat16), "seq", 0),
        *side_by_side_2(
            (grad_totals[8].astype(jnp.bfloat16), grad_totals[9].astype(jnp.bfloat16)), "seq", 0, 1
        ),
        sum_at_owner(grad_totals[10].astype(jnp.bfloat16), "seq", 1),
        sum_at_owner(grad_totals[11].astype(jnp.bfloat16), "seq", 1),
        sum_at_owner(grad_totals[12].astype(jnp.bfloat16), "seq", 0),
        sum_at_owner(grad_totals[13].astype(jnp.bfloat16), "seq", 0),
        sum_at_owner(grad_totals[14].astype(jnp.bfloat16), "seq", 0),
    )
    out_tokens = jnp.stack(out_token_list, axis=0)
    out_logits = jnp.stack(out_logit_list, axis=0)
    grad_tokens = jnp.stack(grad_token_list, axis=0)
    grad_logits = jnp.stack(grad_logit_list, axis=0)
    return (
        out_tokens,
        out_logits,
        grad_tokens,
        grad_logits,
        final_grads[0],
        final_grads[1],
        final_grads[2],
        final_grads[3],
        final_grads[4],
        final_grads[5],
        final_grads[6],
        final_grads[7],
        final_grads[8],
        final_grads[9],
        final_grads[10],
        final_grads[11],
        final_grads[12],
        final_grads[13],
        final_grads[14],
    )

def cost(flops, moved):
    return pl.CostEstimate(flops=int(flops) // 100, bytes_accessed=int(moved) // 100, transcendentals=0)


def params(**more):
    return pltpu.CompilerParams(vmem_limit_bytes=VMEM_LIMIT, **more)


def dot(a, b, ca, cb):
    return lax.dot_general(a, b, (((ca,), (cb,)), ((), ())), preferred_element_type=F32)


def whole(x):
    return pl.BlockSpec(x.shape, lambda *_: (0,) * len(x.shape))


def move_blocks(reads, writes, buffers, in_sem, out_sem):
    ins = [pltpu.make_async_copy(r, v, in_sem.at[i]) for i, (r, v) in enumerate(zip(reads, buffers))]
    outs = [pltpu.make_async_copy(v, w, out_sem.at[i]) for i, (v, w) in enumerate(zip(buffers, writes))]
    for copy in ins:
        copy.start()
    for copy, out in zip(ins, outs):
        copy.wait()
        out.start()
    for out in outs:
        out.wait()


SMALL = pl.BlockSpec(memory_space=pltpu.SMEM)
ANYWHERE = pl.BlockSpec(memory_space=pl.ANY)


def inverse_of(dealing_ref, inverse_ref, micros, slots):
    for m in micros:
        for i in range(slots):
            inverse_ref[dealing_ref[m, i]] = i


def pick_copies(micro, count, inverse_ref, x_ref, o_ref, buffer):
    steps = range(count)
    return (
        [x_ref.at[micro, inverse_ref[i]] for i in steps],
        [o_ref.at[i] for i in steps],
        [buffer.at[i] for i in steps],
    )


def pick_kernel(micro, count, dealing_ref, x_ref, o_ref, buffer, inverse_ref, in_sem, out_sem):
    inverse_of(dealing_ref, inverse_ref, [micro], count)
    move_blocks(*pick_copies(micro, count, inverse_ref, x_ref, o_ref, buffer), in_sem, out_sem)


def pick_blocks(stacked, micro, dealing):
    count = stacked.shape[1]
    block = stacked.shape[2:]
    dma = pltpu.SemaphoreType.DMA
    return pl.pallas_call(
        functools.partial(pick_kernel, micro, count),
        out_shape=jax.ShapeDtypeStruct((count, *block), stacked.dtype),
        in_specs=[SMALL, ANYWHERE],
        out_specs=ANYWHERE,
        scratch_shapes=[
            pltpu.VMEM((count, *block), stacked.dtype),
            pltpu.SMEM((count,), jnp.int32),
            dma((count,)),
            dma((count,)),
        ],
        compiler_params=params(),
        cost_estimate=cost(0, 4 * stacked.size // stacked.shape[0]),
        name="pick_blocks",
    )(dealing, stacked)


PLAIN, QUERY_AT, VALUE_AT, UP_AT, VECTOR_ROWS = 6, 8, 16, 24, 32


def prepare_kernel(
    micros, slots, groups, dealing_ref, prev_ref, tokens_ref, cot_ref,
    wq_ref, wk_ref, wv_ref, wo_ref, wu_ref, wd_ref, bq_ref, bv_ref, bu_ref, plain_refs,
    send_ref, piece_ref, pack_ref, block_buffer, piece_buffer, vector_scr, inverse_refs, in_sem, out_sem,
):
    here, head = lax.axis_index("seq"), lax.axis_index("head")
    for m in range(micros):
        inverse_of(dealing_ref, inverse_refs[m], [m], slots)
    reads, writes, buffers = [], [], []
    for step in range(2):
        slot = lax.rem(head - here // 2 + groups, groups) + groups * lax.rem(here + step, 2)
        for a, array_ref in enumerate((tokens_ref, cot_ref)):
            for m in range(micros):
                n = a * micros + m
                reads.append(array_ref.at[m, inverse_refs[m][slot]])
                writes.append(piece_ref.at[step, n])
                buffers.append(piece_buffer.at[step, n])
    blocks = pick_copies(0, slots, inverse_refs[0], prev_ref, send_ref, block_buffer)
    reads, writes, buffers = reads + blocks[0], writes + blocks[1], buffers + blocks[2]
    for i, (source, target) in enumerate(zip(reads, buffers)):
        pltpu.make_async_copy(source, target, in_sem.at[i]).start()

    at = 0
    for ref in (wq_ref, wk_ref, wv_ref, wo_ref, wu_ref, wd_ref):
        pack_ref[:, at : at + ref.shape[1]] = ref[...]
        at += ref.shape[1]
    vector_scr[...] = jnp.zeros_like(vector_scr)
    for i, ref in enumerate(plain_refs):
        vector_scr[i : i + 1, : ref.shape[1]] = ref[...].astype(F32)
    for first, ref in ((QUERY_AT, bq_ref), (VALUE_AT, bv_ref), (UP_AT, bu_ref)):
        vector_scr[first : first + ref.shape[0], : ref.shape[1]] = ref[...].astype(F32)
    pack_ref[:VECTOR_ROWS, at:] = vector_scr[...].astype(BF16)
    pack_ref[VECTOR_ROWS:, at:] = jnp.zeros_like(pack_ref[VECTOR_ROWS:, at:])

    for i, (source, target, buffer) in enumerate(zip(reads, writes, buffers)):
        pltpu.make_async_copy(source, buffer, in_sem.at[i]).wait()
        pltpu.make_async_copy(buffer, target, out_sem.at[i]).start()
    for i, (target, buffer) in enumerate(zip(writes, buffers)):
        pltpu.make_async_copy(buffer, target, out_sem.at[i]).wait()


def prepare(dealing, prev, tokens, cot_tokens, weights, head_vectors, plain_vectors, groups):
    micros, slots = prev.shape[:2]
    block, row = prev.shape[2:], tokens.shape[2:]
    dma = pltpu.SemaphoreType.DMA
    copies = slots + 4 * micros
    columns = sum(w.shape[1] for w in weights) + 128
    in_vmem = pl.BlockSpec(memory_space=pltpu.VMEM)
    flat = [*weights, *head_vectors]

    def body(*refs):
        fixed = 4 + len(flat)
        plain_refs = refs[fixed : fixed + len(plain_vectors)]
        rest = refs[fixed + len(plain_vectors) :]
        send_ref, piece_ref, pack_ref, block_buffer, piece_buffer, vector_scr = rest[:6]
        prepare_kernel(
            micros, slots, groups, *refs[:fixed], plain_refs, send_ref, piece_ref, pack_ref,
            block_buffer, piece_buffer, vector_scr, rest[6 : 6 + micros], *rest[6 + micros :],
        )

    return pl.pallas_call(
        body,
        out_shape=(
            jax.ShapeDtypeStruct((slots, *block), prev.dtype),
            jax.ShapeDtypeStruct((2, 2 * micros, *row), tokens.dtype),
            jax.ShapeDtypeStruct((weights[0].shape[0], columns), BF16),
        ),
        in_specs=[SMALL, ANYWHERE, ANYWHERE, ANYWHERE] + [in_vmem] * (len(flat) + len(plain_vectors)),
        out_specs=(ANYWHERE, ANYWHERE, in_vmem),
        scratch_shapes=[
            pltpu.VMEM((slots, *block), prev.dtype),
            pltpu.VMEM((2, 2 * micros, *row), tokens.dtype),
            pltpu.VMEM((VECTOR_ROWS, 128), F32),
        ]
        + [pltpu.SMEM((slots,), jnp.int32)] * micros
        + [dma((copies,)), dma((copies,))],
        compiler_params=params(),
        cost_estimate=cost(0, 4 * prev.size // micros),
        name="prepare",
    )(dealing, prev, tokens, cot_tokens, *flat, *plain_vectors)


def unpack_kernel(heads, x_ref, qkv_ref, up_ref, plain_ref):
    groups, slots = x_ref.shape[:2]
    width = heads * HEAD_DIM
    qkv_ref[...] = jnp.zeros_like(qkv_ref)
    lanes = plain_ref.shape[1] // slots
    per_head = HEAD_DIM // slots
    unit = up_ref.shape[2] // heads
    per_unit = unit // slots
    for s in range(slots):
        for h in range(groups):
            block = x_ref[h, s].astype(F32)
            if h == 0:
                plain_ref[:, s * lanes : (s + 1) * lanes] = block[:8, :lanes]
            for j in range(heads):
                at = j * HEAD_DIM + s * per_head
                qkv_ref[h, :, at : at + per_head] = block[QUERY_AT + j : QUERY_AT + j + 1, :per_head]
                at += 2 * width
                qkv_ref[h, :, at : at + per_head] = block[VALUE_AT + j : VALUE_AT + j + 1, :per_head]
                at = j * unit + s * per_unit
                up_ref[h, :, at : at + per_unit] = block[UP_AT + j : UP_AT + j + 1, :per_unit]


def unpack_vectors(shards, heads, width, unit, model):
    groups, slots, _, columns = shards.shape
    last = columns // 128 - 1
    shape = jax.ShapeDtypeStruct
    return pl.pallas_call(
        functools.partial(unpack_kernel, heads),
        out_shape=(
            shape((groups, 1, 3 * width), F32),
            shape((groups, 1, unit), F32),
            shape((8, model), F32),
        ),
        grid=(1,),
        in_specs=[pl.BlockSpec((groups, slots, VECTOR_ROWS, 128), lambda i: (0, 0, 0, last))],
        out_specs=(
            pl.BlockSpec((groups, 1, 3 * width), lambda i: (0, 0, 0)),
            pl.BlockSpec((groups, 1, unit), lambda i: (0, 0, 0)),
            pl.BlockSpec((8, model), lambda i: (0, 0)),
        ),
        compiler_params=params(),
        cost_estimate=cost(0, 4 * groups * slots * VECTOR_ROWS * 128),
        name="unpack_vectors",
    )(shards)


def place_kernel(micro, count, index_ref, x_ref, *rest):
    o_ref, buffer, in_sem, out_sem = rest[-4:]
    steps = range(count)
    move_blocks(
        [x_ref.at[index_ref[i]] for i in steps],
        [o_ref.at[micro, i] for i in steps],
        [buffer.at[i] for i in steps],
        in_sem,
        out_sem,
    )


def place_blocks(blocks, micro, micros, index, into):
    count = blocks.shape[0]
    others = [] if into is None else [into]
    dma = pltpu.SemaphoreType.DMA
    return pl.pallas_call(
        functools.partial(place_kernel, micro, count),
        out_shape=jax.ShapeDtypeStruct((micros, *blocks.shape), blocks.dtype),
        in_specs=[SMALL, ANYWHERE] + [ANYWHERE for _ in others],
        out_specs=ANYWHERE,
        scratch_shapes=[pltpu.VMEM(blocks.shape, blocks.dtype), dma((count,)), dma((count,))],
        input_output_aliases={2: 0} if others else {},
        compiler_params=params(),
        cost_estimate=cost(0, 4 * blocks.size),
        name="place_blocks",
    )(index, blocks, *others)


def project_kernel(x_ref, w_ref, b_ref, *outs):
    columns = outs[0].shape[2]
    for m, o_ref in enumerate(outs):
        o_ref[0] = (dot(x_ref[m], w_ref[0, :, :columns], 1, 0) + b_ref[0]).astype(BF16)


def project(x, weights, bias):
    micros, rows, width = x.shape
    groups, _, columns = bias.shape
    return pl.pallas_call(
        project_kernel,
        out_shape=(jax.ShapeDtypeStruct((groups, rows, columns), BF16),) * micros,
        grid=(groups,),
        in_specs=[
            whole(x),
            pl.BlockSpec((1, width, width), lambda h: (h, 0, 0)),
            pl.BlockSpec((1, 1, columns), lambda h: (h, 0, 0)),
        ],
        out_specs=(pl.BlockSpec((1, rows, columns), lambda h: (h, 0, 0)),) * micros,
        compiler_params=params(),
        cost_estimate=cost(2 * micros * groups * rows * width * columns, 2 * groups * columns * (width + rows)),
        name="project",
    )(x, weights, bias)


def head_mask(shape, head):
    lane = lax.broadcasted_iota(jnp.int32, shape, len(shape) - 1)
    return lane // HEAD_DIM == head


def gather_rows(info_ref, qkv_ref, groups, rows, width, q_scr, k_scr, v_scr):
    for g in range(groups):
        block = qkv_ref[(info_ref[1] + g) % groups]
        q_scr[g * rows : (g + 1) * rows] = block[:, :width]
        k_scr[g * rows : (g + 1) * rows] = block[:, width : 2 * width]
        v_scr[g * rows : (g + 1) * rows] = block[:, 2 * width :]


def forward_kernel(heads, info_ref, qkv_ref, prev_ref, *rest):
    logit_ref, attend_ref, context_ref, q_scr, k_scr, v_scr = rest[-6:]
    step = pl.program_id(0)
    groups, rows, columns = qkv_ref.shape
    piece, extent = prev_ref.shape[2:]
    width = columns // 3

    @pl.when(step == 0)
    def _():
        gather_rows(info_ref, qkv_ref, groups, rows, width, q_scr, k_scr, v_scr)

    q = q_scr[pl.ds(pl.multiple_of(step * piece, 16), piece), :]
    key_valid = lax.broadcasted_iota(jnp.int32, (1, extent), 1) < info_ref[0]
    total = jnp.zeros((piece, width), F32)
    for h in range(heads):
        mine = head_mask((1, width), h)
        q_head = jnp.where(mine, q, jnp.zeros_like(q))
        raw = dot(q_head, k_scr[...], 1, 1) * HEAD_DIM ** (-0.5) + prev_ref[0, h].astype(F32)
        logit_ref[0, h] = raw.astype(BF16)
        masked = jnp.where(key_valid, raw, -jnp.inf)
        top = jnp.max(masked, axis=-1, keepdims=True)
        grown = jnp.exp(masked - top)
        attend = grown * (1.0 / jnp.sum(grown, axis=-1, keepdims=True))
        low = attend.astype(BF16)
        attend_ref[0, h] = low
        total = total + jnp.where(mine, dot(low, v_scr[...], 1, 0), 0.0)
    context_ref[0] = total.astype(BF16)


def attention_forward(info, qkv, prev, micro, micros, logits_into):
    groups, rows, columns = qkv.shape
    pieces, heads, piece, extent = prev.shape
    width = columns // 3
    per = rows // piece
    others = [] if logits_into is None else [logits_into]
    return pl.pallas_call(
        functools.partial(forward_kernel, heads),
        out_shape=(
            jax.ShapeDtypeStruct((micros, heads, extent, extent), BF16),
            jax.ShapeDtypeStruct(prev.shape, BF16),
            jax.ShapeDtypeStruct((groups, rows, width), BF16),
        ),
        grid_spec=pltpu.PrefetchScalarGridSpec(
            num_scalar_prefetch=1,
            grid=(pieces,),
            in_specs=[
                pl.BlockSpec((groups, rows, columns), lambda j, i: (0, 0, 0)),
                pl.BlockSpec((1, heads, piece, extent), lambda j, i: (j, 0, 0, 0)),
            ]
            + [pl.BlockSpec(memory_space=pl.ANY) for _ in others],
            out_specs=(
                pl.BlockSpec((1, heads, piece, extent), lambda j, i: (micro, 0, j, 0)),
                pl.BlockSpec((1, heads, piece, extent), lambda j, i: (j, 0, 0, 0)),
                pl.BlockSpec((1, piece, width), lambda j, i: ((j // per + i[1]) % groups, j % per, 0)),
            ),
            scratch_shapes=[pltpu.VMEM((extent, width), BF16)] * 3,
        ),
        input_output_aliases={3: 0} if others else {},
        compiler_params=params(),
        cost_estimate=cost(4 * heads * extent * extent * HEAD_DIM * 4, 6 * heads * extent * extent),
        name="attention_forward",
    )(info, qkv, prev, *others)


def backward_kernel(
    heads, info_ref, qkv_ref, attend_ref, context_ref, dcon_ref, cot_ref,
    send_ref, dqkv_ref, sums_ref, q_scr, k_scr, v_scr, dq_scr, dk_scr, dv_scr,
):
    step = pl.program_id(0)
    groups, rows, columns = qkv_ref.shape
    piece, extent = attend_ref.shape[2:]
    width = columns // 3
    scale = HEAD_DIM ** (-0.5)

    @pl.when(step == 0)
    def _():
        gather_rows(info_ref, qkv_ref, groups, rows, width, q_scr, k_scr, v_scr)
        dk_scr[...] = jnp.zeros_like(dk_scr)
        dv_scr[...] = jnp.zeros_like(dv_scr)

    here = pl.ds(pl.multiple_of(step * piece, 16), piece)
    q = q_scr[here, :]
    dcon = dcon_ref[0]
    both = dcon.astype(F32) * context_ref[0].astype(F32)
    dq = jnp.zeros((piece, width), F32)
    for h in range(heads):
        mine = head_mask((1, width), h)
        dcon_head = jnp.where(mine, dcon, jnp.zeros_like(dcon))
        q_head = jnp.where(mine, q, jnp.zeros_like(q))
        low = attend_ref[0, h]
        delta = jnp.sum(jnp.where(mine, both, 0.0), axis=-1, keepdims=True)
        dprob = dot(dcon_head, v_scr[...], 1, 1)
        dscore = low.astype(F32) * (dprob - delta) + cot_ref[0, h].astype(F32)
        dlow = dscore.astype(BF16)
        send_ref[0, h] = dlow
        dq = dq + jnp.where(mine, dot(dlow, k_scr[...], 1, 0), 0.0)
        dk_scr[...] += dot(dlow, q_head, 0, 0)
        dv_scr[...] += dot(low, dcon_head, 0, 0)
    dq_scr[here, :] = dq * scale

    @pl.when(step == pl.num_programs(0) - 1)
    def _():
        sums_ref[0:1, :] = jnp.sum(dq_scr[...], axis=0, keepdims=True)
        sums_ref[1:2, :] = jnp.sum(dv_scr[...], axis=0, keepdims=True)
        for g in range(groups):
            part = slice(g * rows, (g + 1) * rows)
            dqkv_ref[(info_ref[1] + g) % groups] = jnp.concatenate(
                [dq_scr[part], dk_scr[part] * scale, dv_scr[part]], axis=1
            ).astype(BF16)


def attention_backward(info, qkv, attend, context, dcontext, cot, micro):
    groups, rows, columns = qkv.shape
    pieces, heads, piece, extent = attend.shape
    width = columns // 3
    per = rows // piece
    rotated = pl.BlockSpec((1, piece, width), lambda j, i: ((j // per + i[1]) % groups, j % per, 0))
    square = pl.BlockSpec((1, heads, piece, extent), lambda j, i: (j, 0, 0, 0))
    return pl.pallas_call(
        functools.partial(backward_kernel, heads),
        out_shape=(
            jax.ShapeDtypeStruct(attend.shape, BF16),
            jax.ShapeDtypeStruct((groups, rows, columns), BF16),
            jax.ShapeDtypeStruct((2, width), F32),
        ),
        grid_spec=pltpu.PrefetchScalarGridSpec(
            num_scalar_prefetch=1,
            grid=(pieces,),
            in_specs=[
                pl.BlockSpec((groups, rows, columns), lambda j, i: (0, 0, 0)),
                square,
                rotated,
                rotated,
                pl.BlockSpec((1, heads, piece, extent), lambda j, i: (micro, 0, j, 0)),
            ],
            out_specs=(
                square,
                pl.BlockSpec((groups, rows, columns), lambda j, i: (0, 0, 0)),
                pl.BlockSpec((2, width), lambda j, i: (0, 0)),
            ),
            scratch_shapes=[pltpu.VMEM((extent, width), BF16)] * 3
            + [pltpu.VMEM((extent, width), F32)] * 3,
        ),
        compiler_params=params(),
        cost_estimate=cost(8 * heads * extent * extent * HEAD_DIM * 4, 6 * heads * extent * extent),
        name="attention_backward",
    )(info, qkv, attend, context, dcontext, cot)


def normal(values):
    center = values - jnp.mean(values, axis=-1, keepdims=True)
    spread = jnp.mean(center * center, axis=-1, keepdims=True)
    inverse = lax.rsqrt(spread + epsilon)
    return center * inverse, inverse


def normal_back(grad, gain, unit, inverse):
    scaled = grad * gain
    return inverse * (
        scaled
        - jnp.mean(scaled, axis=-1, keepdims=True)
        - unit * jnp.mean(scaled * unit, axis=-1, keepdims=True)
    )


def rows_kernel(
    cuts, con_ref, x_ref, cot_ref, w_ref, bup_ref, vec_ref,
    y_ref, dz_ref, dcon_ref, h1_ref, act_ref, b1_ref, b2_ref, b0_ref, sums_ref, dbup_ref,
    slope, acc, hidden, unit_scr, inv_scr,
):
    groups, rows, width = con_ref.shape
    qkv_end, out_end, up_end, down_end = cuts
    b_out, gain_one, shift_one = vec_ref[0:1, :], vec_ref[1:2, :], vec_ref[2:3, :]
    b_down, gain_two, shift_two = vec_ref[3:4, :], vec_ref[4:5, :], vec_ref[5:6, :]

    branch = b_out + x_ref[...].astype(F32)
    for h in range(groups):
        branch = branch + dot(con_ref[h], w_ref[h, :, qkv_end:out_end], 1, 1)
    unit_one, inverse_one = normal(branch)
    unit_scr[...] = unit_one
    inv_scr[...] = inverse_one
    hid = unit_one * gain_one + shift_one
    hidden[...] = hid
    h1_ref[...] = hid.astype(BF16)
    acc[...] = hid + b_down

    def up(h, carry):
        u = dot(h1_ref[...], w_ref[h, :, out_end:up_end], 1, 0) + bup_ref[h]
        half = 0.5 * (1.0 + lax.erf(u * 0.7071067811865476))
        act_ref[h] = (u * half).astype(BF16)
        slope[h] = half + u * (jnp.exp(u * u * -0.5) * 0.3989422804014327)
        acc[...] += dot(act_ref[h], w_ref[h, :, up_end:down_end], 1, 1)
        return carry

    lax.fori_loop(0, groups, up, 0)
    unit_two, inverse_two = normal(acc[...])
    y_ref[...] = (unit_two * gain_two + shift_two).astype(BF16)
    cot = cot_ref[...].astype(F32)
    sums_ref[4:5, :] = jnp.sum(cot * unit_two, axis=0, keepdims=True)
    sums_ref[5:6, :] = jnp.sum(cot, axis=0, keepdims=True)
    dz_two = normal_back(cot, gain_two, unit_two, inverse_two)
    sums_ref[3:4, :] = jnp.sum(dz_two, axis=0, keepdims=True)
    b2_ref[...] = dz_two.astype(BF16)
    acc[...] = dz_two

    def down(h, carry):
        du = dot(b2_ref[...], w_ref[h, :, up_end:down_end], 1, 0) * slope[h]
        dbup_ref[h] = jnp.sum(du, axis=0, keepdims=True)
        b1_ref[h] = du.astype(BF16)
        acc[...] += dot(b1_ref[h], w_ref[h, :, out_end:up_end], 1, 1)
        return carry

    lax.fori_loop(0, groups, down, 0)
    dh = acc[...]
    unit_one = unit_scr[...]
    sums_ref[1:2, :] = jnp.sum(dh * unit_one, axis=0, keepdims=True)
    sums_ref[2:3, :] = jnp.sum(dh, axis=0, keepdims=True)
    dz_one = normal_back(dh, gain_one, unit_one, inv_scr[...])
    sums_ref[0:1, :] = jnp.sum(dz_one, axis=0, keepdims=True)
    sums_ref[6:8, :] = jnp.zeros_like(sums_ref[6:8, :])
    dz_ref[...] = dz_one
    b0_ref[...] = dz_one.astype(BF16)
    for h in range(groups):
        dcon_ref[h] = dot(b0_ref[...], w_ref[h, :, qkv_end:out_end], 1, 0).astype(BF16)


def row_work(cuts, context, x, cot, weights, bias_up, vectors):
    groups, rows, width = context.shape
    model = x.shape[1]
    unit = bias_up.shape[2]
    shape = jax.ShapeDtypeStruct
    args = (context, x, cot, weights, bias_up, vectors)
    return pl.pallas_call(
        functools.partial(rows_kernel, cuts),
        out_shape=(
            shape((rows, model), BF16),
            shape((rows, model), F32),
            shape(context.shape, BF16),
            shape((rows, model), BF16),
            shape((groups, rows, unit), BF16),
            shape((groups, rows, unit), BF16),
            shape((rows, model), BF16),
            shape((rows, model), BF16),
            shape((8, model), F32),
            shape((groups, 1, unit), F32),
        ),
        in_specs=[pl.BlockSpec(memory_space=pltpu.VMEM)] * len(args),
        out_specs=(pl.BlockSpec(memory_space=pltpu.VMEM),) * 10,
        scratch_shapes=[
            pltpu.VMEM((groups, rows, unit), F32),
            pltpu.VMEM((rows, model), F32),
            pltpu.VMEM((rows, model), F32),
            pltpu.VMEM((rows, model), F32),
            pltpu.VMEM((rows, 1), F32),
        ],
        compiler_params=params(),
        cost_estimate=cost(8 * groups * rows * model * (unit + width), 2 * weights.size),
        name="row_work",
    )(*args)


def input_kernel(dqkv_ref, w_ref, dz_ref, o_ref):
    total = dz_ref[...]
    for h in range(dqkv_ref.shape[0]):
        total = total + dot(dqkv_ref[h], w_ref[h, :, : dqkv_ref.shape[2]], 1, 1)
    share = o_ref.shape[2]
    for h in range(o_ref.shape[0]):
        o_ref[h] = total[:, h * share : (h + 1) * share].astype(BF16)


def input_grad(dqkv, weights, dz):
    groups, rows, columns = dqkv.shape
    model = dz.shape[1]
    return pl.pallas_call(
        input_kernel,
        out_shape=jax.ShapeDtypeStruct((groups, rows, model // groups), BF16),
        grid=(1,),
        in_specs=[
            whole(dqkv),
            pl.BlockSpec((groups, model, model), lambda i: (0, 0, 0)),
            whole(dz),
        ],
        out_specs=pl.BlockSpec((groups, rows, model // groups), lambda i: (0, 0, 0)),
        compiler_params=params(),
        cost_estimate=cost(2 * groups * rows * columns * model, 2 * groups * columns * model),
        name="input_grad",
    )(dqkv, weights, dz)


def weight_kernel(cuts, micros, heads, slots, *refs):
    out_ref, vector_scr = refs[-2:]
    qkv_end, out_end, up_end, down_end = cuts

    def summed(family):
        total = family[0][...]
        for ref in family[1:]:
            total = total + ref[...]
        return total

    def product(lefts, rights):
        total = None
        for left, right in zip(lefts, rights):
            term = dot(left[...], right[0], 0, 0)
            total = term if total is None else total + term
        return total.astype(BF16)

    x, b0, h1, b2, dqkv, con, b1, act, own, plain, up = (
        refs[i * micros : (i + 1) * micros] for i in range(11)
    )
    out_ref[0, :, 0:qkv_end] = product(x, dqkv)
    out_ref[0, :, qkv_end:out_end] = product(b0, con)
    out_ref[0, :, out_end:up_end] = product(h1, b1)
    out_ref[0, :, up_end:down_end] = product(b2, act)

    own_sum = jnp.where(pl.program_id(0) == lax.axis_index("head"), summed(own), 0.0)
    plain_sum, up_sum = summed(plain), summed(up)[0]
    rows = out_ref.shape[1] // slots
    lanes = plain_sum.shape[1] // slots
    unit = up_sum.shape[1] // heads
    vector_scr[...] = jnp.zeros_like(vector_scr)
    for s in range(slots):
        vector_scr[:8, :lanes] = plain_sum[:, s * lanes : (s + 1) * lanes]
        for j in range(heads):
            at, step = j * HEAD_DIM + s * (HEAD_DIM // slots), HEAD_DIM // slots
            vector_scr[QUERY_AT + j : QUERY_AT + j + 1, :step] = own_sum[0:1, at : at + step]
            vector_scr[VALUE_AT + j : VALUE_AT + j + 1, :step] = own_sum[1:2, at : at + step]
            at, step = j * unit + s * (unit // slots), unit // slots
            vector_scr[UP_AT + j : UP_AT + j + 1, :step] = up_sum[:, at : at + step]
        out_ref[0, s * rows : s * rows + VECTOR_ROWS, down_end:] = vector_scr[...].astype(BF16)
        out_ref[0, s * rows + VECTOR_ROWS : (s + 1) * rows, down_end:] = jnp.zeros(
            (rows - VECTOR_ROWS, 128), BF16
        )


def weight_grads(cuts, heads, slots, lefts, rights, own, plain, up):
    micros = len(lefts[0])
    groups = rights[0][0].shape[0]
    model = lefts[0][0].shape[1]
    flat_left = [a for family in lefts for a in family]
    flat_right = [a for family in rights for a in family]
    rows = flat_left[0].shape[0]
    columns = cuts[-1] + 128

    def per_group(a):
        return pl.BlockSpec((1, *a.shape[1:]), lambda h: (h, 0, 0))

    return pl.pallas_call(
        functools.partial(weight_kernel, cuts, micros, heads, slots),
        out_shape=jax.ShapeDtypeStruct((groups, model, columns), BF16),
        grid=(groups,),
        in_specs=[whole(a) for a in flat_left]
        + [per_group(a) for a in flat_right]
        + [whole(a) for a in (*own, *plain)]
        + [per_group(a) for a in up],
        out_specs=pl.BlockSpec((1, model, columns), lambda h: (h, 0, 0)),
        scratch_shapes=[pltpu.VMEM((VECTOR_ROWS, 128), F32)],
        compiler_params=params(),
        cost_estimate=cost(2 * micros * groups * rows * model * cuts[-1], 2 * groups * model * cuts[-1]),
        name="weight_grads",
    )(*flat_left, *flat_right, *own, *plain, *up)


MESH = pl.DeviceIdType.MESH
SIDE = 2


def remote(source, target, send_sem, recv_sem, device):
    return pltpu.make_async_remote_copy(
        src_ref=source,
        dst_ref=target,
        send_sem=send_sem,
        recv_sem=recv_sem,
        device_id=device,
        device_id_type=MESH,
    )


def signal(device):
    pl.semaphore_signal(
        pltpu.get_barrier_semaphore(), inc=1, device_id=device, device_id_type=MESH
    )


def greet(devices):
    for device in devices:
        signal(device)
    pl.semaphore_wait(pltpu.get_barrier_semaphore(), len(devices))


def cross_kernel(groups, x_ref, o_ref, send_sem, recv_sem, own_sem):
    me = lax.axis_index("head")
    peers = [lax.rem(me + i, groups) for i in range(1, groups)]
    greet([{"head": peer} for peer in peers])
    copies = []
    for i, peer in enumerate(peers):
        copy = remote(x_ref.at[peer], o_ref.at[me], send_sem.at[i], recv_sem.at[i], {"head": peer})
        copy.start()
        copies.append(copy)
    own = pltpu.make_async_copy(x_ref.at[me], o_ref.at[me], own_sem)
    own.start()
    own.wait()
    for copy in copies:
        copy.wait()


def across_heads(x, number):
    groups = x.shape[0]
    return pl.pallas_call(
        functools.partial(cross_kernel, groups),
        out_shape=jax.ShapeDtypeStruct(x.shape, x.dtype),
        in_specs=[pl.BlockSpec(memory_space=pltpu.VMEM)],
        out_specs=pl.BlockSpec(memory_space=pl.ANY),
        scratch_shapes=[
            pltpu.SemaphoreType.DMA((groups - 1,)),
            pltpu.SemaphoreType.DMA((groups - 1,)),
            pltpu.SemaphoreType.DMA,
        ],
        compiler_params=params(collective_id=number, has_side_effects=True),
        cost_estimate=cost(0, 40 * x.size),
        name="across_heads",
    )(x)


SIDES = 2
LINE = 4


class Place:
    def __init__(self):
        self.here, self.head = lax.axis_index("seq"), lax.axis_index("head")
        self.z, self.x = self.here // SIDES, lax.rem(self.here, SIDES)
        self.y, self.c = self.head // 2, lax.rem(self.head, 2)
        self.up, self.down = {"seq": self.here + SIDES}, {"seq": self.here - SIDES}
        self.across = {"seq": self.z * SIDES + (1 - self.x)}
        self.over = {"head": (1 - self.y) * 2 + self.c}
        self.beside = {"head": self.y * 2 + (1 - self.c)}
        self.not_last, self.not_first = self.z < LINE - 1, self.z > 0
        half = (LINE - 1 - self.z) // 2
        self.order = [self.z, self.z + 1 - 2 * lax.rem(self.z, 2), 1 + half, (LINE - 1) * half]

    def greet_neighbours(self):
        pl.when(self.not_last)(lambda: signal(self.up))
        pl.when(self.not_first)(lambda: signal(self.down))
        for device in (self.across, self.over, self.beside):
            signal(device)
        return 3 + self.not_last.astype(jnp.int32) + self.not_first.astype(jnp.int32)


def arrived(block, send_sem, recv_sem, device):
    remote(block, block, send_sem, recv_sem, device).wait_recv()


def line_kernel(
    slots, groups, pack_ref, piece_ref, all_ref, rows_ref,
    z_s, z_r, x_s, x_r, y_s, y_r, piece_s, piece_r, own_sem,
):
    me = Place()
    here, head, x, y, c = me.here, me.head, me.x, me.y, me.c
    group = lax.rem(head - here + slots, groups)
    homes = [group * SIDE + p for p in range(SIDE)]
    targets = [
        lax.rem(head - me.z + groups, groups) + groups * lax.rem(here + step, 2) for step in range(2)
    ]
    expected = me.greet_neighbours()
    for home in homes:
        pl.when(home != here)(lambda home=home: signal({"seq": home}))
    for target in targets:
        expected = expected + (target != here).astype(jnp.int32)
    pl.semaphore_wait(pltpu.get_barrier_semaphore(), expected)

    def at(i, side, row):
        return all_ref.at[row * 2 + c, i * SIDES + side]

    def source(k):
        return pack_ref if k == 0 else at(me.order[k], x, y)

    def upward(k):
        i = me.order[k]
        return remote(source(k), at(i, x, y), z_s.at[i], z_r.at[i], me.up)

    def downward(k):
        i = me.order[k]
        return remote(source(k), at(i, x, y), z_s.at[LINE + i], z_r.at[i], me.down)

    def over_x(k):
        i = me.order[k]
        return remote(source(k), at(i, x, y), x_s.at[i], x_r.at[i], me.across)

    def over_y(k):
        i = me.order[k]
        return remote(source(k), at(i, x, y), y_s.at[i], y_r.at[i], me.over)

    def goes_up(k):
        return (me.order[k] <= me.z) & me.not_last

    def goes_down(k):
        return (me.order[k] >= me.z) & me.not_first

    def piece(step):
        return remote(
            piece_ref.at[step], rows_ref.at[:, x], piece_s.at[step], piece_r.at[x], {"seq": targets[step]}
        )

    def piece_here(step):
        return pltpu.make_async_copy(piece_ref.at[step], rows_ref.at[:, x], own_sem.at[1])

    own = pltpu.make_async_copy(pack_ref, at(me.z, x, y), own_sem.at[0])
    own.start()
    for k in range(LINE):
        i = me.order[k]
        if k:
            arrived(at(i, x, y), z_s.at[i], z_r.at[i], me.up)
        pl.when(goes_up(k))(lambda k=k: upward(k).start())
        pl.when(goes_down(k))(lambda k=k: downward(k).start())
        over_x(k).start()
        over_y(k).start()
        if k == 2:
            for step, target in enumerate(targets):
                pl.when(target != here)(lambda step=step: piece(step).start())
                pl.when(target == here)(lambda step=step: piece_here(step).start())
    for k in range(LINE):
        i = me.order[k]
        arrived(at(i, 1 - x, y), x_s.at[i], x_r.at[i], me.across)
        arrived(at(i, x, 1 - y), y_s.at[i], y_r.at[i], me.over)
    for p, home in enumerate(homes):
        block = rows_ref.at[:, p]
        pl.when(home != here)(
            lambda block=block, p=p, home=home: arrived(
                block, piece_s.at[p], piece_r.at[p], {"seq": home}
            )
        )
    for step, target in enumerate(targets):
        pl.when(target != here)(lambda step=step: piece(step).wait_send())
        pl.when(target == here)(lambda step=step: piece_here(step).wait())
    own.wait()
    for k in range(LINE):
        pl.when(goes_up(k))(lambda k=k: upward(k).wait_send())
        pl.when(goes_down(k))(lambda k=k: downward(k).wait_send())
        over_x(k).wait_send()
        over_y(k).wait_send()


def gather_line(packed, pieces, slots, groups, number):
    dma = pltpu.SemaphoreType.DMA
    return pl.pallas_call(
        functools.partial(line_kernel, slots, groups),
        out_shape=(
            jax.ShapeDtypeStruct((groups, slots, *packed.shape), packed.dtype),
            jax.ShapeDtypeStruct((pieces.shape[1], SIDE, *pieces.shape[2:]), pieces.dtype),
        ),
        in_specs=[pl.BlockSpec(memory_space=pltpu.VMEM)] * 2,
        out_specs=(ANYWHERE,) * 2,
        scratch_shapes=[dma((2 * LINE,)), dma((LINE,))] + [dma((LINE,))] * 4 + [dma((2,))] * 3,
        compiler_params=params(collective_id=number, has_side_effects=True),
        cost_estimate=cost(0, 3000000 * 20),
        name="gather_line",
    )(packed, pieces)


def plane_kernel(in_ref, all_ref, y_s, y_r, c_s, c_r):
    me = Place()
    x, y, c = me.x, me.y, me.c
    greet([me.over, me.beside])

    def at(i, side, row, core=c):
        return all_ref.at[row * 2 + core, i * SIDES + side]

    def over_y(i):
        block = at(i, 1 - x, y)
        return remote(block, block, y_s.at[i], y_r.at[i], me.over)

    places = ((x, y), (1 - x, y), (x, 1 - y), (1 - x, 1 - y))

    def to_core(i, kind):
        n = kind * LINE + i
        block = at(i, *places[kind])
        return remote(block, block, c_s.at[n], c_r.at[n], me.beside)

    for i in range(LINE):
        over_y(i).start()
    for kind in range(3):
        for i in range(LINE):
            to_core(i, kind).start()
    for i in range(LINE):
        arrived(at(i, 1 - x, 1 - y), y_s.at[i], y_r.at[i], me.over)
        to_core(i, 3).start()
    for kind, (side, row) in enumerate(places):
        for i in range(LINE):
            n = kind * LINE + i
            arrived(at(i, side, row, 1 - c), c_s.at[n], c_r.at[n], me.beside)
    for i in range(LINE):
        over_y(i).wait_send()
        for kind in range(4):
            to_core(i, kind).wait_send()


def gather_plane(shards, number):
    dma = pltpu.SemaphoreType.DMA
    return pl.pallas_call(
        plane_kernel,
        out_shape=jax.ShapeDtypeStruct(shards.shape, shards.dtype),
        in_specs=[ANYWHERE],
        out_specs=ANYWHERE,
        scratch_shapes=[dma((LINE,))] * 2 + [dma((4 * LINE,))] * 2,
        input_output_aliases={0: 0},
        compiler_params=params(collective_id=number, has_side_effects=True),
        cost_estimate=cost(0, 3000000 * 40),
        name="gather_plane",
    )(shards)


def add_into(target, terms, shape):
    rows = shape[-2]
    tile = 16
    steps = rows // tile
    outer = 1
    for n in shape[:-2]:
        outer *= n

    def body(i, carry):
        at = pl.ds(pl.multiple_of(lax.rem(i, steps) * tile, tile), tile)
        rest = i // steps
        index = []
        for n in reversed(shape[:-2]):
            index.insert(0, lax.rem(rest, n))
            rest = rest // n
        index = (*index, at)
        total = terms[0][index].astype(F32)
        for term in terms[1:]:
            total = total + term[index].astype(F32)
        target[index] = total.astype(target.dtype)
        return carry

    lax.fori_loop(0, outer * steps, body, 0)


def finish_kernel(
    slots, groups, micros, part_ref, y_ref, dx_ref, sum_ref, tokens_ref, grads_ref,
    held, first, second, line,
    c_s, c_r, x_s, x_r, y_s, y_r, z_s, z_r, home_s, home_r, over_s, over_r, near_s, near_r, pass_s, pass_r,
    grad_s, grad_r, own_sem,
):
    me = Place()
    here, head, x, y, z, c = me.here, me.head, me.x, me.y, me.z, me.c
    order = me.order[::-1]
    group = lax.rem(head - here + slots, groups)
    homes = [group * SIDE + p for p in range(SIDE)]
    mine = lax.rem(head - z + groups, groups)
    senders = [lax.rem(slot + z, groups) for slot in range(slots)]

    def is_me(slot, other):
        return (slot == here) & (other == head)

    expected = me.greet_neighbours()
    for slot in range(slots):
        pl.when(jnp.logical_not(is_me(slot, senders[slot])))(
            lambda slot=slot: signal({"seq": slot, "head": senders[slot]})
        )
    for home in homes:
        for h in range(groups):
            expected = expected + 1 - is_me(home, h).astype(jnp.int32)
    pl.semaphore_wait(pltpu.get_barrier_semaphore(), expected)

    def to_core(k, row):
        i = order[k]
        n = row * LINE + i
        return remote(
            part_ref.at[row * 2 + (1 - c), i], held.at[i, row], c_s.at[n], c_r.at[n], me.beside
        )

    sides = (1 - x, x)

    def over_y(k, n):
        i = order[k]
        at = n * LINE + i
        return remote(
            held.at[i, 1 - y, sides[n]], first.at[i, sides[n]], y_s.at[at], y_r.at[at], me.over
        )

    def over_x(k):
        i = order[k]
        return remote(held.at[i, y, 1 - x], second.at[i], x_s.at[i], x_r.at[i], me.across)

    def upward(k):
        i = order[k]
        return remote(held.at[i, y, x], line.at[0, i], z_s.at[i], z_r.at[i], me.up)

    def downward(k):
        i = order[k]
        n = LINE + i
        return remote(held.at[i, y, x], line.at[1, i], z_s.at[n], z_r.at[n], me.down)

    rows, columns = sum_ref.shape

    def begin(k):
        i = order[k]
        for row in (1 - y, y):
            n = row * LINE + i
            arrived(held.at[i, row], c_s.at[n], c_r.at[n], me.beside)
        block = held.at[i, 1 - y]
        add_into(block, [block, part_ref.at[(1 - y) * 2 + c, i]], (SIDES, rows, columns))
        over_y(k, 0).start()
        over_y(k, 1).start()
        block = held.at[i, y]
        add_into(block, [block, part_ref.at[y * 2 + c, i]], (SIDES, rows, columns))

    def middle(k):
        i = order[k]
        for n, side in enumerate(sides):
            at = n * LINE + i
            arrived(first.at[i, side], y_s.at[at], y_r.at[at], me.over)
            block = held.at[i, y, side]
            add_into(block, [block, first.at[i, side]], (rows, columns))
            if n == 0:
                over_x(k).start()

    def end(k):
        i = order[k]
        n = LINE + i
        last = k == LINE - 1
        arrived(second.at[i], x_s.at[i], x_r.at[i], me.across)
        target = sum_ref if last else held.at[i, y, x]
        add_into(target, [held.at[i, y, x], second.at[i]], (rows, columns))

        def below():
            arrived(line.at[0, i], z_s.at[i], z_r.at[i], me.up)
            add_into(target, [target, line.at[0, i]], (rows, columns))

        def above():
            arrived(line.at[1, i], z_s.at[n], z_r.at[n], me.up)
            add_into(target, [target, line.at[1, i]], (rows, columns))

        pl.when((i >= z) & me.not_first)(below)
        pl.when((i <= z) & me.not_last)(above)
        if not last:
            pl.when(i > z)(lambda: upward(k).start())
            pl.when(i < z)(lambda: downward(k).start())

    def home_copy(m, p):
        n = m * SIDE + p
        return remote(
            y_ref.at[m, p], tokens_ref.at[m, here], home_s.at[n], home_r.at[m * 2 + here // groups], {"seq": homes[p]}
        )

    def home_here(m, p):
        return pltpu.make_async_copy(y_ref.at[m, p], tokens_ref.at[m, here], own_sem.at[m])

    def grad_copy(m, p, h):
        n = (m * SIDE + p) * groups + h
        return remote(
            dx_ref.at[m, h, p], grads_ref.at[m, here], grad_s.at[n], grad_r.at[m * slots + here],
            {"seq": homes[p], "head": h},
        )

    def grad_here(m, p, h):
        return pltpu.make_async_copy(dx_ref.at[m, h, p], grads_ref.at[m, here], own_sem.at[micros + m])

    def slot_of(other, j):
        return lax.rem(other - z + groups, groups) + groups * j

    far_head, near_head = (1 - y) * 2 + c, y * 2 + (1 - c)
    last_head = (1 - y) * 2 + (1 - c)

    def far(m, j):
        n, block = m * 2 + j, tokens_ref.at[m, slot_of(head, j)]
        return remote(block, block, over_s.at[n], over_r.at[n], me.over)

    def near(m, j):
        n, block = m * 2 + j, tokens_ref.at[m, slot_of(head, j)]
        return remote(block, block, near_s.at[n], near_r.at[n], me.beside)

    def passed(m, j):
        n, block = m * 2 + j, tokens_ref.at[m, slot_of(far_head, j)]
        return remote(block, block, pass_s.at[n], pass_r.at[n], me.beside)

    for k in range(LINE):
        for row in range(2):
            to_core(k, row).start()
    for m in range(micros):
        for p, home in enumerate(homes):
            pl.when(home != here)(lambda m=m, p=p: home_copy(m, p).start())
            pl.when(home == here)(lambda m=m, p=p: home_here(m, p).start())
            for h in range(groups):
                same = is_me(home, h)
                pl.when(jnp.logical_not(same))(lambda m=m, p=p, h=h: grad_copy(m, p, h).start())
                pl.when(same)(lambda m=m, p=p, h=h: grad_here(m, p, h).start())
    for k in range(LINE):
        begin(k)
        if k >= 1:
            middle(k - 1)
        if k >= 2:
            end(k - 2)
    middle(LINE - 1)
    end(LINE - 2)
    for m in range(micros):
        for p, home in enumerate(homes):
            pl.when(home == here)(lambda m=m, p=p: home_here(m, p).wait())
        for j in range(2):
            slot = slot_of(head, j)
            pl.when(slot != here)(
                lambda m=m, j=j, slot=slot: arrived(
                    tokens_ref.at[m, slot], home_s.at[m * 2 + j], home_r.at[m * 2 + j], {"seq": slot}
                )
            )
            far(m, j).start()
            near(m, j).start()
    end(LINE - 1)
    for m in range(micros):
        for j in range(2):
            n = m * 2 + j
            arrived(tokens_ref.at[m, slot_of(far_head, j)], over_s.at[n], over_r.at[n], me.over)
            passed(m, j).start()
    for m in range(micros):
        for j in range(2):
            n = m * 2 + j
            arrived(tokens_ref.at[m, slot_of(near_head, j)], near_s.at[n], near_r.at[n], me.beside)
            arrived(tokens_ref.at[m, slot_of(last_head, j)], pass_s.at[n], pass_r.at[n], me.beside)
        for slot in range(slots):
            n = m * slots + slot
            pl.when(jnp.logical_not(is_me(slot, senders[slot])))(
                lambda m=m, n=n, slot=slot: arrived(
                    grads_ref.at[m, slot], grad_s.at[0], grad_r.at[n], {"seq": slot, "head": senders[slot]}
                )
            )
    for m in range(micros):
        for p, home in enumerate(homes):
            pl.when(home != here)(lambda m=m, p=p: home_copy(m, p).wait_send())
            for h in range(groups):
                same = is_me(home, h)
                pl.when(jnp.logical_not(same))(lambda m=m, p=p, h=h: grad_copy(m, p, h).wait_send())
                pl.when(same)(lambda m=m, p=p, h=h: grad_here(m, p, h).wait())
        for j in range(2):
            far(m, j).wait_send()
            near(m, j).wait_send()
            passed(m, j).wait_send()
    for k in range(LINE):
        for row in range(2):
            to_core(k, row).wait_send()
        over_y(k, 0).wait_send()
        over_y(k, 1).wait_send()
        over_x(k).wait_send()
        if k < LINE - 1:
            i = order[k]
            pl.when(i > z)(lambda k=k: upward(k).wait_send())
            pl.when(i < z)(lambda k=k: downward(k).wait_send())


def finish(part, y, dx, slots, groups, number):
    columns = part.shape[-1]
    micros, _, piece, model = y.shape
    rows = part.shape[-2]
    dma = pltpu.SemaphoreType.DMA
    vmem = pltpu.VMEM
    part = part.reshape(groups, LINE, SIDES, rows, columns)
    return pl.pallas_call(
        functools.partial(finish_kernel, slots, groups, micros),
        out_shape=(
            jax.ShapeDtypeStruct((rows, columns), F32),
            jax.ShapeDtypeStruct((micros, slots, piece, model), BF16),
            jax.ShapeDtypeStruct((micros, slots, piece, dx.shape[-1]), BF16),
        ),
        in_specs=[pl.BlockSpec(memory_space=pltpu.VMEM)] * 3,
        out_specs=(pl.BlockSpec(memory_space=pltpu.VMEM),) + (pl.BlockSpec(memory_space=pl.ANY),) * 2,
        scratch_shapes=[
            vmem((LINE, 2, SIDES, rows, columns), BF16),
            vmem((LINE, SIDES, rows, columns), BF16),
            vmem((LINE, rows, columns), BF16),
            vmem((2, LINE, rows, columns), BF16),
        ]
        + [dma((2 * LINE,))] * 8
        + [dma((2 * micros,))] * 8
        + [dma((2 * groups * micros,)), dma((slots * micros,)), dma((2 * micros,))],
        compiler_params=params(collective_id=number, has_side_effects=True),
        cost_estimate=cost(0, 3000000 * 40),
        name="finish",
    )(part, y, dx)


def order_kernel(micros, slots, index_ref, *refs):
    count = (len(refs) - 2) // 3
    inputs, outputs, buffers = refs[:count], refs[count : 2 * count], refs[2 * count : 3 * count]
    in_sem, out_sem = refs[-2:]
    where = [(n, m, i) for m in range(micros) for n in range(count) for i in range(slots)]
    move_blocks(
        [inputs[n].at[m, index_ref[m, i]] for n, m, i in where],
        [outputs[n].at[m, i] for n, m, i in where],
        [buffers[n].at[m, i] for n, m, i in where],
        in_sem,
        out_sem,
    )


def in_order(arrays, index):
    micros, slots = arrays[0].shape[:2]
    total = len(arrays) * micros * slots
    dma = pltpu.SemaphoreType.DMA
    return pl.pallas_call(
        functools.partial(order_kernel, micros, slots),
        out_shape=tuple(jax.ShapeDtypeStruct(a.shape, a.dtype) for a in arrays),
        in_specs=[SMALL] + [ANYWHERE for _ in arrays],
        out_specs=tuple(ANYWHERE for _ in arrays),
        scratch_shapes=[pltpu.VMEM(a.shape, a.dtype) for a in arrays] + [dma((total,)), dma((total,))],
        compiler_params=params(),
        cost_estimate=cost(0, 4 * sum(a.size for a in arrays)),
        name="in_order",
    )(index, *arrays)


def fits(mesh):
    return dict(mesh.shape) == {"seq": 8, "head": 4}


def on_device(
    tokens,
    prev_logits,
    lengths,
    dealing,
    w_query,
    b_query,
    w_key,
    w_value,
    b_value,
    w_out,
    b_out,
    gain_one,
    shift_one,
    w_up,
    b_up,
    w_down,
    b_down,
    gain_two,
    shift_two,
    cot_tokens,
    cot_logits,
):
    slots, groups = lax.axis_size("seq"), lax.axis_size("head")
    grid = ("seq", "head")
    here, head = lax.axis_index("seq"), lax.axis_index("head")
    micros, _, piece, model = tokens.shape
    heads = prev_logits.shape[3]
    extent = piece * slots
    width = heads * HEAD_DIM
    unit = w_up.shape[1]
    per = slots // groups
    cuts = (3 * width, 3 * width + width, 3 * width + width + unit, 3 * width + width + 2 * unit)
    own_rows = model // slots

    inverse = [
        jnp.sum(
            jnp.where(
                dealing[m][None, :] == jnp.arange(slots, dtype=jnp.int32)[:, None],
                jnp.arange(slots, dtype=jnp.int32)[None, :],
                0,
            ),
            axis=1,
        ).astype(jnp.int32)
        for m in range(micros)
    ]
    info = [
        jnp.stack([lengths[m, inverse[m][here]], here % groups]).astype(jnp.int32)
        for m in range(micros)
    ]
    prev = jnp.transpose(prev_logits, (0, 1, 3, 2, 4))
    cot_square = jnp.transpose(cot_logits[:, 0], (0, 2, 1, 3))

    first_send, pieces, packed = prepare(
        dealing,
        prev,
        tokens,
        cot_tokens,
        (w_query, w_key, w_value, w_out.T, w_up, w_down.T),
        (b_query, b_value, b_up),
        [v.reshape(1, -1) for v in (b_out, gain_one, shift_one, b_down, gain_two, shift_two)],
        groups,
    )
    line, arrived_rows = gather_line(packed, pieces, slots, groups, 1)
    rows = per * piece
    rows_all = arrived_rows.reshape(2 * micros, rows, model)
    rows_in, cot_rows = rows_all[:micros], rows_all[micros:]

    weights = gather_plane(line, 2)
    weights = weights.reshape(groups, slots, own_rows, -1)
    bias_qkv, bias_up, row_vectors = unpack_vectors(weights, heads, width, unit, model)
    weights = weights.reshape(groups, model, -1)

    projected = project(rows_in, weights, bias_qkv)
    first_qkv = across_heads(projected[0], 3)
    got_prev, after = [], arrived_rows
    for m in range(micros):
        send = pick_blocks(prev, m, dealing) if m else first_send
        send, _ = lax.optimization_barrier((send, after))
        got = lax.all_to_all(send, "seq", split_axis=0, concat_axis=0, tiled=True)
        got_prev.append(got)
        after = (got, first_qkv)

    second_qkv = [across_heads(projected[m], 3) for m in range(1, micros)]
    logits, grad_logits = None, None
    kept, sums_own, sums_rows, sums_up, returned, sent = [], [], [], [], [], []
    for m in range(micros):
        qkv = second_qkv[m - 1] if m else first_qkv
        logits, attend, context = attention_forward(info[m], qkv, got_prev[m], m, micros, logits)
        context_rows = across_heads(context, 4)
        y, dz, dcon, h1, act, b1, b2, b0, sums, dbup = row_work(
            cuts, context_rows, rows_in[m], cot_rows[m], weights, bias_up, row_vectors
        )
        dcontext = across_heads(dcon, 4)
        send, dqkv, own = attention_backward(
            info[m], qkv, attend, context, dcontext, cot_square, m
        )
        dqkv = across_heads(dqkv, 5)
        dx = input_grad(dqkv, weights, dz)
        kept.append((rows_in[m], b0, h1, b2, dqkv, context_rows, b1, act))
        sums_own.append(own)
        sums_rows.append(sums)
        sums_up.append(dbup)
        returned.append((y, dx))
        if m == 0:
            send, _ = lax.optimization_barrier((send, (dx, second_qkv)))
            after = lax.all_to_all(send, "seq", split_axis=0, concat_axis=0, tiled=True)
            sent.append(after)
        else:
            sent.append(send)

    families = list(zip(*kept))
    part = weight_grads(cuts, heads, slots, families[:4], families[4:], sums_own, sums_rows, sums_up)
    for m in range(micros):
        if m:
            send, _ = lax.optimization_barrier((sent[m], (sent[m - 1], part)))
            sent[m] = lax.all_to_all(send, "seq", split_axis=0, concat_axis=0, tiled=True)
        grad_logits = place_blocks(sent[m], m, micros, dealing[m], grad_logits)
    ys = jnp.stack([y for y, _ in returned]).reshape(micros, per, piece, model)
    dxs = jnp.stack([dx for _, dx in returned]).reshape(micros, groups, per, piece, -1)
    part = part.reshape(groups, slots, own_rows, -1)
    part, all_y, all_dx = finish(part, ys, dxs, slots, groups, 7)
    out_tokens, grad_tokens = in_order((all_y, all_dx), dealing)

    def plain_out(i):
        return part[i, cuts[-1] : cuts[-1] + own_rows]

    def head_out(first, count):
        return part[first : first + heads, cuts[-1] : cuts[-1] + count]

    def columns(start, count):
        return part[:, start : start + count]

    return (
        out_tokens,
        jnp.transpose(logits, (0, 2, 1, 3))[:, None],
        grad_tokens,
        jnp.transpose(grad_logits, (0, 1, 3, 2, 4)),
        columns(0, width),
        head_out(QUERY_AT, HEAD_DIM // slots),
        columns(width, width),
        columns(2 * width, width),
        head_out(VALUE_AT, HEAD_DIM // slots),
        columns(3 * width, width).T,
        plain_out(0),
        plain_out(1),
        plain_out(2),
        columns(cuts[1], unit),
        head_out(UP_AT, unit // heads // slots),
        columns(cuts[2], unit).T,
        plain_out(3),
        plain_out(4),
        plain_out(5),
    )


def solution(mesh):
    placed = (
        P(None, None, "seq", None),
        P(None, None, "seq", "head", None),
        P(),
        P(),
        P("seq", "head"),
        P("head", "seq"),
        P("seq", "head"),
        P("seq", "head"),
        P("head", "seq"),
        P("head", "seq"),
        P("seq"),
        P("seq"),
        P("seq"),
        P("seq", "head"),
        P("head", "seq"),
        P("head", "seq"),
        P("seq"),
        P("seq"),
        P("seq"),
        P(None, None, "seq", None),
        P(None, "seq", None, "head", None),
    )
    return jax.shard_map(
        on_device if fits(mesh) else on_device_general,
        mesh=mesh,
        in_specs=placed,
        out_specs=(
            P(None, None, "seq", None),
            P(None, "seq", None, "head", None),
            P(None, None, "seq", "head"),
            P(None, None, "seq", "head", None),
            P("seq", "head"),
            P("head", "seq"),
            P("seq", "head"),
            P("seq", "head"),
            P("head", "seq"),
            P("head", "seq"),
            P("seq"),
            P("seq"),
            P("seq"),
            P("seq", "head"),
            P("head", "seq"),
            P("head", "seq"),
            P("seq"),
            P("seq"),
            P("seq"),
        ),
        check_vma=False,
    )
```

```python
import functools

import jax
import jax.numpy as jnp
from jax import lax
from jax.experimental import pallas as pl
from jax.experimental.pallas import tpu as pltpu
from jax.sharding import PartitionSpec as P

HEAD_DIM = 64
BF16, F32 = jnp.bfloat16, jnp.float32
VMEM_LIMIT = 60 * 1024 * 1024


epsilon = 1e-12


def cut_along(x, dim, peers):
    before, after = (x.shape[:dim], x.shape[dim + 1 :])
    return jnp.moveaxis(x.reshape(*before, peers, -1, *after), dim, 0)


def sum_at_owner(x, axis, dim):
    blocks = cut_along(x, dim, lax.axis_size(axis))
    arrived = lax.all_to_all(blocks, axis, split_axis=0, concat_axis=0, tiled=True)
    return arrived.astype(jnp.float32).sum(axis=0)


def side_by_side(arrays, axis, dim, along):
    both = jnp.concatenate(arrays, axis=along)
    result, at, finished = (sum_at_owner(both, axis, dim), 0, [])
    for a in arrays:
        finished.append(lax.slice_in_dim(result, at, at + a.shape[along], axis=along))
        at += a.shape[along]
    return tuple(finished)


def side_by_side_2(arrays, axis, dim, along):
    columns = [a.reshape(*a.shape[:along], -1) for a in arrays]
    both = jnp.concatenate(columns, axis=along)
    result, at, finished = (sum_at_owner(both, axis, dim), 0, [])
    for a, column in zip(arrays, columns):
        slab = result[..., at : at + column.shape[along]]
        finished.append(slab.reshape(*slab.shape[:along], *a.shape[along:]))
        at += column.shape[along]
    return tuple(finished)


def layer_norm(values, gain, shift):
    center = values - jnp.mean(values, axis=-1, keepdims=True)
    spread = jnp.mean(center * center, axis=-1, keepdims=True)
    return center * lax.rsqrt(spread + epsilon) * gain + shift


def exact_gelu(values):
    return jax.nn.gelu(values, approximate=False)


def mask_scores(raw_scores, length):
    key_valid = jnp.arange(raw_scores.shape[2]) < length
    return jnp.where(key_valid[None, None, :], raw_scores, -jnp.inf)


def on_device_general(
    tokens,
    prev_logits,
    lengths,
    dealing,
    w_query,
    b_query,
    w_key,
    w_value,
    b_value,
    w_out,
    b_out,
    gain_one,
    shift_one,
    w_up,
    b_up,
    w_down,
    b_down,
    gain_two,
    shift_two,
    cot_tokens,
    cot_logits,
):
    micro_count = tokens.shape[0]
    seq_count = tokens.shape[1]
    piece_rows = tokens.shape[2]
    model_width = tokens.shape[3]
    extent = piece_rows * seq_count
    heads_here = prev_logits.shape[3]
    width_here = model_width // lax.axis_size("head")
    score_scale = HEAD_DIM ** (-0.5)
    owner_slot = lax.axis_index("seq")
    head_slot = lax.axis_index("head")
    zero_shift = jnp.zeros((model_width,), jnp.float32)
    out_token_list = []
    out_logit_list = []
    grad_token_list = []
    grad_logit_list = []
    grad_totals = None
    for micro_batch in range(micro_count):
        full_weights = (
            lax.all_gather(w_query, "seq", axis=0, tiled=True),
            lax.all_gather(w_key, "seq", axis=0, tiled=True),
            lax.all_gather(w_value, "seq", axis=0, tiled=True),
            lax.all_gather(w_out, "seq", axis=1, tiled=True),
            lax.all_gather(w_up, "seq", axis=0, tiled=True),
            lax.all_gather(w_down, "seq", axis=1, tiled=True),
            lax.all_gather(b_query, "seq", axis=1, tiled=True),
            lax.all_gather(b_value, "seq", axis=1, tiled=True),
            lax.all_gather(b_out, "seq", axis=0, tiled=True),
            lax.all_gather(gain_one, "seq", axis=0, tiled=True),
            lax.all_gather(shift_one, "seq", axis=0, tiled=True),
            lax.all_gather(b_up, "seq", axis=1, tiled=True),
            lax.all_gather(b_down, "seq", axis=0, tiled=True),
            lax.all_gather(gain_two, "seq", axis=0, tiled=True),
            lax.all_gather(shift_two, "seq", axis=0, tiled=True),
        )
        (
            query_full,
            key_full,
            value_full,
            out_full,
            up_full,
            down_full,
            bias_query,
            bias_value,
            bias_out,
            gain_first,
            shift_first,
            bias_up,
            bias_down,
            gain_second,
            shift_second,
        ) = full_weights
        inverse = (
            jnp.zeros((seq_count,), jnp.int32)
            .at[dealing[micro_batch]]
            .set(jnp.arange(seq_count, dtype=jnp.int32))
        )
        own_sequence = inverse[owner_slot]
        own_length = lengths[micro_batch, own_sequence]
        send_tokens = jnp.take(tokens[micro_batch], inverse, axis=0)
        send_prev = jnp.take(prev_logits[micro_batch], inverse, axis=0).reshape(
            seq_count, piece_rows, heads_here * extent
        )
        send_cot = jnp.take(cot_tokens[micro_batch], inverse, axis=0)
        got_tokens, got_prev, got_cot = (
            lax.all_to_all(send_tokens, "seq", split_axis=0, concat_axis=1, tiled=True),
            lax.all_to_all(send_prev, "seq", split_axis=0, concat_axis=1, tiled=True),
            lax.all_to_all(send_cot, "seq", split_axis=0, concat_axis=1, tiled=True),
        )
        rows_in = got_tokens.reshape(extent, model_width)
        prev_rows = got_prev.reshape(extent, heads_here, extent).astype(jnp.float32)
        cot_rows = got_cot.reshape(extent, model_width).astype(jnp.float32)
        query_pre = jnp.dot(rows_in, query_full, preferred_element_type=jnp.float32)
        queries = (query_pre + bias_query.reshape(-1).astype(jnp.float32)).astype(jnp.bfloat16)
        keys_all = jnp.dot(rows_in, key_full, preferred_element_type=jnp.float32).astype(
            jnp.bfloat16
        )
        value_pre = jnp.dot(rows_in, value_full, preferred_element_type=jnp.float32)
        values = (value_pre + bias_value.reshape(-1).astype(jnp.float32)).astype(jnp.bfloat16)
        query_heads = queries.reshape(extent, heads_here, HEAD_DIM)
        key_heads = keys_all.reshape(extent, heads_here, HEAD_DIM)
        value_heads = values.reshape(extent, heads_here, HEAD_DIM)
        raw_scores = (
            jnp.einsum("qhd,khd->qhk", query_heads, key_heads, preferred_element_type=jnp.float32)
            * score_scale
            + prev_rows
        )
        masked = mask_scores(raw_scores, own_length)
        row_top = jnp.max(masked, axis=-1, keepdims=True)
        shifted_exp = jnp.exp(masked - row_top)
        row_total = jnp.sum(shifted_exp, axis=-1, keepdims=True)
        attend = shifted_exp / row_total
        log_total = row_top + jnp.log(row_total)
        out_logit_list.append(raw_scores.astype(jnp.bfloat16)[None])
        context = (
            jnp.einsum(
                "qhk,khd->qhd",
                attend.astype(jnp.bfloat16),
                value_heads,
                preferred_element_type=jnp.float32,
            )
            .astype(jnp.bfloat16)
            .reshape(extent, heads_here * HEAD_DIM)
        )
        out_part = jnp.dot(context, out_full, preferred_element_type=jnp.float32)
        branch = lax.psum(out_part, "head") + bias_out.astype(jnp.float32)
        resid_one = rows_in.astype(jnp.float32) + branch
        hidden = layer_norm(
            resid_one, gain_first.astype(jnp.float32), shift_first.astype(jnp.float32)
        )
        hidden_low = hidden.astype(jnp.bfloat16)
        before_gelu = jnp.dot(
            hidden_low, up_full, preferred_element_type=jnp.float32
        ) + bias_up.reshape(-1).astype(jnp.float32)
        active = exact_gelu(before_gelu).astype(jnp.bfloat16)
        down_part = jnp.dot(active, down_full, preferred_element_type=jnp.float32)
        resid_two = hidden + (
            lax.psum(down_part.astype(jnp.bfloat16), "head").astype(jnp.float32)
            + bias_down.astype(jnp.float32)
        )
        result = layer_norm(
            resid_two, gain_second.astype(jnp.float32), shift_second.astype(jnp.float32)
        )
        out_rows = result.astype(jnp.bfloat16)
        (
            back_query,
            back_key,
            back_value,
            back_out,
            back_up,
            back_down,
            back_gain_first,
            back_gain_second,
        ) = (
            lax.all_gather(w_query, "seq", axis=0, tiled=True),
            lax.all_gather(w_key, "seq", axis=0, tiled=True),
            lax.all_gather(w_value, "seq", axis=0, tiled=True),
            lax.all_gather(w_out, "seq", axis=1, tiled=True),
            lax.all_gather(w_up, "seq", axis=0, tiled=True),
            lax.all_gather(w_down, "seq", axis=1, tiled=True),
            lax.all_gather(gain_one, "seq", axis=0, tiled=True),
            lax.all_gather(gain_two, "seq", axis=0, tiled=True),
        )
        norm_two_value, norm_two_back = jax.vjp(
            layer_norm, resid_two, back_gain_second.astype(jnp.float32), zero_shift
        )
        d_resid_two, d_gain_two, d_shift_two = norm_two_back(cot_rows)
        d_b_down = jnp.sum(d_resid_two, axis=0)
        grad_two_low = d_resid_two.astype(jnp.bfloat16)
        d_w_down = jnp.einsum("rf,rd->fd", active, grad_two_low, preferred_element_type=jnp.float32)
        d_active = jnp.einsum(
            "rd,fd->rf", grad_two_low, back_down, preferred_element_type=jnp.float32
        )
        gelu_value, gelu_back = jax.vjp(exact_gelu, before_gelu)
        d_before = gelu_back(d_active)[0]
        d_b_up = jnp.sum(d_before, axis=0).reshape(heads_here, -1)
        before_low = d_before.astype(jnp.bfloat16)
        d_w_up = jnp.einsum("rd,rf->df", hidden_low, before_low, preferred_element_type=jnp.float32)
        up_part = jnp.einsum("rf,df->rd", before_low, back_up, preferred_element_type=jnp.float32)
        d_hidden = d_resid_two + lax.psum(up_part.astype(jnp.bfloat16), "head").astype(jnp.float32)
        norm_one_value, norm_one_back = jax.vjp(
            layer_norm, resid_one, back_gain_first.astype(jnp.float32), zero_shift
        )
        d_resid_one, d_gain_one, d_shift_one = norm_one_back(d_hidden)
        d_b_out = jnp.sum(d_resid_one, axis=0)
        grad_one_low = d_resid_one.astype(jnp.bfloat16)
        d_w_out = jnp.einsum("rc,rd->cd", context, grad_one_low, preferred_element_type=jnp.float32)
        d_context = (
            jnp.einsum("rd,cd->rc", grad_one_low, back_out, preferred_element_type=jnp.float32)
            .astype(jnp.bfloat16)
            .reshape(extent, heads_here, HEAD_DIM)
        )
        raw_again = (
            jnp.einsum("qhd,khd->qhk", query_heads, key_heads, preferred_element_type=jnp.float32)
            * score_scale
            + prev_rows
        )
        attend_again = jnp.exp(mask_scores(raw_again, own_length) - log_total)
        d_attend = jnp.einsum(
            "qhd,khd->qhk", d_context, value_heads, preferred_element_type=jnp.float32
        )
        d_values = jnp.einsum(
            "qhk,qhd->khd",
            attend_again.astype(jnp.bfloat16),
            d_context,
            preferred_element_type=jnp.float32,
        )
        d_scores = attend_again * (
            d_attend - jnp.sum(attend_again * d_attend, axis=-1, keepdims=True)
        ) + cot_logits[micro_batch, 0].astype(jnp.float32)
        scores_low = d_scores.astype(jnp.bfloat16)
        d_queries = (
            jnp.einsum("qhk,khd->qhd", scores_low, key_heads, preferred_element_type=jnp.float32)
            * score_scale
        )
        d_keys = (
            jnp.einsum("qhk,qhd->khd", scores_low, query_heads, preferred_element_type=jnp.float32)
            * score_scale
        )
        d_b_query = jnp.sum(d_queries, axis=0)
        d_b_value = jnp.sum(d_values, axis=0)
        queries_low = d_queries.astype(jnp.bfloat16).reshape(extent, heads_here * HEAD_DIM)
        keys_low = d_keys.astype(jnp.bfloat16).reshape(extent, heads_here * HEAD_DIM)
        values_low = d_values.astype(jnp.bfloat16).reshape(extent, heads_here * HEAD_DIM)
        d_w_query = jnp.einsum(
            "rd,rc->dc", rows_in, queries_low, preferred_element_type=jnp.float32
        )
        d_w_key = jnp.einsum("rd,rc->dc", rows_in, keys_low, preferred_element_type=jnp.float32)
        d_w_value = jnp.einsum("rd,rc->dc", rows_in, values_low, preferred_element_type=jnp.float32)
        input_part = jnp.einsum(
            "rc,dc->rd", queries_low, back_query, preferred_element_type=jnp.float32
        )
        input_part = input_part + jnp.einsum(
            "rc,dc->rd", keys_low, back_key, preferred_element_type=jnp.float32
        )
        input_part = input_part + jnp.einsum(
            "rc,dc->rd", values_low, back_value, preferred_element_type=jnp.float32
        )
        input_share = lax.psum_scatter(
            input_part.astype(jnp.bfloat16), "head", scatter_dimension=1, tiled=True
        ).astype(jnp.float32)
        resid_share = lax.dynamic_slice_in_dim(d_resid_one, head_slot * width_here, width_here, 1)
        grad_rows = (resid_share + input_share).astype(jnp.bfloat16)
        back_tokens, back_grads, back_logits = (
            lax.all_to_all(
                out_rows.reshape(seq_count, piece_rows, model_width),
                "seq",
                split_axis=0,
                concat_axis=0,
                tiled=True,
            ),
            lax.all_to_all(
                grad_rows.reshape(seq_count, piece_rows, width_here),
                "seq",
                split_axis=0,
                concat_axis=0,
                tiled=True,
            ),
            lax.all_to_all(
                scores_low.reshape(seq_count, piece_rows, heads_here * extent),
                "seq",
                split_axis=0,
                concat_axis=0,
                tiled=True,
            ),
        )
        out_token_list.append(jnp.take(back_tokens, dealing[micro_batch], axis=0))
        grad_token_list.append(jnp.take(back_grads, dealing[micro_batch], axis=0))
        grad_logit_list.append(
            jnp.take(back_logits, dealing[micro_batch], axis=0).reshape(
                seq_count, piece_rows, heads_here, extent
            )
        )
        local_grads = (
            d_w_query,
            d_b_query,
            d_w_key,
            d_w_value,
            d_b_value,
            d_w_out,
            d_b_out,
            d_gain_one,
            d_shift_one,
            d_w_up,
            d_b_up,
            d_w_down,
            d_b_down,
            d_gain_two,
            d_shift_two,
        )
        if grad_totals is None:
            grad_totals = local_grads
        else:
            grad_totals = tuple((total + extra for total, extra in zip(grad_totals, local_grads)))
    final_grads = (
        sum_at_owner(grad_totals[0].astype(jnp.bfloat16), "seq", 0),
        sum_at_owner(grad_totals[1].astype(jnp.bfloat16), "seq", 1),
        *side_by_side(
            (grad_totals[2].astype(jnp.bfloat16), grad_totals[3].astype(jnp.bfloat16)), "seq", 0, 1
        ),
        sum_at_owner(grad_totals[4].astype(jnp.bfloat16), "seq", 1),
        sum_at_owner(grad_totals[5].astype(jnp.bfloat16), "seq", 1),
        sum_at_owner(grad_totals[6].astype(jnp.bfloat16), "seq", 0),
        sum_at_owner(grad_totals[7].astype(jnp.bfloat16), "seq", 0),
        *side_by_side_2(
            (grad_totals[8].astype(jnp.bfloat16), grad_totals[9].astype(jnp.bfloat16)), "seq", 0, 1
        ),
        sum_at_owner(grad_totals[10].astype(jnp.bfloat16), "seq", 1),
        sum_at_owner(grad_totals[11].astype(jnp.bfloat16), "seq", 1),
        sum_at_owner(grad_totals[12].astype(jnp.bfloat16), "seq", 0),
        sum_at_owner(grad_totals[13].astype(jnp.bfloat16), "seq", 0),
        sum_at_owner(grad_totals[14].astype(jnp.bfloat16), "seq", 0),
    )
    out_tokens = jnp.stack(out_token_list, axis=0)
    out_logits = jnp.stack(out_logit_list, axis=0)
    grad_tokens = jnp.stack(grad_token_list, axis=0)
    grad_logits = jnp.stack(grad_logit_list, axis=0)
    return (
        out_tokens,
        out_logits,
        grad_tokens,
        grad_logits,
        final_grads[0],
        final_grads[1],
        final_grads[2],
        final_grads[3],
        final_grads[4],
        final_grads[5],
        final_grads[6],
        final_grads[7],
        final_grads[8],
        final_grads[9],
        final_grads[10],
        final_grads[11],
        final_grads[12],
        final_grads[13],
        final_grads[14],
    )

def cost(flops, moved):
    return pl.CostEstimate(flops=int(flops) // 100, bytes_accessed=int(moved) // 100, transcendentals=0)


def params(**more):
    return pltpu.CompilerParams(vmem_limit_bytes=VMEM_LIMIT, **more)


def dot(a, b, ca, cb):
    return lax.dot_general(a, b, (((ca,), (cb,)), ((), ())), preferred_element_type=F32)


def whole(x):
    return pl.BlockSpec(x.shape, lambda *_: (0,) * len(x.shape))


def move_blocks(reads, writes, buffers, in_sem, out_sem):
    ins = [pltpu.make_async_copy(r, v, in_sem.at[i]) for i, (r, v) in enumerate(zip(reads, buffers))]
    outs = [pltpu.make_async_copy(v, w, out_sem.at[i]) for i, (v, w) in enumerate(zip(buffers, writes))]
    for copy in ins:
        copy.start()
    for copy, out in zip(ins, outs):
        copy.wait()
        out.start()
    for out in outs:
        out.wait()


SMALL = pl.BlockSpec(memory_space=pltpu.SMEM)
ANYWHERE = pl.BlockSpec(memory_space=pl.ANY)


def inverse_of(dealing_ref, inverse_ref, micros, slots):
    for m in micros:
        for i in range(slots):
            inverse_ref[dealing_ref[m, i]] = i


def pick_copies(micro, count, inverse_ref, x_ref, o_ref, buffer):
    steps = range(count)
    return (
        [x_ref.at[micro, inverse_ref[i]] for i in steps],
        [o_ref.at[i] for i in steps],
        [buffer.at[i] for i in steps],
    )


def pick_kernel(micro, count, dealing_ref, x_ref, o_ref, buffer, inverse_ref, in_sem, out_sem):
    inverse_of(dealing_ref, inverse_ref, [micro], count)
    move_blocks(*pick_copies(micro, count, inverse_ref, x_ref, o_ref, buffer), in_sem, out_sem)


def pick_blocks(stacked, micro, dealing):
    count = stacked.shape[1]
    block = stacked.shape[2:]
    dma = pltpu.SemaphoreType.DMA
    return pl.pallas_call(
        functools.partial(pick_kernel, micro, count),
        out_shape=jax.ShapeDtypeStruct((count, *block), stacked.dtype),
        in_specs=[SMALL, ANYWHERE],
        out_specs=ANYWHERE,
        scratch_shapes=[
            pltpu.VMEM((count, *block), stacked.dtype),
            pltpu.SMEM((count,), jnp.int32),
            dma((count,)),
            dma((count,)),
        ],
        compiler_params=params(),
        cost_estimate=cost(0, 4 * stacked.size // stacked.shape[0]),
        name="pick_blocks",
    )(dealing, stacked)


PLAIN, QUERY_AT, VALUE_AT, UP_AT, VECTOR_ROWS = 6, 8, 16, 24, 32


def prepare_kernel(
    micros, slots, groups, dealing_ref, prev_ref, tokens_ref, cot_ref,
    wq_ref, wk_ref, wv_ref, wo_ref, wu_ref, wd_ref, bq_ref, bv_ref, bu_ref, plain_refs,
    send_ref, piece_ref, pack_ref, info_ref, block_buffer, piece_buffer, vector_scr, inverse_refs, in_sem, out_sem,
    lengths_ref,
):
    here, head = lax.axis_index("seq"), lax.axis_index("head")
    for m in range(micros):
        inverse_of(dealing_ref, inverse_refs[m], [m], slots)
        info_ref[m, 0] = lengths_ref[m, inverse_refs[m][here]]
        info_ref[m, 1] = lax.rem(here, groups)
    reads, writes, buffers = [], [], []
    for step in range(2):
        slot = lax.rem(head - here // 2 + groups, groups) + groups * lax.rem(here + step, 2)
        for a, array_ref in enumerate((tokens_ref, cot_ref)):
            for m in range(micros):
                n = a * micros + m
                reads.append(array_ref.at[m, inverse_refs[m][slot]])
                writes.append(piece_ref.at[step, n])
                buffers.append(piece_buffer.at[step, n])
    blocks = pick_copies(0, slots, inverse_refs[0], prev_ref, send_ref, block_buffer)
    reads, writes, buffers = reads + blocks[0], writes + blocks[1], buffers + blocks[2]
    for i, (source, target) in enumerate(zip(reads, buffers)):
        pltpu.make_async_copy(source, target, in_sem.at[i]).start()

    at = 0
    turned = wo_ref[...].astype(F32).T.astype(BF16)
    for block in (wq_ref[...], wk_ref[...], wv_ref[...], turned, wu_ref[...], wd_ref[...]):
        pack_ref[:, at : at + block.shape[1]] = block
        at += block.shape[1]
    vector_scr[...] = jnp.zeros_like(vector_scr)
    for i, ref in enumerate(plain_refs):
        vector_scr[i : i + 1, : ref.shape[1]] = ref[...].astype(F32)
    for first, ref in ((QUERY_AT, bq_ref), (VALUE_AT, bv_ref), (UP_AT, bu_ref)):
        vector_scr[first : first + ref.shape[0], : ref.shape[1]] = ref[...].astype(F32)
    pack_ref[:VECTOR_ROWS, at:] = vector_scr[...].astype(BF16)
    pack_ref[VECTOR_ROWS:, at:] = jnp.zeros_like(pack_ref[VECTOR_ROWS:, at:])

    for i, (source, target, buffer) in enumerate(zip(reads, writes, buffers)):
        pltpu.make_async_copy(source, buffer, in_sem.at[i]).wait()
        pltpu.make_async_copy(buffer, target, out_sem.at[i]).start()
    for i, (target, buffer) in enumerate(zip(writes, buffers)):
        pltpu.make_async_copy(buffer, target, out_sem.at[i]).wait()


def prepare(lengths, dealing, prev, tokens, cot_tokens, weights, head_vectors, plain_vectors, groups):
    micros, slots = prev.shape[:2]
    block, row = prev.shape[2:], tokens.shape[2:]
    dma = pltpu.SemaphoreType.DMA
    copies = slots + 4 * micros
    columns = sum(w.size for w in weights) // weights[0].shape[0] + 128
    in_vmem = pl.BlockSpec(memory_space=pltpu.VMEM)
    flat = [*weights, *head_vectors]

    def body(lengths_ref, *refs):
        fixed = 4 + len(flat)
        plain_refs = refs[fixed : fixed + len(plain_vectors)]
        rest = refs[fixed + len(plain_vectors) :]
        made, buffers = rest[:4], rest[4:7]
        prepare_kernel(
            micros, slots, groups, *refs[:fixed], plain_refs, *made, *buffers,
            rest[7 : 7 + micros], *rest[7 + micros :], lengths_ref,
        )

    return pl.pallas_call(
        body,
        out_shape=(
            jax.ShapeDtypeStruct((slots, *block), prev.dtype),
            jax.ShapeDtypeStruct((2, 2 * micros, *row), tokens.dtype),
            jax.ShapeDtypeStruct((weights[0].shape[0], columns), BF16),
            jax.ShapeDtypeStruct((micros, 2), jnp.int32),
        ),
        in_specs=[SMALL, SMALL, ANYWHERE, ANYWHERE, ANYWHERE] + [in_vmem] * (len(flat) + len(plain_vectors)),
        out_specs=(ANYWHERE, ANYWHERE, in_vmem, SMALL),
        scratch_shapes=[
            pltpu.VMEM((slots, *block), prev.dtype),
            pltpu.VMEM((2, 2 * micros, *row), tokens.dtype),
            pltpu.VMEM((VECTOR_ROWS, 128), F32),
        ]
        + [pltpu.SMEM((slots,), jnp.int32)] * micros
        + [dma((copies,)), dma((copies,))],
        compiler_params=params(),
        cost_estimate=cost(0, 4 * prev.size // micros),
        name="prepare",
    )(lengths, dealing, prev, tokens, cot_tokens, *flat, *plain_vectors)


def unpack_kernel(heads, x_ref, qkv_ref, up_ref, plain_ref):
    groups, slots = x_ref.shape[:2]
    width = heads * HEAD_DIM
    qkv_ref[...] = jnp.zeros_like(qkv_ref)
    lanes = plain_ref.shape[1] // slots
    per_head = HEAD_DIM // slots
    unit = up_ref.shape[2] // heads
    per_unit = unit // slots
    for s in range(slots):
        for h in range(groups):
            block = x_ref[h, s].astype(F32)
            if h == 0:
                plain_ref[:, s * lanes : (s + 1) * lanes] = block[:8, :lanes]
            for j in range(heads):
                at = j * HEAD_DIM + s * per_head
                qkv_ref[h, :, at : at + per_head] = block[QUERY_AT + j : QUERY_AT + j + 1, :per_head]
                at += 2 * width
                qkv_ref[h, :, at : at + per_head] = block[VALUE_AT + j : VALUE_AT + j + 1, :per_head]
                at = j * unit + s * per_unit
                up_ref[h, :, at : at + per_unit] = block[UP_AT + j : UP_AT + j + 1, :per_unit]


def unpack_vectors(shards, heads, width, unit, model):
    groups, slots, _, columns = shards.shape
    last = columns // 128 - 1
    shape = jax.ShapeDtypeStruct
    return pl.pallas_call(
        functools.partial(unpack_kernel, heads),
        out_shape=(
            shape((groups, 1, 3 * width), F32),
            shape((groups, 1, unit), F32),
            shape((8, model), F32),
        ),
        grid=(1,),
        in_specs=[pl.BlockSpec((groups, slots, VECTOR_ROWS, 128), lambda i: (0, 0, 0, last))],
        out_specs=(
            pl.BlockSpec((groups, 1, 3 * width), lambda i: (0, 0, 0)),
            pl.BlockSpec((groups, 1, unit), lambda i: (0, 0, 0)),
            pl.BlockSpec((8, model), lambda i: (0, 0)),
        ),
        compiler_params=params(),
        cost_estimate=cost(0, 4 * groups * slots * VECTOR_ROWS * 128),
        name="unpack_vectors",
    )(shards)


def place_kernel(micro, count, index_ref, x_ref, *rest):
    o_ref, buffer, in_sem, out_sem = rest[-4:]
    steps = range(count)
    move_blocks(
        [x_ref.at[index_ref[micro, i]] for i in steps],
        [o_ref.at[micro, i] for i in steps],
        [buffer.at[i] for i in steps],
        in_sem,
        out_sem,
    )


def place_blocks(blocks, micro, micros, index, into):
    count = blocks.shape[0]
    others = [] if into is None else [into]
    dma = pltpu.SemaphoreType.DMA
    return pl.pallas_call(
        functools.partial(place_kernel, micro, count),
        out_shape=jax.ShapeDtypeStruct((micros, *blocks.shape), blocks.dtype),
        in_specs=[SMALL, ANYWHERE] + [ANYWHERE for _ in others],
        out_specs=ANYWHERE,
        scratch_shapes=[pltpu.VMEM(blocks.shape, blocks.dtype), dma((count,)), dma((count,))],
        input_output_aliases={2: 0} if others else {},
        compiler_params=params(),
        cost_estimate=cost(0, 4 * blocks.size),
        name="place_blocks",
    )(index, blocks, *others)


def project_kernel(x_ref, w_ref, b_ref, *outs):
    columns = outs[0].shape[2]
    for m, o_ref in enumerate(outs):
        o_ref[0] = (dot(x_ref[m], w_ref[0, :, :columns], 1, 0) + b_ref[0]).astype(BF16)


def project(x, weights, bias):
    micros, rows, width = x.shape[0] // 2, *x.shape[1:]
    groups, _, columns = bias.shape
    return pl.pallas_call(
        project_kernel,
        out_shape=(jax.ShapeDtypeStruct((groups, rows, columns), BF16),) * micros,
        grid=(groups,),
        in_specs=[
            pl.BlockSpec((micros, rows, width), lambda h: (0, 0, 0)),
            pl.BlockSpec((1, width, width), lambda h: (h, 0, 0)),
            pl.BlockSpec((1, 1, columns), lambda h: (h, 0, 0)),
        ],
        out_specs=(pl.BlockSpec((1, rows, columns), lambda h: (h, 0, 0)),) * micros,
        compiler_params=params(),
        cost_estimate=cost(2 * micros * groups * rows * width * columns, 2 * groups * columns * (width + rows)),
        name="project",
    )(x, weights, bias)


def head_mask(shape, head):
    lane = lax.broadcasted_iota(jnp.int32, shape, len(shape) - 1)
    return lane // HEAD_DIM == head


def gather_rows(shift, qkv_ref, groups, rows, width, q_scr, k_scr, v_scr):
    for g in range(groups):
        block = qkv_ref[(shift + g) % groups]
        q_scr[g * rows : (g + 1) * rows] = block[:, :width]
        k_scr[g * rows : (g + 1) * rows] = block[:, width : 2 * width]
        v_scr[g * rows : (g + 1) * rows] = block[:, 2 * width :]


def forward_kernel(heads, micro, info_ref, qkv_ref, prev_ref, *rest):
    logit_ref, attend_ref, context_ref, q_scr, k_scr, v_scr = rest[-6:]
    step = pl.program_id(0)
    groups, rows, columns = qkv_ref.shape
    piece, extent = prev_ref.shape[2:]
    width = columns // 3

    @pl.when(step == 0)
    def _():
        gather_rows(info_ref[micro, 1], qkv_ref, groups, rows, width, q_scr, k_scr, v_scr)

    q = q_scr[pl.ds(pl.multiple_of(step * piece, 16), piece), :]
    key_valid = lax.broadcasted_iota(jnp.int32, (1, extent), 1) < info_ref[micro, 0]
    total = jnp.zeros((piece, width), F32)
    for h in range(heads):
        mine = head_mask((1, width), h)
        q_head = jnp.where(mine, q, jnp.zeros_like(q))
        raw = dot(q_head, k_scr[...], 1, 1) * HEAD_DIM ** (-0.5) + prev_ref[0, h].astype(F32)
        logit_ref[0, h] = raw.astype(BF16)
        masked = jnp.where(key_valid, raw, -jnp.inf)
        top = jnp.max(masked, axis=-1, keepdims=True)
        grown = jnp.exp(masked - top)
        attend = grown * (1.0 / jnp.sum(grown, axis=-1, keepdims=True))
        low = attend.astype(BF16)
        attend_ref[0, h] = low
        total = total + jnp.where(mine, dot(low, v_scr[...], 1, 0), 0.0)
    context_ref[0] = total.astype(BF16)


def attention_forward(info, qkv, prev, micro, micros, logits_into):
    groups, rows, columns = qkv.shape
    pieces, heads, piece, extent = prev.shape
    width = columns // 3
    per = rows // piece
    others = [] if logits_into is None else [logits_into]
    return pl.pallas_call(
        functools.partial(forward_kernel, heads, micro),
        out_shape=(
            jax.ShapeDtypeStruct((micros, heads, extent, extent), BF16),
            jax.ShapeDtypeStruct(prev.shape, BF16),
            jax.ShapeDtypeStruct((groups, rows, width), BF16),
        ),
        grid_spec=pltpu.PrefetchScalarGridSpec(
            num_scalar_prefetch=1,
            grid=(pieces,),
            in_specs=[
                pl.BlockSpec((groups, rows, columns), lambda j, i: (0, 0, 0)),
                pl.BlockSpec((1, heads, piece, extent), lambda j, i: (j, 0, 0, 0)),
            ]
            + [pl.BlockSpec(memory_space=pl.ANY) for _ in others],
            out_specs=(
                pl.BlockSpec((1, heads, piece, extent), lambda j, i: (micro, 0, j, 0)),
                pl.BlockSpec((1, heads, piece, extent), lambda j, i: (j, 0, 0, 0)),
                pl.BlockSpec((1, piece, width), lambda j, i: ((j // per + i[micro, 1]) % groups, j % per, 0)),
            ),
            scratch_shapes=[pltpu.VMEM((extent, width), BF16)] * 3,
        ),
        input_output_aliases={3: 0} if others else {},
        compiler_params=params(),
        cost_estimate=cost(4 * heads * extent * extent * HEAD_DIM * 4, 6 * heads * extent * extent),
        name="attention_forward",
    )(info, qkv, prev, *others)


def backward_kernel(
    heads, micro, info_ref, qkv_ref, attend_ref, context_ref, dcon_ref, cot_ref,
    send_ref, dqkv_ref, sums_ref, q_scr, k_scr, v_scr, dq_scr, dk_scr, dv_scr,
):
    step = pl.program_id(0)
    groups, rows, columns = qkv_ref.shape
    piece, extent = attend_ref.shape[2:]
    width = columns // 3
    scale = HEAD_DIM ** (-0.5)

    @pl.when(step == 0)
    def _():
        gather_rows(info_ref[micro, 1], qkv_ref, groups, rows, width, q_scr, k_scr, v_scr)
        dk_scr[...] = jnp.zeros_like(dk_scr)
        dv_scr[...] = jnp.zeros_like(dv_scr)

    here = pl.ds(pl.multiple_of(step * piece, 16), piece)
    q = q_scr[here, :]
    dcon = dcon_ref[0]
    both = dcon.astype(F32) * context_ref[0].astype(F32)
    dq = jnp.zeros((piece, width), F32)
    for h in range(heads):
        mine = head_mask((1, width), h)
        dcon_head = jnp.where(mine, dcon, jnp.zeros_like(dcon))
        q_head = jnp.where(mine, q, jnp.zeros_like(q))
        low = attend_ref[0, h]
        delta = jnp.sum(jnp.where(mine, both, 0.0), axis=-1, keepdims=True)
        dprob = dot(dcon_head, v_scr[...], 1, 1)
        dscore = low.astype(F32) * (dprob - delta) + cot_ref[0, h].astype(F32)
        dlow = dscore.astype(BF16)
        send_ref[0, h] = dlow
        dq = dq + jnp.where(mine, dot(dlow, k_scr[...], 1, 0), 0.0)
        dk_scr[...] += dot(dlow, q_head, 0, 0)
        dv_scr[...] += dot(low, dcon_head, 0, 0)
    dq_scr[here, :] = dq * scale

    @pl.when(step == pl.num_programs(0) - 1)
    def _():
        sums_ref[0:1, :] = jnp.sum(dq_scr[...], axis=0, keepdims=True)
        sums_ref[1:2, :] = jnp.sum(dv_scr[...], axis=0, keepdims=True)
        for g in range(groups):
            part = slice(g * rows, (g + 1) * rows)
            dqkv_ref[(info_ref[micro, 1] + g) % groups] = jnp.concatenate(
                [dq_scr[part], dk_scr[part] * scale, dv_scr[part]], axis=1
            ).astype(BF16)


def attention_backward(info, qkv, attend, context, dcontext, cot, micro):
    groups, rows, columns = qkv.shape
    pieces, heads, piece, extent = attend.shape
    width = columns // 3
    per = rows // piece
    rotated = pl.BlockSpec((1, piece, width), lambda j, i: ((j // per + i[micro, 1]) % groups, j % per, 0))
    square = pl.BlockSpec((1, heads, piece, extent), lambda j, i: (j, 0, 0, 0))
    return pl.pallas_call(
        functools.partial(backward_kernel, heads, micro),
        out_shape=(
            jax.ShapeDtypeStruct(attend.shape, BF16),
            jax.ShapeDtypeStruct((groups, rows, columns), BF16),
            jax.ShapeDtypeStruct((2, width), F32),
        ),
        grid_spec=pltpu.PrefetchScalarGridSpec(
            num_scalar_prefetch=1,
            grid=(pieces,),
            in_specs=[
                pl.BlockSpec((groups, rows, columns), lambda j, i: (0, 0, 0)),
                square,
                rotated,
                rotated,
                pl.BlockSpec((1, heads, piece, extent), lambda j, i: (micro, 0, j, 0)),
            ],
            out_specs=(
                square,
                pl.BlockSpec((groups, rows, columns), lambda j, i: (0, 0, 0)),
                pl.BlockSpec((2, width), lambda j, i: (0, 0)),
            ),
            scratch_shapes=[pltpu.VMEM((extent, width), BF16)] * 3
            + [pltpu.VMEM((extent, width), F32)] * 3,
        ),
        compiler_params=params(),
        cost_estimate=cost(8 * heads * extent * extent * HEAD_DIM * 4, 6 * heads * extent * extent),
        name="attention_backward",
    )(info, qkv, attend, context, dcontext, cot)


def normal(values):
    center = values - jnp.mean(values, axis=-1, keepdims=True)
    spread = jnp.mean(center * center, axis=-1, keepdims=True)
    inverse = lax.rsqrt(spread + epsilon)
    return center * inverse, inverse


def normal_back(grad, gain, unit, inverse):
    scaled = grad * gain
    return inverse * (
        scaled
        - jnp.mean(scaled, axis=-1, keepdims=True)
        - unit * jnp.mean(scaled * unit, axis=-1, keepdims=True)
    )


def rows_kernel(
    cuts, micro, con_ref, x_ref, w_ref, bup_ref, vec_ref,
    y_ref, dz_ref, dcon_ref, h1_ref, act_ref, b1_ref, b2_ref, b0_ref, sums_ref, dbup_ref,
    slope, acc, hidden, unit_scr, inv_scr,
):
    groups, rows, width = con_ref.shape
    qkv_end, out_end, up_end, down_end = cuts
    b_out, gain_one, shift_one = vec_ref[0:1, :], vec_ref[1:2, :], vec_ref[2:3, :]
    b_down, gain_two, shift_two = vec_ref[3:4, :], vec_ref[4:5, :], vec_ref[5:6, :]

    branch = b_out + x_ref[micro].astype(F32)
    for h in range(groups):
        branch = branch + dot(con_ref[h], w_ref[h, :, qkv_end:out_end], 1, 1)
    unit_one, inverse_one = normal(branch)
    unit_scr[...] = unit_one
    inv_scr[...] = inverse_one
    hid = unit_one * gain_one + shift_one
    hidden[...] = hid
    h1_ref[...] = hid.astype(BF16)
    acc[...] = hid + b_down

    def up(h, carry):
        u = dot(h1_ref[...], w_ref[h, :, out_end:up_end], 1, 0) + bup_ref[h]
        half = 0.5 * (1.0 + lax.erf(u * 0.7071067811865476))
        act_ref[h] = (u * half).astype(BF16)
        slope[h] = half + u * (jnp.exp(u * u * -0.5) * 0.3989422804014327)
        acc[...] += dot(act_ref[h], w_ref[h, :, up_end:down_end], 1, 1)
        return carry

    lax.fori_loop(0, groups, up, 0)
    unit_two, inverse_two = normal(acc[...])
    y_ref[...] = (unit_two * gain_two + shift_two).astype(BF16)
    cot = x_ref[x_ref.shape[0] // 2 + micro].astype(F32)
    sums_ref[4:5, :] = jnp.sum(cot * unit_two, axis=0, keepdims=True)
    sums_ref[5:6, :] = jnp.sum(cot, axis=0, keepdims=True)
    dz_two = normal_back(cot, gain_two, unit_two, inverse_two)
    sums_ref[3:4, :] = jnp.sum(dz_two, axis=0, keepdims=True)
    b2_ref[...] = dz_two.astype(BF16)
    acc[...] = dz_two

    def down(h, carry):
        du = dot(b2_ref[...], w_ref[h, :, up_end:down_end], 1, 0) * slope[h]
        dbup_ref[h] = jnp.sum(du, axis=0, keepdims=True)
        b1_ref[h] = du.astype(BF16)
        acc[...] += dot(b1_ref[h], w_ref[h, :, out_end:up_end], 1, 1)
        return carry

    lax.fori_loop(0, groups, down, 0)
    dh = acc[...]
    unit_one = unit_scr[...]
    sums_ref[1:2, :] = jnp.sum(dh * unit_one, axis=0, keepdims=True)
    sums_ref[2:3, :] = jnp.sum(dh, axis=0, keepdims=True)
    dz_one = normal_back(dh, gain_one, unit_one, inv_scr[...])
    sums_ref[0:1, :] = jnp.sum(dz_one, axis=0, keepdims=True)
    sums_ref[6:8, :] = jnp.zeros_like(sums_ref[6:8, :])
    dz_ref[...] = dz_one
    b0_ref[...] = dz_one.astype(BF16)
    for h in range(groups):
        dcon_ref[h] = dot(b0_ref[...], w_ref[h, :, qkv_end:out_end], 1, 0).astype(BF16)


def row_work(cuts, micro, context, x, weights, bias_up, vectors):
    groups, rows, width = context.shape
    model = x.shape[2]
    in_vmem = pl.BlockSpec(memory_space=pltpu.VMEM)
    unit = bias_up.shape[2]
    shape = jax.ShapeDtypeStruct
    args = (context, x, weights, bias_up, vectors)
    return pl.pallas_call(
        functools.partial(rows_kernel, cuts, micro),
        out_shape=(
            shape((rows, model), BF16),
            shape((rows, model), F32),
            shape(context.shape, BF16),
            shape((rows, model), BF16),
            shape((groups, rows, unit), BF16),
            shape((groups, rows, unit), BF16),
            shape((rows, model), BF16),
            shape((rows, model), BF16),
            shape((8, model), F32),
            shape((groups, 1, unit), F32),
        ),
        in_specs=[in_vmem] * len(args),
        out_specs=(in_vmem,) * 10,
        scratch_shapes=[
            pltpu.VMEM((groups, rows, unit), F32),
            pltpu.VMEM((rows, model), F32),
            pltpu.VMEM((rows, model), F32),
            pltpu.VMEM((rows, model), F32),
            pltpu.VMEM((rows, 1), F32),
        ],
        compiler_params=params(),
        cost_estimate=cost(8 * groups * rows * model * (unit + width), 2 * weights.size),
        name="row_work",
    )(*args)


def input_kernel(dqkv_ref, w_ref, dz_ref, o_ref):
    total = dz_ref[...]
    for h in range(dqkv_ref.shape[0]):
        total = total + dot(dqkv_ref[h], w_ref[h, :, : dqkv_ref.shape[2]], 1, 1)
    share = o_ref.shape[2]
    for h in range(o_ref.shape[0]):
        o_ref[h] = total[:, h * share : (h + 1) * share].astype(BF16)


def input_grad(dqkv, weights, dz):
    groups, rows, columns = dqkv.shape
    model = dz.shape[1]
    return pl.pallas_call(
        input_kernel,
        out_shape=jax.ShapeDtypeStruct((groups, rows, model // groups), BF16),
        grid=(1,),
        in_specs=[
            whole(dqkv),
            pl.BlockSpec((groups, model, model), lambda i: (0, 0, 0)),
            whole(dz),
        ],
        out_specs=pl.BlockSpec((groups, rows, model // groups), lambda i: (0, 0, 0)),
        compiler_params=params(),
        cost_estimate=cost(2 * groups * rows * columns * model, 2 * groups * columns * model),
        name="input_grad",
    )(dqkv, weights, dz)


def weight_kernel(cuts, micros, heads, slots, *refs):
    out_ref, vector_scr = refs[-2:]
    qkv_end, out_end, up_end, down_end = cuts

    def summed(family):
        total = family[0][...]
        for ref in family[1:]:
            total = total + ref[...]
        return total

    def product(lefts, rights):
        total = None
        for left, right in zip(lefts, rights):
            term = dot(left[...].reshape(left.shape[-2:]), right[0], 0, 0)
            total = term if total is None else total + term
        return total.astype(BF16)

    x, b0, h1, b2, dqkv, con, b1, act, own, plain, up = (
        refs[i * micros : (i + 1) * micros] for i in range(11)
    )
    out_ref[0, :, 0:qkv_end] = product(x, dqkv)
    out_ref[0, :, qkv_end:out_end] = product(b0, con)
    out_ref[0, :, out_end:up_end] = product(h1, b1)
    out_ref[0, :, up_end:down_end] = product(b2, act)

    own_sum = jnp.where(pl.program_id(0) == lax.axis_index("head"), summed(own), 0.0)
    plain_sum, up_sum = summed(plain), summed(up)[0]
    rows = out_ref.shape[1] // slots
    lanes = plain_sum.shape[1] // slots
    unit = up_sum.shape[1] // heads
    vector_scr[...] = jnp.zeros_like(vector_scr)
    for s in range(slots):
        vector_scr[:8, :lanes] = plain_sum[:, s * lanes : (s + 1) * lanes]
        for j in range(heads):
            at, step = j * HEAD_DIM + s * (HEAD_DIM // slots), HEAD_DIM // slots
            vector_scr[QUERY_AT + j : QUERY_AT + j + 1, :step] = own_sum[0:1, at : at + step]
            vector_scr[VALUE_AT + j : VALUE_AT + j + 1, :step] = own_sum[1:2, at : at + step]
            at, step = j * unit + s * (unit // slots), unit // slots
            vector_scr[UP_AT + j : UP_AT + j + 1, :step] = up_sum[:, at : at + step]
        out_ref[0, s * rows : s * rows + VECTOR_ROWS, down_end:] = vector_scr[...].astype(BF16)
        out_ref[0, s * rows + VECTOR_ROWS : (s + 1) * rows, down_end:] = jnp.zeros(
            (rows - VECTOR_ROWS, 128), BF16
        )


def weight_grads(cuts, heads, slots, x, lefts, rights, own, plain, up):
    micros = len(lefts[0])
    groups = rights[0][0].shape[0]
    model = lefts[0][0].shape[1]
    flat_left = [a for family in lefts for a in family]
    flat_right = [a for family in rights for a in family]
    rows = flat_left[0].shape[0]
    columns = cuts[-1] + 128

    def of_micro(m):
        return pl.BlockSpec((1, rows, model), lambda h: (m, 0, 0))

    def per_group(a):
        return pl.BlockSpec((1, *a.shape[1:]), lambda h: (h, 0, 0))

    return pl.pallas_call(
        functools.partial(weight_kernel, cuts, micros, heads, slots),
        out_shape=jax.ShapeDtypeStruct((groups, model, columns), BF16),
        grid=(groups,),
        in_specs=[of_micro(m) for m in range(micros)]
        + [whole(a) for a in flat_left]
        + [per_group(a) for a in flat_right]
        + [whole(a) for a in (*own, *plain)]
        + [per_group(a) for a in up],
        out_specs=pl.BlockSpec((1, model, columns), lambda h: (h, 0, 0)),
        scratch_shapes=[pltpu.VMEM((VECTOR_ROWS, 128), F32)],
        compiler_params=params(),
        cost_estimate=cost(2 * micros * groups * rows * model * cuts[-1], 2 * groups * model * cuts[-1]),
        name="weight_grads",
    )(*([x] * micros), *flat_left, *flat_right, *own, *plain, *up)


MESH = pl.DeviceIdType.MESH
SIDE = 2


def remote(source, target, send_sem, recv_sem, device):
    return pltpu.make_async_remote_copy(
        src_ref=source,
        dst_ref=target,
        send_sem=send_sem,
        recv_sem=recv_sem,
        device_id=device,
        device_id_type=MESH,
    )


def signal(device):
    pl.semaphore_signal(
        pltpu.get_barrier_semaphore(), inc=1, device_id=device, device_id_type=MESH
    )


def greet(devices):
    for device in devices:
        signal(device)
    pl.semaphore_wait(pltpu.get_barrier_semaphore(), len(devices))


def cross_kernel(groups, x_ref, o_ref, send_sem, recv_sem, own_sem):
    me = lax.axis_index("head")
    peers = [lax.rem(me + i, groups) for i in range(1, groups)]
    greet([{"head": peer} for peer in peers])
    copies = []
    for i, peer in enumerate(peers):
        copy = remote(x_ref.at[peer], o_ref.at[me], send_sem.at[i], recv_sem.at[i], {"head": peer})
        copy.start()
        copies.append(copy)
    own = pltpu.make_async_copy(x_ref.at[me], o_ref.at[me], own_sem)
    own.start()
    own.wait()
    for copy in copies:
        copy.wait()


def across_heads(x, number):
    groups = x.shape[0]
    return pl.pallas_call(
        functools.partial(cross_kernel, groups),
        out_shape=jax.ShapeDtypeStruct(x.shape, x.dtype),
        in_specs=[pl.BlockSpec(memory_space=pltpu.VMEM)],
        out_specs=pl.BlockSpec(memory_space=pl.ANY),
        scratch_shapes=[
            pltpu.SemaphoreType.DMA((groups - 1,)),
            pltpu.SemaphoreType.DMA((groups - 1,)),
            pltpu.SemaphoreType.DMA,
        ],
        compiler_params=params(collective_id=number, has_side_effects=True),
        cost_estimate=cost(0, 40 * x.size),
        name="across_heads",
    )(x)


SIDES = 2
LINE = 4


class Place:
    def __init__(self):
        self.here, self.head = lax.axis_index("seq"), lax.axis_index("head")
        self.z, self.x = self.here // SIDES, lax.rem(self.here, SIDES)
        self.y, self.c = self.head // 2, lax.rem(self.head, 2)
        self.up, self.down = {"seq": self.here + SIDES}, {"seq": self.here - SIDES}
        self.across = {"seq": self.z * SIDES + (1 - self.x)}
        self.over = {"head": (1 - self.y) * 2 + self.c}
        self.beside = {"head": self.y * 2 + (1 - self.c)}
        self.not_last, self.not_first = self.z < LINE - 1, self.z > 0
        self.is_end = jnp.logical_or(jnp.logical_not(self.not_last), jnp.logical_not(self.not_first))
        half = (LINE - 1 - self.z) // 2
        self.order = [self.z, self.z + 1 - 2 * lax.rem(self.z, 2), 1 + half, (LINE - 1) * half]

    def greet_neighbours(self):
        pl.when(self.not_last)(lambda: signal(self.up))
        pl.when(self.not_first)(lambda: signal(self.down))
        for device in (self.across, self.over, self.beside):
            signal(device)
        return 3 + self.not_last.astype(jnp.int32) + self.not_first.astype(jnp.int32)


def arrived(block, send_sem, recv_sem, device):
    remote(block, block, send_sem, recv_sem, device).wait_recv()


def line_kernel(
    slots, groups, pack_ref, piece_ref, all_ref, rows_ref,
    z_s, z_r, x_s, x_r, y_s, y_r, piece_s, piece_r, own_sem,
):
    me = Place()
    here, head, x, y, c = me.here, me.head, me.x, me.y, me.c
    group = lax.rem(head - here + slots, groups)
    homes = [group * SIDE + p for p in range(SIDE)]
    targets = [
        lax.rem(head - me.z + groups, groups) + groups * lax.rem(here + step, 2) for step in range(2)
    ]
    expected = me.greet_neighbours()
    for home in homes:
        pl.when(home != here)(lambda home=home: signal({"seq": home}))
    for target in targets:
        expected = expected + (target != here).astype(jnp.int32)
    pl.semaphore_wait(pltpu.get_barrier_semaphore(), expected)

    def at(i, side, row):
        return all_ref.at[row * 2 + c, i * SIDES + side]

    def source(k):
        return pack_ref if k == 0 else at(me.order[k], x, y)

    def upward(k):
        i = me.order[k]
        return remote(source(k), at(i, x, y), z_s.at[i], z_r.at[i], me.up)

    def downward(k):
        i = me.order[k]
        return remote(source(k), at(i, x, y), z_s.at[LINE + i], z_r.at[i], me.down)

    def over_x(k):
        i = me.order[k]
        return remote(source(k), at(i, x, y), x_s.at[i], x_r.at[i], me.across)

    def over_y(k):
        i = me.order[k]
        return remote(source(k), at(i, x, y), y_s.at[i], y_r.at[i], me.over)

    def goes_up(k):
        return (me.order[k] <= me.z) & me.not_last

    def goes_down(k):
        return (me.order[k] >= me.z) & me.not_first

    def piece(step):
        return remote(
            piece_ref.at[step], rows_ref.at[:, x], piece_s.at[step], piece_r.at[x], {"seq": targets[step]}
        )

    def piece_here(step):
        return pltpu.make_async_copy(piece_ref.at[step], rows_ref.at[:, x], own_sem.at[1])

    own = pltpu.make_async_copy(pack_ref, at(me.z, x, y), own_sem.at[0])
    own.start()
    for k in range(LINE):
        i = me.order[k]
        if k:
            arrived(at(i, x, y), z_s.at[i], z_r.at[i], me.up)
        pl.when(goes_up(k))(lambda k=k: upward(k).start())
        pl.when(goes_down(k))(lambda k=k: downward(k).start())
        over_x(k).start()
        over_y(k).start()
        turn = {0: me.is_end, LINE - 1: jnp.logical_not(me.is_end)}.get(k)
        if turn is not None:
            for step, target in enumerate(targets):
                pl.when(turn & (target != here))(lambda step=step: piece(step).start())
                pl.when(turn & (target == here))(lambda step=step: piece_here(step).start())
    for k in range(LINE):
        i = me.order[k]
        arrived(at(i, 1 - x, y), x_s.at[i], x_r.at[i], me.across)
        arrived(at(i, x, 1 - y), y_s.at[i], y_r.at[i], me.over)
    for p, home in enumerate(homes):
        block = rows_ref.at[:, p]
        pl.when(home != here)(
            lambda block=block, p=p, home=home: arrived(
                block, piece_s.at[p], piece_r.at[p], {"seq": home}
            )
        )
    for step, target in enumerate(targets):
        pl.when(target != here)(lambda step=step: piece(step).wait_send())
        pl.when(target == here)(lambda step=step: piece_here(step).wait())
    own.wait()
    for k in range(LINE):
        pl.when(goes_up(k))(lambda k=k: upward(k).wait_send())
        pl.when(goes_down(k))(lambda k=k: downward(k).wait_send())
        over_x(k).wait_send()
        over_y(k).wait_send()


def gather_line(packed, pieces, slots, groups, number):
    dma = pltpu.SemaphoreType.DMA
    return pl.pallas_call(
        functools.partial(line_kernel, slots, groups),
        out_shape=(
            jax.ShapeDtypeStruct((groups, slots, *packed.shape), packed.dtype),
            jax.ShapeDtypeStruct((pieces.shape[1], SIDE, *pieces.shape[2:]), pieces.dtype),
        ),
        in_specs=[pl.BlockSpec(memory_space=pltpu.VMEM)] * 2,
        out_specs=(ANYWHERE,) * 2,
        scratch_shapes=[dma((2 * LINE,)), dma((LINE,))] + [dma((LINE,))] * 4 + [dma((2,))] * 3,
        compiler_params=params(collective_id=number, has_side_effects=True),
        cost_estimate=cost(0, 3000000 * 20),
        name="gather_line",
    )(packed, pieces)


def plane_kernel(in_ref, all_ref, y_s, y_r, c_s, c_r):
    me = Place()
    x, y, c = me.x, me.y, me.c
    greet([me.over, me.beside])

    def at(i, side, row, core=c):
        return all_ref.at[row * 2 + core, i * SIDES + side]

    def over_y(i):
        block = at(i, 1 - x, y)
        return remote(block, block, y_s.at[i], y_r.at[i], me.over)

    places = ((x, y), (1 - x, y), (x, 1 - y), (1 - x, 1 - y))

    def to_core(i, kind):
        n = kind * LINE + i
        block = at(i, *places[kind])
        return remote(block, block, c_s.at[n], c_r.at[n], me.beside)

    for i in range(LINE):
        over_y(i).start()
    for kind in range(3):
        for i in range(LINE):
            to_core(i, kind).start()
    for i in range(LINE):
        arrived(at(i, 1 - x, 1 - y), y_s.at[i], y_r.at[i], me.over)
        to_core(i, 3).start()
    for kind, (side, row) in enumerate(places):
        for i in range(LINE):
            n = kind * LINE + i
            arrived(at(i, side, row, 1 - c), c_s.at[n], c_r.at[n], me.beside)
    for i in range(LINE):
        over_y(i).wait_send()
        for kind in range(4):
            to_core(i, kind).wait_send()


def gather_plane(shards, number):
    dma = pltpu.SemaphoreType.DMA
    return pl.pallas_call(
        plane_kernel,
        out_shape=jax.ShapeDtypeStruct(shards.shape, shards.dtype),
        in_specs=[ANYWHERE],
        out_specs=ANYWHERE,
        scratch_shapes=[dma((LINE,))] * 2 + [dma((4 * LINE,))] * 2,
        input_output_aliases={0: 0},
        compiler_params=params(collective_id=number, has_side_effects=True),
        cost_estimate=cost(0, 3000000 * 40),
        name="gather_plane",
    )(shards)


def add_into(target, terms, shape):
    rows = shape[-2]
    tile = 16
    steps = rows // tile
    outer = 1
    for n in shape[:-2]:
        outer *= n

    def body(i, carry):
        at = pl.ds(pl.multiple_of(lax.rem(i, steps) * tile, tile), tile)
        rest = i // steps
        index = []
        for n in reversed(shape[:-2]):
            index.insert(0, lax.rem(rest, n))
            rest = rest // n
        index = (*index, at)
        total = terms[0][index].astype(F32)
        for term in terms[1:]:
            total = total + term[index].astype(F32)
        target[index] = total.astype(target.dtype)
        return carry

    lax.fori_loop(0, outer * steps, body, 0)


def finish_kernel(
    slots, groups, micros, part_ref, y_refs, dx_refs, sum_ref, tokens_ref, grads_ref,
    held, first, second, line,
    c_s, c_r, x_s, x_r, y_s, y_r, z_s, z_r, home_s, home_r, over_s, over_r, near_s, near_r, pass_s, pass_r,
    grad_s, grad_r, own_sem,
):
    me = Place()
    here, head, x, y, z, c = me.here, me.head, me.x, me.y, me.z, me.c
    order = me.order[::-1]
    group = lax.rem(head - here + slots, groups)
    homes = [group * SIDE + p for p in range(SIDE)]
    mine = lax.rem(head - z + groups, groups)
    senders = [lax.rem(slot + z, groups) for slot in range(slots)]

    def is_me(slot, other):
        return (slot == here) & (other == head)

    expected = me.greet_neighbours()
    for slot in range(slots):
        pl.when(jnp.logical_not(is_me(slot, senders[slot])))(
            lambda slot=slot: signal({"seq": slot, "head": senders[slot]})
        )
    for home in homes:
        for h in range(groups):
            expected = expected + 1 - is_me(home, h).astype(jnp.int32)
    pl.semaphore_wait(pltpu.get_barrier_semaphore(), expected)

    def to_core(k, row):
        i = order[k]
        n = row * LINE + i
        return remote(
            part_ref.at[row * 2 + (1 - c), i], held.at[i, row], c_s.at[n], c_r.at[n], me.beside
        )

    sides = (1 - x, x)

    def over_y(k, n):
        i = order[k]
        at = n * LINE + i
        return remote(
            held.at[i, 1 - y, sides[n]], first.at[i, sides[n]], y_s.at[at], y_r.at[at], me.over
        )

    def over_x(k):
        i = order[k]
        return remote(held.at[i, y, 1 - x], second.at[i], x_s.at[i], x_r.at[i], me.across)

    def upward(k):
        i = order[k]
        return remote(held.at[i, y, x], line.at[0, i], z_s.at[i], z_r.at[i], me.up)

    def downward(k):
        i = order[k]
        n = LINE + i
        return remote(held.at[i, y, x], line.at[1, i], z_s.at[n], z_r.at[n], me.down)

    rows, columns = sum_ref.shape

    def begin(k):
        i = order[k]
        for row in (1 - y, y):
            n = row * LINE + i
            arrived(held.at[i, row], c_s.at[n], c_r.at[n], me.beside)
        block = held.at[i, 1 - y]
        add_into(block, [block, part_ref.at[(1 - y) * 2 + c, i]], (SIDES, rows, columns))
        over_y(k, 0).start()
        over_y(k, 1).start()
        block = held.at[i, y]
        add_into(block, [block, part_ref.at[y * 2 + c, i]], (SIDES, rows, columns))

    def middle(k):
        i = order[k]
        for n, side in enumerate(sides):
            at = n * LINE + i
            arrived(first.at[i, side], y_s.at[at], y_r.at[at], me.over)
            block = held.at[i, y, side]
            add_into(block, [block, first.at[i, side]], (rows, columns))
            if n == 0:
                over_x(k).start()

    def end(k):
        i = order[k]
        n = LINE + i
        last = k == LINE - 1
        arrived(second.at[i], x_s.at[i], x_r.at[i], me.across)
        target = sum_ref if last else held.at[i, y, x]
        add_into(target, [held.at[i, y, x], second.at[i]], (rows, columns))

        def below():
            arrived(line.at[0, i], z_s.at[i], z_r.at[i], me.up)
            add_into(target, [target, line.at[0, i]], (rows, columns))

        def above():
            arrived(line.at[1, i], z_s.at[n], z_r.at[n], me.up)
            add_into(target, [target, line.at[1, i]], (rows, columns))

        pl.when((i >= z) & me.not_first)(below)
        pl.when((i <= z) & me.not_last)(above)
        if not last:
            pl.when(i > z)(lambda: upward(k).start())
            pl.when(i < z)(lambda: downward(k).start())

    def home_copy(m, p):
        n = m * SIDE + p
        return remote(
            y_refs[m].at[p], tokens_ref.at[m, here], home_s.at[n], home_r.at[m * 2 + here // groups], {"seq": homes[p]}
        )

    def home_here(m, p):
        return pltpu.make_async_copy(y_refs[m].at[p], tokens_ref.at[m, here], own_sem.at[m])

    def grad_copy(m, p, h):
        n = (m * SIDE + p) * groups + h
        return remote(
            dx_refs[m].at[h, p], grads_ref.at[m, here], grad_s.at[n], grad_r.at[m * slots + here],
            {"seq": homes[p], "head": h},
        )

    def grad_here(m, p, h):
        return pltpu.make_async_copy(dx_refs[m].at[h, p], grads_ref.at[m, here], own_sem.at[micros + m])

    def slot_of(other, j):
        return lax.rem(other - z + groups, groups) + groups * j

    far_head, near_head = (1 - y) * 2 + c, y * 2 + (1 - c)
    last_head = (1 - y) * 2 + (1 - c)

    def far(m, j):
        n, block = m * 2 + j, tokens_ref.at[m, slot_of(head, j)]
        return remote(block, block, over_s.at[n], over_r.at[n], me.over)

    def near(m, j):
        n, block = m * 2 + j, tokens_ref.at[m, slot_of(head, j)]
        return remote(block, block, near_s.at[n], near_r.at[n], me.beside)

    def passed(m, j):
        n, block = m * 2 + j, tokens_ref.at[m, slot_of(far_head, j)]
        return remote(block, block, pass_s.at[n], pass_r.at[n], me.beside)

    for k in range(LINE):
        for row in range(2):
            to_core(k, row).start()
    for m in range(micros):
        for p, home in enumerate(homes):
            pl.when(home != here)(lambda m=m, p=p: home_copy(m, p).start())
            pl.when(home == here)(lambda m=m, p=p: home_here(m, p).start())
            for h in range(groups):
                same = is_me(home, h)
                pl.when(jnp.logical_not(same))(lambda m=m, p=p, h=h: grad_copy(m, p, h).start())
                pl.when(same)(lambda m=m, p=p, h=h: grad_here(m, p, h).start())
    for k in range(LINE):
        begin(k)
        if k >= 1:
            middle(k - 1)
        if k >= 2:
            end(k - 2)
    middle(LINE - 1)
    end(LINE - 2)
    for m in range(micros):
        for p, home in enumerate(homes):
            pl.when(home == here)(lambda m=m, p=p: home_here(m, p).wait())
        for j in range(2):
            slot = slot_of(head, j)
            pl.when(slot != here)(
                lambda m=m, j=j, slot=slot: arrived(
                    tokens_ref.at[m, slot], home_s.at[m * 2 + j], home_r.at[m * 2 + j], {"seq": slot}
                )
            )
            far(m, j).start()
            near(m, j).start()
    end(LINE - 1)
    for m in range(micros):
        for j in range(2):
            n = m * 2 + j
            arrived(tokens_ref.at[m, slot_of(far_head, j)], over_s.at[n], over_r.at[n], me.over)
            passed(m, j).start()
    for m in range(micros):
        for j in range(2):
            n = m * 2 + j
            arrived(tokens_ref.at[m, slot_of(near_head, j)], near_s.at[n], near_r.at[n], me.beside)
            arrived(tokens_ref.at[m, slot_of(last_head, j)], pass_s.at[n], pass_r.at[n], me.beside)
        for slot in range(slots):
            n = m * slots + slot
            pl.when(jnp.logical_not(is_me(slot, senders[slot])))(
                lambda m=m, n=n, slot=slot: arrived(
                    grads_ref.at[m, slot], grad_s.at[0], grad_r.at[n], {"seq": slot, "head": senders[slot]}
                )
            )
    for m in range(micros):
        for p, home in enumerate(homes):
            pl.when(home != here)(lambda m=m, p=p: home_copy(m, p).wait_send())
            for h in range(groups):
                same = is_me(home, h)
                pl.when(jnp.logical_not(same))(lambda m=m, p=p, h=h: grad_copy(m, p, h).wait_send())
                pl.when(same)(lambda m=m, p=p, h=h: grad_here(m, p, h).wait())
        for j in range(2):
            far(m, j).wait_send()
            near(m, j).wait_send()
            passed(m, j).wait_send()
    for k in range(LINE):
        for row in range(2):
            to_core(k, row).wait_send()
        over_y(k, 0).wait_send()
        over_y(k, 1).wait_send()
        over_x(k).wait_send()
        if k < LINE - 1:
            i = order[k]
            pl.when(i > z)(lambda k=k: upward(k).wait_send())
            pl.when(i < z)(lambda k=k: downward(k).wait_send())


def finish(part, ys, dxs, slots, groups, number):
    columns = part.shape[-1]
    micros = len(ys)
    _, piece, model = ys[0].shape

    def body(part_ref, *refs):
        finish_kernel(
            slots, groups, micros, part_ref, refs[:micros], refs[micros : 2 * micros], *refs[2 * micros :]
        )

    rows = part.shape[-2]
    dma = pltpu.SemaphoreType.DMA
    vmem = pltpu.VMEM
    part = part.reshape(groups, LINE, SIDES, rows, columns)
    return pl.pallas_call(
        body,
        out_shape=(
            jax.ShapeDtypeStruct((rows, columns), F32),
            jax.ShapeDtypeStruct((micros, slots, piece, model), BF16),
            jax.ShapeDtypeStruct((micros, slots, piece, dxs[0].shape[-1]), BF16),
        ),
        in_specs=[pl.BlockSpec(memory_space=pltpu.VMEM)] * (1 + 2 * micros),
        out_specs=(pl.BlockSpec(memory_space=pltpu.VMEM),) + (pl.BlockSpec(memory_space=pl.ANY),) * 2,
        scratch_shapes=[
            vmem((LINE, 2, SIDES, rows, columns), BF16),
            vmem((LINE, SIDES, rows, columns), BF16),
            vmem((LINE, rows, columns), BF16),
            vmem((2, LINE, rows, columns), BF16),
        ]
        + [dma((2 * LINE,))] * 8
        + [dma((2 * micros,))] * 8
        + [dma((2 * groups * micros,)), dma((slots * micros,)), dma((2 * micros,))],
        compiler_params=params(collective_id=number, has_side_effects=True),
        cost_estimate=cost(0, 3000000 * 40),
        name="finish",
    )(part, *ys, *dxs)


def deliver_kernel(
    cuts, micros, slots, index_ref, sum_ref, y_ref, dx_ref, out_ref, grad_ref,
    q_ref, k_ref, v_ref, wo_ref, wu_ref, wd_ref, bq_ref, bv_ref, bu_ref, *rest,
):
    plain_refs = rest[:PLAIN]
    y_buffer, dx_buffer, in_sem, out_sem, dx_sem = rest[PLAIN:]
    where = [(m, i) for m in range(micros) for i in range(slots)]

    def take(n):
        m, i = where[n]
        return pltpu.make_async_copy(y_ref.at[m, index_ref[m, i]], y_buffer.at[m, i], in_sem.at[n])

    def give(n):
        m, i = where[n]
        return pltpu.make_async_copy(y_buffer.at[m, i], out_ref.at[m, i], out_sem.at[n])

    def take_dx(n):
        m, i = where[n]
        return pltpu.make_async_copy(dx_ref.at[m, index_ref[m, i]], dx_buffer.at[m, i], dx_sem.at[n])

    for n in range(len(where)):
        take(n).start()
    for n in range(len(where)):
        take_dx(n).start()
    width = q_ref.shape[1]
    for n, ref in enumerate((q_ref, k_ref, v_ref)):
        ref[...] = sum_ref[:, n * width : (n + 1) * width]
    wo_ref[...] = sum_ref[:, cuts[0] : cuts[1]].T
    wu_ref[...] = sum_ref[:, cuts[1] : cuts[2]]
    wd_ref[...] = sum_ref[:, cuts[2] : cuts[3]]
    block = sum_ref[:VECTOR_ROWS, cuts[3] :]
    for i, ref in enumerate(plain_refs):
        ref[...] = block[i : i + 1, : ref.shape[1]]
    for first, ref in ((QUERY_AT, bq_ref), (VALUE_AT, bv_ref), (UP_AT, bu_ref)):
        ref[...] = block[first : first + ref.shape[0], : ref.shape[1]]
    for n in range(len(where)):
        take(n).wait()
        give(n).start()
    for n, (m, i) in enumerate(where):
        take_dx(n).wait()
        grad_ref[m, i] = dx_buffer[m, i].astype(F32).T.astype(BF16)
    for n in range(len(where)):
        give(n).wait()


def deliver(cuts, heads, unit, index, sums, y, dx):
    micros, slots, piece, share = dx.shape
    rows, width = sums.shape[0], heads * HEAD_DIM
    total = micros * slots
    dma = pltpu.SemaphoreType.DMA
    in_vmem = pl.BlockSpec(memory_space=pltpu.VMEM)

    def f32(*shape):
        return jax.ShapeDtypeStruct(shape, F32)

    return pl.pallas_call(
        functools.partial(deliver_kernel, cuts, micros, slots),
        out_shape=(
            jax.ShapeDtypeStruct(y.shape, BF16),
            jax.ShapeDtypeStruct((micros, slots, share, piece), BF16),
            f32(rows, width),
            f32(rows, width),
            f32(rows, width),
            f32(width, rows),
            f32(rows, unit),
            f32(rows, unit),
            f32(heads, HEAD_DIM // slots),
            f32(heads, HEAD_DIM // slots),
            f32(heads, unit // heads // slots),
        )
        + (f32(1, rows),) * PLAIN,
        in_specs=[SMALL, in_vmem, ANYWHERE, ANYWHERE],
        out_specs=(ANYWHERE,) + (in_vmem,) * (10 + PLAIN),
        scratch_shapes=[
            pltpu.VMEM(y.shape, BF16),
            pltpu.VMEM(dx.shape, BF16),
            dma((total,)),
            dma((total,)),
            dma((total,)),
        ],
        compiler_params=params(),
        cost_estimate=cost(0, 4 * y.size),
        name="deliver",
    )(index, sums, y, dx)


def fits(mesh):
    return dict(mesh.shape) == {"seq": 8, "head": 4}


def on_device(
    tokens,
    prev_logits,
    lengths,
    dealing,
    w_query,
    b_query,
    w_key,
    w_value,
    b_value,
    w_out,
    b_out,
    gain_one,
    shift_one,
    w_up,
    b_up,
    w_down,
    b_down,
    gain_two,
    shift_two,
    cot_tokens,
    cot_logits,
):
    slots, groups = lax.axis_size("seq"), lax.axis_size("head")
    grid = ("seq", "head")
    here, head = lax.axis_index("seq"), lax.axis_index("head")
    micros, _, piece, model = tokens.shape
    heads = prev_logits.shape[3]
    extent = piece * slots
    width = heads * HEAD_DIM
    unit = w_up.shape[1]
    per = slots // groups
    cuts = (3 * width, 3 * width + width, 3 * width + width + unit, 3 * width + width + 2 * unit)
    own_rows = model // slots

    prev = jnp.transpose(prev_logits, (0, 1, 3, 2, 4))
    cot_square = jnp.transpose(cot_logits[:, 0], (0, 2, 1, 3))

    first_send, pieces, packed, info = prepare(
        lengths,
        dealing,
        prev,
        tokens,
        cot_tokens,
        (w_query, w_key, w_value, w_out, w_up, w_down.T),
        (b_query, b_value, b_up),
        [v.reshape(1, -1) for v in (b_out, gain_one, shift_one, b_down, gain_two, shift_two)],
        groups,
    )
    line, arrived_rows = gather_line(packed, pieces, slots, groups, 1)
    rows = per * piece
    rows_all = arrived_rows.reshape(2 * micros, rows, model)

    weights = gather_plane(line, 2)
    weights = weights.reshape(groups, slots, own_rows, -1)
    bias_qkv, bias_up, row_vectors = unpack_vectors(weights, heads, width, unit, model)
    weights = weights.reshape(groups, model, -1)

    projected = project(rows_all, weights, bias_qkv)
    first_qkv = across_heads(projected[0], 3)
    second_qkv = [across_heads(projected[m], 3) for m in range(1, micros)]
    got_prev, after = [], arrived_rows
    for m in range(micros):
        send = pick_blocks(prev, m, dealing) if m else first_send
        send, _ = lax.optimization_barrier((send, after))
        got = lax.all_to_all(send, "seq", split_axis=0, concat_axis=0, tiled=True)
        got_prev.append(got)
        after = (got, first_qkv, second_qkv)

    logits, grad_logits = None, None
    kept, sums_own, sums_rows, sums_up, returned, sent = [], [], [], [], [], []
    for m in range(micros):
        qkv = second_qkv[m - 1] if m else first_qkv
        logits, attend, context = attention_forward(info, qkv, got_prev[m], m, micros, logits)
        context_rows = across_heads(context, 4)
        y, dz, dcon, h1, act, b1, b2, b0, sums, dbup = row_work(
            cuts, m, context_rows, rows_all, weights, bias_up, row_vectors
        )
        dcontext = across_heads(dcon, 4)
        send, dqkv, own = attention_backward(
            info, qkv, attend, context, dcontext, cot_square, m
        )
        dqkv = across_heads(dqkv, 5)
        dx = input_grad(dqkv, weights, dz)
        kept.append((b0, h1, b2, dqkv, context_rows, b1, act))
        sums_own.append(own)
        sums_rows.append(sums)
        sums_up.append(dbup)
        returned.append((y, dx))
        if m == 0:
            send, _ = lax.optimization_barrier((send, dx))
            after = lax.all_to_all(send, "seq", split_axis=0, concat_axis=0, tiled=True)
            sent.append(after)
        else:
            sent.append(send)

    families = list(zip(*kept))
    part = weight_grads(cuts, heads, slots, rows_all, families[:3], families[3:], sums_own, sums_rows, sums_up)
    for m in range(micros):
        if m:
            send, _ = lax.optimization_barrier((sent[m], (sent[m - 1], part)))
            sent[m] = lax.all_to_all(send, "seq", split_axis=0, concat_axis=0, tiled=True)
        if m == 0:
            grad_logits = place_blocks(sent[m], m, micros, dealing, grad_logits)
    ys = [y.reshape(per, piece, model) for y, _ in returned]
    dxs = [dx.reshape(groups, per, piece, -1) for _, dx in returned]
    part = part.reshape(groups, slots, own_rows, -1)
    part, _ = lax.optimization_barrier((part, grad_logits))
    part, all_y, all_dx = finish(part, ys, dxs, slots, groups, 7)
    out_tokens, grad_tokens, dq, dk, dv, dwo, dwu, dwd, dbq, dbv, dbu, *plain = deliver(
        cuts, heads, unit, dealing, part, all_y, all_dx
    )
    for m in range(1, micros):
        grad_logits = place_blocks(sent[m], m, micros, dealing, grad_logits)

    plain = [row.reshape(-1) for row in plain]
    return (
        out_tokens,
        jnp.transpose(logits, (0, 2, 1, 3))[:, None],
        jnp.transpose(grad_tokens, (0, 1, 3, 2)),
        jnp.transpose(grad_logits, (0, 1, 3, 2, 4)),
        dq,
        dbq,
        dk,
        dv,
        dbv,
        dwo,
        *plain[:3],
        dwu,
        dbu,
        dwd.T,
        *plain[3:],
    )


def solution(mesh):
    placed = (
        P(None, None, "seq", None),
        P(None, None, "seq", "head", None),
        P(),
        P(),
        P("seq", "head"),
        P("head", "seq"),
        P("seq", "head"),
        P("seq", "head"),
        P("head", "seq"),
        P("head", "seq"),
        P("seq"),
        P("seq"),
        P("seq"),
        P("seq", "head"),
        P("head", "seq"),
        P("head", "seq"),
        P("seq"),
        P("seq"),
        P("seq"),
        P(None, None, "seq", None),
        P(None, "seq", None, "head", None),
    )
    return jax.shard_map(
        on_device if fits(mesh) else on_device_general,
        mesh=mesh,
        in_specs=placed,
        out_specs=(
            P(None, None, "seq", None),
            P(None, "seq", None, "head", None),
            P(None, None, "seq", "head"),
            P(None, None, "seq", "head", None),
            P("seq", "head"),
            P("head", "seq"),
            P("seq", "head"),
            P("seq", "head"),
            P("head", "seq"),
            P("head", "seq"),
            P("seq"),
            P("seq"),
            P("seq"),
            P("seq", "head"),
            P("head", "seq"),
            P("head", "seq"),
            P("seq"),
            P("seq"),
            P("seq"),
        ),
        check_vma=False,
    )
```

```python
import functools

import jax
import jax.numpy as jnp
from jax import lax
from jax.experimental import pallas as pl
from jax.experimental.pallas import tpu as pltpu
from jax.sharding import PartitionSpec as P

HEAD_DIM = 64
BF16, F32 = jnp.bfloat16, jnp.float32
VMEM_LIMIT = 60 * 1024 * 1024


epsilon = 1e-12


def cut_along(x, dim, peers):
    before, after = (x.shape[:dim], x.shape[dim + 1 :])
    return jnp.moveaxis(x.reshape(*before, peers, -1, *after), dim, 0)


def sum_at_owner(x, axis, dim):
    blocks = cut_along(x, dim, lax.axis_size(axis))
    arrived = lax.all_to_all(blocks, axis, split_axis=0, concat_axis=0, tiled=True)
    return arrived.astype(jnp.float32).sum(axis=0)


def side_by_side(arrays, axis, dim, along):
    both = jnp.concatenate(arrays, axis=along)
    result, at, finished = (sum_at_owner(both, axis, dim), 0, [])
    for a in arrays:
        finished.append(lax.slice_in_dim(result, at, at + a.shape[along], axis=along))
        at += a.shape[along]
    return tuple(finished)


def side_by_side_2(arrays, axis, dim, along):
    columns = [a.reshape(*a.shape[:along], -1) for a in arrays]
    both = jnp.concatenate(columns, axis=along)
    result, at, finished = (sum_at_owner(both, axis, dim), 0, [])
    for a, column in zip(arrays, columns):
        slab = result[..., at : at + column.shape[along]]
        finished.append(slab.reshape(*slab.shape[:along], *a.shape[along:]))
        at += column.shape[along]
    return tuple(finished)


def layer_norm(values, gain, shift):
    center = values - jnp.mean(values, axis=-1, keepdims=True)
    spread = jnp.mean(center * center, axis=-1, keepdims=True)
    return center * lax.rsqrt(spread + epsilon) * gain + shift


def exact_gelu(values):
    return jax.nn.gelu(values, approximate=False)


def mask_scores(raw_scores, length):
    key_valid = jnp.arange(raw_scores.shape[2]) < length
    return jnp.where(key_valid[None, None, :], raw_scores, -jnp.inf)


def on_device_general(
    tokens,
    prev_logits,
    lengths,
    dealing,
    w_query,
    b_query,
    w_key,
    w_value,
    b_value,
    w_out,
    b_out,
    gain_one,
    shift_one,
    w_up,
    b_up,
    w_down,
    b_down,
    gain_two,
    shift_two,
    cot_tokens,
    cot_logits,
):
    micro_count = tokens.shape[0]
    seq_count = tokens.shape[1]
    piece_rows = tokens.shape[2]
    model_width = tokens.shape[3]
    extent = piece_rows * seq_count
    heads_here = prev_logits.shape[3]
    width_here = model_width // lax.axis_size("head")
    score_scale = HEAD_DIM ** (-0.5)
    owner_slot = lax.axis_index("seq")
    head_slot = lax.axis_index("head")
    zero_shift = jnp.zeros((model_width,), jnp.float32)
    out_token_list = []
    out_logit_list = []
    grad_token_list = []
    grad_logit_list = []
    grad_totals = None
    for micro_batch in range(micro_count):
        full_weights = (
            lax.all_gather(w_query, "seq", axis=0, tiled=True),
            lax.all_gather(w_key, "seq", axis=0, tiled=True),
            lax.all_gather(w_value, "seq", axis=0, tiled=True),
            lax.all_gather(w_out, "seq", axis=1, tiled=True),
            lax.all_gather(w_up, "seq", axis=0, tiled=True),
            lax.all_gather(w_down, "seq", axis=1, tiled=True),
            lax.all_gather(b_query, "seq", axis=1, tiled=True),
            lax.all_gather(b_value, "seq", axis=1, tiled=True),
            lax.all_gather(b_out, "seq", axis=0, tiled=True),
            lax.all_gather(gain_one, "seq", axis=0, tiled=True),
            lax.all_gather(shift_one, "seq", axis=0, tiled=True),
            lax.all_gather(b_up, "seq", axis=1, tiled=True),
            lax.all_gather(b_down, "seq", axis=0, tiled=True),
            lax.all_gather(gain_two, "seq", axis=0, tiled=True),
            lax.all_gather(shift_two, "seq", axis=0, tiled=True),
        )
        (
            query_full,
            key_full,
            value_full,
            out_full,
            up_full,
            down_full,
            bias_query,
            bias_value,
            bias_out,
            gain_first,
            shift_first,
            bias_up,
            bias_down,
            gain_second,
            shift_second,
        ) = full_weights
        inverse = (
            jnp.zeros((seq_count,), jnp.int32)
            .at[dealing[micro_batch]]
            .set(jnp.arange(seq_count, dtype=jnp.int32))
        )
        own_sequence = inverse[owner_slot]
        own_length = lengths[micro_batch, own_sequence]
        send_tokens = jnp.take(tokens[micro_batch], inverse, axis=0)
        send_prev = jnp.take(prev_logits[micro_batch], inverse, axis=0).reshape(
            seq_count, piece_rows, heads_here * extent
        )
        send_cot = jnp.take(cot_tokens[micro_batch], inverse, axis=0)
        got_tokens, got_prev, got_cot = (
            lax.all_to_all(send_tokens, "seq", split_axis=0, concat_axis=1, tiled=True),
            lax.all_to_all(send_prev, "seq", split_axis=0, concat_axis=1, tiled=True),
            lax.all_to_all(send_cot, "seq", split_axis=0, concat_axis=1, tiled=True),
        )
        rows_in = got_tokens.reshape(extent, model_width)
        prev_rows = got_prev.reshape(extent, heads_here, extent).astype(jnp.float32)
        cot_rows = got_cot.reshape(extent, model_width).astype(jnp.float32)
        query_pre = jnp.dot(rows_in, query_full, preferred_element_type=jnp.float32)
        queries = (query_pre + bias_query.reshape(-1).astype(jnp.float32)).astype(jnp.bfloat16)
        keys_all = jnp.dot(rows_in, key_full, preferred_element_type=jnp.float32).astype(
            jnp.bfloat16
        )
        value_pre = jnp.dot(rows_in, value_full, preferred_element_type=jnp.float32)
        values = (value_pre + bias_value.reshape(-1).astype(jnp.float32)).astype(jnp.bfloat16)
        query_heads = queries.reshape(extent, heads_here, HEAD_DIM)
        key_heads = keys_all.reshape(extent, heads_here, HEAD_DIM)
        value_heads = values.reshape(extent, heads_here, HEAD_DIM)
        raw_scores = (
            jnp.einsum("qhd,khd->qhk", query_heads, key_heads, preferred_element_type=jnp.float32)
            * score_scale
            + prev_rows
        )
        masked = mask_scores(raw_scores, own_length)
        row_top = jnp.max(masked, axis=-1, keepdims=True)
        shifted_exp = jnp.exp(masked - row_top)
        row_total = jnp.sum(shifted_exp, axis=-1, keepdims=True)
        attend = shifted_exp / row_total
        log_total = row_top + jnp.log(row_total)
        out_logit_list.append(raw_scores.astype(jnp.bfloat16)[None])
        context = (
            jnp.einsum(
                "qhk,khd->qhd",
                attend.astype(jnp.bfloat16),
                value_heads,
                preferred_element_type=jnp.float32,
            )
            .astype(jnp.bfloat16)
            .reshape(extent, heads_here * HEAD_DIM)
        )
        out_part = jnp.dot(context, out_full, preferred_element_type=jnp.float32)
        branch = lax.psum(out_part, "head") + bias_out.astype(jnp.float32)
        resid_one = rows_in.astype(jnp.float32) + branch
        hidden = layer_norm(
            resid_one, gain_first.astype(jnp.float32), shift_first.astype(jnp.float32)
        )
        hidden_low = hidden.astype(jnp.bfloat16)
        before_gelu = jnp.dot(
            hidden_low, up_full, preferred_element_type=jnp.float32
        ) + bias_up.reshape(-1).astype(jnp.float32)
        active = exact_gelu(before_gelu).astype(jnp.bfloat16)
        down_part = jnp.dot(active, down_full, preferred_element_type=jnp.float32)
        resid_two = hidden + (
            lax.psum(down_part.astype(jnp.bfloat16), "head").astype(jnp.float32)
            + bias_down.astype(jnp.float32)
        )
        result = layer_norm(
            resid_two, gain_second.astype(jnp.float32), shift_second.astype(jnp.float32)
        )
        out_rows = result.astype(jnp.bfloat16)
        (
            back_query,
            back_key,
            back_value,
            back_out,
            back_up,
            back_down,
            back_gain_first,
            back_gain_second,
        ) = (
            lax.all_gather(w_query, "seq", axis=0, tiled=True),
            lax.all_gather(w_key, "seq", axis=0, tiled=True),
            lax.all_gather(w_value, "seq", axis=0, tiled=True),
            lax.all_gather(w_out, "seq", axis=1, tiled=True),
            lax.all_gather(w_up, "seq", axis=0, tiled=True),
            lax.all_gather(w_down, "seq", axis=1, tiled=True),
            lax.all_gather(gain_one, "seq", axis=0, tiled=True),
            lax.all_gather(gain_two, "seq", axis=0, tiled=True),
        )
        norm_two_value, norm_two_back = jax.vjp(
            layer_norm, resid_two, back_gain_second.astype(jnp.float32), zero_shift
        )
        d_resid_two, d_gain_two, d_shift_two = norm_two_back(cot_rows)
        d_b_down = jnp.sum(d_resid_two, axis=0)
        grad_two_low = d_resid_two.astype(jnp.bfloat16)
        d_w_down = jnp.einsum("rf,rd->fd", active, grad_two_low, preferred_element_type=jnp.float32)
        d_active = jnp.einsum(
            "rd,fd->rf", grad_two_low, back_down, preferred_element_type=jnp.float32
        )
        gelu_value, gelu_back = jax.vjp(exact_gelu, before_gelu)
        d_before = gelu_back(d_active)[0]
        d_b_up = jnp.sum(d_before, axis=0).reshape(heads_here, -1)
        before_low = d_before.astype(jnp.bfloat16)
        d_w_up = jnp.einsum("rd,rf->df", hidden_low, before_low, preferred_element_type=jnp.float32)
        up_part = jnp.einsum("rf,df->rd", before_low, back_up, preferred_element_type=jnp.float32)
        d_hidden = d_resid_two + lax.psum(up_part.astype(jnp.bfloat16), "head").astype(jnp.float32)
        norm_one_value, norm_one_back = jax.vjp(
            layer_norm, resid_one, back_gain_first.astype(jnp.float32), zero_shift
        )
        d_resid_one, d_gain_one, d_shift_one = norm_one_back(d_hidden)
        d_b_out = jnp.sum(d_resid_one, axis=0)
        grad_one_low = d_resid_one.astype(jnp.bfloat16)
        d_w_out = jnp.einsum("rc,rd->cd", context, grad_one_low, preferred_element_type=jnp.float32)
        d_context = (
            jnp.einsum("rd,cd->rc", grad_one_low, back_out, preferred_element_type=jnp.float32)
            .astype(jnp.bfloat16)
            .reshape(extent, heads_here, HEAD_DIM)
        )
        raw_again = (
            jnp.einsum("qhd,khd->qhk", query_heads, key_heads, preferred_element_type=jnp.float32)
            * score_scale
            + prev_rows
        )
        attend_again = jnp.exp(mask_scores(raw_again, own_length) - log_total)
        d_attend = jnp.einsum(
            "qhd,khd->qhk", d_context, value_heads, preferred_element_type=jnp.float32
        )
        d_values = jnp.einsum(
            "qhk,qhd->khd",
            attend_again.astype(jnp.bfloat16),
            d_context,
            preferred_element_type=jnp.float32,
        )
        d_scores = attend_again * (
            d_attend - jnp.sum(attend_again * d_attend, axis=-1, keepdims=True)
        ) + cot_logits[micro_batch, 0].astype(jnp.float32)
        scores_low = d_scores.astype(jnp.bfloat16)
        d_queries = (
            jnp.einsum("qhk,khd->qhd", scores_low, key_heads, preferred_element_type=jnp.float32)
            * score_scale
        )
        d_keys = (
            jnp.einsum("qhk,qhd->khd", scores_low, query_heads, preferred_element_type=jnp.float32)
            * score_scale
        )
        d_b_query = jnp.sum(d_queries, axis=0)
        d_b_value = jnp.sum(d_values, axis=0)
        queries_low = d_queries.astype(jnp.bfloat16).reshape(extent, heads_here * HEAD_DIM)
        keys_low = d_keys.astype(jnp.bfloat16).reshape(extent, heads_here * HEAD_DIM)
        values_low = d_values.astype(jnp.bfloat16).reshape(extent, heads_here * HEAD_DIM)
        d_w_query = jnp.einsum(
            "rd,rc->dc", rows_in, queries_low, preferred_element_type=jnp.float32
        )
        d_w_key = jnp.einsum("rd,rc->dc", rows_in, keys_low, preferred_element_type=jnp.float32)
        d_w_value = jnp.einsum("rd,rc->dc", rows_in, values_low, preferred_element_type=jnp.float32)
        input_part = jnp.einsum(
            "rc,dc->rd", queries_low, back_query, preferred_element_type=jnp.float32
        )
        input_part = input_part + jnp.einsum(
            "rc,dc->rd", keys_low, back_key, preferred_element_type=jnp.float32
        )
        input_part = input_part + jnp.einsum(
            "rc,dc->rd", values_low, back_value, preferred_element_type=jnp.float32
        )
        input_share = lax.psum_scatter(
            input_part.astype(jnp.bfloat16), "head", scatter_dimension=1, tiled=True
        ).astype(jnp.float32)
        resid_share = lax.dynamic_slice_in_dim(d_resid_one, head_slot * width_here, width_here, 1)
        grad_rows = (resid_share + input_share).astype(jnp.bfloat16)
        back_tokens, back_grads, back_logits = (
            lax.all_to_all(
                out_rows.reshape(seq_count, piece_rows, model_width),
                "seq",
                split_axis=0,
                concat_axis=0,
                tiled=True,
            ),
            lax.all_to_all(
                grad_rows.reshape(seq_count, piece_rows, width_here),
                "seq",
                split_axis=0,
                concat_axis=0,
                tiled=True,
            ),
            lax.all_to_all(
                scores_low.reshape(seq_count, piece_rows, heads_here * extent),
                "seq",
                split_axis=0,
                concat_axis=0,
                tiled=True,
            ),
        )
        out_token_list.append(jnp.take(back_tokens, dealing[micro_batch], axis=0))
        grad_token_list.append(jnp.take(back_grads, dealing[micro_batch], axis=0))
        grad_logit_list.append(
            jnp.take(back_logits, dealing[micro_batch], axis=0).reshape(
                seq_count, piece_rows, heads_here, extent
            )
        )
        local_grads = (
            d_w_query,
            d_b_query,
            d_w_key,
            d_w_value,
            d_b_value,
            d_w_out,
            d_b_out,
            d_gain_one,
            d_shift_one,
            d_w_up,
            d_b_up,
            d_w_down,
            d_b_down,
            d_gain_two,
            d_shift_two,
        )
        if grad_totals is None:
            grad_totals = local_grads
        else:
            grad_totals = tuple((total + extra for total, extra in zip(grad_totals, local_grads)))
    final_grads = (
        sum_at_owner(grad_totals[0].astype(jnp.bfloat16), "seq", 0),
        sum_at_owner(grad_totals[1].astype(jnp.bfloat16), "seq", 1),
        *side_by_side(
            (grad_totals[2].astype(jnp.bfloat16), grad_totals[3].astype(jnp.bfloat16)), "seq", 0, 1
        ),
        sum_at_owner(grad_totals[4].astype(jnp.bfloat16), "seq", 1),
        sum_at_owner(grad_totals[5].astype(jnp.bfloat16), "seq", 1),
        sum_at_owner(grad_totals[6].astype(jnp.bfloat16), "seq", 0),
        sum_at_owner(grad_totals[7].astype(jnp.bfloat16), "seq", 0),
        *side_by_side_2(
            (grad_totals[8].astype(jnp.bfloat16), grad_totals[9].astype(jnp.bfloat16)), "seq", 0, 1
        ),
        sum_at_owner(grad_totals[10].astype(jnp.bfloat16), "seq", 1),
        sum_at_owner(grad_totals[11].astype(jnp.bfloat16), "seq", 1),
        sum_at_owner(grad_totals[12].astype(jnp.bfloat16), "seq", 0),
        sum_at_owner(grad_totals[13].astype(jnp.bfloat16), "seq", 0),
        sum_at_owner(grad_totals[14].astype(jnp.bfloat16), "seq", 0),
    )
    out_tokens = jnp.stack(out_token_list, axis=0)
    out_logits = jnp.stack(out_logit_list, axis=0)
    grad_tokens = jnp.stack(grad_token_list, axis=0)
    grad_logits = jnp.stack(grad_logit_list, axis=0)
    return (
        out_tokens,
        out_logits,
        grad_tokens,
        grad_logits,
        final_grads[0],
        final_grads[1],
        final_grads[2],
        final_grads[3],
        final_grads[4],
        final_grads[5],
        final_grads[6],
        final_grads[7],
        final_grads[8],
        final_grads[9],
        final_grads[10],
        final_grads[11],
        final_grads[12],
        final_grads[13],
        final_grads[14],
    )

def cost(flops, moved):
    return pl.CostEstimate(flops=int(flops) // 100, bytes_accessed=int(moved) // 100, transcendentals=0)


def params(**more):
    return pltpu.CompilerParams(vmem_limit_bytes=VMEM_LIMIT, **more)


def dot(a, b, ca, cb):
    return lax.dot_general(a, b, (((ca,), (cb,)), ((), ())), preferred_element_type=F32)


def whole(x):
    return pl.BlockSpec(x.shape, lambda *_: (0,) * len(x.shape))


def move_blocks(reads, writes, buffers, in_sem, out_sem):
    ins = [pltpu.make_async_copy(r, v, in_sem.at[i]) for i, (r, v) in enumerate(zip(reads, buffers))]
    outs = [pltpu.make_async_copy(v, w, out_sem.at[i]) for i, (v, w) in enumerate(zip(buffers, writes))]
    for copy in ins:
        copy.start()
    for copy, out in zip(ins, outs):
        copy.wait()
        out.start()
    for out in outs:
        out.wait()


SMALL = pl.BlockSpec(memory_space=pltpu.SMEM)
ANYWHERE = pl.BlockSpec(memory_space=pl.ANY)


def inverse_of(dealing_ref, inverse_ref, micros, slots):
    for m in micros:
        for i in range(slots):
            inverse_ref[dealing_ref[m, i]] = i


def pick_copies(micro, count, inverse_ref, x_ref, o_ref, buffer):
    steps = range(count)
    return (
        [x_ref.at[micro, inverse_ref[i]] for i in steps],
        [o_ref.at[i] for i in steps],
        [buffer.at[i] for i in steps],
    )


def pick_kernel(micro, count, dealing_ref, x_ref, o_ref, buffer, inverse_ref, in_sem, out_sem):
    inverse_of(dealing_ref, inverse_ref, [micro], count)
    move_blocks(*pick_copies(micro, count, inverse_ref, x_ref, o_ref, buffer), in_sem, out_sem)


def pick_blocks(stacked, micro, dealing):
    count = stacked.shape[1]
    block = stacked.shape[2:]
    dma = pltpu.SemaphoreType.DMA
    return pl.pallas_call(
        functools.partial(pick_kernel, micro, count),
        out_shape=jax.ShapeDtypeStruct((count, *block), stacked.dtype),
        in_specs=[SMALL, ANYWHERE],
        out_specs=ANYWHERE,
        scratch_shapes=[
            pltpu.VMEM((count, *block), stacked.dtype),
            pltpu.SMEM((count,), jnp.int32),
            dma((count,)),
            dma((count,)),
        ],
        compiler_params=params(),
        cost_estimate=cost(0, 4 * stacked.size // stacked.shape[0]),
        name="pick_blocks",
    )(dealing, stacked)


PLAIN, QUERY_AT, VALUE_AT, UP_AT, VECTOR_ROWS = 6, 8, 16, 24, 32


def prepare_kernel(
    micros, slots, groups, dealing_ref, prev_ref, tokens_ref, cot_ref,
    wq_ref, wk_ref, wv_ref, wo_ref, wu_ref, wd_ref, bq_ref, bv_ref, bu_ref, plain_refs,
    send_ref, piece_ref, pack_ref, info_ref, block_buffer, piece_buffer, vector_scr, inverse_refs, in_sem, out_sem,
    lengths_ref,
):
    here, head = lax.axis_index("seq"), lax.axis_index("head")
    for m in range(micros):
        inverse_of(dealing_ref, inverse_refs[m], [m], slots)
        info_ref[m, 0] = lengths_ref[m, inverse_refs[m][here]]
        info_ref[m, 1] = lax.rem(here, groups)
    reads, writes, buffers = [], [], []
    for step in range(2):
        slot = lax.rem(head - here // 2 + groups, groups) + groups * lax.rem(here + step, 2)
        for a, array_ref in enumerate((tokens_ref, cot_ref)):
            for m in range(micros):
                n = a * micros + m
                reads.append(array_ref.at[m, inverse_refs[m][slot]])
                writes.append(piece_ref.at[step, n])
                buffers.append(piece_buffer.at[step, n])
    blocks = pick_copies(0, slots, inverse_refs[0], prev_ref, send_ref, block_buffer)
    reads, writes, buffers = reads + blocks[0], writes + blocks[1], buffers + blocks[2]
    for i, (source, target) in enumerate(zip(reads, buffers)):
        pltpu.make_async_copy(source, target, in_sem.at[i]).start()

    at = 0
    turned = wo_ref[...].astype(F32).T.astype(BF16)
    for block in (wq_ref[...], wk_ref[...], wv_ref[...], turned, wu_ref[...], wd_ref[...]):
        pack_ref[:, at : at + block.shape[1]] = block
        at += block.shape[1]
    vector_scr[...] = jnp.zeros_like(vector_scr)
    for i, ref in enumerate(plain_refs):
        vector_scr[i : i + 1, : ref.shape[1]] = ref[...].astype(F32)
    for first, ref in ((QUERY_AT, bq_ref), (VALUE_AT, bv_ref), (UP_AT, bu_ref)):
        vector_scr[first : first + ref.shape[0], : ref.shape[1]] = ref[...].astype(F32)
    pack_ref[:VECTOR_ROWS, at:] = vector_scr[...].astype(BF16)
    pack_ref[VECTOR_ROWS:, at:] = jnp.zeros_like(pack_ref[VECTOR_ROWS:, at:])

    for i, (source, target, buffer) in enumerate(zip(reads, writes, buffers)):
        pltpu.make_async_copy(source, buffer, in_sem.at[i]).wait()
        pltpu.make_async_copy(buffer, target, out_sem.at[i]).start()
    for i, (target, buffer) in enumerate(zip(writes, buffers)):
        pltpu.make_async_copy(buffer, target, out_sem.at[i]).wait()


def prepare(lengths, dealing, prev, tokens, cot_tokens, weights, head_vectors, plain_vectors, groups):
    micros, slots = prev.shape[:2]
    block, row = prev.shape[2:], tokens.shape[2:]
    dma = pltpu.SemaphoreType.DMA
    copies = slots + 4 * micros
    columns = sum(w.size for w in weights) // weights[0].shape[0] + 128
    in_vmem = pl.BlockSpec(memory_space=pltpu.VMEM)
    flat = [*weights, *head_vectors]

    def body(lengths_ref, *refs):
        fixed = 4 + len(flat)
        plain_refs = refs[fixed : fixed + len(plain_vectors)]
        rest = refs[fixed + len(plain_vectors) :]
        made, buffers = rest[:4], rest[4:7]
        prepare_kernel(
            micros, slots, groups, *refs[:fixed], plain_refs, *made, *buffers,
            rest[7 : 7 + micros], *rest[7 + micros :], lengths_ref,
        )

    return pl.pallas_call(
        body,
        out_shape=(
            jax.ShapeDtypeStruct((slots, *block), prev.dtype),
            jax.ShapeDtypeStruct((2, 2 * micros, *row), tokens.dtype),
            jax.ShapeDtypeStruct((weights[0].shape[0], columns), BF16),
            jax.ShapeDtypeStruct((micros, 2), jnp.int32),
        ),
        in_specs=[SMALL, SMALL, ANYWHERE, ANYWHERE, ANYWHERE] + [in_vmem] * (len(flat) + len(plain_vectors)),
        out_specs=(ANYWHERE, ANYWHERE, in_vmem, SMALL),
        scratch_shapes=[
            pltpu.VMEM((slots, *block), prev.dtype),
            pltpu.VMEM((2, 2 * micros, *row), tokens.dtype),
            pltpu.VMEM((VECTOR_ROWS, 128), F32),
        ]
        + [pltpu.SMEM((slots,), jnp.int32)] * micros
        + [dma((copies,)), dma((copies,))],
        compiler_params=params(),
        cost_estimate=cost(0, 4 * prev.size // micros),
        name="prepare",
    )(lengths, dealing, prev, tokens, cot_tokens, *flat, *plain_vectors)


def unpack_kernel(heads, x_ref, qkv_ref, up_ref, plain_ref):
    groups, slots = x_ref.shape[:2]
    width = heads * HEAD_DIM
    qkv_ref[...] = jnp.zeros_like(qkv_ref)
    lanes = plain_ref.shape[1] // slots
    per_head = HEAD_DIM // slots
    unit = up_ref.shape[2] // heads
    per_unit = unit // slots
    for s in range(slots):
        for h in range(groups):
            block = x_ref[h, s].astype(F32)
            if h == 0:
                plain_ref[:, s * lanes : (s + 1) * lanes] = block[:8, :lanes]
            for j in range(heads):
                at = j * HEAD_DIM + s * per_head
                qkv_ref[h, :, at : at + per_head] = block[QUERY_AT + j : QUERY_AT + j + 1, :per_head]
                at += 2 * width
                qkv_ref[h, :, at : at + per_head] = block[VALUE_AT + j : VALUE_AT + j + 1, :per_head]
                at = j * unit + s * per_unit
                up_ref[h, :, at : at + per_unit] = block[UP_AT + j : UP_AT + j + 1, :per_unit]


def unpack_vectors(shards, heads, width, unit, model):
    groups, slots, _, columns = shards.shape
    last = columns // 128 - 1
    shape = jax.ShapeDtypeStruct
    return pl.pallas_call(
        functools.partial(unpack_kernel, heads),
        out_shape=(
            shape((groups, 1, 3 * width), F32),
            shape((groups, 1, unit), F32),
            shape((8, model), F32),
        ),
        grid=(1,),
        in_specs=[pl.BlockSpec((groups, slots, VECTOR_ROWS, 128), lambda i: (0, 0, 0, last))],
        out_specs=(
            pl.BlockSpec((groups, 1, 3 * width), lambda i: (0, 0, 0)),
            pl.BlockSpec((groups, 1, unit), lambda i: (0, 0, 0)),
            pl.BlockSpec((8, model), lambda i: (0, 0)),
        ),
        compiler_params=params(),
        cost_estimate=cost(0, 4 * groups * slots * VECTOR_ROWS * 128),
        name="unpack_vectors",
    )(shards)


def place_kernel(micro, count, index_ref, x_ref, *rest):
    o_ref, buffer, in_sem, out_sem = rest[-4:]
    steps = range(count)
    move_blocks(
        [x_ref.at[index_ref[micro, i]] for i in steps],
        [o_ref.at[micro, i] for i in steps],
        [buffer.at[i] for i in steps],
        in_sem,
        out_sem,
    )


def place_blocks(blocks, micro, micros, index, into):
    count = blocks.shape[0]
    others = [] if into is None else [into]
    dma = pltpu.SemaphoreType.DMA
    return pl.pallas_call(
        functools.partial(place_kernel, micro, count),
        out_shape=jax.ShapeDtypeStruct((micros, *blocks.shape), blocks.dtype),
        in_specs=[SMALL, ANYWHERE] + [ANYWHERE for _ in others],
        out_specs=ANYWHERE,
        scratch_shapes=[pltpu.VMEM(blocks.shape, blocks.dtype), dma((count,)), dma((count,))],
        input_output_aliases={2: 0} if others else {},
        compiler_params=params(),
        cost_estimate=cost(0, 4 * blocks.size),
        name="place_blocks",
    )(index, blocks, *others)


def project_kernel(x_ref, w_ref, b_ref, *outs):
    columns = outs[0].shape[2]
    for m, o_ref in enumerate(outs):
        o_ref[0] = (dot(x_ref[m], w_ref[0, :, :columns], 1, 0) + b_ref[0]).astype(BF16)


def project(x, weights, bias):
    micros, rows, width = x.shape[0] // 2, *x.shape[1:]
    groups, _, columns = bias.shape
    return pl.pallas_call(
        project_kernel,
        out_shape=(jax.ShapeDtypeStruct((groups, rows, columns), BF16),) * micros,
        grid=(groups,),
        in_specs=[
            pl.BlockSpec((micros, rows, width), lambda h: (0, 0, 0)),
            pl.BlockSpec((1, width, width), lambda h: (h, 0, 0)),
            pl.BlockSpec((1, 1, columns), lambda h: (h, 0, 0)),
        ],
        out_specs=(pl.BlockSpec((1, rows, columns), lambda h: (h, 0, 0)),) * micros,
        compiler_params=params(),
        cost_estimate=cost(2 * micros * groups * rows * width * columns, 2 * groups * columns * (width + rows)),
        name="project",
    )(x, weights, bias)


def head_mask(shape, head):
    lane = lax.broadcasted_iota(jnp.int32, shape, len(shape) - 1)
    return lane // HEAD_DIM == head


def gather_rows(shift, qkv_ref, groups, rows, width, q_scr, k_scr, v_scr):
    for g in range(groups):
        block = qkv_ref[(shift + g) % groups]
        q_scr[g * rows : (g + 1) * rows] = block[:, :width]
        k_scr[g * rows : (g + 1) * rows] = block[:, width : 2 * width]
        v_scr[g * rows : (g + 1) * rows] = block[:, 2 * width :]


def forward_kernel(heads, micro, info_ref, qkv_ref, prev_ref, *rest):
    logit_ref, attend_ref, context_ref, q_scr, k_scr, v_scr = rest[-6:]
    step = pl.program_id(0)
    groups, rows, columns = qkv_ref.shape
    piece, extent = prev_ref.shape[2:]
    width = columns // 3

    @pl.when(step == 0)
    def _():
        gather_rows(info_ref[micro, 1], qkv_ref, groups, rows, width, q_scr, k_scr, v_scr)

    q = q_scr[pl.ds(pl.multiple_of(step * piece, 16), piece), :]
    key_valid = lax.broadcasted_iota(jnp.int32, (1, extent), 1) < info_ref[micro, 0]
    total = jnp.zeros((piece, width), F32)
    for h in range(heads):
        mine = head_mask((1, width), h)
        q_head = jnp.where(mine, q, jnp.zeros_like(q))
        raw = dot(q_head, k_scr[...], 1, 1) * HEAD_DIM ** (-0.5) + prev_ref[0, h].astype(F32)
        logit_ref[0, h] = raw.astype(BF16)
        masked = jnp.where(key_valid, raw, -jnp.inf)
        top = jnp.max(masked, axis=-1, keepdims=True)
        grown = jnp.exp(masked - top)
        attend = grown * (1.0 / jnp.sum(grown, axis=-1, keepdims=True))
        low = attend.astype(BF16)
        attend_ref[0, h] = low
        total = total + jnp.where(mine, dot(low, v_scr[...], 1, 0), 0.0)
    context_ref[0] = total.astype(BF16)


def attention_forward(info, qkv, prev, micro, micros, logits_into):
    groups, rows, columns = qkv.shape
    pieces, heads, piece, extent = prev.shape
    width = columns // 3
    per = rows // piece
    others = [] if logits_into is None else [logits_into]
    return pl.pallas_call(
        functools.partial(forward_kernel, heads, micro),
        out_shape=(
            jax.ShapeDtypeStruct((micros, heads, extent, extent), BF16),
            jax.ShapeDtypeStruct(prev.shape, BF16),
            jax.ShapeDtypeStruct((groups, rows, width), BF16),
        ),
        grid_spec=pltpu.PrefetchScalarGridSpec(
            num_scalar_prefetch=1,
            grid=(pieces,),
            in_specs=[
                pl.BlockSpec((groups, rows, columns), lambda j, i: (0, 0, 0)),
                pl.BlockSpec((1, heads, piece, extent), lambda j, i: (j, 0, 0, 0)),
            ]
            + [pl.BlockSpec(memory_space=pl.ANY) for _ in others],
            out_specs=(
                pl.BlockSpec((1, heads, piece, extent), lambda j, i: (micro, 0, j, 0)),
                pl.BlockSpec((1, heads, piece, extent), lambda j, i: (j, 0, 0, 0)),
                pl.BlockSpec((1, piece, width), lambda j, i: ((j // per + i[micro, 1]) % groups, j % per, 0)),
            ),
            scratch_shapes=[pltpu.VMEM((extent, width), BF16)] * 3,
        ),
        input_output_aliases={3: 0} if others else {},
        compiler_params=params(),
        cost_estimate=cost(4 * heads * extent * extent * HEAD_DIM * 4, 6 * heads * extent * extent),
        name="attention_forward",
    )(info, qkv, prev, *others)


def backward_kernel(
    heads, micro, info_ref, qkv_ref, attend_ref, context_ref, dcon_ref, cot_ref,
    send_ref, dqkv_ref, sums_ref, q_scr, k_scr, v_scr, dq_scr, dk_scr, dv_scr,
):
    step = pl.program_id(0)
    groups, rows, columns = qkv_ref.shape
    piece, extent = attend_ref.shape[2:]
    width = columns // 3
    scale = HEAD_DIM ** (-0.5)

    @pl.when(step == 0)
    def _():
        gather_rows(info_ref[micro, 1], qkv_ref, groups, rows, width, q_scr, k_scr, v_scr)
        dk_scr[...] = jnp.zeros_like(dk_scr)
        dv_scr[...] = jnp.zeros_like(dv_scr)

    here = pl.ds(pl.multiple_of(step * piece, 16), piece)
    q = q_scr[here, :]
    dcon = dcon_ref[0]
    both = dcon.astype(F32) * context_ref[0].astype(F32)
    dq = jnp.zeros((piece, width), F32)
    for h in range(heads):
        mine = head_mask((1, width), h)
        dcon_head = jnp.where(mine, dcon, jnp.zeros_like(dcon))
        q_head = jnp.where(mine, q, jnp.zeros_like(q))
        low = attend_ref[0, h]
        delta = jnp.sum(jnp.where(mine, both, 0.0), axis=-1, keepdims=True)
        dprob = dot(dcon_head, v_scr[...], 1, 1)
        dscore = low.astype(F32) * (dprob - delta) + cot_ref[0, h].astype(F32)
        dlow = dscore.astype(BF16)
        send_ref[0, h] = dlow
        dq = dq + jnp.where(mine, dot(dlow, k_scr[...], 1, 0), 0.0)
        dk_scr[...] += dot(dlow, q_head, 0, 0)
        dv_scr[...] += dot(low, dcon_head, 0, 0)
    dq_scr[here, :] = dq * scale

    @pl.when(step == pl.num_programs(0) - 1)
    def _():
        sums_ref[0:1, :] = jnp.sum(dq_scr[...], axis=0, keepdims=True)
        sums_ref[1:2, :] = jnp.sum(dv_scr[...], axis=0, keepdims=True)
        for g in range(groups):
            part = slice(g * rows, (g + 1) * rows)
            dqkv_ref[(info_ref[micro, 1] + g) % groups] = jnp.concatenate(
                [dq_scr[part], dk_scr[part] * scale, dv_scr[part]], axis=1
            ).astype(BF16)


def attention_backward(info, qkv, attend, context, dcontext, cot, micro):
    groups, rows, columns = qkv.shape
    pieces, heads, piece, extent = attend.shape
    width = columns // 3
    per = rows // piece
    rotated = pl.BlockSpec((1, piece, width), lambda j, i: ((j // per + i[micro, 1]) % groups, j % per, 0))
    square = pl.BlockSpec((1, heads, piece, extent), lambda j, i: (j, 0, 0, 0))
    return pl.pallas_call(
        functools.partial(backward_kernel, heads, micro),
        out_shape=(
            jax.ShapeDtypeStruct(attend.shape, BF16),
            jax.ShapeDtypeStruct((groups, rows, columns), BF16),
            jax.ShapeDtypeStruct((2, width), F32),
        ),
        grid_spec=pltpu.PrefetchScalarGridSpec(
            num_scalar_prefetch=1,
            grid=(pieces,),
            in_specs=[
                pl.BlockSpec((groups, rows, columns), lambda j, i: (0, 0, 0)),
                square,
                rotated,
                rotated,
                pl.BlockSpec((1, heads, piece, extent), lambda j, i: (micro, 0, j, 0)),
            ],
            out_specs=(
                square,
                pl.BlockSpec((groups, rows, columns), lambda j, i: (0, 0, 0)),
                pl.BlockSpec((2, width), lambda j, i: (0, 0)),
            ),
            scratch_shapes=[pltpu.VMEM((extent, width), BF16)] * 3
            + [pltpu.VMEM((extent, width), F32)] * 3,
        ),
        compiler_params=params(),
        cost_estimate=cost(8 * heads * extent * extent * HEAD_DIM * 4, 6 * heads * extent * extent),
        name="attention_backward",
    )(info, qkv, attend, context, dcontext, cot)


def normal(values):
    center = values - jnp.mean(values, axis=-1, keepdims=True)
    spread = jnp.mean(center * center, axis=-1, keepdims=True)
    inverse = lax.rsqrt(spread + epsilon)
    return center * inverse, inverse


def normal_back(grad, gain, unit, inverse):
    scaled = grad * gain
    return inverse * (
        scaled
        - jnp.mean(scaled, axis=-1, keepdims=True)
        - unit * jnp.mean(scaled * unit, axis=-1, keepdims=True)
    )


def rows_kernel(
    cuts, micro, con_ref, x_ref, w_ref, bup_ref, vec_ref,
    y_ref, dz_ref, dcon_ref, h1_ref, act_ref, b1_ref, b2_ref, b0_ref, sums_ref, dbup_ref,
    slope, acc, hidden, unit_scr, inv_scr,
):
    groups, rows, width = con_ref.shape
    qkv_end, out_end, up_end, down_end = cuts
    b_out, gain_one, shift_one = vec_ref[0:1, :], vec_ref[1:2, :], vec_ref[2:3, :]
    b_down, gain_two, shift_two = vec_ref[3:4, :], vec_ref[4:5, :], vec_ref[5:6, :]

    branch = b_out + x_ref[micro].astype(F32)
    for h in range(groups):
        branch = branch + dot(con_ref[h], w_ref[h, :, qkv_end:out_end], 1, 1)
    unit_one, inverse_one = normal(branch)
    unit_scr[...] = unit_one
    inv_scr[...] = inverse_one
    hid = unit_one * gain_one + shift_one
    hidden[...] = hid
    h1_ref[...] = hid.astype(BF16)
    acc[...] = hid + b_down

    def up(h, carry):
        u = dot(h1_ref[...], w_ref[h, :, out_end:up_end], 1, 0) + bup_ref[h]
        half = 0.5 * (1.0 + lax.erf(u * 0.7071067811865476))
        act_ref[h] = (u * half).astype(BF16)
        slope[h] = half + u * (jnp.exp(u * u * -0.5) * 0.3989422804014327)
        acc[...] += dot(act_ref[h], w_ref[h, :, up_end:down_end], 1, 1)
        return carry

    lax.fori_loop(0, groups, up, 0)
    unit_two, inverse_two = normal(acc[...])
    y_ref[...] = (unit_two * gain_two + shift_two).astype(BF16)
    cot = x_ref[x_ref.shape[0] // 2 + micro].astype(F32)
    sums_ref[4:5, :] = jnp.sum(cot * unit_two, axis=0, keepdims=True)
    sums_ref[5:6, :] = jnp.sum(cot, axis=0, keepdims=True)
    dz_two = normal_back(cot, gain_two, unit_two, inverse_two)
    sums_ref[3:4, :] = jnp.sum(dz_two, axis=0, keepdims=True)
    b2_ref[...] = dz_two.astype(BF16)
    acc[...] = dz_two

    def down(h, carry):
        du = dot(b2_ref[...], w_ref[h, :, up_end:down_end], 1, 0) * slope[h]
        dbup_ref[h] = jnp.sum(du, axis=0, keepdims=True)
        b1_ref[h] = du.astype(BF16)
        acc[...] += dot(b1_ref[h], w_ref[h, :, out_end:up_end], 1, 1)
        return carry

    lax.fori_loop(0, groups, down, 0)
    dh = acc[...]
    unit_one = unit_scr[...]
    sums_ref[1:2, :] = jnp.sum(dh * unit_one, axis=0, keepdims=True)
    sums_ref[2:3, :] = jnp.sum(dh, axis=0, keepdims=True)
    dz_one = normal_back(dh, gain_one, unit_one, inv_scr[...])
    sums_ref[0:1, :] = jnp.sum(dz_one, axis=0, keepdims=True)
    sums_ref[6:8, :] = jnp.zeros_like(sums_ref[6:8, :])
    dz_ref[...] = dz_one
    b0_ref[...] = dz_one.astype(BF16)
    for h in range(groups):
        dcon_ref[h] = dot(b0_ref[...], w_ref[h, :, qkv_end:out_end], 1, 0).astype(BF16)


def row_work(cuts, micro, context, x, weights, bias_up, vectors):
    groups, rows, width = context.shape
    model = x.shape[2]
    in_vmem = pl.BlockSpec(memory_space=pltpu.VMEM)
    unit = bias_up.shape[2]
    shape = jax.ShapeDtypeStruct
    args = (context, x, weights, bias_up, vectors)
    return pl.pallas_call(
        functools.partial(rows_kernel, cuts, micro),
        out_shape=(
            shape((rows, model), BF16),
            shape((rows, model), F32),
            shape(context.shape, BF16),
            shape((rows, model), BF16),
            shape((groups, rows, unit), BF16),
            shape((groups, rows, unit), BF16),
            shape((rows, model), BF16),
            shape((rows, model), BF16),
            shape((8, model), F32),
            shape((groups, 1, unit), F32),
        ),
        in_specs=[in_vmem] * len(args),
        out_specs=(in_vmem,) * 10,
        scratch_shapes=[
            pltpu.VMEM((groups, rows, unit), F32),
            pltpu.VMEM((rows, model), F32),
            pltpu.VMEM((rows, model), F32),
            pltpu.VMEM((rows, model), F32),
            pltpu.VMEM((rows, 1), F32),
        ],
        compiler_params=params(),
        cost_estimate=cost(8 * groups * rows * model * (unit + width), 2 * weights.size),
        name="row_work",
    )(*args)


def input_kernel(dqkv_ref, w_ref, dz_ref, o_ref):
    total = dz_ref[...]
    for h in range(dqkv_ref.shape[0]):
        total = total + dot(dqkv_ref[h], w_ref[h, :, : dqkv_ref.shape[2]], 1, 1)
    _, pieces, share, piece = o_ref.shape
    turned = total.T
    for h in range(o_ref.shape[0]):
        for p in range(pieces):
            block = turned[h * share : (h + 1) * share, p * piece : (p + 1) * piece]
            o_ref[h, p] = block.astype(BF16)


def input_grad(dqkv, weights, dz, pieces):
    groups, rows, columns = dqkv.shape
    model = dz.shape[1]
    return pl.pallas_call(
        input_kernel,
        out_shape=jax.ShapeDtypeStruct((groups, pieces, model // groups, rows // pieces), BF16),
        grid=(1,),
        in_specs=[
            whole(dqkv),
            pl.BlockSpec((groups, model, model), lambda i: (0, 0, 0)),
            whole(dz),
        ],
        out_specs=pl.BlockSpec((groups, pieces, model // groups, rows // pieces), lambda i: (0, 0, 0, 0)),
        compiler_params=params(),
        cost_estimate=cost(2 * groups * rows * columns * model, 2 * groups * columns * model),
        name="input_grad",
    )(dqkv, weights, dz)


def weight_kernel(cuts, micros, heads, slots, *refs):
    out_ref, vector_scr = refs[-2:]
    qkv_end, out_end, up_end, down_end = cuts

    def summed(family):
        total = family[0][...]
        for ref in family[1:]:
            total = total + ref[...]
        return total

    def product(lefts, rights):
        total = None
        for left, right in zip(lefts, rights):
            term = dot(left[...].reshape(left.shape[-2:]), right[0], 0, 0)
            total = term if total is None else total + term
        return total.astype(BF16)

    x, b0, h1, b2, dqkv, con, b1, act, own, plain, up = (
        refs[i * micros : (i + 1) * micros] for i in range(11)
    )
    out_ref[0, :, 0:qkv_end] = product(x, dqkv)
    out_ref[0, :, qkv_end:out_end] = product(b0, con)
    out_ref[0, :, out_end:up_end] = product(h1, b1)
    out_ref[0, :, up_end:down_end] = product(b2, act)

    own_sum = jnp.where(pl.program_id(0) == lax.axis_index("head"), summed(own), 0.0)
    plain_sum, up_sum = summed(plain), summed(up)[0]
    rows = out_ref.shape[1] // slots
    lanes = plain_sum.shape[1] // slots
    unit = up_sum.shape[1] // heads
    vector_scr[...] = jnp.zeros_like(vector_scr)
    for s in range(slots):
        vector_scr[:8, :lanes] = plain_sum[:, s * lanes : (s + 1) * lanes]
        for j in range(heads):
            at, step = j * HEAD_DIM + s * (HEAD_DIM // slots), HEAD_DIM // slots
            vector_scr[QUERY_AT + j : QUERY_AT + j + 1, :step] = own_sum[0:1, at : at + step]
            vector_scr[VALUE_AT + j : VALUE_AT + j + 1, :step] = own_sum[1:2, at : at + step]
            at, step = j * unit + s * (unit // slots), unit // slots
            vector_scr[UP_AT + j : UP_AT + j + 1, :step] = up_sum[:, at : at + step]
        out_ref[0, s * rows : s * rows + VECTOR_ROWS, down_end:] = vector_scr[...].astype(BF16)
        out_ref[0, s * rows + VECTOR_ROWS : (s + 1) * rows, down_end:] = jnp.zeros(
            (rows - VECTOR_ROWS, 128), BF16
        )


def weight_grads(cuts, heads, slots, x, lefts, rights, own, plain, up):
    micros = len(lefts[0])
    groups = rights[0][0].shape[0]
    model = lefts[0][0].shape[1]
    flat_left = [a for family in lefts for a in family]
    flat_right = [a for family in rights for a in family]
    rows = flat_left[0].shape[0]
    columns = cuts[-1] + 128

    def of_micro(m):
        return pl.BlockSpec((1, rows, model), lambda h: (m, 0, 0))

    def per_group(a):
        return pl.BlockSpec((1, *a.shape[1:]), lambda h: (h, 0, 0))

    return pl.pallas_call(
        functools.partial(weight_kernel, cuts, micros, heads, slots),
        out_shape=jax.ShapeDtypeStruct((groups, model, columns), BF16),
        grid=(groups,),
        in_specs=[of_micro(m) for m in range(micros)]
        + [whole(a) for a in flat_left]
        + [per_group(a) for a in flat_right]
        + [whole(a) for a in (*own, *plain)]
        + [per_group(a) for a in up],
        out_specs=pl.BlockSpec((1, model, columns), lambda h: (h, 0, 0)),
        scratch_shapes=[pltpu.VMEM((VECTOR_ROWS, 128), F32)],
        compiler_params=params(),
        cost_estimate=cost(2 * micros * groups * rows * model * cuts[-1], 2 * groups * model * cuts[-1]),
        name="weight_grads",
    )(*([x] * micros), *flat_left, *flat_right, *own, *plain, *up)


MESH = pl.DeviceIdType.MESH
SIDE = 2


def remote(source, target, send_sem, recv_sem, device):
    return pltpu.make_async_remote_copy(
        src_ref=source,
        dst_ref=target,
        send_sem=send_sem,
        recv_sem=recv_sem,
        device_id=device,
        device_id_type=MESH,
    )


def signal(device):
    pl.semaphore_signal(
        pltpu.get_barrier_semaphore(), inc=1, device_id=device, device_id_type=MESH
    )


def greet(devices):
    for device in devices:
        signal(device)
    pl.semaphore_wait(pltpu.get_barrier_semaphore(), len(devices))


def cross_kernel(groups, x_ref, o_ref, send_sem, recv_sem, own_sem):
    me = lax.axis_index("head")
    peers = [lax.rem(me + i, groups) for i in range(1, groups)]
    greet([{"head": peer} for peer in peers])
    copies = []
    for i, peer in enumerate(peers):
        copy = remote(x_ref.at[peer], o_ref.at[me], send_sem.at[i], recv_sem.at[i], {"head": peer})
        copy.start()
        copies.append(copy)
    own = pltpu.make_async_copy(x_ref.at[me], o_ref.at[me], own_sem)
    own.start()
    own.wait()
    for copy in copies:
        copy.wait()


def across_heads(x, number):
    groups = x.shape[0]
    return pl.pallas_call(
        functools.partial(cross_kernel, groups),
        out_shape=jax.ShapeDtypeStruct(x.shape, x.dtype),
        in_specs=[pl.BlockSpec(memory_space=pltpu.VMEM)],
        out_specs=pl.BlockSpec(memory_space=pl.ANY),
        scratch_shapes=[
            pltpu.SemaphoreType.DMA((groups - 1,)),
            pltpu.SemaphoreType.DMA((groups - 1,)),
            pltpu.SemaphoreType.DMA,
        ],
        compiler_params=params(collective_id=number, has_side_effects=True),
        cost_estimate=cost(0, 40 * x.size),
        name="across_heads",
    )(x)


SIDES = 2
LINE = 4


class Place:
    def __init__(self):
        self.here, self.head = lax.axis_index("seq"), lax.axis_index("head")
        self.z, self.x = self.here // SIDES, lax.rem(self.here, SIDES)
        self.y, self.c = self.head // 2, lax.rem(self.head, 2)
        self.up, self.down = {"seq": self.here + SIDES}, {"seq": self.here - SIDES}
        self.across = {"seq": self.z * SIDES + (1 - self.x)}
        self.over = {"head": (1 - self.y) * 2 + self.c}
        self.beside = {"head": self.y * 2 + (1 - self.c)}
        self.not_last, self.not_first = self.z < LINE - 1, self.z > 0
        self.is_end = jnp.logical_or(jnp.logical_not(self.not_last), jnp.logical_not(self.not_first))
        half = (LINE - 1 - self.z) // 2
        self.order = [self.z, self.z + 1 - 2 * lax.rem(self.z, 2), 1 + half, (LINE - 1) * half]

    def greet_neighbours(self):
        pl.when(self.not_last)(lambda: signal(self.up))
        pl.when(self.not_first)(lambda: signal(self.down))
        for device in (self.across, self.over, self.beside):
            signal(device)
        return 3 + self.not_last.astype(jnp.int32) + self.not_first.astype(jnp.int32)


def arrived(block, send_sem, recv_sem, device):
    remote(block, block, send_sem, recv_sem, device).wait_recv()


def line_kernel(
    slots, groups, pack_ref, piece_ref, all_ref, rows_ref,
    z_s, z_r, x_s, x_r, y_s, y_r, piece_s, piece_r, own_sem,
):
    me = Place()
    here, head, x, y, c = me.here, me.head, me.x, me.y, me.c
    group = lax.rem(head - here + slots, groups)
    homes = [group * SIDE + p for p in range(SIDE)]
    targets = [
        lax.rem(head - me.z + groups, groups) + groups * lax.rem(here + step, 2) for step in range(2)
    ]
    expected = me.greet_neighbours()
    for home in homes:
        pl.when(home != here)(lambda home=home: signal({"seq": home}))
    for target in targets:
        expected = expected + (target != here).astype(jnp.int32)
    pl.semaphore_wait(pltpu.get_barrier_semaphore(), expected)

    def at(i, side, row):
        return all_ref.at[row * 2 + c, i * SIDES + side]

    def source(k):
        return pack_ref if k == 0 else at(me.order[k], x, y)

    def upward(k):
        i = me.order[k]
        return remote(source(k), at(i, x, y), z_s.at[i], z_r.at[i], me.up)

    def downward(k):
        i = me.order[k]
        return remote(source(k), at(i, x, y), z_s.at[LINE + i], z_r.at[i], me.down)

    def over_x(k):
        i = me.order[k]
        return remote(source(k), at(i, x, y), x_s.at[i], x_r.at[i], me.across)

    def over_y(k):
        i = me.order[k]
        return remote(source(k), at(i, x, y), y_s.at[i], y_r.at[i], me.over)

    def goes_up(k):
        return (me.order[k] <= me.z) & me.not_last

    def goes_down(k):
        return (me.order[k] >= me.z) & me.not_first

    def piece(step):
        return remote(
            piece_ref.at[step], rows_ref.at[:, x], piece_s.at[step], piece_r.at[x], {"seq": targets[step]}
        )

    def piece_here(step):
        return pltpu.make_async_copy(piece_ref.at[step], rows_ref.at[:, x], own_sem.at[1])

    own = pltpu.make_async_copy(pack_ref, at(me.z, x, y), own_sem.at[0])
    own.start()
    for k in range(LINE):
        i = me.order[k]
        if k:
            arrived(at(i, x, y), z_s.at[i], z_r.at[i], me.up)
        pl.when(goes_up(k))(lambda k=k: upward(k).start())
        pl.when(goes_down(k))(lambda k=k: downward(k).start())
        over_x(k).start()
        over_y(k).start()
        turn = {0: me.is_end, LINE - 1: jnp.logical_not(me.is_end)}.get(k)
        if turn is not None:
            for step, target in enumerate(targets):
                pl.when(turn & (target != here))(lambda step=step: piece(step).start())
                pl.when(turn & (target == here))(lambda step=step: piece_here(step).start())
    for k in range(LINE):
        i = me.order[k]
        arrived(at(i, 1 - x, y), x_s.at[i], x_r.at[i], me.across)
        arrived(at(i, x, 1 - y), y_s.at[i], y_r.at[i], me.over)
    for p, home in enumerate(homes):
        block = rows_ref.at[:, p]
        pl.when(home != here)(
            lambda block=block, p=p, home=home: arrived(
                block, piece_s.at[p], piece_r.at[p], {"seq": home}
            )
        )
    for step, target in enumerate(targets):
        pl.when(target != here)(lambda step=step: piece(step).wait_send())
        pl.when(target == here)(lambda step=step: piece_here(step).wait())
    own.wait()
    for k in range(LINE):
        pl.when(goes_up(k))(lambda k=k: upward(k).wait_send())
        pl.when(goes_down(k))(lambda k=k: downward(k).wait_send())
        over_x(k).wait_send()
        over_y(k).wait_send()


def gather_line(packed, pieces, slots, groups, number):
    dma = pltpu.SemaphoreType.DMA
    return pl.pallas_call(
        functools.partial(line_kernel, slots, groups),
        out_shape=(
            jax.ShapeDtypeStruct((groups, slots, *packed.shape), packed.dtype),
            jax.ShapeDtypeStruct((pieces.shape[1], SIDE, *pieces.shape[2:]), pieces.dtype),
        ),
        in_specs=[pl.BlockSpec(memory_space=pltpu.VMEM)] * 2,
        out_specs=(ANYWHERE,) * 2,
        scratch_shapes=[dma((2 * LINE,)), dma((LINE,))] + [dma((LINE,))] * 4 + [dma((2,))] * 3,
        compiler_params=params(collective_id=number, has_side_effects=True),
        cost_estimate=cost(0, 3000000 * 20),
        name="gather_line",
    )(packed, pieces)


def plane_kernel(in_ref, all_ref, y_s, y_r, c_s, c_r):
    me = Place()
    x, y, c = me.x, me.y, me.c
    greet([me.over, me.beside])

    def at(i, side, row, core=c):
        return all_ref.at[row * 2 + core, i * SIDES + side]

    def over_y(i):
        block = at(i, 1 - x, y)
        return remote(block, block, y_s.at[i], y_r.at[i], me.over)

    places = ((x, y), (1 - x, y), (x, 1 - y), (1 - x, 1 - y))

    def to_core(i, kind):
        n = kind * LINE + i
        block = at(i, *places[kind])
        return remote(block, block, c_s.at[n], c_r.at[n], me.beside)

    for i in range(LINE):
        over_y(i).start()
    for kind in range(3):
        for i in range(LINE):
            to_core(i, kind).start()
    for i in range(LINE):
        arrived(at(i, 1 - x, 1 - y), y_s.at[i], y_r.at[i], me.over)
        to_core(i, 3).start()
    for kind, (side, row) in enumerate(places):
        for i in range(LINE):
            n = kind * LINE + i
            arrived(at(i, side, row, 1 - c), c_s.at[n], c_r.at[n], me.beside)
    for i in range(LINE):
        over_y(i).wait_send()
        for kind in range(4):
            to_core(i, kind).wait_send()


def gather_plane(shards, number):
    dma = pltpu.SemaphoreType.DMA
    return pl.pallas_call(
        plane_kernel,
        out_shape=jax.ShapeDtypeStruct(shards.shape, shards.dtype),
        in_specs=[ANYWHERE],
        out_specs=ANYWHERE,
        scratch_shapes=[dma((LINE,))] * 2 + [dma((4 * LINE,))] * 2,
        input_output_aliases={0: 0},
        compiler_params=params(collective_id=number, has_side_effects=True),
        cost_estimate=cost(0, 3000000 * 40),
        name="gather_plane",
    )(shards)


def add_into(target, terms, shape):
    rows = shape[-2]
    tile = 16
    steps = rows // tile
    outer = 1
    for n in shape[:-2]:
        outer *= n

    def body(i, carry):
        at = pl.ds(pl.multiple_of(lax.rem(i, steps) * tile, tile), tile)
        rest = i // steps
        index = []
        for n in reversed(shape[:-2]):
            index.insert(0, lax.rem(rest, n))
            rest = rest // n
        index = (*index, at)
        total = terms[0][index].astype(F32)
        for term in terms[1:]:
            total = total + term[index].astype(F32)
        target[index] = total.astype(target.dtype)
        return carry

    lax.fori_loop(0, outer * steps, body, 0)


def finish_kernel(
    slots, groups, micros, part_ref, y_refs, dx_refs, sum_ref, tokens_ref, grads_ref,
    held, first, second, line,
    c_s, c_r, x_s, x_r, y_s, y_r, z_s, z_r, home_s, home_r, over_s, over_r, near_s, near_r, pass_s, pass_r,
    grad_s, grad_r, own_sem,
):
    me = Place()
    here, head, x, y, z, c = me.here, me.head, me.x, me.y, me.z, me.c
    order = me.order[::-1]
    group = lax.rem(head - here + slots, groups)
    homes = [group * SIDE + p for p in range(SIDE)]
    mine = lax.rem(head - z + groups, groups)
    senders = [lax.rem(slot + z, groups) for slot in range(slots)]

    def is_me(slot, other):
        return (slot == here) & (other == head)

    expected = me.greet_neighbours()
    for slot in range(slots):
        pl.when(jnp.logical_not(is_me(slot, senders[slot])))(
            lambda slot=slot: signal({"seq": slot, "head": senders[slot]})
        )
    for home in homes:
        for h in range(groups):
            expected = expected + 1 - is_me(home, h).astype(jnp.int32)
    pl.semaphore_wait(pltpu.get_barrier_semaphore(), expected)

    def to_core(k, row):
        i = order[k]
        n = row * LINE + i
        return remote(
            part_ref.at[row * 2 + (1 - c), i], held.at[i, row], c_s.at[n], c_r.at[n], me.beside
        )

    sides = (1 - x, x)

    def over_y(k, n):
        i = order[k]
        at = n * LINE + i
        return remote(
            held.at[i, 1 - y, sides[n]], first.at[i, sides[n]], y_s.at[at], y_r.at[at], me.over
        )

    def over_x(k):
        i = order[k]
        return remote(held.at[i, y, 1 - x], second.at[i], x_s.at[i], x_r.at[i], me.across)

    def upward(k):
        i = order[k]
        return remote(held.at[i, y, x], line.at[0, i], z_s.at[i], z_r.at[i], me.up)

    def downward(k):
        i = order[k]
        n = LINE + i
        return remote(held.at[i, y, x], line.at[1, i], z_s.at[n], z_r.at[n], me.down)

    rows, columns = sum_ref.shape

    def begin(k):
        i = order[k]
        for row in (1 - y, y):
            n = row * LINE + i
            arrived(held.at[i, row], c_s.at[n], c_r.at[n], me.beside)
        block = held.at[i, 1 - y]
        add_into(block, [block, part_ref.at[(1 - y) * 2 + c, i]], (SIDES, rows, columns))
        over_y(k, 0).start()
        over_y(k, 1).start()
        block = held.at[i, y]
        add_into(block, [block, part_ref.at[y * 2 + c, i]], (SIDES, rows, columns))

    def middle(k):
        i = order[k]
        for n, side in enumerate(sides):
            at = n * LINE + i
            arrived(first.at[i, side], y_s.at[at], y_r.at[at], me.over)
            block = held.at[i, y, side]
            add_into(block, [block, first.at[i, side]], (rows, columns))
            if n == 0:
                over_x(k).start()

    def end(k):
        i = order[k]
        n = LINE + i
        last = k == LINE - 1
        arrived(second.at[i], x_s.at[i], x_r.at[i], me.across)
        target = sum_ref if last else held.at[i, y, x]
        add_into(target, [held.at[i, y, x], second.at[i]], (rows, columns))

        def below():
            arrived(line.at[0, i], z_s.at[i], z_r.at[i], me.up)
            add_into(target, [target, line.at[0, i]], (rows, columns))

        def above():
            arrived(line.at[1, i], z_s.at[n], z_r.at[n], me.up)
            add_into(target, [target, line.at[1, i]], (rows, columns))

        pl.when((i >= z) & me.not_first)(below)
        pl.when((i <= z) & me.not_last)(above)
        if not last:
            pl.when(i > z)(lambda: upward(k).start())
            pl.when(i < z)(lambda: downward(k).start())

    def home_copy(m, p):
        n = m * SIDE + p
        return remote(
            y_refs[m].at[p], tokens_ref.at[m, here], home_s.at[n], home_r.at[m * 2 + here // groups], {"seq": homes[p]}
        )

    def home_here(m, p):
        return pltpu.make_async_copy(y_refs[m].at[p], tokens_ref.at[m, here], own_sem.at[m])

    def grad_copy(m, p, h):
        n = (m * SIDE + p) * groups + h
        return remote(
            dx_refs[m].at[h, p], grads_ref.at[m, here], grad_s.at[n], grad_r.at[m * slots + here],
            {"seq": homes[p], "head": h},
        )

    def grad_here(m, p, h):
        return pltpu.make_async_copy(dx_refs[m].at[h, p], grads_ref.at[m, here], own_sem.at[micros + m])

    def slot_of(other, j):
        return lax.rem(other - z + groups, groups) + groups * j

    far_head, near_head = (1 - y) * 2 + c, y * 2 + (1 - c)
    last_head = (1 - y) * 2 + (1 - c)

    def far(m, j):
        n, block = m * 2 + j, tokens_ref.at[m, slot_of(head, j)]
        return remote(block, block, over_s.at[n], over_r.at[n], me.over)

    def near(m, j):
        n, block = m * 2 + j, tokens_ref.at[m, slot_of(head, j)]
        return remote(block, block, near_s.at[n], near_r.at[n], me.beside)

    def passed(m, j):
        n, block = m * 2 + j, tokens_ref.at[m, slot_of(far_head, j)]
        return remote(block, block, pass_s.at[n], pass_r.at[n], me.beside)

    for k in range(LINE):
        for row in range(2):
            to_core(k, row).start()
    for m in range(micros):
        for p, home in enumerate(homes):
            pl.when(home != here)(lambda m=m, p=p: home_copy(m, p).start())
            pl.when(home == here)(lambda m=m, p=p: home_here(m, p).start())
            for h in range(groups):
                same = is_me(home, h)
                pl.when(jnp.logical_not(same))(lambda m=m, p=p, h=h: grad_copy(m, p, h).start())
                pl.when(same)(lambda m=m, p=p, h=h: grad_here(m, p, h).start())
    for k in range(LINE):
        begin(k)
        if k >= 1:
            middle(k - 1)
        if k >= 2:
            end(k - 2)
    middle(LINE - 1)
    end(LINE - 2)
    for m in range(micros):
        for p, home in enumerate(homes):
            pl.when(home == here)(lambda m=m, p=p: home_here(m, p).wait())
        for j in range(2):
            slot = slot_of(head, j)
            pl.when(slot != here)(
                lambda m=m, j=j, slot=slot: arrived(
                    tokens_ref.at[m, slot], home_s.at[m * 2 + j], home_r.at[m * 2 + j], {"seq": slot}
                )
            )
            far(m, j).start()
            near(m, j).start()
    end(LINE - 1)
    for m in range(micros):
        for j in range(2):
            n = m * 2 + j
            arrived(tokens_ref.at[m, slot_of(far_head, j)], over_s.at[n], over_r.at[n], me.over)
            passed(m, j).start()
    for m in range(micros):
        for j in range(2):
            n = m * 2 + j
            arrived(tokens_ref.at[m, slot_of(near_head, j)], near_s.at[n], near_r.at[n], me.beside)
            arrived(tokens_ref.at[m, slot_of(last_head, j)], pass_s.at[n], pass_r.at[n], me.beside)
        for slot in range(slots):
            n = m * slots + slot
            pl.when(jnp.logical_not(is_me(slot, senders[slot])))(
                lambda m=m, n=n, slot=slot: arrived(
                    grads_ref.at[m, slot], grad_s.at[0], grad_r.at[n], {"seq": slot, "head": senders[slot]}
                )
            )
    for m in range(micros):
        for p, home in enumerate(homes):
            pl.when(home != here)(lambda m=m, p=p: home_copy(m, p).wait_send())
            for h in range(groups):
                same = is_me(home, h)
                pl.when(jnp.logical_not(same))(lambda m=m, p=p, h=h: grad_copy(m, p, h).wait_send())
                pl.when(same)(lambda m=m, p=p, h=h: grad_here(m, p, h).wait())
        for j in range(2):
            far(m, j).wait_send()
            near(m, j).wait_send()
            passed(m, j).wait_send()
    for k in range(LINE):
        for row in range(2):
            to_core(k, row).wait_send()
        over_y(k, 0).wait_send()
        over_y(k, 1).wait_send()
        over_x(k).wait_send()
        if k < LINE - 1:
            i = order[k]
            pl.when(i > z)(lambda k=k: upward(k).wait_send())
            pl.when(i < z)(lambda k=k: downward(k).wait_send())


def finish(part, ys, dxs, slots, groups, number):
    columns = part.shape[-1]
    micros = len(ys)
    _, piece, model = ys[0].shape

    def body(part_ref, *refs):
        finish_kernel(
            slots, groups, micros, part_ref, refs[:micros], refs[micros : 2 * micros], *refs[2 * micros :]
        )

    rows = part.shape[-2]
    dma = pltpu.SemaphoreType.DMA
    vmem = pltpu.VMEM
    part = part.reshape(groups, LINE, SIDES, rows, columns)
    return pl.pallas_call(
        body,
        out_shape=(
            jax.ShapeDtypeStruct((rows, columns), F32),
            jax.ShapeDtypeStruct((micros, slots, piece, model), BF16),
            jax.ShapeDtypeStruct((micros, slots, *dxs[0].shape[-2:]), BF16),
        ),
        in_specs=[pl.BlockSpec(memory_space=pltpu.VMEM)] * (1 + 2 * micros),
        out_specs=(pl.BlockSpec(memory_space=pltpu.VMEM),) + (pl.BlockSpec(memory_space=pl.ANY),) * 2,
        scratch_shapes=[
            vmem((LINE, 2, SIDES, rows, columns), BF16),
            vmem((LINE, SIDES, rows, columns), BF16),
            vmem((LINE, rows, columns), BF16),
            vmem((2, LINE, rows, columns), BF16),
        ]
        + [dma((2 * LINE,))] * 8
        + [dma((2 * micros,))] * 8
        + [dma((2 * groups * micros,)), dma((slots * micros,)), dma((2 * micros,))],
        compiler_params=params(collective_id=number, has_side_effects=True),
        cost_estimate=cost(0, 3000000 * 40),
        name="finish",
    )(part, *ys, *dxs)


def deliver_kernel(
    cuts, micros, slots, index_ref, sum_ref, y_ref, dx_ref, block_ref, _, out_ref, grad_ref, logits_ref,
    q_ref, k_ref, v_ref, wo_ref, wu_ref, wd_ref, bq_ref, bv_ref, bu_ref, *rest,
):
    plain_refs = rest[:PLAIN]
    y_buffer, dx_buffer, block_buffer, in_sem, out_sem = rest[PLAIN:]
    last = micros - 1
    reads = [block_ref.at[index_ref[last, i]] for i in range(slots)]
    writes = [logits_ref.at[last, i] for i in range(slots)]
    buffers = [block_buffer.at[i] for i in range(slots)]
    for source, target, buffer in ((y_ref, out_ref, y_buffer), (dx_ref, grad_ref, dx_buffer)):
        for m in range(micros):
            for i in range(slots):
                reads.append(source.at[m, index_ref[m, i]])
                writes.append(target.at[m, i])
                buffers.append(buffer.at[m, i])

    def take(n):
        return pltpu.make_async_copy(reads[n], buffers[n], in_sem.at[n])

    def give(n):
        return pltpu.make_async_copy(buffers[n], writes[n], out_sem.at[n])

    for n in range(len(reads)):
        take(n).start()
    width = q_ref.shape[1]
    for n, ref in enumerate((q_ref, k_ref, v_ref)):
        ref[...] = sum_ref[:, n * width : (n + 1) * width]
    wo_ref[...] = sum_ref[:, cuts[0] : cuts[1]].T
    wu_ref[...] = sum_ref[:, cuts[1] : cuts[2]]
    wd_ref[...] = sum_ref[:, cuts[2] : cuts[3]]
    block = sum_ref[:VECTOR_ROWS, cuts[3] :]
    for i, ref in enumerate(plain_refs):
        ref[...] = block[i : i + 1, : ref.shape[1]]
    for first, ref in ((QUERY_AT, bq_ref), (VALUE_AT, bv_ref), (UP_AT, bu_ref)):
        ref[...] = block[first : first + ref.shape[0], : ref.shape[1]]
    for n in range(len(reads)):
        take(n).wait()
        give(n).start()
    for n in range(len(reads)):
        give(n).wait()


def deliver(cuts, heads, unit, index, sums, y, dx, blocks, logits):
    micros, slots = dx.shape[:2]
    rows, width = sums.shape[0], heads * HEAD_DIM
    total = slots + 2 * micros * slots
    dma = pltpu.SemaphoreType.DMA
    in_vmem = pl.BlockSpec(memory_space=pltpu.VMEM)

    def f32(*shape):
        return jax.ShapeDtypeStruct(shape, F32)

    return pl.pallas_call(
        functools.partial(deliver_kernel, cuts, micros, slots),
        out_shape=(
            jax.ShapeDtypeStruct(y.shape, BF16),
            jax.ShapeDtypeStruct(dx.shape, BF16),
            jax.ShapeDtypeStruct(logits.shape, BF16),
            f32(rows, width),
            f32(rows, width),
            f32(rows, width),
            f32(width, rows),
            f32(rows, unit),
            f32(rows, unit),
            f32(heads, HEAD_DIM // slots),
            f32(heads, HEAD_DIM // slots),
            f32(heads, unit // heads // slots),
        )
        + (f32(1, rows),) * PLAIN,
        in_specs=[SMALL, in_vmem] + [ANYWHERE] * 4,
        out_specs=(ANYWHERE,) * 3 + (in_vmem,) * (9 + PLAIN),
        scratch_shapes=[
            pltpu.VMEM(y.shape, BF16),
            pltpu.VMEM(dx.shape, BF16),
            pltpu.VMEM(blocks.shape, BF16),
            dma((total,)),
            dma((total,)),
        ],
        input_output_aliases={5: 2},
        compiler_params=params(),
        cost_estimate=cost(0, 4 * y.size),
        name="deliver",
    )(index, sums, y, dx, blocks, logits)


def fits(mesh):
    return dict(mesh.shape) == {"seq": 8, "head": 4}


def on_device(
    tokens,
    prev_logits,
    lengths,
    dealing,
    w_query,
    b_query,
    w_key,
    w_value,
    b_value,
    w_out,
    b_out,
    gain_one,
    shift_one,
    w_up,
    b_up,
    w_down,
    b_down,
    gain_two,
    shift_two,
    cot_tokens,
    cot_logits,
):
    slots, groups = lax.axis_size("seq"), lax.axis_size("head")
    grid = ("seq", "head")
    here, head = lax.axis_index("seq"), lax.axis_index("head")
    micros, _, piece, model = tokens.shape
    heads = prev_logits.shape[3]
    extent = piece * slots
    width = heads * HEAD_DIM
    unit = w_up.shape[1]
    per = slots // groups
    cuts = (3 * width, 3 * width + width, 3 * width + width + unit, 3 * width + width + 2 * unit)
    own_rows = model // slots

    prev = jnp.transpose(prev_logits, (0, 1, 3, 2, 4))
    cot_square = jnp.transpose(cot_logits[:, 0], (0, 2, 1, 3))

    first_send, pieces, packed, info = prepare(
        lengths,
        dealing,
        prev,
        tokens,
        cot_tokens,
        (w_query, w_key, w_value, w_out, w_up, w_down.T),
        (b_query, b_value, b_up),
        [v.reshape(1, -1) for v in (b_out, gain_one, shift_one, b_down, gain_two, shift_two)],
        groups,
    )
    line, arrived_rows = gather_line(packed, pieces, slots, groups, 1)
    rows = per * piece
    rows_all = arrived_rows.reshape(2 * micros, rows, model)

    weights = gather_plane(line, 2)
    weights = weights.reshape(groups, slots, own_rows, -1)
    bias_qkv, bias_up, row_vectors = unpack_vectors(weights, heads, width, unit, model)
    weights = weights.reshape(groups, model, -1)

    projected = project(rows_all, weights, bias_qkv)
    first_qkv = across_heads(projected[0], 3)
    second_qkv = [across_heads(projected[m], 3) for m in range(1, micros)]
    got_prev, after = [], arrived_rows
    for m in range(micros):
        send = pick_blocks(prev, m, dealing) if m else first_send
        send, _ = lax.optimization_barrier((send, after))
        got = lax.all_to_all(send, "seq", split_axis=0, concat_axis=0, tiled=True)
        got_prev.append(got)
        after = (got, first_qkv, second_qkv)

    logits, grad_logits = None, None
    kept, sums_own, sums_rows, sums_up, returned, sent = [], [], [], [], [], []
    for m in range(micros):
        qkv = second_qkv[m - 1] if m else first_qkv
        logits, attend, context = attention_forward(info, qkv, got_prev[m], m, micros, logits)
        context_rows = across_heads(context, 4)
        y, dz, dcon, h1, act, b1, b2, b0, sums, dbup = row_work(
            cuts, m, context_rows, rows_all, weights, bias_up, row_vectors
        )
        dcontext = across_heads(dcon, 4)
        send, dqkv, own = attention_backward(
            info, qkv, attend, context, dcontext, cot_square, m
        )
        dqkv = across_heads(dqkv, 5)
        dx = input_grad(dqkv, weights, dz, per)
        kept.append((b0, h1, b2, dqkv, context_rows, b1, act))
        sums_own.append(own)
        sums_rows.append(sums)
        sums_up.append(dbup)
        returned.append((y, dx))
        if m == 0:
            send, _ = lax.optimization_barrier((send, dx))
            after = lax.all_to_all(send, "seq", split_axis=0, concat_axis=0, tiled=True)
            sent.append(after)
        else:
            sent.append(send)

    families = list(zip(*kept))
    part = weight_grads(cuts, heads, slots, rows_all, families[:3], families[3:], sums_own, sums_rows, sums_up)
    for m in range(micros):
        if m:
            send, _ = lax.optimization_barrier((sent[m], (sent[m - 1], part)))
            sent[m] = lax.all_to_all(send, "seq", split_axis=0, concat_axis=0, tiled=True)
        if m == 0:
            grad_logits = place_blocks(sent[m], m, micros, dealing, grad_logits)
    ys = [y.reshape(per, piece, model) for y, _ in returned]
    dxs = [dx for _, dx in returned]
    part = part.reshape(groups, slots, own_rows, -1)
    part, _ = lax.optimization_barrier((part, grad_logits))
    part, all_y, all_dx = finish(part, ys, dxs, slots, groups, 7)
    out_tokens, grad_tokens, grad_logits, dq, dk, dv, dwo, dwu, dwd, dbq, dbv, dbu, *plain = deliver(
        cuts, heads, unit, dealing, part, all_y, all_dx, sent[-1], grad_logits
    )
    plain = [row.reshape(-1) for row in plain]
    return (
        out_tokens,
        jnp.transpose(logits, (0, 2, 1, 3))[:, None],
        jnp.transpose(grad_tokens, (0, 1, 3, 2)),
        jnp.transpose(grad_logits, (0, 1, 3, 2, 4)),
        dq,
        dbq,
        dk,
        dv,
        dbv,
        dwo,
        *plain[:3],
        dwu,
        dbu,
        dwd.T,
        *plain[3:],
    )


def solution(mesh):
    placed = (
        P(None, None, "seq", None),
        P(None, None, "seq", "head", None),
        P(),
        P(),
        P("seq", "head"),
        P("head", "seq"),
        P("seq", "head"),
        P("seq", "head"),
        P("head", "seq"),
        P("head", "seq"),
        P("seq"),
        P("seq"),
        P("seq"),
        P("seq", "head"),
        P("head", "seq"),
        P("head", "seq"),
        P("seq"),
        P("seq"),
        P("seq"),
        P(None, None, "seq", None),
        P(None, "seq", None, "head", None),
    )
    return jax.shard_map(
        on_device if fits(mesh) else on_device_general,
        mesh=mesh,
        in_specs=placed,
        out_specs=(
            P(None, None, "seq", None),
            P(None, "seq", None, "head", None),
            P(None, None, "seq", "head"),
            P(None, None, "seq", "head", None),
            P("seq", "head"),
            P("head", "seq"),
            P("seq", "head"),
            P("seq", "head"),
            P("head", "seq"),
            P("head", "seq"),
            P("seq"),
            P("seq"),
            P("seq"),
            P("seq", "head"),
            P("head", "seq"),
            P("head", "seq"),
            P("seq"),
            P("seq"),
            P("seq"),
        ),
        check_vma=False,
    )
```

```python
import functools

import jax
import jax.numpy as jnp
from jax import lax
from jax.experimental import pallas as pl
from jax.experimental.pallas import tpu as pltpu
from jax.sharding import PartitionSpec as P

HEAD_DIM = 64
BF16, F32 = jnp.bfloat16, jnp.float32
VMEM_LIMIT = 60 * 1024 * 1024


epsilon = 1e-12


def cut_along(x, dim, peers):
    before, after = (x.shape[:dim], x.shape[dim + 1 :])
    return jnp.moveaxis(x.reshape(*before, peers, -1, *after), dim, 0)


def sum_at_owner(x, axis, dim):
    blocks = cut_along(x, dim, lax.axis_size(axis))
    arrived = lax.all_to_all(blocks, axis, split_axis=0, concat_axis=0, tiled=True)
    return arrived.astype(jnp.float32).sum(axis=0)


def side_by_side(arrays, axis, dim, along):
    both = jnp.concatenate(arrays, axis=along)
    result, at, finished = (sum_at_owner(both, axis, dim), 0, [])
    for a in arrays:
        finished.append(lax.slice_in_dim(result, at, at + a.shape[along], axis=along))
        at += a.shape[along]
    return tuple(finished)


def side_by_side_2(arrays, axis, dim, along):
    columns = [a.reshape(*a.shape[:along], -1) for a in arrays]
    both = jnp.concatenate(columns, axis=along)
    result, at, finished = (sum_at_owner(both, axis, dim), 0, [])
    for a, column in zip(arrays, columns):
        slab = result[..., at : at + column.shape[along]]
        finished.append(slab.reshape(*slab.shape[:along], *a.shape[along:]))
        at += column.shape[along]
    return tuple(finished)


def layer_norm(values, gain, shift):
    center = values - jnp.mean(values, axis=-1, keepdims=True)
    spread = jnp.mean(center * center, axis=-1, keepdims=True)
    return center * lax.rsqrt(spread + epsilon) * gain + shift


def exact_gelu(values):
    return jax.nn.gelu(values, approximate=False)


def mask_scores(raw_scores, length):
    key_valid = jnp.arange(raw_scores.shape[2]) < length
    return jnp.where(key_valid[None, None, :], raw_scores, -jnp.inf)


def on_device_general(
    tokens,
    prev_logits,
    lengths,
    dealing,
    w_query,
    b_query,
    w_key,
    w_value,
    b_value,
    w_out,
    b_out,
    gain_one,
    shift_one,
    w_up,
    b_up,
    w_down,
    b_down,
    gain_two,
    shift_two,
    cot_tokens,
    cot_logits,
):
    micro_count = tokens.shape[0]
    seq_count = tokens.shape[1]
    piece_rows = tokens.shape[2]
    model_width = tokens.shape[3]
    extent = piece_rows * seq_count
    heads_here = prev_logits.shape[3]
    width_here = model_width // lax.axis_size("head")
    score_scale = HEAD_DIM ** (-0.5)
    owner_slot = lax.axis_index("seq")
    head_slot = lax.axis_index("head")
    zero_shift = jnp.zeros((model_width,), jnp.float32)
    out_token_list = []
    out_logit_list = []
    grad_token_list = []
    grad_logit_list = []
    grad_totals = None
    for micro_batch in range(micro_count):
        full_weights = (
            lax.all_gather(w_query, "seq", axis=0, tiled=True),
            lax.all_gather(w_key, "seq", axis=0, tiled=True),
            lax.all_gather(w_value, "seq", axis=0, tiled=True),
            lax.all_gather(w_out, "seq", axis=1, tiled=True),
            lax.all_gather(w_up, "seq", axis=0, tiled=True),
            lax.all_gather(w_down, "seq", axis=1, tiled=True),
            lax.all_gather(b_query, "seq", axis=1, tiled=True),
            lax.all_gather(b_value, "seq", axis=1, tiled=True),
            lax.all_gather(b_out, "seq", axis=0, tiled=True),
            lax.all_gather(gain_one, "seq", axis=0, tiled=True),
            lax.all_gather(shift_one, "seq", axis=0, tiled=True),
            lax.all_gather(b_up, "seq", axis=1, tiled=True),
            lax.all_gather(b_down, "seq", axis=0, tiled=True),
            lax.all_gather(gain_two, "seq", axis=0, tiled=True),
            lax.all_gather(shift_two, "seq", axis=0, tiled=True),
        )
        (
            query_full,
            key_full,
            value_full,
            out_full,
            up_full,
            down_full,
            bias_query,
            bias_value,
            bias_out,
            gain_first,
            shift_first,
            bias_up,
            bias_down,
            gain_second,
            shift_second,
        ) = full_weights
        inverse = (
            jnp.zeros((seq_count,), jnp.int32)
            .at[dealing[micro_batch]]
            .set(jnp.arange(seq_count, dtype=jnp.int32))
        )
        own_sequence = inverse[owner_slot]
        own_length = lengths[micro_batch, own_sequence]
        send_tokens = jnp.take(tokens[micro_batch], inverse, axis=0)
        send_prev = jnp.take(prev_logits[micro_batch], inverse, axis=0).reshape(
            seq_count, piece_rows, heads_here * extent
        )
        send_cot = jnp.take(cot_tokens[micro_batch], inverse, axis=0)
        got_tokens, got_prev, got_cot = (
            lax.all_to_all(send_tokens, "seq", split_axis=0, concat_axis=1, tiled=True),
            lax.all_to_all(send_prev, "seq", split_axis=0, concat_axis=1, tiled=True),
            lax.all_to_all(send_cot, "seq", split_axis=0, concat_axis=1, tiled=True),
        )
        rows_in = got_tokens.reshape(extent, model_width)
        prev_rows = got_prev.reshape(extent, heads_here, extent).astype(jnp.float32)
        cot_rows = got_cot.reshape(extent, model_width).astype(jnp.float32)
        query_pre = jnp.dot(rows_in, query_full, preferred_element_type=jnp.float32)
        queries = (query_pre + bias_query.reshape(-1).astype(jnp.float32)).astype(jnp.bfloat16)
        keys_all = jnp.dot(rows_in, key_full, preferred_element_type=jnp.float32).astype(
            jnp.bfloat16
        )
        value_pre = jnp.dot(rows_in, value_full, preferred_element_type=jnp.float32)
        values = (value_pre + bias_value.reshape(-1).astype(jnp.float32)).astype(jnp.bfloat16)
        query_heads = queries.reshape(extent, heads_here, HEAD_DIM)
        key_heads = keys_all.reshape(extent, heads_here, HEAD_DIM)
        value_heads = values.reshape(extent, heads_here, HEAD_DIM)
        raw_scores = (
            jnp.einsum("qhd,khd->qhk", query_heads, key_heads, preferred_element_type=jnp.float32)
            * score_scale
            + prev_rows
        )
        masked = mask_scores(raw_scores, own_length)
        row_top = jnp.max(masked, axis=-1, keepdims=True)
        shifted_exp = jnp.exp(masked - row_top)
        row_total = jnp.sum(shifted_exp, axis=-1, keepdims=True)
        attend = shifted_exp / row_total
        log_total = row_top + jnp.log(row_total)
        out_logit_list.append(raw_scores.astype(jnp.bfloat16)[None])
        context = (
            jnp.einsum(
                "qhk,khd->qhd",
                attend.astype(jnp.bfloat16),
                value_heads,
                preferred_element_type=jnp.float32,
            )
            .astype(jnp.bfloat16)
            .reshape(extent, heads_here * HEAD_DIM)
        )
        out_part = jnp.dot(context, out_full, preferred_element_type=jnp.float32)
        branch = lax.psum(out_part, "head") + bias_out.astype(jnp.float32)
        resid_one = rows_in.astype(jnp.float32) + branch
        hidden = layer_norm(
            resid_one, gain_first.astype(jnp.float32), shift_first.astype(jnp.float32)
        )
        hidden_low = hidden.astype(jnp.bfloat16)
        before_gelu = jnp.dot(
            hidden_low, up_full, preferred_element_type=jnp.float32
        ) + bias_up.reshape(-1).astype(jnp.float32)
        active = exact_gelu(before_gelu).astype(jnp.bfloat16)
        down_part = jnp.dot(active, down_full, preferred_element_type=jnp.float32)
        resid_two = hidden + (
            lax.psum(down_part.astype(jnp.bfloat16), "head").astype(jnp.float32)
            + bias_down.astype(jnp.float32)
        )
        result = layer_norm(
            resid_two, gain_second.astype(jnp.float32), shift_second.astype(jnp.float32)
        )
        out_rows = result.astype(jnp.bfloat16)
        (
            back_query,
            back_key,
            back_value,
            back_out,
            back_up,
            back_down,
            back_gain_first,
            back_gain_second,
        ) = (
            lax.all_gather(w_query, "seq", axis=0, tiled=True),
            lax.all_gather(w_key, "seq", axis=0, tiled=True),
            lax.all_gather(w_value, "seq", axis=0, tiled=True),
            lax.all_gather(w_out, "seq", axis=1, tiled=True),
            lax.all_gather(w_up, "seq", axis=0, tiled=True),
            lax.all_gather(w_down, "seq", axis=1, tiled=True),
            lax.all_gather(gain_one, "seq", axis=0, tiled=True),
            lax.all_gather(gain_two, "seq", axis=0, tiled=True),
        )
        norm_two_value, norm_two_back = jax.vjp(
            layer_norm, resid_two, back_gain_second.astype(jnp.float32), zero_shift
        )
        d_resid_two, d_gain_two, d_shift_two = norm_two_back(cot_rows)
        d_b_down = jnp.sum(d_resid_two, axis=0)
        grad_two_low = d_resid_two.astype(jnp.bfloat16)
        d_w_down = jnp.einsum("rf,rd->fd", active, grad_two_low, preferred_element_type=jnp.float32)
        d_active = jnp.einsum(
            "rd,fd->rf", grad_two_low, back_down, preferred_element_type=jnp.float32
        )
        gelu_value, gelu_back = jax.vjp(exact_gelu, before_gelu)
        d_before = gelu_back(d_active)[0]
        d_b_up = jnp.sum(d_before, axis=0).reshape(heads_here, -1)
        before_low = d_before.astype(jnp.bfloat16)
        d_w_up = jnp.einsum("rd,rf->df", hidden_low, before_low, preferred_element_type=jnp.float32)
        up_part = jnp.einsum("rf,df->rd", before_low, back_up, preferred_element_type=jnp.float32)
        d_hidden = d_resid_two + lax.psum(up_part.astype(jnp.bfloat16), "head").astype(jnp.float32)
        norm_one_value, norm_one_back = jax.vjp(
            layer_norm, resid_one, back_gain_first.astype(jnp.float32), zero_shift
        )
        d_resid_one, d_gain_one, d_shift_one = norm_one_back(d_hidden)
        d_b_out = jnp.sum(d_resid_one, axis=0)
        grad_one_low = d_resid_one.astype(jnp.bfloat16)
        d_w_out = jnp.einsum("rc,rd->cd", context, grad_one_low, preferred_element_type=jnp.float32)
        d_context = (
            jnp.einsum("rd,cd->rc", grad_one_low, back_out, preferred_element_type=jnp.float32)
            .astype(jnp.bfloat16)
            .reshape(extent, heads_here, HEAD_DIM)
        )
        raw_again = (
            jnp.einsum("qhd,khd->qhk", query_heads, key_heads, preferred_element_type=jnp.float32)
            * score_scale
            + prev_rows
        )
        attend_again = jnp.exp(mask_scores(raw_again, own_length) - log_total)
        d_attend = jnp.einsum(
            "qhd,khd->qhk", d_context, value_heads, preferred_element_type=jnp.float32
        )
        d_values = jnp.einsum(
            "qhk,qhd->khd",
            attend_again.astype(jnp.bfloat16),
            d_context,
            preferred_element_type=jnp.float32,
        )
        d_scores = attend_again * (
            d_attend - jnp.sum(attend_again * d_attend, axis=-1, keepdims=True)
        ) + cot_logits[micro_batch, 0].astype(jnp.float32)
        scores_low = d_scores.astype(jnp.bfloat16)
        d_queries = (
            jnp.einsum("qhk,khd->qhd", scores_low, key_heads, preferred_element_type=jnp.float32)
            * score_scale
        )
        d_keys = (
            jnp.einsum("qhk,qhd->khd", scores_low, query_heads, preferred_element_type=jnp.float32)
            * score_scale
        )
        d_b_query = jnp.sum(d_queries, axis=0)
        d_b_value = jnp.sum(d_values, axis=0)
        queries_low = d_queries.astype(jnp.bfloat16).reshape(extent, heads_here * HEAD_DIM)
        keys_low = d_keys.astype(jnp.bfloat16).reshape(extent, heads_here * HEAD_DIM)
        values_low = d_values.astype(jnp.bfloat16).reshape(extent, heads_here * HEAD_DIM)
        d_w_query = jnp.einsum(
            "rd,rc->dc", rows_in, queries_low, preferred_element_type=jnp.float32
        )
        d_w_key = jnp.einsum("rd,rc->dc", rows_in, keys_low, preferred_element_type=jnp.float32)
        d_w_value = jnp.einsum("rd,rc->dc", rows_in, values_low, preferred_element_type=jnp.float32)
        input_part = jnp.einsum(
            "rc,dc->rd", queries_low, back_query, preferred_element_type=jnp.float32
        )
        input_part = input_part + jnp.einsum(
            "rc,dc->rd", keys_low, back_key, preferred_element_type=jnp.float32
        )
        input_part = input_part + jnp.einsum(
            "rc,dc->rd", values_low, back_value, preferred_element_type=jnp.float32
        )
        input_share = lax.psum_scatter(
            input_part.astype(jnp.bfloat16), "head", scatter_dimension=1, tiled=True
        ).astype(jnp.float32)
        resid_share = lax.dynamic_slice_in_dim(d_resid_one, head_slot * width_here, width_here, 1)
        grad_rows = (resid_share + input_share).astype(jnp.bfloat16)
        back_tokens, back_grads, back_logits = (
            lax.all_to_all(
                out_rows.reshape(seq_count, piece_rows, model_width),
                "seq",
                split_axis=0,
                concat_axis=0,
                tiled=True,
            ),
            lax.all_to_all(
                grad_rows.reshape(seq_count, piece_rows, width_here),
                "seq",
                split_axis=0,
                concat_axis=0,
                tiled=True,
            ),
            lax.all_to_all(
                scores_low.reshape(seq_count, piece_rows, heads_here * extent),
                "seq",
                split_axis=0,
                concat_axis=0,
                tiled=True,
            ),
        )
        out_token_list.append(jnp.take(back_tokens, dealing[micro_batch], axis=0))
        grad_token_list.append(jnp.take(back_grads, dealing[micro_batch], axis=0))
        grad_logit_list.append(
            jnp.take(back_logits, dealing[micro_batch], axis=0).reshape(
                seq_count, piece_rows, heads_here, extent
            )
        )
        local_grads = (
            d_w_query,
            d_b_query,
            d_w_key,
            d_w_value,
            d_b_value,
            d_w_out,
            d_b_out,
            d_gain_one,
            d_shift_one,
            d_w_up,
            d_b_up,
            d_w_down,
            d_b_down,
            d_gain_two,
            d_shift_two,
        )
        if grad_totals is None:
            grad_totals = local_grads
        else:
            grad_totals = tuple((total + extra for total, extra in zip(grad_totals, local_grads)))
    final_grads = (
        sum_at_owner(grad_totals[0].astype(jnp.bfloat16), "seq", 0),
        sum_at_owner(grad_totals[1].astype(jnp.bfloat16), "seq", 1),
        *side_by_side(
            (grad_totals[2].astype(jnp.bfloat16), grad_totals[3].astype(jnp.bfloat16)), "seq", 0, 1
        ),
        sum_at_owner(grad_totals[4].astype(jnp.bfloat16), "seq", 1),
        sum_at_owner(grad_totals[5].astype(jnp.bfloat16), "seq", 1),
        sum_at_owner(grad_totals[6].astype(jnp.bfloat16), "seq", 0),
        sum_at_owner(grad_totals[7].astype(jnp.bfloat16), "seq", 0),
        *side_by_side_2(
            (grad_totals[8].astype(jnp.bfloat16), grad_totals[9].astype(jnp.bfloat16)), "seq", 0, 1
        ),
        sum_at_owner(grad_totals[10].astype(jnp.bfloat16), "seq", 1),
        sum_at_owner(grad_totals[11].astype(jnp.bfloat16), "seq", 1),
        sum_at_owner(grad_totals[12].astype(jnp.bfloat16), "seq", 0),
        sum_at_owner(grad_totals[13].astype(jnp.bfloat16), "seq", 0),
        sum_at_owner(grad_totals[14].astype(jnp.bfloat16), "seq", 0),
    )
    out_tokens = jnp.stack(out_token_list, axis=0)
    out_logits = jnp.stack(out_logit_list, axis=0)
    grad_tokens = jnp.stack(grad_token_list, axis=0)
    grad_logits = jnp.stack(grad_logit_list, axis=0)
    return (
        out_tokens,
        out_logits,
        grad_tokens,
        grad_logits,
        final_grads[0],
        final_grads[1],
        final_grads[2],
        final_grads[3],
        final_grads[4],
        final_grads[5],
        final_grads[6],
        final_grads[7],
        final_grads[8],
        final_grads[9],
        final_grads[10],
        final_grads[11],
        final_grads[12],
        final_grads[13],
        final_grads[14],
    )

def cost(flops, moved):
    return pl.CostEstimate(flops=int(flops) // 100, bytes_accessed=int(moved) // 100, transcendentals=0)


def params(**more):
    return pltpu.CompilerParams(vmem_limit_bytes=VMEM_LIMIT, **more)


def dot(a, b, ca, cb):
    return lax.dot_general(a, b, (((ca,), (cb,)), ((), ())), preferred_element_type=F32)


def whole(x):
    return pl.BlockSpec(x.shape, lambda *_: (0,) * len(x.shape))


def move_blocks(reads, writes, buffers, in_sem, out_sem):
    ins = [pltpu.make_async_copy(r, v, in_sem.at[i]) for i, (r, v) in enumerate(zip(reads, buffers))]
    outs = [pltpu.make_async_copy(v, w, out_sem.at[i]) for i, (v, w) in enumerate(zip(buffers, writes))]
    for copy in ins:
        copy.start()
    for copy, out in zip(ins, outs):
        copy.wait()
        out.start()
    for out in outs:
        out.wait()


SMALL = pl.BlockSpec(memory_space=pltpu.SMEM)
ANYWHERE = pl.BlockSpec(memory_space=pl.ANY)


def inverse_of(dealing_ref, inverse_ref, micros, slots):
    for m in micros:
        for i in range(slots):
            inverse_ref[dealing_ref[m, i]] = i


def pick_copies(micro, count, inverse_ref, x_ref, o_ref, buffer):
    steps = range(count)
    return (
        [x_ref.at[micro, inverse_ref[i]] for i in steps],
        [o_ref.at[i] for i in steps],
        [buffer.at[i] for i in steps],
    )


def pick_kernel(micro, count, dealing_ref, x_ref, o_ref, buffer, inverse_ref, in_sem, out_sem):
    inverse_of(dealing_ref, inverse_ref, [micro], count)
    move_blocks(*pick_copies(micro, count, inverse_ref, x_ref, o_ref, buffer), in_sem, out_sem)


def pick_blocks(stacked, micro, dealing):
    count = stacked.shape[1]
    block = stacked.shape[2:]
    dma = pltpu.SemaphoreType.DMA
    return pl.pallas_call(
        functools.partial(pick_kernel, micro, count),
        out_shape=jax.ShapeDtypeStruct((count, *block), stacked.dtype),
        in_specs=[SMALL, ANYWHERE],
        out_specs=ANYWHERE,
        scratch_shapes=[
            pltpu.VMEM((count, *block), stacked.dtype),
            pltpu.SMEM((count,), jnp.int32),
            dma((count,)),
            dma((count,)),
        ],
        compiler_params=params(),
        cost_estimate=cost(0, 4 * stacked.size // stacked.shape[0]),
        name="pick_blocks",
    )(dealing, stacked)


PLAIN, QUERY_AT, VALUE_AT, UP_AT, VECTOR_ROWS = 6, 8, 16, 24, 32


def prepare_kernel(
    micros, slots, groups, dealing_ref, prev_ref, tokens_ref, cot_ref,
    wq_ref, wk_ref, wv_ref, wo_ref, wu_ref, wd_ref, bq_ref, bv_ref, bu_ref, plain_refs,
    send_ref, piece_ref, pack_ref, info_ref, block_buffer, piece_buffer, vector_scr, inverse_refs, in_sem, out_sem,
    lengths_ref,
):
    here, head = lax.axis_index("seq"), lax.axis_index("head")
    for m in range(micros):
        inverse_of(dealing_ref, inverse_refs[m], [m], slots)
        info_ref[m, 0] = lengths_ref[m, inverse_refs[m][here]]
        info_ref[m, 1] = lax.rem(here, groups)
    reads, writes, buffers = [], [], []
    for step in range(2):
        slot = lax.rem(head - here // 2 + groups, groups) + groups * lax.rem(here + step, 2)
        for a, array_ref in enumerate((tokens_ref, cot_ref)):
            for m in range(micros):
                n = a * micros + m
                reads.append(array_ref.at[m, inverse_refs[m][slot]])
                writes.append(piece_ref.at[step, n])
                buffers.append(piece_buffer.at[step, n])
    blocks = pick_copies(0, slots, inverse_refs[0], prev_ref, send_ref, block_buffer)
    reads, writes, buffers = reads + blocks[0], writes + blocks[1], buffers + blocks[2]
    for i, (source, target) in enumerate(zip(reads, buffers)):
        pltpu.make_async_copy(source, target, in_sem.at[i]).start()

    at = 0
    turned = wo_ref[...].astype(F32).T.astype(BF16)
    for block in (wq_ref[...], wk_ref[...], wv_ref[...], turned, wu_ref[...], wd_ref[...]):
        pack_ref[:, at : at + block.shape[1]] = block
        at += block.shape[1]
    vector_scr[...] = jnp.zeros_like(vector_scr)
    for i, ref in enumerate(plain_refs):
        vector_scr[i : i + 1, : ref.shape[1]] = ref[...].astype(F32)
    for first, ref in ((QUERY_AT, bq_ref), (VALUE_AT, bv_ref), (UP_AT, bu_ref)):
        vector_scr[first : first + ref.shape[0], : ref.shape[1]] = ref[...].astype(F32)
    pack_ref[:VECTOR_ROWS, at:] = vector_scr[...].astype(BF16)
    pack_ref[VECTOR_ROWS:, at:] = jnp.zeros_like(pack_ref[VECTOR_ROWS:, at:])

    for i, (source, target, buffer) in enumerate(zip(reads, writes, buffers)):
        pltpu.make_async_copy(source, buffer, in_sem.at[i]).wait()
        pltpu.make_async_copy(buffer, target, out_sem.at[i]).start()
    for i, (target, buffer) in enumerate(zip(writes, buffers)):
        pltpu.make_async_copy(buffer, target, out_sem.at[i]).wait()


def prepare(lengths, dealing, prev, tokens, cot_tokens, weights, head_vectors, plain_vectors, groups):
    micros, slots = prev.shape[:2]
    block, row = prev.shape[2:], tokens.shape[2:]
    dma = pltpu.SemaphoreType.DMA
    copies = slots + 4 * micros
    columns = sum(w.size for w in weights) // weights[0].shape[0] + 128
    in_vmem = pl.BlockSpec(memory_space=pltpu.VMEM)
    flat = [*weights, *head_vectors]

    def body(lengths_ref, *refs):
        fixed = 4 + len(flat)
        plain_refs = refs[fixed : fixed + len(plain_vectors)]
        rest = refs[fixed + len(plain_vectors) :]
        made, buffers = rest[:4], rest[4:7]
        prepare_kernel(
            micros, slots, groups, *refs[:fixed], plain_refs, *made, *buffers,
            rest[7 : 7 + micros], *rest[7 + micros :], lengths_ref,
        )

    return pl.pallas_call(
        body,
        out_shape=(
            jax.ShapeDtypeStruct((slots, *block), prev.dtype),
            jax.ShapeDtypeStruct((2, 2 * micros, *row), tokens.dtype),
            jax.ShapeDtypeStruct((weights[0].shape[0], columns), BF16),
            jax.ShapeDtypeStruct((micros, 2), jnp.int32),
        ),
        in_specs=[SMALL, SMALL, ANYWHERE, ANYWHERE, ANYWHERE] + [in_vmem] * (len(flat) + len(plain_vectors)),
        out_specs=(ANYWHERE, ANYWHERE, in_vmem, SMALL),
        scratch_shapes=[
            pltpu.VMEM((slots, *block), prev.dtype),
            pltpu.VMEM((2, 2 * micros, *row), tokens.dtype),
            pltpu.VMEM((VECTOR_ROWS, 128), F32),
        ]
        + [pltpu.SMEM((slots,), jnp.int32)] * micros
        + [dma((copies,)), dma((copies,))],
        compiler_params=params(),
        cost_estimate=cost(0, 4 * prev.size // micros),
        name="prepare",
    )(lengths, dealing, prev, tokens, cot_tokens, *flat, *plain_vectors)


def unpack_kernel(heads, x_ref, qkv_ref, up_ref, plain_ref):
    groups, slots = x_ref.shape[:2]
    width = heads * HEAD_DIM
    qkv_ref[...] = jnp.zeros_like(qkv_ref)
    lanes = plain_ref.shape[1] // slots
    per_head = HEAD_DIM // slots
    unit = up_ref.shape[2] // heads
    per_unit = unit // slots
    for s in range(slots):
        for h in range(groups):
            block = x_ref[h, s].astype(F32)
            if h == 0:
                plain_ref[:, s * lanes : (s + 1) * lanes] = block[:8, :lanes]
            for j in range(heads):
                at = j * HEAD_DIM + s * per_head
                qkv_ref[h, :, at : at + per_head] = block[QUERY_AT + j : QUERY_AT + j + 1, :per_head]
                at += 2 * width
                qkv_ref[h, :, at : at + per_head] = block[VALUE_AT + j : VALUE_AT + j + 1, :per_head]
                at = j * unit + s * per_unit
                up_ref[h, :, at : at + per_unit] = block[UP_AT + j : UP_AT + j + 1, :per_unit]


def unpack_vectors(shards, heads, width, unit, model):
    groups, slots, _, columns = shards.shape
    last = columns // 128 - 1
    shape = jax.ShapeDtypeStruct
    return pl.pallas_call(
        functools.partial(unpack_kernel, heads),
        out_shape=(
            shape((groups, 1, 3 * width), F32),
            shape((groups, 1, unit), F32),
            shape((8, model), F32),
        ),
        grid=(1,),
        in_specs=[pl.BlockSpec((groups, slots, VECTOR_ROWS, 128), lambda i: (0, 0, 0, last))],
        out_specs=(
            pl.BlockSpec((groups, 1, 3 * width), lambda i: (0, 0, 0)),
            pl.BlockSpec((groups, 1, unit), lambda i: (0, 0, 0)),
            pl.BlockSpec((8, model), lambda i: (0, 0)),
        ),
        compiler_params=params(),
        cost_estimate=cost(0, 4 * groups * slots * VECTOR_ROWS * 128),
        name="unpack_vectors",
    )(shards)


def place_kernel(micro, count, index_ref, x_ref, *rest):
    o_ref, buffer, in_sem, out_sem = rest[-4:]
    steps = range(count)
    move_blocks(
        [x_ref.at[index_ref[micro, i]] for i in steps],
        [o_ref.at[micro, i] for i in steps],
        [buffer.at[i] for i in steps],
        in_sem,
        out_sem,
    )


def place_blocks(blocks, micro, micros, index, into):
    count = blocks.shape[0]
    others = [] if into is None else [into]
    dma = pltpu.SemaphoreType.DMA
    return pl.pallas_call(
        functools.partial(place_kernel, micro, count),
        out_shape=jax.ShapeDtypeStruct((micros, *blocks.shape), blocks.dtype),
        in_specs=[SMALL, ANYWHERE] + [ANYWHERE for _ in others],
        out_specs=ANYWHERE,
        scratch_shapes=[pltpu.VMEM(blocks.shape, blocks.dtype), dma((count,)), dma((count,))],
        input_output_aliases={2: 0} if others else {},
        compiler_params=params(),
        cost_estimate=cost(0, 4 * blocks.size),
        name="place_blocks",
    )(index, blocks, *others)


def project_kernel(x_ref, w_ref, b_ref, *outs):
    columns = outs[0].shape[2]
    for m, o_ref in enumerate(outs):
        o_ref[0] = (dot(x_ref[m], w_ref[0, :, :columns], 1, 0) + b_ref[0]).astype(BF16)


def project(x, weights, bias):
    micros, rows, width = x.shape[0] // 2, *x.shape[1:]
    groups, _, columns = bias.shape
    return pl.pallas_call(
        project_kernel,
        out_shape=(jax.ShapeDtypeStruct((groups, rows, columns), BF16),) * micros,
        grid=(groups,),
        in_specs=[
            pl.BlockSpec((micros, rows, width), lambda h: (0, 0, 0)),
            pl.BlockSpec((1, width, width), lambda h: (h, 0, 0)),
            pl.BlockSpec((1, 1, columns), lambda h: (h, 0, 0)),
        ],
        out_specs=(pl.BlockSpec((1, rows, columns), lambda h: (h, 0, 0)),) * micros,
        compiler_params=params(),
        cost_estimate=cost(2 * micros * groups * rows * width * columns, 2 * groups * columns * (width + rows)),
        name="project",
    )(x, weights, bias)


def head_mask(shape, head):
    lane = lax.broadcasted_iota(jnp.int32, shape, len(shape) - 1)
    return lane // HEAD_DIM == head


def gather_rows(shift, qkv_ref, groups, rows, width, q_scr, k_scr, v_scr):
    for g in range(groups):
        block = qkv_ref[(shift + g) % groups]
        q_scr[g * rows : (g + 1) * rows] = block[:, :width]
        k_scr[g * rows : (g + 1) * rows] = block[:, width : 2 * width]
        v_scr[g * rows : (g + 1) * rows] = block[:, 2 * width :]


def forward_kernel(heads, micro, info_ref, qkv_ref, prev_ref, *rest):
    logit_ref, attend_ref, context_ref, q_scr, k_scr, v_scr = rest[-6:]
    step = pl.program_id(0)
    groups, rows, columns = qkv_ref.shape
    piece, extent = prev_ref.shape[2:]
    width = columns // 3

    @pl.when(step == 0)
    def _():
        gather_rows(info_ref[micro, 1], qkv_ref, groups, rows, width, q_scr, k_scr, v_scr)

    q = q_scr[pl.ds(pl.multiple_of(step * piece, 16), piece), :]
    key_valid = lax.broadcasted_iota(jnp.int32, (1, extent), 1) < info_ref[micro, 0]
    total = jnp.zeros((piece, width), F32)
    for h in range(heads):
        mine = head_mask((1, width), h)
        q_head = jnp.where(mine, q, jnp.zeros_like(q))
        raw = dot(q_head, k_scr[...], 1, 1) * HEAD_DIM ** (-0.5) + prev_ref[0, h].astype(F32)
        logit_ref[0, h] = raw.astype(BF16)
        masked = jnp.where(key_valid, raw, -jnp.inf)
        top = jnp.max(masked, axis=-1, keepdims=True)
        grown = jnp.exp(masked - top)
        attend = grown * (1.0 / jnp.sum(grown, axis=-1, keepdims=True))
        low = attend.astype(BF16)
        attend_ref[0, h] = low
        total = total + jnp.where(mine, dot(low, v_scr[...], 1, 0), 0.0)
    context_ref[0] = total.astype(BF16)


def attention_forward(info, qkv, prev, micro, micros, logits_into):
    groups, rows, columns = qkv.shape
    pieces, heads, piece, extent = prev.shape
    width = columns // 3
    per = rows // piece
    others = [] if logits_into is None else [logits_into]
    return pl.pallas_call(
        functools.partial(forward_kernel, heads, micro),
        out_shape=(
            jax.ShapeDtypeStruct((micros, heads, extent, extent), BF16),
            jax.ShapeDtypeStruct(prev.shape, BF16),
            jax.ShapeDtypeStruct((groups, rows, width), BF16),
        ),
        grid_spec=pltpu.PrefetchScalarGridSpec(
            num_scalar_prefetch=1,
            grid=(pieces,),
            in_specs=[
                pl.BlockSpec((groups, rows, columns), lambda j, i: (0, 0, 0)),
                pl.BlockSpec((1, heads, piece, extent), lambda j, i: (j, 0, 0, 0)),
            ]
            + [pl.BlockSpec(memory_space=pl.ANY) for _ in others],
            out_specs=(
                pl.BlockSpec((1, heads, piece, extent), lambda j, i: (micro, 0, j, 0)),
                pl.BlockSpec((1, heads, piece, extent), lambda j, i: (j, 0, 0, 0)),
                pl.BlockSpec((1, piece, width), lambda j, i: ((j // per + i[micro, 1]) % groups, j % per, 0)),
            ),
            scratch_shapes=[pltpu.VMEM((extent, width), BF16)] * 3,
        ),
        input_output_aliases={3: 0} if others else {},
        compiler_params=params(),
        cost_estimate=cost(4 * heads * extent * extent * HEAD_DIM * 4, 6 * heads * extent * extent),
        name="attention_forward",
    )(info, qkv, prev, *others)


def backward_kernel(
    heads, micro, info_ref, qkv_ref, attend_ref, context_ref, dcon_ref, cot_ref,
    send_ref, dqkv_ref, sums_ref, q_scr, k_scr, v_scr, dq_scr, dk_scr, dv_scr,
):
    step = pl.program_id(0)
    groups, rows, columns = qkv_ref.shape
    piece, extent = attend_ref.shape[2:]
    width = columns // 3
    scale = HEAD_DIM ** (-0.5)

    @pl.when(step == 0)
    def _():
        gather_rows(info_ref[micro, 1], qkv_ref, groups, rows, width, q_scr, k_scr, v_scr)
        dk_scr[...] = jnp.zeros_like(dk_scr)
        dv_scr[...] = jnp.zeros_like(dv_scr)

    here = pl.ds(pl.multiple_of(step * piece, 16), piece)
    q = q_scr[here, :]
    dcon = dcon_ref[0]
    both = dcon.astype(F32) * context_ref[0].astype(F32)
    dq = jnp.zeros((piece, width), F32)
    for h in range(heads):
        mine = head_mask((1, width), h)
        dcon_head = jnp.where(mine, dcon, jnp.zeros_like(dcon))
        q_head = jnp.where(mine, q, jnp.zeros_like(q))
        low = attend_ref[0, h]
        delta = jnp.sum(jnp.where(mine, both, 0.0), axis=-1, keepdims=True)
        dprob = dot(dcon_head, v_scr[...], 1, 1)
        dscore = low.astype(F32) * (dprob - delta) + cot_ref[0, h].astype(F32)
        dlow = dscore.astype(BF16)
        send_ref[0, h] = dlow
        dq = dq + jnp.where(mine, dot(dlow, k_scr[...], 1, 0), 0.0)
        dk_scr[...] += dot(dlow, q_head, 0, 0)
        dv_scr[...] += dot(low, dcon_head, 0, 0)
    dq_scr[here, :] = dq * scale

    @pl.when(step == pl.num_programs(0) - 1)
    def _():
        sums_ref[0:1, :] = jnp.sum(dq_scr[...], axis=0, keepdims=True)
        sums_ref[1:2, :] = jnp.sum(dv_scr[...], axis=0, keepdims=True)
        for g in range(groups):
            part = slice(g * rows, (g + 1) * rows)
            dqkv_ref[(info_ref[micro, 1] + g) % groups] = jnp.concatenate(
                [dq_scr[part], dk_scr[part] * scale, dv_scr[part]], axis=1
            ).astype(BF16)


def attention_backward(info, qkv, attend, context, dcontext, cot, micro):
    groups, rows, columns = qkv.shape
    pieces, heads, piece, extent = attend.shape
    width = columns // 3
    per = rows // piece
    rotated = pl.BlockSpec((1, piece, width), lambda j, i: ((j // per + i[micro, 1]) % groups, j % per, 0))
    square = pl.BlockSpec((1, heads, piece, extent), lambda j, i: (j, 0, 0, 0))
    return pl.pallas_call(
        functools.partial(backward_kernel, heads, micro),
        out_shape=(
            jax.ShapeDtypeStruct(attend.shape, BF16),
            jax.ShapeDtypeStruct((groups, rows, columns), BF16),
            jax.ShapeDtypeStruct((2, width), F32),
        ),
        grid_spec=pltpu.PrefetchScalarGridSpec(
            num_scalar_prefetch=1,
            grid=(pieces,),
            in_specs=[
                pl.BlockSpec((groups, rows, columns), lambda j, i: (0, 0, 0)),
                square,
                rotated,
                rotated,
                pl.BlockSpec((1, heads, piece, extent), lambda j, i: (micro, 0, j, 0)),
            ],
            out_specs=(
                square,
                pl.BlockSpec((groups, rows, columns), lambda j, i: (0, 0, 0)),
                pl.BlockSpec((2, width), lambda j, i: (0, 0)),
            ),
            scratch_shapes=[pltpu.VMEM((extent, width), BF16)] * 3
            + [pltpu.VMEM((extent, width), F32)] * 3,
        ),
        compiler_params=params(),
        cost_estimate=cost(8 * heads * extent * extent * HEAD_DIM * 4, 6 * heads * extent * extent),
        name="attention_backward",
    )(info, qkv, attend, context, dcontext, cot)


def normal(values):
    center = values - jnp.mean(values, axis=-1, keepdims=True)
    spread = jnp.mean(center * center, axis=-1, keepdims=True)
    inverse = lax.rsqrt(spread + epsilon)
    return center * inverse, inverse


def normal_back(grad, gain, unit, inverse):
    scaled = grad * gain
    return inverse * (
        scaled
        - jnp.mean(scaled, axis=-1, keepdims=True)
        - unit * jnp.mean(scaled * unit, axis=-1, keepdims=True)
    )


def rows_kernel(
    cuts, micro, con_ref, x_ref, w_ref, bup_ref, vec_ref,
    y_ref, dz_ref, dcon_ref, h1_ref, act_ref, b1_ref, b2_ref, b0_ref, sums_ref, dbup_ref,
    slope, acc, hidden, unit_scr, inv_scr,
):
    groups, rows, width = con_ref.shape
    qkv_end, out_end, up_end, down_end = cuts
    b_out, gain_one, shift_one = vec_ref[0:1, :], vec_ref[1:2, :], vec_ref[2:3, :]
    b_down, gain_two, shift_two = vec_ref[3:4, :], vec_ref[4:5, :], vec_ref[5:6, :]

    branch = b_out + x_ref[micro].astype(F32)
    for h in range(groups):
        branch = branch + dot(con_ref[h], w_ref[h, :, qkv_end:out_end], 1, 1)
    unit_one, inverse_one = normal(branch)
    unit_scr[...] = unit_one
    inv_scr[...] = inverse_one
    hid = unit_one * gain_one + shift_one
    hidden[...] = hid
    h1_ref[...] = hid.astype(BF16)
    acc[...] = hid + b_down

    def up(h, carry):
        u = dot(h1_ref[...], w_ref[h, :, out_end:up_end], 1, 0) + bup_ref[h]
        half = 0.5 * (1.0 + lax.erf(u * 0.7071067811865476))
        act_ref[h] = (u * half).astype(BF16)
        slope[h] = half + u * (jnp.exp(u * u * -0.5) * 0.3989422804014327)
        acc[...] += dot(act_ref[h], w_ref[h, :, up_end:down_end], 1, 1)
        return carry

    lax.fori_loop(0, groups, up, 0)
    unit_two, inverse_two = normal(acc[...])
    y_ref[...] = (unit_two * gain_two + shift_two).astype(BF16)
    cot = x_ref[x_ref.shape[0] // 2 + micro].astype(F32)
    sums_ref[4:5, :] = jnp.sum(cot * unit_two, axis=0, keepdims=True)
    sums_ref[5:6, :] = jnp.sum(cot, axis=0, keepdims=True)
    dz_two = normal_back(cot, gain_two, unit_two, inverse_two)
    sums_ref[3:4, :] = jnp.sum(dz_two, axis=0, keepdims=True)
    b2_ref[...] = dz_two.astype(BF16)
    acc[...] = dz_two

    def down(h, carry):
        du = dot(b2_ref[...], w_ref[h, :, up_end:down_end], 1, 0) * slope[h]
        dbup_ref[h] = jnp.sum(du, axis=0, keepdims=True)
        b1_ref[h] = du.astype(BF16)
        acc[...] += dot(b1_ref[h], w_ref[h, :, out_end:up_end], 1, 1)
        return carry

    lax.fori_loop(0, groups, down, 0)
    dh = acc[...]
    unit_one = unit_scr[...]
    sums_ref[1:2, :] = jnp.sum(dh * unit_one, axis=0, keepdims=True)
    sums_ref[2:3, :] = jnp.sum(dh, axis=0, keepdims=True)
    dz_one = normal_back(dh, gain_one, unit_one, inv_scr[...])
    sums_ref[0:1, :] = jnp.sum(dz_one, axis=0, keepdims=True)
    sums_ref[6:8, :] = jnp.zeros_like(sums_ref[6:8, :])
    dz_ref[...] = dz_one
    b0_ref[...] = dz_one.astype(BF16)
    for h in range(groups):
        dcon_ref[h] = dot(b0_ref[...], w_ref[h, :, qkv_end:out_end], 1, 0).astype(BF16)


def row_work(cuts, micro, context, x, weights, bias_up, vectors):
    groups, rows, width = context.shape
    model = x.shape[2]
    in_vmem = pl.BlockSpec(memory_space=pltpu.VMEM)
    unit = bias_up.shape[2]
    shape = jax.ShapeDtypeStruct
    args = (context, x, weights, bias_up, vectors)
    return pl.pallas_call(
        functools.partial(rows_kernel, cuts, micro),
        out_shape=(
            shape((rows, model), BF16),
            shape((rows, model), F32),
            shape(context.shape, BF16),
            shape((rows, model), BF16),
            shape((groups, rows, unit), BF16),
            shape((groups, rows, unit), BF16),
            shape((rows, model), BF16),
            shape((rows, model), BF16),
            shape((8, model), F32),
            shape((groups, 1, unit), F32),
        ),
        in_specs=[in_vmem] * len(args),
        out_specs=(in_vmem,) * 10,
        scratch_shapes=[
            pltpu.VMEM((groups, rows, unit), F32),
            pltpu.VMEM((rows, model), F32),
            pltpu.VMEM((rows, model), F32),
            pltpu.VMEM((rows, model), F32),
            pltpu.VMEM((rows, 1), F32),
        ],
        compiler_params=params(),
        cost_estimate=cost(8 * groups * rows * model * (unit + width), 2 * weights.size),
        name="row_work",
    )(*args)


def input_kernel(dqkv_ref, w_ref, dz_ref, o_ref):
    total = dz_ref[...]
    for h in range(dqkv_ref.shape[0]):
        total = total + dot(dqkv_ref[h], w_ref[h, :, : dqkv_ref.shape[2]], 1, 1)
    _, pieces, share, piece = o_ref.shape
    turned = total.T
    for h in range(o_ref.shape[0]):
        for p in range(pieces):
            block = turned[h * share : (h + 1) * share, p * piece : (p + 1) * piece]
            o_ref[h, p] = block.astype(BF16)


def input_grad(dqkv, weights, dz, pieces):
    groups, rows, columns = dqkv.shape
    model = dz.shape[1]
    return pl.pallas_call(
        input_kernel,
        out_shape=jax.ShapeDtypeStruct((groups, pieces, model // groups, rows // pieces), BF16),
        grid=(1,),
        in_specs=[
            whole(dqkv),
            pl.BlockSpec((groups, model, model), lambda i: (0, 0, 0)),
            whole(dz),
        ],
        out_specs=pl.BlockSpec((groups, pieces, model // groups, rows // pieces), lambda i: (0, 0, 0, 0)),
        compiler_params=params(),
        cost_estimate=cost(2 * groups * rows * columns * model, 2 * groups * columns * model),
        name="input_grad",
    )(dqkv, weights, dz)


def weight_kernel(cuts, micros, heads, slots, *refs):
    out_ref, vector_scr = refs[-2:]
    qkv_end, out_end, up_end, down_end = cuts

    def summed(family):
        total = family[0][...]
        for ref in family[1:]:
            total = total + ref[...]
        return total

    def product(lefts, rights):
        total = None
        for left, right in zip(lefts, rights):
            term = dot(left[...].reshape(left.shape[-2:]), right[0], 0, 0)
            total = term if total is None else total + term
        return total.astype(BF16)

    x, b0, h1, b2, dqkv, con, b1, act, own, plain, up = (
        refs[i * micros : (i + 1) * micros] for i in range(11)
    )
    out_ref[0, :, 0:qkv_end] = product(x, dqkv)
    out_ref[0, :, qkv_end:out_end] = product(b0, con)
    out_ref[0, :, out_end:up_end] = product(h1, b1)
    out_ref[0, :, up_end:down_end] = product(b2, act)

    own_sum = jnp.where(pl.program_id(0) == lax.axis_index("head"), summed(own), 0.0)
    plain_sum, up_sum = summed(plain), summed(up)[0]
    rows = out_ref.shape[1] // slots
    lanes = plain_sum.shape[1] // slots
    unit = up_sum.shape[1] // heads
    vector_scr[...] = jnp.zeros_like(vector_scr)
    for s in range(slots):
        vector_scr[:8, :lanes] = plain_sum[:, s * lanes : (s + 1) * lanes]
        for j in range(heads):
            at, step = j * HEAD_DIM + s * (HEAD_DIM // slots), HEAD_DIM // slots
            vector_scr[QUERY_AT + j : QUERY_AT + j + 1, :step] = own_sum[0:1, at : at + step]
            vector_scr[VALUE_AT + j : VALUE_AT + j + 1, :step] = own_sum[1:2, at : at + step]
            at, step = j * unit + s * (unit // slots), unit // slots
            vector_scr[UP_AT + j : UP_AT + j + 1, :step] = up_sum[:, at : at + step]
        out_ref[0, s * rows : s * rows + VECTOR_ROWS, down_end:] = vector_scr[...].astype(BF16)
        out_ref[0, s * rows + VECTOR_ROWS : (s + 1) * rows, down_end:] = jnp.zeros(
            (rows - VECTOR_ROWS, 128), BF16
        )


def weight_grads(cuts, heads, slots, x, lefts, rights, own, plain, up):
    micros = len(lefts[0])
    groups = rights[0][0].shape[0]
    model = lefts[0][0].shape[1]
    flat_left = [a for family in lefts for a in family]
    flat_right = [a for family in rights for a in family]
    rows = flat_left[0].shape[0]
    columns = cuts[-1] + 128

    def of_micro(m):
        return pl.BlockSpec((1, rows, model), lambda h: (m, 0, 0))

    def per_group(a):
        return pl.BlockSpec((1, *a.shape[1:]), lambda h: (h, 0, 0))

    return pl.pallas_call(
        functools.partial(weight_kernel, cuts, micros, heads, slots),
        out_shape=jax.ShapeDtypeStruct((groups, model, columns), BF16),
        grid=(groups,),
        in_specs=[of_micro(m) for m in range(micros)]
        + [whole(a) for a in flat_left]
        + [per_group(a) for a in flat_right]
        + [whole(a) for a in (*own, *plain)]
        + [per_group(a) for a in up],
        out_specs=pl.BlockSpec((1, model, columns), lambda h: (h, 0, 0)),
        scratch_shapes=[pltpu.VMEM((VECTOR_ROWS, 128), F32)],
        compiler_params=params(),
        cost_estimate=cost(2 * micros * groups * rows * model * cuts[-1], 2 * groups * model * cuts[-1]),
        name="weight_grads",
    )(*([x] * micros), *flat_left, *flat_right, *own, *plain, *up)


MESH = pl.DeviceIdType.MESH
SIDE = 2


def remote(source, target, send_sem, recv_sem, device):
    return pltpu.make_async_remote_copy(
        src_ref=source,
        dst_ref=target,
        send_sem=send_sem,
        recv_sem=recv_sem,
        device_id=device,
        device_id_type=MESH,
    )


def signal(device):
    pl.semaphore_signal(
        pltpu.get_barrier_semaphore(), inc=1, device_id=device, device_id_type=MESH
    )


def greet(devices):
    for device in devices:
        signal(device)
    pl.semaphore_wait(pltpu.get_barrier_semaphore(), len(devices))


def cross_kernel(groups, x_ref, o_ref, send_sem, recv_sem, own_sem):
    me = lax.axis_index("head")
    peers = [lax.rem(me + i, groups) for i in range(1, groups)]
    greet([{"head": peer} for peer in peers])
    copies = []
    for i, peer in enumerate(peers):
        copy = remote(x_ref.at[peer], o_ref.at[me], send_sem.at[i], recv_sem.at[i], {"head": peer})
        copy.start()
        copies.append(copy)
    own = pltpu.make_async_copy(x_ref.at[me], o_ref.at[me], own_sem)
    own.start()
    own.wait()
    for copy in copies:
        copy.wait()


def across_heads(x, number):
    groups = x.shape[0]
    return pl.pallas_call(
        functools.partial(cross_kernel, groups),
        out_shape=jax.ShapeDtypeStruct(x.shape, x.dtype),
        in_specs=[pl.BlockSpec(memory_space=pltpu.VMEM)],
        out_specs=pl.BlockSpec(memory_space=pl.ANY),
        scratch_shapes=[
            pltpu.SemaphoreType.DMA((groups - 1,)),
            pltpu.SemaphoreType.DMA((groups - 1,)),
            pltpu.SemaphoreType.DMA,
        ],
        compiler_params=params(collective_id=number, has_side_effects=True),
        cost_estimate=cost(0, 40 * x.size),
        name="across_heads",
    )(x)


SIDES = 2
LINE = 4


class Place:
    def __init__(self):
        self.here, self.head = lax.axis_index("seq"), lax.axis_index("head")
        self.z, self.x = self.here // SIDES, lax.rem(self.here, SIDES)
        self.y, self.c = self.head // 2, lax.rem(self.head, 2)
        self.up, self.down = {"seq": self.here + SIDES}, {"seq": self.here - SIDES}
        self.across = {"seq": self.z * SIDES + (1 - self.x)}
        self.over = {"head": (1 - self.y) * 2 + self.c}
        self.beside = {"head": self.y * 2 + (1 - self.c)}
        self.not_last, self.not_first = self.z < LINE - 1, self.z > 0
        self.is_end = jnp.logical_or(jnp.logical_not(self.not_last), jnp.logical_not(self.not_first))
        half = (LINE - 1 - self.z) // 2
        self.order = [self.z, self.z + 1 - 2 * lax.rem(self.z, 2), 1 + half, (LINE - 1) * half]

    def greet_neighbours(self):
        pl.when(self.not_last)(lambda: signal(self.up))
        pl.when(self.not_first)(lambda: signal(self.down))
        for device in (self.across, self.over, self.beside):
            signal(device)
        return 3 + self.not_last.astype(jnp.int32) + self.not_first.astype(jnp.int32)


def arrived(block, send_sem, recv_sem, device):
    remote(block, block, send_sem, recv_sem, device).wait_recv()


def line_kernel(
    slots, groups, pack_ref, piece_ref, all_ref, rows_ref,
    z_s, z_r, x_s, x_r, y_s, y_r, piece_s, piece_r, own_sem,
):
    me = Place()
    here, head, x, y, c = me.here, me.head, me.x, me.y, me.c
    group = lax.rem(head - here + slots, groups)
    homes = [group * SIDE + p for p in range(SIDE)]
    targets = [
        lax.rem(head - me.z + groups, groups) + groups * lax.rem(here + step, 2) for step in range(2)
    ]
    expected = me.greet_neighbours()
    for home in homes:
        pl.when(home != here)(lambda home=home: signal({"seq": home}))
    for target in targets:
        expected = expected + (target != here).astype(jnp.int32)
    pl.semaphore_wait(pltpu.get_barrier_semaphore(), expected)

    def at(i, side, row):
        return all_ref.at[row * 2 + c, i * SIDES + side]

    def source(k):
        return pack_ref if k == 0 else at(me.order[k], x, y)

    def upward(k):
        i = me.order[k]
        return remote(source(k), at(i, x, y), z_s.at[i], z_r.at[i], me.up)

    def downward(k):
        i = me.order[k]
        return remote(source(k), at(i, x, y), z_s.at[LINE + i], z_r.at[i], me.down)

    def over_x(k):
        i = me.order[k]
        return remote(source(k), at(i, x, y), x_s.at[i], x_r.at[i], me.across)

    def over_y(k):
        i = me.order[k]
        return remote(source(k), at(i, x, y), y_s.at[i], y_r.at[i], me.over)

    def goes_up(k):
        return (me.order[k] <= me.z) & me.not_last

    def goes_down(k):
        return (me.order[k] >= me.z) & me.not_first

    def piece(step):
        return remote(
            piece_ref.at[step], rows_ref.at[:, x], piece_s.at[step], piece_r.at[x], {"seq": targets[step]}
        )

    def piece_here(step):
        return pltpu.make_async_copy(piece_ref.at[step], rows_ref.at[:, x], own_sem.at[1])

    own = pltpu.make_async_copy(pack_ref, at(me.z, x, y), own_sem.at[0])
    own.start()
    for k in range(LINE):
        i = me.order[k]
        if k:
            arrived(at(i, x, y), z_s.at[i], z_r.at[i], me.up)
        pl.when(goes_up(k))(lambda k=k: upward(k).start())
        pl.when(goes_down(k))(lambda k=k: downward(k).start())
        over_x(k).start()
        over_y(k).start()
        turn = {0: me.is_end, LINE - 1: jnp.logical_not(me.is_end)}.get(k)
        if turn is not None:
            for step, target in enumerate(targets):
                pl.when(turn & (target != here))(lambda step=step: piece(step).start())
                pl.when(turn & (target == here))(lambda step=step: piece_here(step).start())
    for k in range(LINE):
        i = me.order[k]
        arrived(at(i, 1 - x, y), x_s.at[i], x_r.at[i], me.across)
        arrived(at(i, x, 1 - y), y_s.at[i], y_r.at[i], me.over)
    for p, home in enumerate(homes):
        block = rows_ref.at[:, p]
        pl.when(home != here)(
            lambda block=block, p=p, home=home: arrived(
                block, piece_s.at[p], piece_r.at[p], {"seq": home}
            )
        )
    for step, target in enumerate(targets):
        pl.when(target != here)(lambda step=step: piece(step).wait_send())
        pl.when(target == here)(lambda step=step: piece_here(step).wait())
    own.wait()
    for k in range(LINE):
        pl.when(goes_up(k))(lambda k=k: upward(k).wait_send())
        pl.when(goes_down(k))(lambda k=k: downward(k).wait_send())
        over_x(k).wait_send()
        over_y(k).wait_send()


def gather_line(packed, pieces, slots, groups, number):
    dma = pltpu.SemaphoreType.DMA
    return pl.pallas_call(
        functools.partial(line_kernel, slots, groups),
        out_shape=(
            jax.ShapeDtypeStruct((groups, slots, *packed.shape), packed.dtype),
            jax.ShapeDtypeStruct((pieces.shape[1], SIDE, *pieces.shape[2:]), pieces.dtype),
        ),
        in_specs=[pl.BlockSpec(memory_space=pltpu.VMEM)] * 2,
        out_specs=(ANYWHERE,) * 2,
        scratch_shapes=[dma((2 * LINE,)), dma((LINE,))] + [dma((LINE,))] * 4 + [dma((2,))] * 3,
        compiler_params=params(collective_id=number, has_side_effects=True),
        cost_estimate=cost(0, 3000000 * 20),
        name="gather_line",
    )(packed, pieces)


def plane_kernel(in_ref, all_ref, y_s, y_r, c_s, c_r):
    me = Place()
    x, y, c = me.x, me.y, me.c
    greet([me.over, me.beside])

    def at(i, side, row, core=c):
        return all_ref.at[row * 2 + core, i * SIDES + side]

    def over_y(i):
        block = at(i, 1 - x, y)
        return remote(block, block, y_s.at[i], y_r.at[i], me.over)

    places = ((x, y), (1 - x, y), (x, 1 - y), (1 - x, 1 - y))

    def to_core(i, kind):
        n = kind * LINE + i
        block = at(i, *places[kind])
        return remote(block, block, c_s.at[n], c_r.at[n], me.beside)

    for i in range(LINE):
        over_y(i).start()
    for kind in range(3):
        for i in range(LINE):
            to_core(i, kind).start()
    for i in range(LINE):
        arrived(at(i, 1 - x, 1 - y), y_s.at[i], y_r.at[i], me.over)
        to_core(i, 3).start()
    for kind, (side, row) in enumerate(places):
        for i in range(LINE):
            n = kind * LINE + i
            arrived(at(i, side, row, 1 - c), c_s.at[n], c_r.at[n], me.beside)
    for i in range(LINE):
        over_y(i).wait_send()
        for kind in range(4):
            to_core(i, kind).wait_send()


def gather_plane(shards, number):
    dma = pltpu.SemaphoreType.DMA
    return pl.pallas_call(
        plane_kernel,
        out_shape=jax.ShapeDtypeStruct(shards.shape, shards.dtype),
        in_specs=[ANYWHERE],
        out_specs=ANYWHERE,
        scratch_shapes=[dma((LINE,))] * 2 + [dma((4 * LINE,))] * 2,
        input_output_aliases={0: 0},
        compiler_params=params(collective_id=number, has_side_effects=True),
        cost_estimate=cost(0, 3000000 * 40),
        name="gather_plane",
    )(shards)


def add_into(target, terms, shape):
    rows = shape[-2]
    tile = 16
    steps = rows // tile
    outer = 1
    for n in shape[:-2]:
        outer *= n

    def body(i, carry):
        at = pl.ds(pl.multiple_of(lax.rem(i, steps) * tile, tile), tile)
        rest = i // steps
        index = []
        for n in reversed(shape[:-2]):
            index.insert(0, lax.rem(rest, n))
            rest = rest // n
        index = (*index, at)
        total = terms[0][index].astype(F32)
        for term in terms[1:]:
            total = total + term[index].astype(F32)
        target[index] = total.astype(target.dtype)
        return carry

    lax.fori_loop(0, outer * steps, body, 0)


def finish_kernel(
    slots, groups, micros, part_ref, y_refs, dx_refs, sum_ref, tokens_ref, grads_ref,
    held, first, second, line,
    c_s, c_r, x_s, x_r, y_s, y_r, z_s, z_r, home_s, home_r, over_s, over_r, near_s, near_r, pass_s, pass_r,
    grad_s, grad_r, own_sem,
):
    me = Place()
    here, head, x, y, z, c = me.here, me.head, me.x, me.y, me.z, me.c
    order = me.order[::-1]
    group = lax.rem(head - here + slots, groups)
    homes = [group * SIDE + p for p in range(SIDE)]
    mine = lax.rem(head - z + groups, groups)
    senders = [lax.rem(slot + z, groups) for slot in range(slots)]

    def is_me(slot, other):
        return (slot == here) & (other == head)

    expected = me.greet_neighbours()
    for slot in range(slots):
        pl.when(jnp.logical_not(is_me(slot, senders[slot])))(
            lambda slot=slot: signal({"seq": slot, "head": senders[slot]})
        )
    for home in homes:
        for h in range(groups):
            expected = expected + 1 - is_me(home, h).astype(jnp.int32)
    pl.semaphore_wait(pltpu.get_barrier_semaphore(), expected)

    def to_core(k, row):
        i = order[k]
        n = row * LINE + i
        return remote(
            part_ref.at[row * 2 + (1 - c), i], held.at[i, row], c_s.at[n], c_r.at[n], me.beside
        )

    sides = (1 - x, x)

    def over_y(k, n):
        i = order[k]
        at = n * LINE + i
        return remote(
            held.at[i, 1 - y, sides[n]], first.at[i, sides[n]], y_s.at[at], y_r.at[at], me.over
        )

    def over_x(k):
        i = order[k]
        return remote(held.at[i, y, 1 - x], second.at[i], x_s.at[i], x_r.at[i], me.across)

    def upward(k):
        i = order[k]
        return remote(held.at[i, y, x], line.at[0, i], z_s.at[i], z_r.at[i], me.up)

    def downward(k):
        i = order[k]
        n = LINE + i
        return remote(held.at[i, y, x], line.at[1, i], z_s.at[n], z_r.at[n], me.down)

    rows, columns = sum_ref.shape

    def begin(k):
        i = order[k]
        for row in (1 - y, y):
            n = row * LINE + i
            arrived(held.at[i, row], c_s.at[n], c_r.at[n], me.beside)
        block = held.at[i, 1 - y]
        add_into(block, [block, part_ref.at[(1 - y) * 2 + c, i]], (SIDES, rows, columns))
        over_y(k, 0).start()
        over_y(k, 1).start()
        block = held.at[i, y]
        add_into(block, [block, part_ref.at[y * 2 + c, i]], (SIDES, rows, columns))

    def middle(k):
        i = order[k]
        for n, side in enumerate(sides):
            at = n * LINE + i
            arrived(first.at[i, side], y_s.at[at], y_r.at[at], me.over)
            block = held.at[i, y, side]
            add_into(block, [block, first.at[i, side]], (rows, columns))
            if n == 0:
                over_x(k).start()

    def end(k):
        i = order[k]
        n = LINE + i
        last = k == LINE - 1
        arrived(second.at[i], x_s.at[i], x_r.at[i], me.across)
        target = sum_ref if last else held.at[i, y, x]
        add_into(target, [held.at[i, y, x], second.at[i]], (rows, columns))

        def below():
            arrived(line.at[0, i], z_s.at[i], z_r.at[i], me.up)
            add_into(target, [target, line.at[0, i]], (rows, columns))

        def above():
            arrived(line.at[1, i], z_s.at[n], z_r.at[n], me.up)
            add_into(target, [target, line.at[1, i]], (rows, columns))

        pl.when((i >= z) & me.not_first)(below)
        pl.when((i <= z) & me.not_last)(above)
        if not last:
            pl.when(i > z)(lambda: upward(k).start())
            pl.when(i < z)(lambda: downward(k).start())

    def home_copy(m, p):
        n = m * SIDE + p
        return remote(
            y_refs[m].at[p], tokens_ref.at[m, here], home_s.at[n], home_r.at[m * 2 + here // groups], {"seq": homes[p]}
        )

    def home_here(m, p):
        return pltpu.make_async_copy(y_refs[m].at[p], tokens_ref.at[m, here], own_sem.at[m])

    def grad_copy(m, p, h):
        n = (m * SIDE + p) * groups + h
        return remote(
            dx_refs[m].at[h, p], grads_ref.at[m, here], grad_s.at[n], grad_r.at[m * slots + here],
            {"seq": homes[p], "head": h},
        )

    def grad_here(m, p, h):
        return pltpu.make_async_copy(dx_refs[m].at[h, p], grads_ref.at[m, here], own_sem.at[micros + m])

    def slot_of(other, j):
        return lax.rem(other - z + groups, groups) + groups * j

    far_head, near_head = (1 - y) * 2 + c, y * 2 + (1 - c)
    last_head = (1 - y) * 2 + (1 - c)

    def far(m, j):
        n, block = m * 2 + j, tokens_ref.at[m, slot_of(head, j)]
        return remote(block, block, over_s.at[n], over_r.at[n], me.over)

    def near(m, j):
        n, block = m * 2 + j, tokens_ref.at[m, slot_of(head, j)]
        return remote(block, block, near_s.at[n], near_r.at[n], me.beside)

    def passed(m, j):
        n, block = m * 2 + j, tokens_ref.at[m, slot_of(far_head, j)]
        return remote(block, block, pass_s.at[n], pass_r.at[n], me.beside)

    for k in range(LINE):
        for row in range(2):
            to_core(k, row).start()
    for m in range(micros):
        for p, home in enumerate(homes):
            pl.when(home != here)(lambda m=m, p=p: home_copy(m, p).start())
            pl.when(home == here)(lambda m=m, p=p: home_here(m, p).start())
    for k in range(LINE):
        begin(k)
        if k >= 1:
            middle(k - 1)
        if k >= 2:
            end(k - 2)
        if k == 2:
            for m in range(micros):
                for p, home in enumerate(homes):
                    for h in range(groups):
                        same = is_me(home, h)
                        pl.when(jnp.logical_not(same))(lambda m=m, p=p, h=h: grad_copy(m, p, h).start())
                        pl.when(same)(lambda m=m, p=p, h=h: grad_here(m, p, h).start())
    middle(LINE - 1)
    end(LINE - 2)
    for m in range(micros):
        for p, home in enumerate(homes):
            pl.when(home == here)(lambda m=m, p=p: home_here(m, p).wait())
        for j in range(2):
            slot = slot_of(head, j)
            pl.when(slot != here)(
                lambda m=m, j=j, slot=slot: arrived(
                    tokens_ref.at[m, slot], home_s.at[m * 2 + j], home_r.at[m * 2 + j], {"seq": slot}
                )
            )
            far(m, j).start()
            near(m, j).start()
    end(LINE - 1)
    for m in range(micros):
        for j in range(2):
            n = m * 2 + j
            arrived(tokens_ref.at[m, slot_of(far_head, j)], over_s.at[n], over_r.at[n], me.over)
            passed(m, j).start()
    for m in range(micros):
        for j in range(2):
            n = m * 2 + j
            arrived(tokens_ref.at[m, slot_of(near_head, j)], near_s.at[n], near_r.at[n], me.beside)
            arrived(tokens_ref.at[m, slot_of(last_head, j)], pass_s.at[n], pass_r.at[n], me.beside)
        for slot in range(slots):
            n = m * slots + slot
            pl.when(jnp.logical_not(is_me(slot, senders[slot])))(
                lambda m=m, n=n, slot=slot: arrived(
                    grads_ref.at[m, slot], grad_s.at[0], grad_r.at[n], {"seq": slot, "head": senders[slot]}
                )
            )
    for m in range(micros):
        for p, home in enumerate(homes):
            pl.when(home != here)(lambda m=m, p=p: home_copy(m, p).wait_send())
            for h in range(groups):
                same = is_me(home, h)
                pl.when(jnp.logical_not(same))(lambda m=m, p=p, h=h: grad_copy(m, p, h).wait_send())
                pl.when(same)(lambda m=m, p=p, h=h: grad_here(m, p, h).wait())
        for j in range(2):
            far(m, j).wait_send()
            near(m, j).wait_send()
            passed(m, j).wait_send()
    for k in range(LINE):
        for row in range(2):
            to_core(k, row).wait_send()
        over_y(k, 0).wait_send()
        over_y(k, 1).wait_send()
        over_x(k).wait_send()
        if k < LINE - 1:
            i = order[k]
            pl.when(i > z)(lambda k=k: upward(k).wait_send())
            pl.when(i < z)(lambda k=k: downward(k).wait_send())


def finish(part, ys, dxs, slots, groups, number):
    columns = part.shape[-1]
    micros = len(ys)
    _, piece, model = ys[0].shape

    def body(part_ref, *refs):
        finish_kernel(
            slots, groups, micros, part_ref, refs[:micros], refs[micros : 2 * micros], *refs[2 * micros :]
        )

    rows = part.shape[-2]
    dma = pltpu.SemaphoreType.DMA
    vmem = pltpu.VMEM
    part = part.reshape(groups, LINE, SIDES, rows, columns)
    return pl.pallas_call(
        body,
        out_shape=(
            jax.ShapeDtypeStruct((rows, columns), F32),
            jax.ShapeDtypeStruct((micros, slots, piece, model), BF16),
            jax.ShapeDtypeStruct((micros, slots, *dxs[0].shape[-2:]), BF16),
        ),
        in_specs=[pl.BlockSpec(memory_space=pltpu.VMEM)] * (1 + 2 * micros),
        out_specs=(pl.BlockSpec(memory_space=pltpu.VMEM),) + (pl.BlockSpec(memory_space=pl.ANY),) * 2,
        scratch_shapes=[
            vmem((LINE, 2, SIDES, rows, columns), BF16),
            vmem((LINE, SIDES, rows, columns), BF16),
            vmem((LINE, rows, columns), BF16),
            vmem((2, LINE, rows, columns), BF16),
        ]
        + [dma((2 * LINE,))] * 8
        + [dma((2 * micros,))] * 8
        + [dma((2 * groups * micros,)), dma((slots * micros,)), dma((2 * micros,))],
        compiler_params=params(collective_id=number, has_side_effects=True),
        cost_estimate=cost(0, 3000000 * 40),
        name="finish",
    )(part, *ys, *dxs)


def deliver_kernel(
    cuts, micros, slots, index_ref, sum_ref, y_ref, dx_ref, block_ref, _, out_ref, grad_ref, logits_ref,
    q_ref, k_ref, v_ref, wo_ref, wu_ref, wd_ref, bq_ref, bv_ref, bu_ref, *rest,
):
    plain_refs = rest[:PLAIN]
    y_buffer, dx_buffer, block_buffer, in_sem, out_sem = rest[PLAIN:]
    last = micros - 1
    reads = [block_ref.at[index_ref[last, i]] for i in range(slots)]
    writes = [logits_ref.at[last, i] for i in range(slots)]
    buffers = [block_buffer.at[i] for i in range(slots)]
    for source, target, buffer in ((y_ref, out_ref, y_buffer), (dx_ref, grad_ref, dx_buffer)):
        for m in range(micros):
            for i in range(slots):
                reads.append(source.at[m, index_ref[m, i]])
                writes.append(target.at[m, i])
                buffers.append(buffer.at[m, i])

    def take(n):
        return pltpu.make_async_copy(reads[n], buffers[n], in_sem.at[n])

    def give(n):
        return pltpu.make_async_copy(buffers[n], writes[n], out_sem.at[n])

    for n in range(len(reads)):
        take(n).start()
    width = q_ref.shape[1]
    for n, ref in enumerate((q_ref, k_ref, v_ref)):
        ref[...] = sum_ref[:, n * width : (n + 1) * width]
    wo_ref[...] = sum_ref[:, cuts[0] : cuts[1]].T
    wu_ref[...] = sum_ref[:, cuts[1] : cuts[2]]
    wd_ref[...] = sum_ref[:, cuts[2] : cuts[3]]
    block = sum_ref[:VECTOR_ROWS, cuts[3] :]
    for i, ref in enumerate(plain_refs):
        ref[...] = block[i : i + 1, : ref.shape[1]]
    for first, ref in ((QUERY_AT, bq_ref), (VALUE_AT, bv_ref), (UP_AT, bu_ref)):
        ref[...] = block[first : first + ref.shape[0], : ref.shape[1]]
    for n in range(len(reads)):
        take(n).wait()
        give(n).start()
    for n in range(len(reads)):
        give(n).wait()


def deliver(cuts, heads, unit, index, sums, y, dx, blocks, logits):
    micros, slots = dx.shape[:2]
    rows, width = sums.shape[0], heads * HEAD_DIM
    total = slots + 2 * micros * slots
    dma = pltpu.SemaphoreType.DMA
    in_vmem = pl.BlockSpec(memory_space=pltpu.VMEM)

    def f32(*shape):
        return jax.ShapeDtypeStruct(shape, F32)

    return pl.pallas_call(
        functools.partial(deliver_kernel, cuts, micros, slots),
        out_shape=(
            jax.ShapeDtypeStruct(y.shape, BF16),
            jax.ShapeDtypeStruct(dx.shape, BF16),
            jax.ShapeDtypeStruct(logits.shape, BF16),
            f32(rows, width),
            f32(rows, width),
            f32(rows, width),
            f32(width, rows),
            f32(rows, unit),
            f32(rows, unit),
            f32(heads, HEAD_DIM // slots),
            f32(heads, HEAD_DIM // slots),
            f32(heads, unit // heads // slots),
        )
        + (f32(1, rows),) * PLAIN,
        in_specs=[SMALL, in_vmem] + [ANYWHERE] * 4,
        out_specs=(ANYWHERE,) * 3 + (in_vmem,) * (9 + PLAIN),
        scratch_shapes=[
            pltpu.VMEM(y.shape, BF16),
            pltpu.VMEM(dx.shape, BF16),
            pltpu.VMEM(blocks.shape, BF16),
            dma((total,)),
            dma((total,)),
        ],
        input_output_aliases={5: 2},
        compiler_params=params(),
        cost_estimate=cost(0, 4 * y.size),
        name="deliver",
    )(index, sums, y, dx, blocks, logits)


def fits(mesh):
    return dict(mesh.shape) == {"seq": 8, "head": 4}


def on_device(
    tokens,
    prev_logits,
    lengths,
    dealing,
    w_query,
    b_query,
    w_key,
    w_value,
    b_value,
    w_out,
    b_out,
    gain_one,
    shift_one,
    w_up,
    b_up,
    w_down,
    b_down,
    gain_two,
    shift_two,
    cot_tokens,
    cot_logits,
):
    slots, groups = lax.axis_size("seq"), lax.axis_size("head")
    grid = ("seq", "head")
    here, head = lax.axis_index("seq"), lax.axis_index("head")
    micros, _, piece, model = tokens.shape
    heads = prev_logits.shape[3]
    extent = piece * slots
    width = heads * HEAD_DIM
    unit = w_up.shape[1]
    per = slots // groups
    cuts = (3 * width, 3 * width + width, 3 * width + width + unit, 3 * width + width + 2 * unit)
    own_rows = model // slots

    prev = jnp.transpose(prev_logits, (0, 1, 3, 2, 4))
    cot_square = jnp.transpose(cot_logits[:, 0], (0, 2, 1, 3))

    first_send, pieces, packed, info = prepare(
        lengths,
        dealing,
        prev,
        tokens,
        cot_tokens,
        (w_query, w_key, w_value, w_out, w_up, w_down.T),
        (b_query, b_value, b_up),
        [v.reshape(1, -1) for v in (b_out, gain_one, shift_one, b_down, gain_two, shift_two)],
        groups,
    )
    line, arrived_rows = gather_line(packed, pieces, slots, groups, 1)
    rows = per * piece
    rows_all = arrived_rows.reshape(2 * micros, rows, model)

    weights = gather_plane(line, 2)
    weights = weights.reshape(groups, slots, own_rows, -1)
    bias_qkv, bias_up, row_vectors = unpack_vectors(weights, heads, width, unit, model)
    weights = weights.reshape(groups, model, -1)

    projected = project(rows_all, weights, bias_qkv)
    first_qkv = across_heads(projected[0], 3)
    second_qkv = [across_heads(projected[m], 3) for m in range(1, micros)]
    got_prev, after = [], arrived_rows
    for m in range(micros):
        send = pick_blocks(prev, m, dealing) if m else first_send
        send, _ = lax.optimization_barrier((send, after))
        got = lax.all_to_all(send, "seq", split_axis=0, concat_axis=0, tiled=True)
        got_prev.append(got)
        after = (got, first_qkv, second_qkv)

    logits, grad_logits = None, None
    kept, sums_own, sums_rows, sums_up, returned, sent = [], [], [], [], [], []
    for m in range(micros):
        qkv = second_qkv[m - 1] if m else first_qkv
        logits, attend, context = attention_forward(info, qkv, got_prev[m], m, micros, logits)
        context_rows = across_heads(context, 4)
        y, dz, dcon, h1, act, b1, b2, b0, sums, dbup = row_work(
            cuts, m, context_rows, rows_all, weights, bias_up, row_vectors
        )
        dcontext = across_heads(dcon, 4)
        send, dqkv, own = attention_backward(
            info, qkv, attend, context, dcontext, cot_square, m
        )
        dqkv = across_heads(dqkv, 5)
        dx = input_grad(dqkv, weights, dz, per)
        kept.append((b0, h1, b2, dqkv, context_rows, b1, act))
        sums_own.append(own)
        sums_rows.append(sums)
        sums_up.append(dbup)
        returned.append((y, dx))
        if m == 0:
            send, _ = lax.optimization_barrier((send, dx))
            after = lax.all_to_all(send, "seq", split_axis=0, concat_axis=0, tiled=True)
            sent.append(after)
        else:
            sent.append(send)

    families = list(zip(*kept))
    part = weight_grads(cuts, heads, slots, rows_all, families[:3], families[3:], sums_own, sums_rows, sums_up)
    for m in range(micros):
        if m:
            send, _ = lax.optimization_barrier((sent[m], (sent[m - 1], part)))
            sent[m] = lax.all_to_all(send, "seq", split_axis=0, concat_axis=0, tiled=True)
        if m == 0:
            grad_logits = place_blocks(sent[m], m, micros, dealing, grad_logits)
    ys = [y.reshape(per, piece, model) for y, _ in returned]
    dxs = [dx for _, dx in returned]
    part = part.reshape(groups, slots, own_rows, -1)
    part, _ = lax.optimization_barrier((part, grad_logits))
    part, all_y, all_dx = finish(part, ys, dxs, slots, groups, 7)
    out_tokens, grad_tokens, grad_logits, dq, dk, dv, dwo, dwu, dwd, dbq, dbv, dbu, *plain = deliver(
        cuts, heads, unit, dealing, part, all_y, all_dx, sent[-1], grad_logits
    )
    plain = [row.reshape(-1) for row in plain]
    return (
        out_tokens,
        jnp.transpose(logits, (0, 2, 1, 3))[:, None],
        jnp.transpose(grad_tokens, (0, 1, 3, 2)),
        jnp.transpose(grad_logits, (0, 1, 3, 2, 4)),
        dq,
        dbq,
        dk,
        dv,
        dbv,
        dwo,
        *plain[:3],
        dwu,
        dbu,
        dwd.T,
        *plain[3:],
    )


def solution(mesh):
    placed = (
        P(None, None, "seq", None),
        P(None, None, "seq", "head", None),
        P(),
        P(),
        P("seq", "head"),
        P("head", "seq"),
        P("seq", "head"),
        P("seq", "head"),
        P("head", "seq"),
        P("head", "seq"),
        P("seq"),
        P("seq"),
        P("seq"),
        P("seq", "head"),
        P("head", "seq"),
        P("head", "seq"),
        P("seq"),
        P("seq"),
        P("seq"),
        P(None, None, "seq", None),
        P(None, "seq", None, "head", None),
    )
    return jax.shard_map(
        on_device if fits(mesh) else on_device_general,
        mesh=mesh,
        in_specs=placed,
        out_specs=(
            P(None, None, "seq", None),
            P(None, "seq", None, "head", None),
            P(None, None, "seq", "head"),
            P(None, None, "seq", "head", None),
            P("seq", "head"),
            P("head", "seq"),
            P("seq", "head"),
            P("seq", "head"),
            P("head", "seq"),
            P("head", "seq"),
            P("seq"),
            P("seq"),
            P("seq"),
            P("seq", "head"),
            P("head", "seq"),
            P("head", "seq"),
            P("seq"),
            P("seq"),
            P("seq"),
        ),
        check_vma=False,
    )
```
